32 devices in a mesh: dp: 16 (over z, x, core), tensor: 2 (over y).
Axes of the slice: x: 2, y: 2, z: 4, core: 2. Of those that a mesh axis runs over, the one named last changes fastest.
Arguments:
- inputs: float32 [32, 680, 1024], P('dp', 'tensor'), may hold values from -6 to 6
- labels: int32 [32], P('dp'), may hold values from 0 to 999
- scale_ids: int32 [32, 680], P('dp'), may hold values from 0 to 9, never falling along the last dimension, each value on 1 to 256 neighbouring positions
- cotangent: float32 [32, 680, 1024], P('dp', 'tensor'), may hold values from -6 to 6
- table: float32 [1000, 1024], P(None, 'dp'), may hold values from -6 to 6
- w_ada: float32 [1024, 6, 1024], P('dp'), may hold values from -0.1875 to 0.1875
- w_qkv: float32 [1024, 3, 1024], P('dp', None, 'tensor'), may hold values from -0.1875 to 0.1875
- head_scale: float32 [16], P('tensor'), may hold values from 6 to 12
- w_proj: float32 [1024, 1024], P('tensor', 'dp'), may hold values from -0.375 to 0.375
- w_fc1: float32 [1024, 4096], P('dp', 'tensor'), may hold values from -0.1875 to 0.1875
- w_fc2: float32 [4096, 1024], P('tensor', 'dp'), may hold values from -0.125 to 0.125
Outputs:
- output: float32 [32, 680, 1024], P('dp', 'tensor')
- d_inputs: float32 [32, 680, 1024], P('dp', 'tensor')
- d_table: float32 [1000, 1024], P(None, 'dp')
- d_ada: float32 [1024, 6, 1024], P('dp')
- d_qkv: float32 [1024, 3, 1024], P('dp', None, 'tensor')
- d_scale: float32 [16], P('tensor')
- d_proj: float32 [1024, 1024], P('tensor', 'dp')
- d_fc1: float32 [1024, 4096], P('dp', 'tensor')
- d_fc2: float32 [4096, 1024], P('tensor', 'dp')
The draws below stay inside these ranges and needn't reach their ends.
Inputs may be any that keep to these rules, and one draw needn't show every extreme that they name: `scale_ids`: each image's scale ids never fall along its tokens; every scale occurs, with 1 to 256 tokens, one scale with exactly 256; the scales' lengths vary from image to image, a generalization of VAR's fixed pyramid.
All inputs are finite; a program needn't handle non-finite values.
Results may differ from the reference program's by a relative error of at most 0.03.
Values may be sent and summed in bfloat16 or wider, within the bound.
No kernel may reach another device: no remote copies, remote signals or barrier semaphores. Data moves between devices by JAX's collectives and lax.ppermute only.
A program may use at most 256 MiB of HBM per device.

```python
import math
import jax
import jax.numpy as jnp
import numpy as np
from jax import lax

D = 1024
H = 16
HD = 64
FF = 4096
CLASSES = 1000
L = 680
SCALES = 10
SCALE_MOST = 256
IMAGES = 32
N_TENSOR = 2


def plant(values, own_key, low, high):
    longest = values.shape.index(max(values.shape))
    spots = []
    for shift in (0, 1):
        where = [jax.random.randint(jax.random.fold_in(own_key, axis), (), 0, length) for axis, length in enumerate(values.shape)]
        where[longest] = (where[longest] + shift) % values.shape[longest]
        spots.append(tuple(where))
    return values.at[spots[0]].set(low).at[spots[1]].set(high)


def level_of(key, dims, cuts, low, top_value):
    def one(axis_at, parts):
        heights = jax.random.uniform(jax.random.fold_in(jax.random.fold_in(key, 6), axis_at), (parts,), jnp.float32, low / len(cuts), top_value / len(cuts))
        return jnp.repeat(jnp.exp(heights), dims[axis_at] // parts).reshape((-1,) + (1,) * (len(dims) - axis_at - 1))

    gain = one(*cuts[0])
    for cut in cuts[1:]:
        gain = gain * one(*cut)
    return gain


def profile(number_of, total, limit, slope):
    portions = [(1 << 20) // math.isqrt(rank ** slope) + 1 for rank in range(2, number_of + 1)]
    surplus, holding = total - limit - (number_of - 1), [1] * (number_of - 1)
    while surplus > 0:
        candidates = [i for i in range(number_of - 1) if holding[i] < limit]
        pool, left = sum([portions[i] for i in candidates]), surplus
        for i in candidates:
            more = min(limit - holding[i], max(1, left * portions[i] // pool), surplus)
            holding[i] = holding[i] + more
            surplus = surplus - more
    return np.array([limit] + holding)


def uneven(rng, amount, total, bound, lean):
    if amount == 2:
        one = jax.random.randint(rng, (), max(1, total - bound), min(bound, total - 1) + 1)
        return jnp.stack([one, total - one])
    sizes = jnp.asarray(profile(amount, total, bound, lean), jnp.int32)
    couples = (amount - 1) // 2
    donor, receiver = sizes[1:1 + 2 * couples:2], sizes[2:2 + 2 * couples:2]
    margin = jnp.minimum(donor - 1, bound - receiver)
    moved = jax.random.randint(jax.random.fold_in(rng, 1), (couples,), 0, 1 << 20) % (margin + 1)
    sizes = sizes.at[1:1 + 2 * couples:2].set(donor - moved).at[2:2 + 2 * couples:2].set(receiver + moved)
    return sizes[jax.random.permutation(jax.random.fold_in(rng, 2), amount)]


def noise(stream_key, dims, scale, most, cuts=(), dtype=jnp.bfloat16):
    entries = jax.random.normal(stream_key, dims, jnp.float32) * scale
    if len(cuts) > 0:
        entries = level_of(stream_key, dims, cuts, -0.22, 0.18) * entries
    return jnp.clip(entries, min=-most, max=most).astype(dtype)


def setup_inputs(seed: int = 0) -> dict:
    arg_keys = jax.random.split(jax.random.key(seed), 12)
    inputs = noise(arg_keys[0], (IMAGES, L, D), 1.0, 6.0, ((0, 16), (1, 2)), jnp.float32)
    labels = plant(jax.random.randint(arg_keys[1], (IMAGES,), 0, CLASSES), jax.random.fold_in(arg_keys[1], 1), 0, CLASSES - 1).astype(jnp.int32)
    scale_ids = jax.vmap(lambda own: jnp.searchsorted(jnp.cumsum(uneven(own, SCALES, L, SCALE_MOST, 0)), jnp.arange(L), side="right"))(jax.random.split(arg_keys[2], IMAGES)).reshape((IMAGES, L)).astype(jnp.int32)
    cotangent = noise(arg_keys[3], (IMAGES, L, D), 1.0, 6.0, ((0, 16), (1, 2)), jnp.float32)
    table = noise(arg_keys[4], (CLASSES, D), 1.0, 6.0, ((1, 16),), jnp.float32)
    w_ada = noise(arg_keys[5], (D, 6, D), D ** -0.5, 0.1875, ((0, 16),), jnp.float32)
    w_qkv = noise(arg_keys[6], (D, 3, D), D ** -0.5, 0.1875, ((0, 16), (2, 2)), jnp.float32)
    head_scale = jnp.clip(jnp.exp(math.log(12.0) - 0.6931472 * jax.random.uniform(arg_keys[7], (H,), jnp.float32) ** level_of(arg_keys[7], (H,), ((0, 2),), -0.2, 0.2)), 6.0, 12.0)
    w_proj = noise(arg_keys[8], (D, D), (D // 4) ** -0.5, 0.375, ((0, 2), (1, 16)), jnp.float32)
    w_fc1 = noise(arg_keys[9], (D, FF), D ** -0.5, 0.1875, ((0, 16), (1, 2)), jnp.float32)
    w_fc2 = noise(arg_keys[10], (FF, D), (FF // 2) ** -0.5, 0.125, ((0, 2), (1, 16)), jnp.float32)
    return {"inputs": inputs, "labels": labels, "scale_ids": scale_ids, "cotangent": cotangent, "table": table, "w_ada": w_ada, "w_qkv": w_qkv, "head_scale": head_scale, "w_proj": w_proj, "w_fc1": w_fc1, "w_fc2": w_fc2}


@jax.custom_vjp
def low(v):
    return lax.optimization_barrier(v.astype(jnp.bfloat16)).astype(jnp.float32)

@jax.custom_vjp
def low_back(v):
    return v

def low_keep(v):
    return (low(v), None)

def low_pass(kept, grad):
    return (grad,)

def back_keep(v):
    return (v, None)

def back_low(kept, grad):
    return (low(grad),)
low.defvjp(low_keep, low_pass)
low_back.defvjp(back_keep, back_low)
EPSILON = 1e-06
HIGHEST = lax.Precision.HIGHEST

def layer_norm(values):
    average = lax.optimization_barrier(jnp.mean(values, axis=-1, keepdims=True))
    centred = values - average
    return centred * lax.rsqrt(lax.optimization_barrier(jnp.mean(centred * centred, axis=-1, keepdims=True)) + EPSILON)

def unit_rows(values):
    return values * lax.rsqrt(lax.optimization_barrier(jnp.sum(values * values, axis=-1, keepdims=True)) + EPSILON)

def attend_image(pieces):
    queries, keys_in, values_in, scale_row = pieces
    scores = low_back(jnp.einsum('qhd,khd->hqk', queries, keys_in, precision=HIGHEST))
    visible = scale_row[None, :] <= scale_row[:, None]
    scores = jnp.where(visible[None], scores, -1e+30)
    largest = lax.optimization_barrier(jnp.max(scores, axis=-1, keepdims=True))
    exponent = jnp.exp(scores - largest)
    attn_probs = exponent / lax.optimization_barrier(jnp.sum(exponent, axis=-1, keepdims=True))
    mixed = jnp.einsum('hqk,khd->qhd', low(attn_probs), values_in, precision=HIGHEST)
    return low(low_back(mixed))

def reference(inputs, labels, scale_ids, cotangent, table, w_ada, w_qkv, head_scale, w_proj, w_fc1, w_fc2):
    per_step = math.gcd(IMAGES, 4)
    step_count = IMAGES // per_step
    groups = N_TENSOR

    def forward(inputs, table, w_ada, w_qkv, head_scale, w_proj, w_fc1, w_fc2):
        table_low = low(table)
        ada_low = low(w_ada).reshape(D, 6 * D)
        qkv_groups = low(w_qkv).reshape(D, 3, groups, D // groups)
        proj_groups = low(w_proj).reshape(groups, D // groups, D)
        fc1_groups = low(w_fc1).reshape(D, groups, FF // groups)
        fc2_groups = low(w_fc2).reshape(groups, FF // groups, D)
        condition = table_low[labels]
        silu_low = low(jax.nn.silu(condition))
        modulation = jnp.dot(silu_low, ada_low, precision=HIGHEST).reshape(IMAGES, 6, D)

        def group_step(running, pieces):
            tokens, mod_rows, scale_rows = pieces
            gain_attn = mod_rows[:, 0, None, :]
            gain_mlp = mod_rows[:, 1, None, :]
            scale_attn = mod_rows[:, 2, None, :]
            scale_mlp = mod_rows[:, 3, None, :]
            shift_attn = mod_rows[:, 4, None, :]
            shift_mlp = mod_rows[:, 5, None, :]
            hidden_one = low(layer_norm(tokens) * (1.0 + scale_attn) + shift_attn)
            copies_one = low_back(jnp.broadcast_to(hidden_one[:, None], (per_step, groups, L, D)))
            projected = low_back(jnp.einsum('bgld,dtgc->bltgc', copies_one, qkv_groups, precision=HIGHEST))
            projected = projected.reshape(per_step, L, 3, H, HD)
            q_hat = low(unit_rows(projected[:, :, 0]) * head_scale[:, None])
            k_hat = low(unit_rows(projected[:, :, 1]))
            v_hat = low(projected[:, :, 2])
            mixed = lax.map(attend_image, (q_hat, k_hat, v_hat, scale_rows))
            mixed_groups = mixed.reshape(per_step, L, groups, D // groups)
            attn_terms = low(jnp.einsum('blgc,gcd->bgld', mixed_groups, proj_groups, precision=HIGHEST))
            attended = low_back(lax.optimization_barrier(jnp.sum(attn_terms, axis=1)))
            middle = tokens + gain_attn * attended
            hidden_two = low(layer_norm(middle) * (1.0 + scale_mlp) + shift_mlp)
            copies_two = low_back(jnp.broadcast_to(hidden_two[:, None], (per_step, groups, L, D)))
            before = low_back(jnp.einsum('bgld,dgf->blgf', copies_two, fc1_groups, precision=HIGHEST))
            active = low(jax.nn.gelu(before, approximate=True))
            branch_terms = low(jnp.einsum('blgf,gfd->bgld', active, fc2_groups, precision=HIGHEST))
            branch = low_back(lax.optimization_barrier(jnp.sum(branch_terms, axis=1)))
            return (running, middle + gain_mlp * branch)
        _, results = lax.scan(jax.checkpoint(group_step), jnp.zeros((), jnp.float32), (inputs.reshape(step_count, per_step, L, D), modulation.reshape(step_count, per_step, 6, D), scale_ids.reshape(step_count, per_step, L)))
        return results.reshape(IMAGES, L, D)
    output, pull_back = jax.vjp(forward, inputs, table, w_ada, w_qkv, head_scale, w_proj, w_fc1, w_fc2)
    grads = pull_back(cotangent)
    return (output, grads[0], grads[1], grads[2], grads[3], grads[4], grads[5], grads[6], grads[7])
```

```python
import functools

import jax
import jax.numpy as jnp
from jax import lax
from jax.experimental import pallas as pl
from jax.experimental.pallas import tpu as pltpu
from jax.sharding import PartitionSpec as P

EPSILON = 1e-06
HIGHEST = lax.Precision.HIGHEST


def layer_norm(values):
    average = jnp.mean(values, axis=-1, keepdims=True)
    centred = values - average
    inverse = lax.rsqrt(jnp.mean(centred * centred, axis=-1, keepdims=True) + EPSILON)
    return (centred * inverse, inverse)


def norm_back(d_normed, normed, inverse):
    return inverse * (
        d_normed
        - jnp.mean(d_normed, axis=-1, keepdims=True)
        - normed * jnp.mean(d_normed * normed, axis=-1, keepdims=True)
    )


def unit_rows(values):
    inverse = lax.rsqrt(jnp.sum(values * values, axis=-1, keepdims=True) + EPSILON)
    return (values * inverse, inverse)


def unit_back(d_unit, unit, inverse):
    return inverse * (d_unit - unit * jnp.sum(d_unit * unit, axis=-1, keepdims=True))


def spread(values):
    return lax.all_gather(values, "tensor", axis=1, tiled=True)


def collect(terms):
    return lax.psum_scatter(
        terms.astype(jnp.bfloat16), "tensor", scatter_dimension=1, tiled=True
    ).astype(jnp.float32)


def masked_scores(queries, keys_in, scale_row):
    scores = jnp.einsum("qhd,khd->hqk", queries, keys_in, preferred_element_type=jnp.float32)
    visible = scale_row[None, :] <= scale_row[:, None]
    return jnp.where(visible[None], scores, -1e30)


def attend_forward(pieces):
    queries, keys_in, values_in, scale_row = pieces
    scores = masked_scores(queries, keys_in, scale_row)
    largest = jnp.max(scores, axis=-1, keepdims=True)
    exponent = jnp.exp(scores - largest)
    denominator = jnp.sum(exponent, axis=-1, keepdims=True)
    attn_probs = (exponent / denominator).astype(jnp.bfloat16)
    mixed = jnp.einsum("hqk,khd->qhd", attn_probs, values_in, preferred_element_type=jnp.float32)
    return (mixed.astype(jnp.bfloat16), (largest + jnp.log(denominator))[..., 0])


def attend_backward(pieces):
    queries, keys_in, values_in, scale_row, log_total, d_mixed = pieces
    scores = masked_scores(queries, keys_in, scale_row)
    attn_probs = jnp.exp(scores - log_total[..., None])
    d_probs = jnp.einsum("qhd,khd->hqk", d_mixed, values_in, preferred_element_type=jnp.float32)
    offset = jnp.sum(attn_probs * d_probs, axis=-1, keepdims=True)
    d_scores = (attn_probs * (d_probs - offset)).astype(jnp.bfloat16)
    d_queries = jnp.einsum("hqk,khd->qhd", d_scores, keys_in, preferred_element_type=jnp.float32)
    d_keys = jnp.einsum("hqk,qhd->khd", d_scores, queries, preferred_element_type=jnp.float32)
    d_values = jnp.einsum(
        "hqk,qhd->khd", attn_probs.astype(jnp.bfloat16), d_mixed, preferred_element_type=jnp.float32
    )
    return (d_queries, d_keys, d_values)


def on_device_general(
    inputs, labels, scale_ids, cotangent, table, w_ada, w_qkv, head_scale, w_proj, w_fc1, w_fc2
):
    images, local_len, model_width = inputs.shape
    full_len = scale_ids.shape[1]
    local_heads = head_scale.shape[0]
    head_dim = w_qkv.shape[2] // local_heads
    classes = table.shape[0]
    gathered = (
        lax.all_gather(table.astype(jnp.bfloat16), "dp", axis=1, tiled=True),
        lax.all_gather(w_qkv.astype(jnp.bfloat16), "dp", axis=0, tiled=True),
        lax.all_gather(w_proj.astype(jnp.bfloat16), "dp", axis=1, tiled=True),
        lax.all_gather(w_fc1.astype(jnp.bfloat16), "dp", axis=0, tiled=True),
        lax.all_gather(w_fc2.astype(jnp.bfloat16), "dp", axis=1, tiled=True),
    )
    table_low, qkv_low, proj_low, fc1_low, fc2_low = gathered
    qkv_flat = qkv_low.reshape(model_width, -1)
    one_hot = labels[:, None] == jnp.arange(classes)[None, :]
    condition = jnp.dot(one_hot.astype(jnp.bfloat16), table_low, preferred_element_type=jnp.float32)
    silu_low = jax.nn.silu(condition).astype(jnp.bfloat16)
    ada_full = lax.all_gather(w_ada.astype(jnp.bfloat16), "dp", axis=0, tiled=True).reshape(
        model_width, 6 * model_width
    )
    modulation = jnp.dot(silu_low, ada_full, preferred_element_type=jnp.float32)
    modulation = modulation.reshape(images, 6, model_width)
    gain_attn = modulation[:, 0, None, :]
    gain_mlp = modulation[:, 1, None, :]
    scale_attn = modulation[:, 2, None, :]
    scale_mlp = modulation[:, 3, None, :]
    shift_attn = modulation[:, 4, None, :]
    shift_mlp = modulation[:, 5, None, :]
    normed_one, inverse_one = layer_norm(inputs)
    hidden_one = spread((normed_one * (1.0 + scale_attn) + shift_attn).astype(jnp.bfloat16))
    projected = jnp.einsum("bld,dc->blc", hidden_one, qkv_flat, preferred_element_type=jnp.float32)
    projected = projected.reshape(images, full_len, 3, local_heads, head_dim)
    q_unit, q_inverse = unit_rows(projected[:, :, 0])
    k_unit, k_inverse = unit_rows(projected[:, :, 1])
    q_hat = (q_unit * head_scale[:, None]).astype(jnp.bfloat16)
    k_hat = k_unit.astype(jnp.bfloat16)
    v_hat = projected[:, :, 2].astype(jnp.bfloat16)
    mixed, log_total = lax.map(attend_forward, (q_hat, k_hat, v_hat, scale_ids))
    mixed_flat = mixed.reshape(images, full_len, local_heads * head_dim)
    attended = collect(
        jnp.einsum("blc,cd->bld", mixed_flat, proj_low, preferred_element_type=jnp.float32)
    )
    middle = inputs + gain_attn * attended
    normed_two, inverse_two = layer_norm(middle)
    hidden_two = spread((normed_two * (1.0 + scale_mlp) + shift_mlp).astype(jnp.bfloat16))
    before = jnp.einsum("bld,df->blf", hidden_two, fc1_low, preferred_element_type=jnp.float32)
    gelu_fn = functools.partial(jax.nn.gelu, approximate=True)
    active_f, gelu_pull = jax.vjp(gelu_fn, before)
    active = active_f.astype(jnp.bfloat16)
    branch = collect(jnp.einsum("blf,fd->bld", active, fc2_low, preferred_element_type=jnp.float32))
    output = middle + gain_mlp * branch
    again = (
        lax.all_gather(w_qkv.astype(jnp.bfloat16), "dp", axis=0, tiled=True),
        lax.all_gather(w_proj.astype(jnp.bfloat16), "dp", axis=1, tiled=True),
        lax.all_gather(w_fc1.astype(jnp.bfloat16), "dp", axis=0, tiled=True),
        lax.all_gather(w_fc2.astype(jnp.bfloat16), "dp", axis=1, tiled=True),
    )
    qkv_back, proj_back, fc1_back, fc2_back = again
    d_gain_mlp = jnp.sum(cotangent * branch, axis=1)
    d_branch = spread((gain_mlp * cotangent).astype(jnp.bfloat16))
    grad_fc2 = jnp.einsum("blf,bld->fd", active, d_branch, preferred_element_type=jnp.float32)
    d_active = jnp.einsum("bld,fd->blf", d_branch, fc2_back, preferred_element_type=jnp.float32)
    d_before = gelu_pull(d_active)[0].astype(jnp.bfloat16)
    grad_fc1 = jnp.einsum("bld,blf->df", hidden_two, d_before, preferred_element_type=jnp.float32)
    d_hidden_two = collect(
        jnp.einsum("blf,df->bld", d_before, fc1_back, preferred_element_type=jnp.float32)
    )
    d_scale_mlp = jnp.sum(d_hidden_two * normed_two, axis=1)
    d_shift_mlp = jnp.sum(d_hidden_two, axis=1)
    d_middle = cotangent + norm_back(d_hidden_two * (1.0 + scale_mlp), normed_two, inverse_two)
    d_gain_attn = jnp.sum(d_middle * attended, axis=1)
    d_attended = spread((gain_attn * d_middle).astype(jnp.bfloat16))
    grad_proj = jnp.einsum(
        "blc,bld->cd", mixed_flat, d_attended, preferred_element_type=jnp.float32
    )
    d_mixed = jnp.einsum("bld,cd->blc", d_attended, proj_back, preferred_element_type=jnp.float32)
    d_mixed = d_mixed.astype(jnp.bfloat16).reshape(images, full_len, local_heads, head_dim)
    d_q_hat, d_k_hat, d_v_hat = lax.map(
        attend_backward, (q_hat, k_hat, v_hat, scale_ids, log_total, d_mixed)
    )
    scale_terms = jnp.sum(d_q_hat * q_unit, axis=(0, 1, 3))
    d_query = unit_back(d_q_hat * head_scale[:, None], q_unit, q_inverse)
    d_key = unit_back(d_k_hat, k_unit, k_inverse)
    d_raw = jnp.stack([d_query, d_key, d_v_hat], axis=2).astype(jnp.bfloat16)
    d_raw = d_raw.reshape(images, full_len, 3 * local_heads * head_dim)
    grad_qkv = jnp.einsum("bld,blc->dc", hidden_one, d_raw, preferred_element_type=jnp.float32)
    grad_qkv = grad_qkv.reshape(model_width, 3, local_heads * head_dim)
    d_hidden_one = collect(
        jnp.einsum(
            "blc,dc->bld",
            d_raw,
            qkv_back.reshape(model_width, -1),
            preferred_element_type=jnp.float32,
        )
    )
    d_scale_attn = jnp.sum(d_hidden_one * normed_one, axis=1)
    d_shift_attn = jnp.sum(d_hidden_one, axis=1)
    d_inputs = d_middle + norm_back(d_hidden_one * (1.0 + scale_attn), normed_one, inverse_one)
    mod_terms_back = jnp.stack(
        [d_gain_attn, d_gain_mlp, d_scale_attn, d_scale_mlp, d_shift_attn, d_shift_mlp], axis=1
    )
    d_modulation = lax.psum(mod_terms_back.astype(jnp.bfloat16), "tensor").astype(jnp.float32)
    d_mod_flat = d_modulation.reshape(images, 6 * model_width)
    grad_scale = lax.psum(scale_terms, "dp")
    ada_terms = jnp.dot(silu_low.astype(jnp.float32).T, d_mod_flat, precision=HIGHEST)
    grad_ada = lax.psum_scatter(
        ada_terms.reshape(model_width, 6, model_width).astype(jnp.bfloat16),
        "dp",
        scatter_dimension=0,
        tiled=True,
    ).astype(jnp.float32)
    d_silu = jnp.dot(d_mod_flat, ada_full.astype(jnp.float32).T, precision=HIGHEST)
    _, silu_pull = jax.vjp(jax.nn.silu, condition)
    d_condition = silu_pull(d_silu)[0]
    table_terms = jnp.dot(one_hot.astype(jnp.float32).T, d_condition, precision=HIGHEST)
    summed = (
        lax.psum_scatter(
            table_terms.astype(jnp.bfloat16), "dp", scatter_dimension=1, tiled=True
        ).astype(jnp.float32),
        lax.psum_scatter(
            grad_qkv.astype(jnp.bfloat16), "dp", scatter_dimension=0, tiled=True
        ).astype(jnp.float32),
        lax.psum_scatter(
            grad_proj.astype(jnp.bfloat16), "dp", scatter_dimension=1, tiled=True
        ).astype(jnp.float32),
        lax.psum_scatter(
            grad_fc1.astype(jnp.bfloat16), "dp", scatter_dimension=0, tiled=True
        ).astype(jnp.float32),
        lax.psum_scatter(
            grad_fc2.astype(jnp.bfloat16), "dp", scatter_dimension=1, tiled=True
        ).astype(jnp.float32),
    )
    grad_table, grad_qkv_own, grad_proj_own, grad_fc1_own, grad_fc2_own = summed
    return (
        output,
        d_inputs,
        grad_table,
        grad_ada,
        grad_qkv_own,
        grad_scale,
        grad_proj_own,
        grad_fc1_own,
        grad_fc2_own,
    )


BF16 = jnp.bfloat16
F32 = jnp.float32
ZS, XS, CS, TS = 4, 2, 2, 2
BOTH = ("dp", "tensor")
NN = (((1,), (0,)), ((), ()))
NT = (((1,), (1,)), ((), ()))
TN = (((0,), (0,)), ((), ()))
HIDDEN = -1e30
VMEM_LIMIT = 60 * 1024 * 1024


def perm_of(step):
    pairs = []
    for z in range(ZS):
        for x in range(XS):
            for c in range(CS):
                for t in range(TS):
                    nz, nx, nc, nt = step(z, x, c, t)
                    source = ((z * XS + x) * CS + c) * TS + t
                    target = ((nz * XS + nx) * CS + nc) * TS + nt
                    pairs.append((source, target))
    return pairs


def send(values, step):
    return lax.ppermute(values, BOTH, perm_of(step))


def to_core(z, x, c, t):
    return (z, x, 1 - c, t)


def to_x(z, x, c, t):
    return (z, 1 - x, c, t)


def to_t(z, x, c, t):
    return (z, x, c, 1 - t)


def to_z(k):
    return lambda z, x, c, t: ((z + k) % ZS, x, c, t)


def to_near(z, x, c, t):
    return (z, 1 - x, c, t) if c == 0 else (z, x, c, 1 - t)


def to_far(z, x, c, t):
    return (z, x, c, 1 - t) if c == 0 else (z, 1 - x, c, t)


def pick(values, index, axis=0):
    return lax.dynamic_index_in_dim(values, index, axis, keepdims=False)


def place():
    dp = lax.axis_index("dp")
    t = lax.axis_index("tensor")
    return dp // (XS * CS), (dp // CS) % XS, dp % CS, t


def matmul(left, right, dims):
    return lax.dot_general(left, right, dims, preferred_element_type=F32)


def gather_near_first(rows):
    rows = jnp.concatenate([rows, send(rows, to_core)])
    rows = jnp.concatenate([rows, send(rows, to_x)])
    return jnp.concatenate([rows] + [send(rows, to_z(k)) for k in range(1, ZS)])


def reduce_near_first(terms):
    terms = terms[:, :, 0] + send(terms[:, :, 1], to_core)
    terms = terms[:, 0] + send(terms[:, 1], to_x)
    total = terms[0]
    for k in range(1, ZS):
        total = total + send(terms[ZS - k], to_z(k))
    return total


def gather_pieces(keep, give):
    two = jnp.stack([keep, send(give, to_core)])
    four = jnp.stack([two] + [send(two, to_z(k)) for k in range(1, ZS)])
    near = send(four, to_near)
    mine = [four, near, send(four, to_far), send(near, to_far)]
    return mine + [send(piece, to_core) for piece in mine]


def assemble_kernel(parts, where_ref, *refs):
    pieces, outs, sem = refs[:8], refs[8:-1], refs[-1]
    z, x, c, t = where_ref[0], where_ref[1], where_ref[2], where_ref[3]
    for number, piece in enumerate(pieces):
        owner = c if number < 4 else 1 - c
        slot = number % 4
        if slot == 0:
            dx, dt = 0, 0
        elif slot == 1:
            dx, dt = 1 - owner, owner
        elif slot == 2:
            dx, dt = owner, 1 - owner
        else:
            dx, dt = 1, 1
        sx, st = x ^ dx, t ^ dt
        for dz in range(ZS):
            for dc in range(CS):
                sz = (z + ZS - dz) % ZS
                sc = owner ^ dc
                row = pl.multiple_of(((sz * XS + sx) * CS + sc) * 64, 64)
                for which, base, stride_t, stride_h, start, width in parts:
                    column = pl.multiple_of(base + st * stride_t + owner * stride_h, 128)
                    pltpu.make_async_copy(
                        piece.at[dz, dc, :, pl.ds(start, width)],
                        outs[which].at[pl.ds(row, 64), pl.ds(column, width)],
                        sem.at[which],
                    ).start()
    for which, out in enumerate(outs):
        pltpu.make_async_copy(out, out, sem.at[which]).wait()


def assemble(pieces, position, parts, widths):
    rows = ZS * XS * CS * 64
    outs = [jax.ShapeDtypeStruct((rows, width), BF16) for width in widths]
    return pl.pallas_call(
        functools.partial(assemble_kernel, parts),
        out_shape=outs,
        in_specs=[pl.BlockSpec(memory_space=pltpu.SMEM)]
        + [pl.BlockSpec(memory_space=pl.ANY)] * 8,
        out_specs=[pl.BlockSpec(memory_space=pltpu.VMEM)] * len(outs),
        scratch_shapes=[pltpu.SemaphoreType.DMA((len(outs),))],
        compiler_params=pltpu.CompilerParams(vmem_limit_bytes=VMEM_LIMIT),
    )(position, *pieces)


def product_kernel(*refs):
    left = jnp.concatenate([ref[...] for ref in refs[1 : 1 + ZS]], axis=1)
    right = refs[1 + ZS][...]
    out = refs[-1]
    total = matmul(left, right.reshape(right.shape[-2:]), TN)
    if len(refs) == ZS + 4:
        total = total + refs[2 + ZS][...].astype(F32)
    out[...] = total.astype(out.dtype)


def product(rows, columns, quarter, choice, added=None):
    tokens = rows.shape[0]
    span = CS * 64
    if columns.ndim == 3:
        parts = columns.shape[0]
        right = pl.BlockSpec((1, tokens, quarter), lambda p, s: (p, 0, s[1]))
    else:
        parts = 1
        right = pl.BlockSpec((tokens, quarter), lambda p, s: (0, s[1]))
    lefts = [
        pl.BlockSpec((tokens, span), functools.partial(lambda n, p, s: (0, n * XS + s[0]), n))
        for n in range(ZS)
    ]
    block = pl.BlockSpec((ZS * span, quarter), lambda p, s: (0, p))
    extra = [] if added is None else [added]
    return pl.pallas_call(
        product_kernel,
        out_shape=jax.ShapeDtypeStruct((ZS * span, parts * quarter), BF16),
        grid_spec=pltpu.PrefetchScalarGridSpec(
            num_scalar_prefetch=1,
            grid=(parts,),
            in_specs=lefts + [right] + [block] * len(extra),
            out_specs=block,
        ),
        cost_estimate=pl.CostEstimate(
            flops=2 * tokens * ZS * span * parts * quarter,
            bytes_accessed=2 * (tokens + ZS * span) * (ZS * span + parts * quarter),
            transcendentals=0,
        ),
        compiler_params=pltpu.CompilerParams(vmem_limit_bytes=VMEM_LIMIT),
    )(choice, *([rows] * ZS), columns, *extra)


def scatter_sum(rows, columns, quarter, z, x, c, t):
    def block(dx, dt, dh, added=None):
        choice = jnp.stack([x ^ dx, (t ^ dt) * 2 + (c ^ dh)]).astype(jnp.int32)
        return product(rows, columns, quarter, choice, added)

    def on_chip(dx, dt, other_dx, other_dt):
        return block(dx, dt, 0, send(block(other_dx, other_dt, 1), to_core))

    flag = 1 - c
    far_both = send(on_chip(1, 1, 1, 1), to_far)
    far_one = send(on_chip(c, flag, flag, c), to_far)
    near = on_chip(flag, c, c, flag).astype(F32) + far_both.astype(F32)
    near = send(near.astype(BF16), to_near)
    whole = on_chip(0, 0, 0, 0).astype(F32) + far_one.astype(F32) + near.astype(F32)
    whole = whole.astype(BF16).reshape(ZS, CS, 64, whole.shape[-1])
    total = pick(whole, z).astype(F32)
    for k in range(1, ZS):
        total = total + send(pick(whole, (z + k) % ZS), to_z(k)).astype(F32)
    return pick(total, c), send(pick(total, 1 - c).astype(BF16), to_core).astype(F32)


def in_order(own, other, bit):
    return jnp.where(bit == 0, own, other), jnp.where(bit == 0, other, own)


def whole_image(values, t):
    own = pick(values, t)
    other = send(pick(values, 1 - t).astype(BF16), to_t).astype(F32)
    return jnp.concatenate(in_order(own, other, t), axis=0)


def split_image(values, t):
    half = values.shape[0] // 2
    own = lax.dynamic_slice_in_dim(values, t * half, half, axis=0)
    give = lax.dynamic_slice_in_dim(values, (1 - t) * half, half, axis=0)
    other = send(give.astype(BF16), to_t).astype(F32)
    return jnp.stack(in_order(own, other, t))


def unit_of(values, mask):
    squares = jnp.where(mask, values * values, 0.0)
    inverse = lax.rsqrt(jnp.sum(squares, axis=-1, keepdims=True) + EPSILON)
    return jnp.where(mask, values * inverse, 0.0), inverse


def head_masks(shape, head_dim):
    lane = lax.broadcasted_iota(jnp.int32, shape, 1)
    return [(lane >= n * head_dim) & (lane < (n + 1) * head_dim) for n in range(2)]


def attend_kernel(head_dim, scale_ref, row_ref, column_ref, q_ref, k_ref, v_ref, out_ref, bias_ref):
    pair = pl.program_id(0)

    @pl.when(pair == 0)
    def _():
        bias_ref[...] = jnp.where(row_ref[...] <= column_ref[...], 0.0, HIDDEN)

    q, k = q_ref[...].astype(F32), k_ref[...].astype(F32)
    v = v_ref[...]
    values = jnp.concatenate([v, jnp.ones_like(v)], axis=1)
    masks = head_masks(q.shape, head_dim)
    k_hat = (unit_of(k, masks[0])[0] + unit_of(k, masks[1])[0]).astype(BF16)
    result = None
    for n in range(2):
        scale = scale_ref[2 * pair + n]
        q_hat = (unit_of(q, masks[n])[0] * scale).astype(BF16)
        scores = matmul(q_hat, k_hat, NT) + (bias_ref[...] - jnp.abs(scale))
        weights = jnp.exp(scores).astype(BF16)
        mixed = matmul(weights, values, NN)
        mixed = mixed[:, : 2 * head_dim] / mixed[:, 2 * head_dim :]
        result = mixed if result is None else jnp.where(masks[n], mixed, result)
    out_ref[...] = result.astype(out_ref.dtype)


def attend_whole(raw, scale_row, all_scale):
    tokens, width = raw.shape[0], raw.shape[1] // 3
    head_dim = width // all_scale.shape[0]
    lanes = 2 * head_dim
    pairs = width // lanes

    def block(part):
        return pl.BlockSpec((tokens, lanes), lambda n: (0, part * pairs + n))

    return pl.pallas_call(
        functools.partial(attend_kernel, head_dim),
        out_shape=jax.ShapeDtypeStruct((tokens, width), BF16),
        grid=(pairs,),
        in_specs=[
            pl.BlockSpec(memory_space=pltpu.SMEM),
            pl.BlockSpec((1, tokens), lambda n: (0, 0)),
            pl.BlockSpec((tokens, 1), lambda n: (0, 0)),
            block(0),
            block(1),
            block(2),
        ],
        out_specs=pl.BlockSpec((tokens, lanes), lambda n: (0, n)),
        scratch_shapes=[pltpu.VMEM((tokens, tokens), F32)],
        cost_estimate=pl.CostEstimate(
            flops=4 * tokens * tokens * width,
            bytes_accessed=8 * tokens * width,
            transcendentals=tokens * tokens * all_scale.shape[0],
        ),
        compiler_params=pltpu.CompilerParams(vmem_limit_bytes=VMEM_LIMIT),
    )(all_scale, scale_row[None, :], scale_row[:, None], raw, raw, raw)


def attend_back_kernel(
    head_dim,
    scale_ref,
    row_ref,
    column_ref,
    q_ref,
    k_ref,
    v_ref,
    mixed_ref,
    d_mixed_ref,
    out_ref,
    term_ref,
    bias_ref,
):
    pair = pl.program_id(0)

    @pl.when(pair == 0)
    def _():
        bias_ref[...] = jnp.where(column_ref[...] <= row_ref[...], 0.0, HIDDEN)

    q, k = q_ref[...].astype(F32), k_ref[...].astype(F32)
    v, d_mixed = v_ref[...], d_mixed_ref[...]
    masks = head_masks(q.shape, head_dim)
    k_units = [unit_of(k, mask) for mask in masks]
    k_hat = (k_units[0][0] + k_units[1][0]).astype(BF16)
    products = d_mixed.astype(F32) * mixed_ref[...].astype(F32)
    d_q_all = d_k_all = d_v_all = None
    for n in range(2):
        mask = masks[n]
        scale = scale_ref[2 * pair + n]
        q_unit, q_inverse = unit_of(q, mask)
        q_hat = (q_unit * scale).astype(BF16)
        d_out = jnp.where(mask, d_mixed, jnp.zeros_like(d_mixed))
        offset = jnp.sum(jnp.where(mask, products, 0.0), axis=-1, keepdims=True)
        offset = jnp.transpose(jnp.broadcast_to(offset, products.shape))[:1]
        scores = matmul(k_hat, q_hat, NT) + (bias_ref[...] - jnp.abs(scale))
        weights = jnp.exp(scores)
        weights = weights * (1.0 / jnp.sum(weights, axis=0, keepdims=True))
        d_weights = matmul(v, d_out, NT)
        d_scores = (weights * (d_weights - offset)).astype(BF16)
        d_v = matmul(weights.astype(BF16), d_out, NN)
        d_k = matmul(d_scores, q_hat, NN)
        d_q = jnp.where(mask, matmul(d_scores, k_hat, TN), 0.0)
        d_k = jnp.where(mask, d_k, 0.0)
        k_unit, k_inverse = k_units[n]
        term = d_q * q_unit
        term_n = jnp.sum(term, axis=0, keepdims=True)
        d_q = q_inverse * scale * (d_q - q_unit * jnp.sum(term, axis=-1, keepdims=True))
        d_k = k_inverse * (d_k - k_unit * jnp.sum(d_k * k_unit, axis=-1, keepdims=True))
        if n == 0:
            d_q_all, d_k_all, d_v_all, term_all = d_q, d_k, d_v, term_n
        else:
            d_q_all, d_k_all = d_q_all + d_q, d_k_all + d_k
            d_v_all, term_all = d_v_all + d_v, term_all + term_n
    out_ref[0] = d_q_all.astype(out_ref.dtype)
    out_ref[1] = d_k_all.astype(out_ref.dtype)
    out_ref[2] = d_v_all.astype(out_ref.dtype)
    term_ref[...] = jnp.broadcast_to(term_all, term_ref.shape)


def attend_back_whole(raw, mixed, d_mixed, scale_row, all_scale):
    tokens, width = mixed.shape
    heads = all_scale.shape[0]
    head_dim = width // heads
    lanes = 2 * head_dim
    pairs = width // lanes

    def block(part):
        return pl.BlockSpec((tokens, lanes), lambda n: (0, part * pairs + n))

    d_raw, terms = pl.pallas_call(
        functools.partial(attend_back_kernel, head_dim),
        out_shape=[
            jax.ShapeDtypeStruct((3, tokens, width), BF16),
            jax.ShapeDtypeStruct((8, width), F32),
        ],
        grid=(pairs,),
        in_specs=[
            pl.BlockSpec(memory_space=pltpu.SMEM),
            pl.BlockSpec((1, tokens), lambda n: (0, 0)),
            pl.BlockSpec((tokens, 1), lambda n: (0, 0)),
            block(0),
            block(1),
            block(2),
            block(0),
            block(0),
        ],
        out_specs=[
            pl.BlockSpec((3, tokens, lanes), lambda n: (0, 0, n)),
            pl.BlockSpec((8, lanes), lambda n: (0, n)),
        ],
        scratch_shapes=[pltpu.VMEM((tokens, tokens), F32)],
        cost_estimate=pl.CostEstimate(
            flops=10 * tokens * tokens * width,
            bytes_accessed=16 * tokens * width,
            transcendentals=tokens * tokens * heads,
        ),
        compiler_params=pltpu.CompilerParams(vmem_limit_bytes=VMEM_LIMIT),
    )(all_scale, scale_row[None, :], scale_row[:, None], raw, raw, raw, mixed, d_mixed)
    return d_raw, jnp.sum(terms[0].reshape(heads, head_dim), axis=1)


def halves(values, c, half):
    keep = lax.dynamic_slice_in_dim(values, c * half, half, axis=1)
    give = lax.dynamic_slice_in_dim(values, (1 - c) * half, half, axis=1)
    return keep, give


def on_device_whole(
    inputs, labels, scale_ids, cotangent, table, w_ada, w_qkv, head_scale, w_proj, w_fc1, w_fc2
):
    width = inputs.shape[2]
    classes, rows = table.shape
    heads = TS * head_scale.shape[0]
    quarter = w_qkv.shape[2] // 2
    hidden_quarter = w_fc1.shape[1] // 2
    z, x, c, t = place()
    position = jnp.stack([z, x, c, t]).astype(jnp.int32)

    qkv_parts = [halves(w_qkv[:, n].astype(BF16), c, quarter) for n in range(3)]
    proj_parts = halves(w_proj.astype(BF16).T, c, quarter)
    fc1_parts = halves(w_fc1.astype(BF16), c, hidden_quarter)
    fc2_parts = halves(w_fc2.astype(BF16).T, c, hidden_quarter)
    pieces_qkv = gather_pieces(
        *[jnp.concatenate([part[n] for part in qkv_parts], axis=1) for n in range(2)]
    )
    pieces_mid = gather_pieces(
        *[jnp.concatenate([proj_parts[n], fc1_parts[n]], axis=1) for n in range(2)]
    )
    pieces_fc2 = gather_pieces(*fc2_parts)
    (qkv_low,) = assemble(
        pieces_qkv,
        position,
        [(0, n * width, 2 * quarter, quarter, n * quarter, quarter) for n in range(3)],
        [3 * width],
    )
    proj_low, fc1_low = assemble(
        pieces_mid,
        position,
        [
            (0, 0, 2 * quarter, quarter, 0, quarter),
            (1, 0, 2 * hidden_quarter, hidden_quarter, quarter, hidden_quarter),
        ],
        [width, 4 * hidden_quarter],
    )
    (fc2_low,) = assemble(
        pieces_fc2,
        position,
        [(0, 0, 2 * hidden_quarter, hidden_quarter, 0, hidden_quarter)],
        [4 * hidden_quarter],
    )

    label_pair = jnp.stack(in_order(labels[0], labels[1], t)).astype(F32)
    label_tile = jnp.broadcast_to(label_pair[:, None], (2, 128))
    all_labels = gather_near_first(label_tile)[:, 0].astype(jnp.int32)
    one_hot = (all_labels[:, None] == jnp.arange(classes)[None, :]).astype(BF16)
    condition = matmul(one_hot, table.astype(BF16), NN)
    silu_low = jax.nn.silu(condition).astype(BF16)
    ada_low = w_ada.astype(BF16).reshape(rows, 6 * width)
    silu_own = silu_low.reshape(-1, TS, rows)[:, 0]
    partial = matmul(silu_own, ada_low, NN).reshape(ZS, XS, CS, 6 * width)
    modulation = reduce_near_first(partial).reshape(6, 1, width)
    gain_attn, gain_mlp, scale_attn, scale_mlp, shift_attn, shift_mlp = modulation

    tokens_in = whole_image(inputs, t)
    upstream = whole_image(cotangent, t)
    scale_row = pick(scale_ids, t)
    other_scale = send(jnp.broadcast_to(head_scale[None, :], (8, head_scale.shape[0])), to_t)[0]
    all_scale = jnp.concatenate(in_order(head_scale, other_scale, t))

    normed_one, inverse_one = layer_norm(tokens_in)
    hidden_one = (normed_one * (1.0 + scale_attn) + shift_attn).astype(BF16)
    raw = matmul(hidden_one, qkv_low, NN).astype(BF16)
    mixed = attend_whole(raw, scale_row, all_scale)
    attended = matmul(mixed, proj_low, NT)
    middle = tokens_in + gain_attn * attended
    normed_two, inverse_two = layer_norm(middle)
    hidden_two = (normed_two * (1.0 + scale_mlp) + shift_mlp).astype(BF16)
    before = matmul(hidden_two, fc1_low, NN)
    gelu_fn = functools.partial(jax.nn.gelu, approximate=True)
    active_f, gelu_pull = jax.vjp(gelu_fn, before)
    active = active_f.astype(BF16)
    slope = gelu_pull(jnp.ones_like(before))[0].astype(BF16)
    branch = matmul(active, fc2_low, NT)
    output = split_image(middle + gain_mlp * branch, t)

    d_gain_mlp = jnp.sum(upstream * branch, axis=0)
    d_branch = (gain_mlp * upstream).astype(BF16)
    grad_fc2 = scatter_sum(d_branch, active, hidden_quarter, z, x, c, t)
    d_before = (matmul(d_branch, fc2_low, NN) * slope.astype(F32)).astype(BF16)
    grad_fc1 = scatter_sum(hidden_two, d_before, hidden_quarter, z, x, c, t)
    d_hidden_two = matmul(d_before, fc1_low, NT)
    d_scale_mlp = jnp.sum(d_hidden_two * normed_two, axis=0)
    d_shift_mlp = jnp.sum(d_hidden_two, axis=0)
    d_middle = upstream + norm_back(d_hidden_two * (1.0 + scale_mlp), normed_two, inverse_two)
    d_gain_attn = jnp.sum(d_middle * attended, axis=0)
    d_attended = (gain_attn * d_middle).astype(BF16)
    grad_proj = scatter_sum(d_attended, mixed, quarter, z, x, c, t)
    d_mixed = matmul(d_attended, proj_low, NN).astype(BF16)
    d_raw, scale_terms = attend_back_whole(raw, mixed, d_mixed, scale_row, all_scale)
    grad_qkv = scatter_sum(hidden_one, d_raw, quarter, z, x, c, t)
    d_hidden_one = sum(
        matmul(d_raw[n], qkv_low[:, n * width : (n + 1) * width], NT) for n in range(3)
    )
    d_scale_attn = jnp.sum(d_hidden_one * normed_one, axis=0)
    d_shift_attn = jnp.sum(d_hidden_one, axis=0)
    d_inputs = d_middle + norm_back(d_hidden_one * (1.0 + scale_attn), normed_one, inverse_one)
    d_inputs = split_image(d_inputs, t)

    d_modulation = jnp.concatenate(
        [d_gain_attn, d_gain_mlp, d_scale_attn, d_scale_mlp, d_shift_attn, d_shift_mlp]
    )
    scale_high = lax.reduce_precision(scale_terms, 8, 7)
    row = jnp.concatenate(
        [d_modulation, scale_high, scale_terms - scale_high, jnp.zeros((128 - 2 * heads,), F32)]
    ).astype(BF16)[None, :]
    everything = gather_near_first(jnp.concatenate([row, send(row, to_t)]))
    d_mod_all = everything[:, : 6 * width]
    scale_sum = jnp.sum(everything[:, 6 * width : 6 * width + 2 * heads].astype(F32), axis=0)
    scale_sum = (scale_sum[:heads] + scale_sum[heads:]).reshape(TS, heads // TS)
    grad_scale = pick(scale_sum, t)
    grad_ada = matmul(silu_low, d_mod_all, TN).reshape(rows, 6, width)
    d_silu = matmul(d_mod_all, ada_low, NT)
    _, silu_pull = jax.vjp(jax.nn.silu, condition)
    d_condition = silu_pull(d_silu)[0]
    grad_table = jnp.dot(one_hot.astype(F32).T, d_condition, precision=HIGHEST)

    own_qkv, other_qkv = grad_qkv
    grad_qkv = jnp.stack(
        [
            jnp.concatenate(
                in_order(
                    own_qkv[:, n * quarter : (n + 1) * quarter],
                    other_qkv[:, n * quarter : (n + 1) * quarter],
                    c,
                ),
                axis=1,
            )
            for n in range(3)
        ],
        axis=1,
    )
    return (
        output,
        d_inputs,
        grad_table,
        grad_ada,
        grad_qkv,
        grad_scale,
        jnp.concatenate(in_order(*grad_proj, c), axis=1).T,
        jnp.concatenate(in_order(*grad_fc1, c), axis=1),
        jnp.concatenate(in_order(*grad_fc2, c), axis=1).T,
    )


def solution(mesh):
    placed = (
        P("dp", "tensor", None),
        P("dp"),
        P("dp", None),
        P("dp", "tensor", None),
        P(None, "dp"),
        P("dp", None, None),
        P("dp", None, "tensor"),
        P("tensor"),
        P("tensor", "dp"),
        P("dp", "tensor"),
        P("tensor", "dp"),
    )
    fitting = mesh.shape["dp"] == ZS * XS * CS and mesh.shape["tensor"] == TS

    def on_device(inputs, *others):
        fits = fitting and inputs.shape[0] == TS
        return (on_device_whole if fits else on_device_general)(inputs, *others)

    return jax.shard_map(
        on_device,
        mesh=mesh,
        in_specs=placed,
        out_specs=(
            P("dp", "tensor", None),
            P("dp", "tensor", None),
            P(None, "dp"),
            P("dp", None, None),
            P("dp", None, "tensor"),
            P("tensor"),
            P("tensor", "dp"),
            P("dp", "tensor"),
            P("tensor", "dp"),
        ),
        check_vma=False,
    )
```

```python
import functools

import jax
import jax.numpy as jnp
from jax import lax
from jax.experimental import pallas as pl
from jax.experimental.pallas import tpu as pltpu
from jax.sharding import PartitionSpec as P

EPSILON = 1e-06
HIGHEST = lax.Precision.HIGHEST


def layer_norm(values):
    average = jnp.mean(values, axis=-1, keepdims=True)
    centred = values - average
    inverse = lax.rsqrt(jnp.mean(centred * centred, axis=-1, keepdims=True) + EPSILON)
    return (centred * inverse, inverse)


def norm_back(d_normed, normed, inverse):
    return inverse * (
        d_normed
        - jnp.mean(d_normed, axis=-1, keepdims=True)
        - normed * jnp.mean(d_normed * normed, axis=-1, keepdims=True)
    )


def unit_rows(values):
    inverse = lax.rsqrt(jnp.sum(values * values, axis=-1, keepdims=True) + EPSILON)
    return (values * inverse, inverse)


def unit_back(d_unit, unit, inverse):
    return inverse * (d_unit - unit * jnp.sum(d_unit * unit, axis=-1, keepdims=True))


def spread(values):
    return lax.all_gather(values, "tensor", axis=1, tiled=True)


def collect(terms):
    return lax.psum_scatter(
        terms.astype(jnp.bfloat16), "tensor", scatter_dimension=1, tiled=True
    ).astype(jnp.float32)


def masked_scores(queries, keys_in, scale_row):
    scores = jnp.einsum("qhd,khd->hqk", queries, keys_in, preferred_element_type=jnp.float32)
    visible = scale_row[None, :] <= scale_row[:, None]
    return jnp.where(visible[None], scores, -1e30)


def attend_forward(pieces):
    queries, keys_in, values_in, scale_row = pieces
    scores = masked_scores(queries, keys_in, scale_row)
    largest = jnp.max(scores, axis=-1, keepdims=True)
    exponent = jnp.exp(scores - largest)
    denominator = jnp.sum(exponent, axis=-1, keepdims=True)
    attn_probs = (exponent / denominator).astype(jnp.bfloat16)
    mixed = jnp.einsum("hqk,khd->qhd", attn_probs, values_in, preferred_element_type=jnp.float32)
    return (mixed.astype(jnp.bfloat16), (largest + jnp.log(denominator))[..., 0])


def attend_backward(pieces):
    queries, keys_in, values_in, scale_row, log_total, d_mixed = pieces
    scores = masked_scores(queries, keys_in, scale_row)
    attn_probs = jnp.exp(scores - log_total[..., None])
    d_probs = jnp.einsum("qhd,khd->hqk", d_mixed, values_in, preferred_element_type=jnp.float32)
    offset = jnp.sum(attn_probs * d_probs, axis=-1, keepdims=True)
    d_scores = (attn_probs * (d_probs - offset)).astype(jnp.bfloat16)
    d_queries = jnp.einsum("hqk,khd->qhd", d_scores, keys_in, preferred_element_type=jnp.float32)
    d_keys = jnp.einsum("hqk,qhd->khd", d_scores, queries, preferred_element_type=jnp.float32)
    d_values = jnp.einsum(
        "hqk,qhd->khd", attn_probs.astype(jnp.bfloat16), d_mixed, preferred_element_type=jnp.float32
    )
    return (d_queries, d_keys, d_values)


def on_device_general(
    inputs, labels, scale_ids, cotangent, table, w_ada, w_qkv, head_scale, w_proj, w_fc1, w_fc2
):
    images, local_len, model_width = inputs.shape
    full_len = scale_ids.shape[1]
    local_heads = head_scale.shape[0]
    head_dim = w_qkv.shape[2] // local_heads
    classes = table.shape[0]
    gathered = (
        lax.all_gather(table.astype(jnp.bfloat16), "dp", axis=1, tiled=True),
        lax.all_gather(w_qkv.astype(jnp.bfloat16), "dp", axis=0, tiled=True),
        lax.all_gather(w_proj.astype(jnp.bfloat16), "dp", axis=1, tiled=True),
        lax.all_gather(w_fc1.astype(jnp.bfloat16), "dp", axis=0, tiled=True),
        lax.all_gather(w_fc2.astype(jnp.bfloat16), "dp", axis=1, tiled=True),
    )
    table_low, qkv_low, proj_low, fc1_low, fc2_low = gathered
    qkv_flat = qkv_low.reshape(model_width, -1)
    one_hot = labels[:, None] == jnp.arange(classes)[None, :]
    condition = jnp.dot(one_hot.astype(jnp.bfloat16), table_low, preferred_element_type=jnp.float32)
    silu_low = jax.nn.silu(condition).astype(jnp.bfloat16)
    ada_full = lax.all_gather(w_ada.astype(jnp.bfloat16), "dp", axis=0, tiled=True).reshape(
        model_width, 6 * model_width
    )
    modulation = jnp.dot(silu_low, ada_full, preferred_element_type=jnp.float32)
    modulation = modulation.reshape(images, 6, model_width)
    gain_attn = modulation[:, 0, None, :]
    gain_mlp = modulation[:, 1, None, :]
    scale_attn = modulation[:, 2, None, :]
    scale_mlp = modulation[:, 3, None, :]
    shift_attn = modulation[:, 4, None, :]
    shift_mlp = modulation[:, 5, None, :]
    normed_one, inverse_one = layer_norm(inputs)
    hidden_one = spread((normed_one * (1.0 + scale_attn) + shift_attn).astype(jnp.bfloat16))
    projected = jnp.einsum("bld,dc->blc", hidden_one, qkv_flat, preferred_element_type=jnp.float32)
    projected = projected.reshape(images, full_len, 3, local_heads, head_dim)
    q_unit, q_inverse = unit_rows(projected[:, :, 0])
    k_unit, k_inverse = unit_rows(projected[:, :, 1])
    q_hat = (q_unit * head_scale[:, None]).astype(jnp.bfloat16)
    k_hat = k_unit.astype(jnp.bfloat16)
    v_hat = projected[:, :, 2].astype(jnp.bfloat16)
    mixed, log_total = lax.map(attend_forward, (q_hat, k_hat, v_hat, scale_ids))
    mixed_flat = mixed.reshape(images, full_len, local_heads * head_dim)
    attended = collect(
        jnp.einsum("blc,cd->bld", mixed_flat, proj_low, preferred_element_type=jnp.float32)
    )
    middle = inputs + gain_attn * attended
    normed_two, inverse_two = layer_norm(middle)
    hidden_two = spread((normed_two * (1.0 + scale_mlp) + shift_mlp).astype(jnp.bfloat16))
    before = jnp.einsum("bld,df->blf", hidden_two, fc1_low, preferred_element_type=jnp.float32)
    gelu_fn = functools.partial(jax.nn.gelu, approximate=True)
    active_f, gelu_pull = jax.vjp(gelu_fn, before)
    active = active_f.astype(jnp.bfloat16)
    branch = collect(jnp.einsum("blf,fd->bld", active, fc2_low, preferred_element_type=jnp.float32))
    output = middle + gain_mlp * branch
    again = (
        lax.all_gather(w_qkv.astype(jnp.bfloat16), "dp", axis=0, tiled=True),
        lax.all_gather(w_proj.astype(jnp.bfloat16), "dp", axis=1, tiled=True),
        lax.all_gather(w_fc1.astype(jnp.bfloat16), "dp", axis=0, tiled=True),
        lax.all_gather(w_fc2.astype(jnp.bfloat16), "dp", axis=1, tiled=True),
    )
    qkv_back, proj_back, fc1_back, fc2_back = again
    d_gain_mlp = jnp.sum(cotangent * branch, axis=1)
    d_branch = spread((gain_mlp * cotangent).astype(jnp.bfloat16))
    grad_fc2 = jnp.einsum("blf,bld->fd", active, d_branch, preferred_element_type=jnp.float32)
    d_active = jnp.einsum("bld,fd->blf", d_branch, fc2_back, preferred_element_type=jnp.float32)
    d_before = gelu_pull(d_active)[0].astype(jnp.bfloat16)
    grad_fc1 = jnp.einsum("bld,blf->df", hidden_two, d_before, preferred_element_type=jnp.float32)
    d_hidden_two = collect(
        jnp.einsum("blf,df->bld", d_before, fc1_back, preferred_element_type=jnp.float32)
    )
    d_scale_mlp = jnp.sum(d_hidden_two * normed_two, axis=1)
    d_shift_mlp = jnp.sum(d_hidden_two, axis=1)
    d_middle = cotangent + norm_back(d_hidden_two * (1.0 + scale_mlp), normed_two, inverse_two)
    d_gain_attn = jnp.sum(d_middle * attended, axis=1)
    d_attended = spread((gain_attn * d_middle).astype(jnp.bfloat16))
    grad_proj = jnp.einsum(
        "blc,bld->cd", mixed_flat, d_attended, preferred_element_type=jnp.float32
    )
    d_mixed = jnp.einsum("bld,cd->blc", d_attended, proj_back, preferred_element_type=jnp.float32)
    d_mixed = d_mixed.astype(jnp.bfloat16).reshape(images, full_len, local_heads, head_dim)
    d_q_hat, d_k_hat, d_v_hat = lax.map(
        attend_backward, (q_hat, k_hat, v_hat, scale_ids, log_total, d_mixed)
    )
    scale_terms = jnp.sum(d_q_hat * q_unit, axis=(0, 1, 3))
    d_query = unit_back(d_q_hat * head_scale[:, None], q_unit, q_inverse)
    d_key = unit_back(d_k_hat, k_unit, k_inverse)
    d_raw = jnp.stack([d_query, d_key, d_v_hat], axis=2).astype(jnp.bfloat16)
    d_raw = d_raw.reshape(images, full_len, 3 * local_heads * head_dim)
    grad_qkv = jnp.einsum("bld,blc->dc", hidden_one, d_raw, preferred_element_type=jnp.float32)
    grad_qkv = grad_qkv.reshape(model_width, 3, local_heads * head_dim)
    d_hidden_one = collect(
        jnp.einsum(
            "blc,dc->bld",
            d_raw,
            qkv_back.reshape(model_width, -1),
            preferred_element_type=jnp.float32,
        )
    )
    d_scale_attn = jnp.sum(d_hidden_one * normed_one, axis=1)
    d_shift_attn = jnp.sum(d_hidden_one, axis=1)
    d_inputs = d_middle + norm_back(d_hidden_one * (1.0 + scale_attn), normed_one, inverse_one)
    mod_terms_back = jnp.stack(
        [d_gain_attn, d_gain_mlp, d_scale_attn, d_scale_mlp, d_shift_attn, d_shift_mlp], axis=1
    )
    d_modulation = lax.psum(mod_terms_back.astype(jnp.bfloat16), "tensor").astype(jnp.float32)
    d_mod_flat = d_modulation.reshape(images, 6 * model_width)
    grad_scale = lax.psum(scale_terms, "dp")
    ada_terms = jnp.dot(silu_low.astype(jnp.float32).T, d_mod_flat, precision=HIGHEST)
    grad_ada = lax.psum_scatter(
        ada_terms.reshape(model_width, 6, model_width).astype(jnp.bfloat16),
        "dp",
        scatter_dimension=0,
        tiled=True,
    ).astype(jnp.float32)
    d_silu = jnp.dot(d_mod_flat, ada_full.astype(jnp.float32).T, precision=HIGHEST)
    _, silu_pull = jax.vjp(jax.nn.silu, condition)
    d_condition = silu_pull(d_silu)[0]
    table_terms = jnp.dot(one_hot.astype(jnp.float32).T, d_condition, precision=HIGHEST)
    summed = (
        lax.psum_scatter(
            table_terms.astype(jnp.bfloat16), "dp", scatter_dimension=1, tiled=True
        ).astype(jnp.float32),
        lax.psum_scatter(
            grad_qkv.astype(jnp.bfloat16), "dp", scatter_dimension=0, tiled=True
        ).astype(jnp.float32),
        lax.psum_scatter(
            grad_proj.astype(jnp.bfloat16), "dp", scatter_dimension=1, tiled=True
        ).astype(jnp.float32),
        lax.psum_scatter(
            grad_fc1.astype(jnp.bfloat16), "dp", scatter_dimension=0, tiled=True
        ).astype(jnp.float32),
        lax.psum_scatter(
            grad_fc2.astype(jnp.bfloat16), "dp", scatter_dimension=1, tiled=True
        ).astype(jnp.float32),
    )
    grad_table, grad_qkv_own, grad_proj_own, grad_fc1_own, grad_fc2_own = summed
    return (
        output,
        d_inputs,
        grad_table,
        grad_ada,
        grad_qkv_own,
        grad_scale,
        grad_proj_own,
        grad_fc1_own,
        grad_fc2_own,
    )


BF16 = jnp.bfloat16
F32 = jnp.float32
ZS, XS, CS, TS = 4, 2, 2, 2
BOTH = ("dp", "tensor")
NN = (((1,), (0,)), ((), ()))
NT = (((1,), (1,)), ((), ()))
TN = (((0,), (0,)), ((), ()))
HIDDEN = -1e30
VMEM_LIMIT = 60 * 1024 * 1024
BRIEF = pl.CostEstimate(flops=0, bytes_accessed=0, transcendentals=0)


def perm_of(step):
    pairs = []
    for z in range(ZS):
        for x in range(XS):
            for c in range(CS):
                for t in range(TS):
                    nz, nx, nc, nt = step(z, x, c, t)
                    source = ((z * XS + x) * CS + c) * TS + t
                    target = ((nz * XS + nx) * CS + nc) * TS + nt
                    pairs.append((source, target))
    return pairs


def send(values, step):
    return lax.ppermute(values, BOTH, perm_of(step))


def to_core(z, x, c, t):
    return (z, x, 1 - c, t)


def to_x(z, x, c, t):
    return (z, 1 - x, c, t)


def to_t(z, x, c, t):
    return (z, x, c, 1 - t)


def to_z(k):
    return lambda z, x, c, t: ((z + k) % ZS, x, c, t)


def to_near(z, x, c, t):
    return (z, 1 - x, c, t) if c == 0 else (z, x, c, 1 - t)


def to_far(z, x, c, t):
    return (z, x, c, 1 - t) if c == 0 else (z, 1 - x, c, t)


def pick(values, index, axis=0):
    return lax.dynamic_index_in_dim(values, index, axis, keepdims=False)


def place():
    dp = lax.axis_index("dp")
    t = lax.axis_index("tensor")
    return dp // (XS * CS), (dp // CS) % XS, dp % CS, t


def matmul(left, right, dims):
    return lax.dot_general(left, right, dims, preferred_element_type=F32)


def hold(*values):
    return lax.optimization_barrier(values)


def send_z(values):
    return [send(values, to_z(k)) for k in range(1, ZS)]


def send_terms_z(terms):
    return [send(terms[k - 1], to_z(k)) for k in range(1, ZS)]


def assemble_kernel(widths, where_ref, *refs):
    pieces, outs, sem = refs[:4], refs[4:-1], refs[-1]
    z, x, c, t = where_ref[0], where_ref[1], where_ref[2], where_ref[3]
    for slot, piece in enumerate(pieces):
        dx, dt = [(0, 0), (1 - c, c), (c, 1 - c), (1, 1)][slot]
        sx, st = x ^ dx, t ^ dt
        for dz in range(ZS):
            for dc in range(CS):
                sz = (z + ZS - dz) % ZS
                sc = c ^ dc
                row = pl.multiple_of(((sz * XS + sx) * CS + sc) * 64, 64)
                start = 0
                for which, width in enumerate(widths):
                    column = pl.multiple_of(st * width, 128)
                    pltpu.make_async_copy(
                        piece.at[dz, dc, :, pl.ds(start, width)],
                        outs[which].at[pl.ds(row, 64), pl.ds(column, width)],
                        sem.at[which],
                    ).start()
                    start += width
    for which, out in enumerate(outs):
        pltpu.make_async_copy(out, out, sem.at[which]).wait()


def assemble(pieces, position, widths):
    rows = ZS * XS * CS * 64
    return pl.pallas_call(
        functools.partial(assemble_kernel, widths),
        out_shape=[jax.ShapeDtypeStruct((rows, TS * width), BF16) for width in widths],
        in_specs=[pl.BlockSpec(memory_space=pltpu.SMEM)]
        + [pl.BlockSpec(memory_space=pl.ANY)] * 4,
        out_specs=[pl.BlockSpec(memory_space=pltpu.VMEM)] * len(widths),
        scratch_shapes=[pltpu.SemaphoreType.DMA((len(widths),))],
        cost_estimate=BRIEF,
        compiler_params=pltpu.CompilerParams(vmem_limit_bytes=VMEM_LIMIT),
    )(position, *pieces)


def product_kernel(count, with_added, *refs):
    out, start = refs[-1], 0
    for n in range(count):
        left = refs[1 + 2 * n][...]
        left = left.reshape(left.shape[0] * left.shape[1], left.shape[2])
        right = refs[2 + 2 * n][...]
        total = matmul(left, right, NN)
        columns = pl.ds(start, right.shape[1])
        if with_added:
            total = total + refs[1 + 2 * count][0, :, columns].astype(F32)
        out[0, :, columns] = total.astype(out.dtype)
        start += right.shape[1]


def products(factors, choice, added=None):
    tokens = factors[0][0].shape[1]
    span = CS * 64
    operands, specs, width = [], [], 0
    for rows, columns in factors:
        m = columns.shape[1] // TS
        operands += [rows.reshape(ZS, XS * span, tokens), columns]
        specs += [
            pl.BlockSpec((ZS, span, tokens), lambda n, s: (0, s[0, n], 0)),
            pl.BlockSpec((tokens, m), lambda n, s: (0, s[1, n])),
        ]
        width += m
    block = pl.BlockSpec((1, ZS * span, width), lambda n, s: (n, 0, 0))
    extra = [] if added is None else [added]
    return pl.pallas_call(
        functools.partial(product_kernel, len(factors), len(extra) == 1),
        out_shape=jax.ShapeDtypeStruct((4, ZS * span, width), BF16),
        grid_spec=pltpu.PrefetchScalarGridSpec(
            num_scalar_prefetch=1,
            grid=(4,),
            in_specs=specs + [block] * len(extra),
            out_specs=block,
        ),
        cost_estimate=BRIEF,
        compiler_params=pltpu.CompilerParams(vmem_limit_bytes=VMEM_LIMIT),
    )(choice, *operands, *extra)


def block_choice(core, where):
    z, x, c, t = where
    dx = jnp.stack([jnp.ones_like(core), core, 1 - core, jnp.zeros_like(core)])
    dt = jnp.stack([jnp.ones_like(core), 1 - core, core, jnp.zeros_like(core)])
    return jnp.stack([x ^ dx, t ^ dt]).astype(jnp.int32)


def scatter_near(blocks, far):
    return (blocks[2].astype(F32) + far[0].astype(F32)).astype(BF16)


def scatter_z(blocks, far, near, where):
    z = where[0]
    whole = blocks[3].astype(F32) + far[1].astype(F32) + near.astype(F32)
    whole = whole.astype(BF16).reshape(ZS, CS, 64, whole.shape[-1])
    return [pick(whole, (z + k) % ZS) for k in range(ZS)]


def scatter_total(own, others, where):
    c = where[2]
    total = sum(term.astype(F32) for term in [own] + list(others))
    return pick(total, c), pick(total, 1 - c).astype(BF16)


def in_order(own, other, bit):
    return jnp.where(bit == 0, own, other), jnp.where(bit == 0, other, own)


def join_image(values, other, t):
    return jnp.concatenate(in_order(pick(values, t), other.astype(F32), t), axis=0)


def own_and_other(values, t):
    half = values.shape[0] // 2
    own = lax.dynamic_slice_in_dim(values, t * half, half, axis=0)
    give = lax.dynamic_slice_in_dim(values, (1 - t) * half, half, axis=0)
    return own, give.astype(BF16)


def two_images(own, other, t):
    return jnp.stack(in_order(own, other.astype(F32), t))


def unit_of(values, mask):
    squares = jnp.where(mask, values * values, 0.0)
    inverse = lax.rsqrt(jnp.sum(squares, axis=-1, keepdims=True) + EPSILON)
    return jnp.where(mask, values * inverse, 0.0), inverse


def head_masks(shape, head_dim):
    lane = lax.broadcasted_iota(jnp.int32, shape, 1)
    return [(lane >= n * head_dim) & (lane < (n + 1) * head_dim) for n in range(2)]


def attend_kernel(head_dim, scale_ref, row_ref, column_ref, raw_ref, out_ref, bias_ref):
    pair = pl.program_id(0)

    @pl.when(pair == 0)
    def _():
        bias_ref[...] = jnp.where(row_ref[...] <= column_ref[...], 0.0, HIDDEN)

    lanes = 2 * head_dim
    q, k = raw_ref[:, :lanes].astype(F32), raw_ref[:, lanes : 2 * lanes].astype(F32)
    v = raw_ref[:, 2 * lanes :]
    values = jnp.concatenate([v, jnp.ones_like(v)], axis=1)
    masks = head_masks(q.shape, head_dim)
    k_hat = (unit_of(k, masks[0])[0] + unit_of(k, masks[1])[0]).astype(BF16)
    result = None
    for n in range(2):
        scale = scale_ref[2 * pair + n]
        q_hat = (unit_of(q, masks[n])[0] * scale).astype(BF16)
        scores = matmul(q_hat, k_hat, NT) + (bias_ref[...] - jnp.abs(scale))
        weights = jnp.exp(scores).astype(BF16)
        mixed = matmul(weights, values, NN)
        mixed = mixed[:, : 2 * head_dim] / mixed[:, 2 * head_dim :]
        result = mixed if result is None else jnp.where(masks[n], mixed, result)
    out_ref[...] = result.astype(out_ref.dtype)


def attend_whole(raw, scale_row, all_scale):
    tokens, width = raw.shape[0], raw.shape[1] // 3
    head_dim = width // all_scale.shape[0]
    lanes = 2 * head_dim
    pairs = width // lanes

    block = pl.BlockSpec((tokens, lanes), lambda n: (0, n))
    triple = pl.BlockSpec((tokens, 3 * lanes), lambda n: (0, n))
    return pl.pallas_call(
        functools.partial(attend_kernel, head_dim),
        out_shape=jax.ShapeDtypeStruct((tokens, width), BF16),
        grid=(pairs,),
        in_specs=[
            pl.BlockSpec(memory_space=pltpu.SMEM),
            pl.BlockSpec((1, tokens), lambda n: (0, 0)),
            pl.BlockSpec((tokens, 1), lambda n: (0, 0)),
            triple,
        ],
        out_specs=block,
        scratch_shapes=[pltpu.VMEM((tokens, tokens), F32)],
        cost_estimate=BRIEF,
        compiler_params=pltpu.CompilerParams(vmem_limit_bytes=VMEM_LIMIT),
    )(all_scale, scale_row[None, :], scale_row[:, None], raw)


def attend_back_kernel(
    head_dim,
    scale_ref,
    row_ref,
    column_ref,
    raw_ref,
    mixed_ref,
    d_mixed_ref,
    out_ref,
    term_ref,
    bias_ref,
):
    pair = pl.program_id(0)

    @pl.when(pair == 0)
    def _():
        bias_ref[...] = jnp.where(column_ref[...] <= row_ref[...], 0.0, HIDDEN)

    lanes = 2 * head_dim
    q, k = raw_ref[:, :lanes].astype(F32), raw_ref[:, lanes : 2 * lanes].astype(F32)
    v, d_mixed = raw_ref[:, 2 * lanes :], d_mixed_ref[...]
    masks = head_masks(q.shape, head_dim)
    k_units = [unit_of(k, mask) for mask in masks]
    k_hat = (k_units[0][0] + k_units[1][0]).astype(BF16)
    products = d_mixed.astype(F32) * mixed_ref[...].astype(F32)
    d_q_all = d_k_all = d_v_all = None
    for n in range(2):
        mask = masks[n]
        scale = scale_ref[2 * pair + n]
        q_unit, q_inverse = unit_of(q, mask)
        q_hat = (q_unit * scale).astype(BF16)
        d_out = jnp.where(mask, d_mixed, jnp.zeros_like(d_mixed))
        offset = jnp.sum(jnp.where(mask, products, 0.0), axis=-1, keepdims=True)
        offset = jnp.transpose(jnp.broadcast_to(offset, products.shape))[:1]
        scores = matmul(k_hat, q_hat, NT) + (bias_ref[...] - jnp.abs(scale))
        weights = jnp.exp(scores)
        weights = weights * (1.0 / jnp.sum(weights, axis=0, keepdims=True))
        d_weights = matmul(v, d_out, NT)
        d_scores = (weights * (d_weights - offset)).astype(BF16)
        d_v = matmul(weights.astype(BF16), d_out, NN)
        d_k = matmul(d_scores, q_hat, NN)
        d_q = jnp.where(mask, matmul(d_scores, k_hat, TN), 0.0)
        d_k = jnp.where(mask, d_k, 0.0)
        k_unit, k_inverse = k_units[n]
        term = d_q * q_unit
        term_n = jnp.sum(term, axis=0, keepdims=True)
        d_q = q_inverse * scale * (d_q - q_unit * jnp.sum(term, axis=-1, keepdims=True))
        d_k = k_inverse * (d_k - k_unit * jnp.sum(d_k * k_unit, axis=-1, keepdims=True))
        if n == 0:
            d_q_all, d_k_all, d_v_all, term_all = d_q, d_k, d_v, term_n
        else:
            d_q_all, d_k_all = d_q_all + d_q, d_k_all + d_k
            d_v_all, term_all = d_v_all + d_v, term_all + term_n
    out_ref[:, :lanes] = d_q_all.astype(out_ref.dtype)
    out_ref[:, lanes : 2 * lanes] = d_k_all.astype(out_ref.dtype)
    out_ref[:, 2 * lanes :] = d_v_all.astype(out_ref.dtype)
    term_ref[...] = jnp.broadcast_to(term_all, term_ref.shape)


def attend_back_whole(raw, mixed, d_mixed, scale_row, all_scale):
    tokens, width = mixed.shape
    heads = all_scale.shape[0]
    head_dim = width // heads
    lanes = 2 * head_dim
    pairs = width // lanes

    block = pl.BlockSpec((tokens, lanes), lambda n: (0, n))
    triple = pl.BlockSpec((tokens, 3 * lanes), lambda n: (0, n))
    d_raw, terms = pl.pallas_call(
        functools.partial(attend_back_kernel, head_dim),
        out_shape=[
            jax.ShapeDtypeStruct((tokens, 3 * width), BF16),
            jax.ShapeDtypeStruct((8, width), F32),
        ],
        grid=(pairs,),
        in_specs=[
            pl.BlockSpec(memory_space=pltpu.SMEM),
            pl.BlockSpec((1, tokens), lambda n: (0, 0)),
            pl.BlockSpec((tokens, 1), lambda n: (0, 0)),
            triple,
            block,
            block,
        ],
        out_specs=[
            triple,
            pl.BlockSpec((8, lanes), lambda n: (0, n)),
        ],
        scratch_shapes=[pltpu.VMEM((tokens, tokens), F32)],
        cost_estimate=BRIEF,
        compiler_params=pltpu.CompilerParams(vmem_limit_bytes=VMEM_LIMIT),
    )(all_scale, scale_row[None, :], scale_row[:, None], raw, mixed, d_mixed)
    return d_raw, jnp.sum(terms[0].reshape(heads, head_dim), axis=1)


def halves(values, c, half):
    keep = lax.dynamic_slice_in_dim(values, c * half, half, axis=1)
    give = lax.dynamic_slice_in_dim(values, (1 - c) * half, half, axis=1)
    return keep, give


def on_device_whole(
    inputs, labels, scale_ids, cotangent, table, w_ada, w_qkv, head_scale, w_proj, w_fc1, w_fc2
):
    width = inputs.shape[2]
    classes, rows = table.shape
    heads = TS * head_scale.shape[0]
    quarter = w_qkv.shape[2] // 2
    hidden_quarter = w_fc1.shape[1] // 2
    z, x, c, t = place()
    position = jnp.stack([z, x, c, t]).astype(jnp.int32)

    where = (z, x, c, t)

    pair = 2 * width // heads

    choice_given, choice_kept = block_choice(1 - c, where), block_choice(c, where)

    token_other = send(pick(inputs, 1 - t).astype(BF16), to_t)
    label_pair = jnp.stack(in_order(labels[0], labels[1], t)).astype(F32)
    label_tile = jnp.broadcast_to(label_pair[:, None], (2, 128))
    label_z = send_z(label_tile)
    scale_tile = jnp.broadcast_to(head_scale[None, :], (8, head_scale.shape[0]))
    scale_other = send(scale_tile, to_t)
    qkv_halves = []
    for side in (c, 1 - c):
        columns = [
            lax.dynamic_slice_in_dim(w_qkv[:, n].astype(BF16), side * quarter + j * pair, pair, 1)
            for j in range(quarter // pair)
            for n in range(3)
        ]
        qkv_halves.append(jnp.concatenate(columns, axis=1))
    keep_qkv, give_qkv = qkv_halves
    keep_qkv, recv_qkv, label_z, scale_other, rest = hold(
        keep_qkv,
        send(give_qkv, to_core),
        label_z,
        scale_other,
        (cotangent, w_ada, w_proj, w_fc1, w_fc2, table),
    )
    cotangent, w_ada, w_proj, w_fc1, w_fc2, table = rest
    two_qkv = jnp.stack([keep_qkv, recv_qkv])
    z_qkv = send_z(two_qkv)
    scale_row = pick(scale_ids, t)
    scales = jnp.concatenate(in_order(head_scale, scale_other[0], t)).reshape(TS, 2, -1)
    scale_own, scale_oth = pick(scales, c, 1).reshape(-1), pick(scales, 1 - c, 1).reshape(-1)

    label_rows = jnp.concatenate([label_tile] + label_z)
    label_rows = jnp.concatenate([label_rows, send(label_rows, to_x)])
    label_rows = jnp.concatenate([label_rows, send(label_rows, to_core)])
    all_labels = label_rows[:, 0].astype(jnp.int32)
    one_hot = (all_labels[:, None] == jnp.arange(classes)[None, :]).astype(BF16)
    condition = matmul(one_hot, table.astype(BF16), NN)
    silu_low = jax.nn.silu(condition).astype(BF16)
    ada_low = w_ada.astype(BF16).reshape(rows, 6 * width)
    silu_own = silu_low.reshape(-1, TS, rows)[:, 0]
    partial = matmul(silu_own, ada_low, NN).reshape(CS, XS, ZS, 6 * width)
    partial = partial[0] + send(partial[1], to_core)
    own_part, x_part = partial[0], send(partial[1], to_x)
    w_fc1, w_proj_t, w_fc2_t = w_fc1.astype(BF16), w_proj.astype(BF16).T, w_fc2.astype(BF16).T
    rest_halves = [halves(w_proj_t, c, quarter), halves(w_fc1, c, hidden_quarter)]
    rest_halves.append(halves(w_fc2_t, c, hidden_quarter))
    keep_rest, give_rest = [jnp.concatenate([part[n] for part in rest_halves], 1) for n in range(2)]
    cotangent_other = send(pick(cotangent, 1 - t).astype(BF16), to_t)
    z_qkv, own_part, x_part, token_other, recv_rest = hold(
        z_qkv, own_part, x_part, token_other, send(give_rest, to_core)
    )

    partial = own_part + x_part
    four_qkv = jnp.stack([two_qkv] + z_qkv)
    near_qkv, far_qkv = send(four_qkv, to_near), send(four_qkv, to_far)
    mod_z = send_terms_z([partial[ZS - k] for k in range(1, ZS)])
    mod_z, keep_rest = hold(mod_z, keep_rest)
    split = quarter + hidden_quarter
    two_mid = jnp.stack([keep_rest[:, :split], recv_rest[:, :split]])
    two_fc2 = jnp.stack([keep_rest[:, split:], recv_rest[:, split:]])
    mid_2 = send(two_mid, to_z(2))
    modulation = sum(mod_z, partial[0]).reshape(6, 1, width)
    gain_attn, gain_mlp, scale_attn, scale_mlp, shift_attn, shift_mlp = modulation
    tokens_in = join_image(inputs, token_other, t)
    near_qkv, far_qkv, mid_2, two_mid = hold(near_qkv, far_qkv, mid_2, two_mid)
    last_qkv = send(near_qkv, to_far)
    mid_1, mid_3 = send(two_mid, to_z(1)), send(two_mid, to_z(3))
    normed_one, inverse_one = layer_norm(tokens_in)
    hidden_one = (normed_one * (1.0 + scale_attn) + shift_attn).astype(BF16)
    last_qkv, mid_1, mid_3, hidden_one, cotangent_other = hold(
        last_qkv, mid_1, mid_3, hidden_one, cotangent_other
    )
    four_mid = jnp.stack([two_mid, mid_1, mid_2, mid_3])
    near_mid, far_mid = send(four_mid, to_near), send(four_mid, to_far)
    z_fc2 = send_z(two_fc2)
    (qkv_own,) = assemble([four_qkv, near_qkv, far_qkv, last_qkv], position, [3 * quarter])
    raw_own = matmul(hidden_one, qkv_own, NN).astype(BF16)
    raw_own, qkv_oth = hold(raw_own, send(qkv_own, to_core))
    raw_oth = matmul(hidden_one, qkv_oth, NN).astype(BF16)
    mixed_own = attend_whole(raw_own, scale_row, scale_own)
    mixed_own, near_mid, far_mid, z_fc2, raw_oth = hold(mixed_own, near_mid, far_mid, z_fc2, raw_oth)
    last_mid = send(near_mid, to_far)
    mixed_oth = attend_whole(raw_oth, scale_row, scale_oth)
    mixed_oth, last_mid = hold(mixed_oth, last_mid)
    four_fc2 = jnp.stack([two_fc2] + z_fc2)
    near_fc2, far_fc2 = send(four_fc2, to_near), send(four_fc2, to_far)
    proj_own, fc1_own = assemble(
        [four_mid, near_mid, far_mid, last_mid], position, [quarter, hidden_quarter]
    )
    upstream = join_image(cotangent, cotangent_other, t)
    d_branch = (gain_mlp * upstream).astype(BF16)
    proj_oth, d_branch = hold(send(proj_own, to_core), d_branch)
    fc1_oth = send(fc1_own, to_core)
    attended = matmul(mixed_own, proj_own, NT) + matmul(mixed_oth, proj_oth, NT)
    middle = tokens_in + gain_attn * attended
    normed_two, inverse_two = layer_norm(middle)
    hidden_two = (normed_two * (1.0 + scale_mlp) + shift_mlp).astype(BF16)
    hidden_two, fc1_oth = hold(hidden_two, fc1_oth)

    def activate(weights):
        before = matmul(hidden_two, weights, NN)
        active, pull = jax.vjp(functools.partial(jax.nn.gelu, approximate=True), before)
        return active.astype(BF16), pull(jnp.ones_like(before))[0].astype(BF16)

    active_oth, slope_oth = activate(fc1_oth)
    active_oth, slope_oth, near_fc2, far_fc2 = hold(active_oth, slope_oth, near_fc2, far_fc2)
    last_fc2 = send(near_fc2, to_far)
    active_own, slope_own = activate(fc1_own)
    d_branch_t = d_branch.T
    given = products([(d_branch_t, active_oth)], choice_given)
    given, active_own, slope_own, last_fc2 = hold(given, active_own, slope_own, last_fc2)
    added = send(given, to_core)
    (fc2_own,) = assemble([four_fc2, near_fc2, far_fc2, last_fc2], position, [hidden_quarter])
    fc2_own, added = hold(fc2_own, added)
    fc2_oth = send(fc2_own, to_core)
    blocks_fc2 = products([(d_branch_t, active_own)], choice_kept, added)
    blocks_fc2, fc2_oth = hold(blocks_fc2, fc2_oth)
    far_fc2 = send(blocks_fc2[:2], to_far)
    d_before_oth = (matmul(d_branch, fc2_oth, NN) * slope_oth.astype(F32)).astype(BF16)
    d_before_own = (matmul(d_branch, fc2_own, NN) * slope_own.astype(F32)).astype(BF16)
    branch = matmul(active_own, fc2_own, NT) + matmul(active_oth, fc2_oth, NT)
    output_own, output_give = own_and_other(middle + gain_mlp * branch, t)

    d_gain_mlp = jnp.sum(upstream * branch, axis=0)
    d_before_oth, d_before_own, output_give, far_fc2 = hold(
        d_before_oth, d_before_own, output_give, far_fc2
    )
    near_fc2 = send(scatter_near(blocks_fc2, far_fc2), to_near)
    d_hidden_two = matmul(d_before_own, fc1_own, NT) + matmul(d_before_oth, fc1_oth, NT)
    d_scale_mlp = jnp.sum(d_hidden_two * normed_two, axis=0)
    d_shift_mlp = jnp.sum(d_hidden_two, axis=0)
    d_middle = upstream + norm_back(d_hidden_two * (1.0 + scale_mlp), normed_two, inverse_two)
    d_gain_attn = jnp.sum(d_middle * attended, axis=0)
    d_attended = (gain_attn * d_middle).astype(BF16)
    d_attended, near_fc2 = hold(d_attended, near_fc2)
    z_fc2 = scatter_z(blocks_fc2, far_fc2, near_fc2, where)
    own_fc2, others_fc2 = z_fc2[0], send_terms_z(z_fc2[1:])
    hidden_two_t, d_attended_t = hidden_two.T, d_attended.T
    given = products([(d_attended_t, mixed_oth), (hidden_two_t, d_before_oth)], choice_given)
    given, d_attended = hold(given, d_attended)
    d_mixed_oth = matmul(d_attended, proj_oth, NN).astype(BF16)
    d_mixed_own = matmul(d_attended, proj_own, NN).astype(BF16)
    d_mixed_oth, d_mixed_own, added = hold(d_mixed_oth, d_mixed_own, send(given, to_core))
    blocks_mid = products(
        [(d_attended_t, mixed_own), (hidden_two_t, d_before_own)], choice_kept, added
    )
    blocks_mid, d_mixed_oth, others_fc2 = hold(blocks_mid, d_mixed_oth, others_fc2)
    far_mid = send(blocks_mid[:2], to_far)
    d_raw_oth, terms_oth = attend_back_whole(raw_oth, mixed_oth, d_mixed_oth, scale_row, scale_oth)
    hidden_one_t = hidden_one.T
    given = products([(hidden_one_t, d_raw_oth)], choice_given)
    given, far_mid, d_mixed_own = hold(given, far_mid, d_mixed_own)
    near_mid = send(scatter_near(blocks_mid, far_mid), to_near)
    added, output_other = send(given, to_core), send(output_give, to_t)
    d_raw_own, terms_own = attend_back_whole(raw_own, mixed_own, d_mixed_own, scale_row, scale_own)
    d_raw_own, near_mid, added = hold(d_raw_own, near_mid, added)
    z_mid = scatter_z(blocks_mid, far_mid, near_mid, where)
    own_mid, others_mid = z_mid[0], send_terms_z(z_mid[1:])
    blocks_qkv = products([(hidden_one_t, d_raw_own)], choice_kept, added)
    blocks_qkv, d_raw_own = hold(blocks_qkv, d_raw_own)
    far_qkv = send(blocks_qkv[:2], to_far)
    d_hidden_one = matmul(d_raw_own, qkv_own, NT) + matmul(d_raw_oth, qkv_oth, NT)
    d_scale_attn = jnp.sum(d_hidden_one * normed_one, axis=0)
    d_shift_attn = jnp.sum(d_hidden_one, axis=0)
    d_modulation = jnp.concatenate(
        [d_gain_attn, d_gain_mlp, d_scale_attn, d_scale_mlp, d_shift_attn, d_shift_mlp]
    )
    terms = in_order(terms_own.reshape(TS, -1), terms_oth.reshape(TS, -1), c)
    scale_terms = jnp.concatenate(terms, axis=1).reshape(-1)
    scale_high = lax.reduce_precision(scale_terms, 8, 7)
    row = jnp.concatenate(
        [d_modulation, scale_high, scale_terms - scale_high, jnp.zeros((128 - 2 * heads,), F32)]
    ).astype(BF16)[None, :]
    d_inputs = d_middle + norm_back(d_hidden_one * (1.0 + scale_attn), normed_one, inverse_one)
    inputs_own, inputs_give = own_and_other(d_inputs, t)
    row_other = send(row, to_t)
    far_qkv, inputs_give, row_other, output_other, others_mid = hold(
        far_qkv, inputs_give, row_other, output_other, others_mid
    )
    near_qkv = send(scatter_near(blocks_qkv, far_qkv), to_near)
    inputs_other = send(inputs_give, to_t)
    mod_rows = jnp.concatenate([row, row_other])
    half_fc2, other_fc2 = scatter_total(own_fc2, others_fc2, where)
    half_mid, other_mid = scatter_total(own_mid, others_mid, where)
    other_rest = jnp.concatenate([other_mid, other_fc2], axis=1)
    near_qkv, mod_z, other_rest = hold(near_qkv, send_z(mod_rows), send(other_rest, to_core))
    z_qkv = scatter_z(blocks_qkv, far_qkv, near_qkv, where)
    own_qkv, others_qkv = z_qkv[0], send_terms_z(z_qkv[1:])
    mod_rows = jnp.concatenate([mod_rows] + mod_z)
    mod_rows = jnp.concatenate([mod_rows, send(mod_rows, to_x)])
    mod_rows = jnp.concatenate([mod_rows, send(mod_rows, to_core)])

    d_mod_all = mod_rows[:, : 6 * width]
    scale_sum = jnp.sum(mod_rows[:, 6 * width : 6 * width + 2 * heads].astype(F32), axis=0)
    scale_sum = (scale_sum[:heads] + scale_sum[heads:]).reshape(TS, heads // TS)
    grad_scale = pick(scale_sum, t)
    grad_ada = matmul(silu_low, d_mod_all, TN).reshape(rows, 6, width)
    d_silu = matmul(d_mod_all, ada_low, NT)
    _, silu_pull = jax.vjp(jax.nn.silu, condition)
    d_condition = silu_pull(d_silu)[0]
    grad_table = jnp.dot(one_hot.astype(F32).T, d_condition, precision=HIGHEST)

    def joined(own, other):
        return jnp.concatenate(in_order(own, other.astype(F32), c), axis=1)

    grad_proj = joined(half_mid[:, :quarter], other_rest[:, :quarter]).T
    grad_fc1 = joined(half_mid[:, quarter:], other_rest[:, quarter:split])
    grad_fc2 = joined(half_fc2, other_rest[:, split:]).T
    others_qkv, others = hold(
        others_qkv, (grad_ada, grad_table, grad_scale, inputs_other, grad_proj, grad_fc1, grad_fc2)
    )
    grad_ada, grad_table, grad_scale, inputs_other, grad_proj, grad_fc1, grad_fc2 = others
    half_qkv, other_qkv = scatter_total(own_qkv, others_qkv, where)
    other_qkv = send(other_qkv, to_core)

    def part_of(values, n):
        starts = range(n * pair, 3 * quarter, 3 * pair)
        return jnp.concatenate([values[:, start : start + pair] for start in starts], axis=1)

    grad_qkv = [joined(part_of(half_qkv, n), part_of(other_qkv, n)) for n in range(3)]
    return (
        two_images(output_own, output_other, t),
        two_images(inputs_own, inputs_other, t),
        grad_table,
        grad_ada,
        jnp.stack(grad_qkv, axis=1),
        grad_scale,
        grad_proj,
        grad_fc1,
        grad_fc2,
    )


def solution(mesh):
    placed = (
        P("dp", "tensor", None),
        P("dp"),
        P("dp", None),
        P("dp", "tensor", None),
        P(None, "dp"),
        P("dp", None, None),
        P("dp", None, "tensor"),
        P("tensor"),
        P("tensor", "dp"),
        P("dp", "tensor"),
        P("tensor", "dp"),
    )
    fitting = mesh.shape["dp"] == ZS * XS * CS and mesh.shape["tensor"] == TS

    def on_device(inputs, *others):
        fits = fitting and inputs.shape[0] == TS
        return (on_device_whole if fits else on_device_general)(inputs, *others)

    return jax.shard_map(
        on_device,
        mesh=mesh,
        in_specs=placed,
        out_specs=(
            P("dp", "tensor", None),
            P("dp", "tensor", None),
            P(None, "dp"),
            P("dp", None, None),
            P("dp", None, "tensor"),
            P("tensor"),
            P("tensor", "dp"),
            P("dp", "tensor"),
            P("tensor", "dp"),
        ),
        check_vma=False,
    )
```

```python
import functools
import math

import jax
import jax.numpy as jnp
from jax import lax
from jax.experimental import pallas as pl
from jax.experimental.pallas import tpu as pltpu
from jax.sharding import PartitionSpec as P

EPSILON = 1e-06
HIGHEST = lax.Precision.HIGHEST


def layer_norm(values):
    average = jnp.mean(values, axis=-1, keepdims=True)
    centred = values - average
    inverse = lax.rsqrt(jnp.mean(centred * centred, axis=-1, keepdims=True) + EPSILON)
    return (centred * inverse, inverse)


def norm_back(d_normed, normed, inverse):
    return inverse * (
        d_normed
        - jnp.mean(d_normed, axis=-1, keepdims=True)
        - normed * jnp.mean(d_normed * normed, axis=-1, keepdims=True)
    )


def unit_rows(values):
    inverse = lax.rsqrt(jnp.sum(values * values, axis=-1, keepdims=True) + EPSILON)
    return (values * inverse, inverse)


def unit_back(d_unit, unit, inverse):
    return inverse * (d_unit - unit * jnp.sum(d_unit * unit, axis=-1, keepdims=True))


def spread(values):
    return lax.all_gather(values, "tensor", axis=1, tiled=True)


def collect(terms):
    return lax.psum_scatter(
        terms.astype(jnp.bfloat16), "tensor", scatter_dimension=1, tiled=True
    ).astype(jnp.float32)


def masked_scores(queries, keys_in, scale_row):
    scores = jnp.einsum("qhd,khd->hqk", queries, keys_in, preferred_element_type=jnp.float32)
    visible = scale_row[None, :] <= scale_row[:, None]
    return jnp.where(visible[None], scores, -1e30)


def attend_forward(pieces):
    queries, keys_in, values_in, scale_row = pieces
    scores = masked_scores(queries, keys_in, scale_row)
    largest = jnp.max(scores, axis=-1, keepdims=True)
    exponent = jnp.exp(scores - largest)
    denominator = jnp.sum(exponent, axis=-1, keepdims=True)
    attn_probs = (exponent / denominator).astype(jnp.bfloat16)
    mixed = jnp.einsum("hqk,khd->qhd", attn_probs, values_in, preferred_element_type=jnp.float32)
    return (mixed.astype(jnp.bfloat16), (largest + jnp.log(denominator))[..., 0])


def attend_backward(pieces):
    queries, keys_in, values_in, scale_row, log_total, d_mixed = pieces
    scores = masked_scores(queries, keys_in, scale_row)
    attn_probs = jnp.exp(scores - log_total[..., None])
    d_probs = jnp.einsum("qhd,khd->hqk", d_mixed, values_in, preferred_element_type=jnp.float32)
    offset = jnp.sum(attn_probs * d_probs, axis=-1, keepdims=True)
    d_scores = (attn_probs * (d_probs - offset)).astype(jnp.bfloat16)
    d_queries = jnp.einsum("hqk,khd->qhd", d_scores, keys_in, preferred_element_type=jnp.float32)
    d_keys = jnp.einsum("hqk,qhd->khd", d_scores, queries, preferred_element_type=jnp.float32)
    d_values = jnp.einsum(
        "hqk,qhd->khd", attn_probs.astype(jnp.bfloat16), d_mixed, preferred_element_type=jnp.float32
    )
    return (d_queries, d_keys, d_values)


def on_device_general(
    inputs, labels, scale_ids, cotangent, table, w_ada, w_qkv, head_scale, w_proj, w_fc1, w_fc2
):
    images, local_len, model_width = inputs.shape
    full_len = scale_ids.shape[1]
    local_heads = head_scale.shape[0]
    head_dim = w_qkv.shape[2] // local_heads
    classes = table.shape[0]
    gathered = (
        lax.all_gather(table.astype(jnp.bfloat16), "dp", axis=1, tiled=True),
        lax.all_gather(w_qkv.astype(jnp.bfloat16), "dp", axis=0, tiled=True),
        lax.all_gather(w_proj.astype(jnp.bfloat16), "dp", axis=1, tiled=True),
        lax.all_gather(w_fc1.astype(jnp.bfloat16), "dp", axis=0, tiled=True),
        lax.all_gather(w_fc2.astype(jnp.bfloat16), "dp", axis=1, tiled=True),
    )
    table_low, qkv_low, proj_low, fc1_low, fc2_low = gathered
    qkv_flat = qkv_low.reshape(model_width, -1)
    one_hot = labels[:, None] == jnp.arange(classes)[None, :]
    condition = jnp.dot(one_hot.astype(jnp.bfloat16), table_low, preferred_element_type=jnp.float32)
    silu_low = jax.nn.silu(condition).astype(jnp.bfloat16)
    ada_full = lax.all_gather(w_ada.astype(jnp.bfloat16), "dp", axis=0, tiled=True).reshape(
        model_width, 6 * model_width
    )
    modulation = jnp.dot(silu_low, ada_full, preferred_element_type=jnp.float32)
    modulation = modulation.reshape(images, 6, model_width)
    gain_attn = modulation[:, 0, None, :]
    gain_mlp = modulation[:, 1, None, :]
    scale_attn = modulation[:, 2, None, :]
    scale_mlp = modulation[:, 3, None, :]
    shift_attn = modulation[:, 4, None, :]
    shift_mlp = modulation[:, 5, None, :]
    normed_one, inverse_one = layer_norm(inputs)
    hidden_one = spread((normed_one * (1.0 + scale_attn) + shift_attn).astype(jnp.bfloat16))
    projected = jnp.einsum("bld,dc->blc", hidden_one, qkv_flat, preferred_element_type=jnp.float32)
    projected = projected.reshape(images, full_len, 3, local_heads, head_dim)
    q_unit, q_inverse = unit_rows(projected[:, :, 0])
    k_unit, k_inverse = unit_rows(projected[:, :, 1])
    q_hat = (q_unit * head_scale[:, None]).astype(jnp.bfloat16)
    k_hat = k_unit.astype(jnp.bfloat16)
    v_hat = projected[:, :, 2].astype(jnp.bfloat16)
    mixed, log_total = lax.map(attend_forward, (q_hat, k_hat, v_hat, scale_ids))
    mixed_flat = mixed.reshape(images, full_len, local_heads * head_dim)
    attended = collect(
        jnp.einsum("blc,cd->bld", mixed_flat, proj_low, preferred_element_type=jnp.float32)
    )
    middle = inputs + gain_attn * attended
    normed_two, inverse_two = layer_norm(middle)
    hidden_two = spread((normed_two * (1.0 + scale_mlp) + shift_mlp).astype(jnp.bfloat16))
    before = jnp.einsum("bld,df->blf", hidden_two, fc1_low, preferred_element_type=jnp.float32)
    gelu_fn = functools.partial(jax.nn.gelu, approximate=True)
    active_f, gelu_pull = jax.vjp(gelu_fn, before)
    active = active_f.astype(jnp.bfloat16)
    branch = collect(jnp.einsum("blf,fd->bld", active, fc2_low, preferred_element_type=jnp.float32))
    output = middle + gain_mlp * branch
    again = (
        lax.all_gather(w_qkv.astype(jnp.bfloat16), "dp", axis=0, tiled=True),
        lax.all_gather(w_proj.astype(jnp.bfloat16), "dp", axis=1, tiled=True),
        lax.all_gather(w_fc1.astype(jnp.bfloat16), "dp", axis=0, tiled=True),
        lax.all_gather(w_fc2.astype(jnp.bfloat16), "dp", axis=1, tiled=True),
    )
    qkv_back, proj_back, fc1_back, fc2_back = again
    d_gain_mlp = jnp.sum(cotangent * branch, axis=1)
    d_branch = spread((gain_mlp * cotangent).astype(jnp.bfloat16))
    grad_fc2 = jnp.einsum("blf,bld->fd", active, d_branch, preferred_element_type=jnp.float32)
    d_active = jnp.einsum("bld,fd->blf", d_branch, fc2_back, preferred_element_type=jnp.float32)
    d_before = gelu_pull(d_active)[0].astype(jnp.bfloat16)
    grad_fc1 = jnp.einsum("bld,blf->df", hidden_two, d_before, preferred_element_type=jnp.float32)
    d_hidden_two = collect(
        jnp.einsum("blf,df->bld", d_before, fc1_back, preferred_element_type=jnp.float32)
    )
    d_scale_mlp = jnp.sum(d_hidden_two * normed_two, axis=1)
    d_shift_mlp = jnp.sum(d_hidden_two, axis=1)
    d_middle = cotangent + norm_back(d_hidden_two * (1.0 + scale_mlp), normed_two, inverse_two)
    d_gain_attn = jnp.sum(d_middle * attended, axis=1)
    d_attended = spread((gain_attn * d_middle).astype(jnp.bfloat16))
    grad_proj = jnp.einsum(
        "blc,bld->cd", mixed_flat, d_attended, preferred_element_type=jnp.float32
    )
    d_mixed = jnp.einsum("bld,cd->blc", d_attended, proj_back, preferred_element_type=jnp.float32)
    d_mixed = d_mixed.astype(jnp.bfloat16).reshape(images, full_len, local_heads, head_dim)
    d_q_hat, d_k_hat, d_v_hat = lax.map(
        attend_backward, (q_hat, k_hat, v_hat, scale_ids, log_total, d_mixed)
    )
    scale_terms = jnp.sum(d_q_hat * q_unit, axis=(0, 1, 3))
    d_query = unit_back(d_q_hat * head_scale[:, None], q_unit, q_inverse)
    d_key = unit_back(d_k_hat, k_unit, k_inverse)
    d_raw = jnp.stack([d_query, d_key, d_v_hat], axis=2).astype(jnp.bfloat16)
    d_raw = d_raw.reshape(images, full_len, 3 * local_heads * head_dim)
    grad_qkv = jnp.einsum("bld,blc->dc", hidden_one, d_raw, preferred_element_type=jnp.float32)
    grad_qkv = grad_qkv.reshape(model_width, 3, local_heads * head_dim)
    d_hidden_one = collect(
        jnp.einsum(
            "blc,dc->bld",
            d_raw,
            qkv_back.reshape(model_width, -1),
            preferred_element_type=jnp.float32,
        )
    )
    d_scale_attn = jnp.sum(d_hidden_one * normed_one, axis=1)
    d_shift_attn = jnp.sum(d_hidden_one, axis=1)
    d_inputs = d_middle + norm_back(d_hidden_one * (1.0 + scale_attn), normed_one, inverse_one)
    mod_terms_back = jnp.stack(
        [d_gain_attn, d_gain_mlp, d_scale_attn, d_scale_mlp, d_shift_attn, d_shift_mlp], axis=1
    )
    d_modulation = lax.psum(mod_terms_back.astype(jnp.bfloat16), "tensor").astype(jnp.float32)
    d_mod_flat = d_modulation.reshape(images, 6 * model_width)
    grad_scale = lax.psum(scale_terms, "dp")
    ada_terms = jnp.dot(silu_low.astype(jnp.float32).T, d_mod_flat, precision=HIGHEST)
    grad_ada = lax.psum_scatter(
        ada_terms.reshape(model_width, 6, model_width).astype(jnp.bfloat16),
        "dp",
        scatter_dimension=0,
        tiled=True,
    ).astype(jnp.float32)
    d_silu = jnp.dot(d_mod_flat, ada_full.astype(jnp.float32).T, precision=HIGHEST)
    _, silu_pull = jax.vjp(jax.nn.silu, condition)
    d_condition = silu_pull(d_silu)[0]
    table_terms = jnp.dot(one_hot.astype(jnp.float32).T, d_condition, precision=HIGHEST)
    summed = (
        lax.psum_scatter(
            table_terms.astype(jnp.bfloat16), "dp", scatter_dimension=1, tiled=True
        ).astype(jnp.float32),
        lax.psum_scatter(
            grad_qkv.astype(jnp.bfloat16), "dp", scatter_dimension=0, tiled=True
        ).astype(jnp.float32),
        lax.psum_scatter(
            grad_proj.astype(jnp.bfloat16), "dp", scatter_dimension=1, tiled=True
        ).astype(jnp.float32),
        lax.psum_scatter(
            grad_fc1.astype(jnp.bfloat16), "dp", scatter_dimension=0, tiled=True
        ).astype(jnp.float32),
        lax.psum_scatter(
            grad_fc2.astype(jnp.bfloat16), "dp", scatter_dimension=1, tiled=True
        ).astype(jnp.float32),
    )
    grad_table, grad_qkv_own, grad_proj_own, grad_fc1_own, grad_fc2_own = summed
    return (
        output,
        d_inputs,
        grad_table,
        grad_ada,
        grad_qkv_own,
        grad_scale,
        grad_proj_own,
        grad_fc1_own,
        grad_fc2_own,
    )


BF16 = jnp.bfloat16
F32 = jnp.float32
ZS, XS, CS, TS = 4, 2, 2, 2
BOTH = ("dp", "tensor")
NN = (((1,), (0,)), ((), ()))
NT = (((1,), (1,)), ((), ()))
TN = (((0,), (0,)), ((), ()))
HIDDEN = -1e30
VMEM_LIMIT = 60 * 1024 * 1024
BRIEF = pl.CostEstimate(flops=0, bytes_accessed=0, transcendentals=0)


def perm_of(step):
    pairs = []
    for z in range(ZS):
        for x in range(XS):
            for c in range(CS):
                for t in range(TS):
                    nz, nx, nc, nt = step(z, x, c, t)
                    source = ((z * XS + x) * CS + c) * TS + t
                    target = ((nz * XS + nx) * CS + nc) * TS + nt
                    pairs.append((source, target))
    return pairs


def send(values, step):
    return lax.ppermute(values, BOTH, perm_of(step))


def to_core(z, x, c, t):
    return (z, x, 1 - c, t)


def to_x(z, x, c, t):
    return (z, 1 - x, c, t)


def to_t(z, x, c, t):
    return (z, x, c, 1 - t)


def to_z(k):
    return lambda z, x, c, t: ((z + k) % ZS, x, c, t)


def to_near(z, x, c, t):
    return (z, 1 - x, c, t) if c == 0 else (z, x, c, 1 - t)


def to_far(z, x, c, t):
    return (z, x, c, 1 - t) if c == 0 else (z, 1 - x, c, t)


def pick(values, index, axis=0):
    return lax.dynamic_index_in_dim(values, index, axis, keepdims=False)


def place():
    dp = lax.axis_index("dp")
    t = lax.axis_index("tensor")
    return dp // (XS * CS), (dp // CS) % XS, dp % CS, t


def matmul(left, right, dims):
    return lax.dot_general(left, right, dims, preferred_element_type=F32)


def hold(*values):
    return lax.optimization_barrier(values)


def send_z(values):
    return [send(values, to_z(k)) for k in range(1, ZS)]


def send_terms_z(terms):
    return [send(terms[k - 1], to_z(k)) for k in range(1, ZS)]


def assemble_kernel(widths, where_ref, *refs):
    pieces, outs, sem = refs[:4], refs[4:-1], refs[-1]
    z, x, c, t = where_ref[0], where_ref[1], where_ref[2], where_ref[3]
    for slot, piece in enumerate(pieces):
        dx, dt = [(0, 0), (1 - c, c), (c, 1 - c), (1, 1)][slot]
        sx, st = x ^ dx, t ^ dt
        for dz in range(ZS):
            for dc in range(CS):
                sz = (z + ZS - dz) % ZS
                sc = c ^ dc
                row = pl.multiple_of(((sz * XS + sx) * CS + sc) * 64, 64)
                start = 0
                for which, width in enumerate(widths):
                    column = pl.multiple_of(st * width, 128)
                    pltpu.make_async_copy(
                        piece.at[dz, dc, :, pl.ds(start, width)],
                        outs[which].at[pl.ds(row, 64), pl.ds(column, width)],
                        sem.at[which],
                    ).start()
                    start += width
    for which, out in enumerate(outs):
        pltpu.make_async_copy(out, out, sem.at[which]).wait()


def assemble(pieces, position, widths):
    rows = ZS * XS * CS * 64
    return pl.pallas_call(
        functools.partial(assemble_kernel, widths),
        out_shape=[jax.ShapeDtypeStruct((rows, TS * width), BF16) for width in widths],
        in_specs=[pl.BlockSpec(memory_space=pltpu.SMEM)]
        + [pl.BlockSpec(memory_space=pl.ANY)] * 4,
        out_specs=[pl.BlockSpec(memory_space=pltpu.VMEM)] * len(widths),
        scratch_shapes=[pltpu.SemaphoreType.DMA((len(widths),))],
        cost_estimate=BRIEF,
        compiler_params=pltpu.CompilerParams(vmem_limit_bytes=VMEM_LIMIT),
    )(position, *pieces)


def products(factors, added=None):
    terms = [matmul(rows, columns, TN) for rows, columns in factors]
    if added is not None:
        terms = [term + other.astype(F32) for term, other in zip(terms, added)]
    return [term.astype(BF16) for term in terms]


def block(blocks, dx, dt, where):
    z, x, c, t = where
    parts = []
    for values in blocks:
        m = values.shape[1] // TS
        values = lax.dynamic_slice_in_dim(values, (t ^ dt) * m, m, 1)
        values = pick(values.reshape(ZS, XS, CS * 64, m), x ^ dx, 1)
        parts.append(values.reshape(ZS * CS * 64, m))
    return parts[0] if len(parts) == 1 else jnp.concatenate(parts, axis=1)


def scatter_far(blocks, where):
    c = where[2]
    return jnp.stack([block(blocks, 1, 1, where), block(blocks, c, 1 - c, where)])


def scatter_near(blocks, far, where):
    c = where[2]
    return (block(blocks, 1 - c, c, where).astype(F32) + far[0].astype(F32)).astype(BF16)


def scatter_z(blocks, far, near, where):
    z = where[0]
    whole = block(blocks, 0, 0, where).astype(F32) + far[1].astype(F32) + near.astype(F32)
    whole = whole.astype(BF16).reshape(ZS, CS, 64, whole.shape[-1])
    return [pick(whole, (z + k) % ZS) for k in range(ZS)]


def scatter_total(own, others, where):
    c = where[2]
    total = sum(term.astype(F32) for term in [own] + list(others))
    return pick(total, c), pick(total, 1 - c).astype(BF16)


def in_order(own, other, bit):
    return jnp.where(bit == 0, own, other), jnp.where(bit == 0, other, own)


def join_image(values, other, t):
    return jnp.concatenate(in_order(pick(values, t), other.astype(F32), t), axis=0)


def own_and_other(values, t):
    half = values.shape[0] // 2
    own = lax.dynamic_slice_in_dim(values, t * half, half, axis=0)
    give = lax.dynamic_slice_in_dim(values, (1 - t) * half, half, axis=0)
    return own, give.astype(BF16)


def two_images(own, other, t):
    return jnp.stack(in_order(own, other.astype(F32), t))


def unit_of(values, mask):
    squares = jnp.where(mask, values * values, 0.0)
    inverse = lax.rsqrt(jnp.sum(squares, axis=-1, keepdims=True) + EPSILON)
    return jnp.where(mask, values * inverse, 0.0), inverse


def head_masks(shape, head_dim):
    lane = lax.broadcasted_iota(jnp.int32, shape, 1)
    return [(lane >= n * head_dim) & (lane < (n + 1) * head_dim) for n in range(2)]


def attend_kernel(head_dim, scale_ref, row_ref, column_ref, raw_ref, out_ref, bias_ref):
    pair = pl.program_id(0)

    @pl.when(pair == 0)
    def _():
        bias_ref[...] = jnp.where(row_ref[...] <= column_ref[...], 0.0, HIDDEN)

    lanes = 2 * head_dim
    q, k = raw_ref[:, :lanes].astype(F32), raw_ref[:, lanes : 2 * lanes].astype(F32)
    v = raw_ref[:, 2 * lanes :]
    values = jnp.concatenate([v, jnp.ones_like(v)], axis=1)
    masks = head_masks(q.shape, head_dim)
    k_hat = (unit_of(k, masks[0])[0] + unit_of(k, masks[1])[0]).astype(BF16)
    result = None
    for n in range(2):
        scale = scale_ref[2 * pair + n]
        q_hat = (unit_of(q, masks[n])[0] * scale).astype(BF16)
        scores = matmul(q_hat, k_hat, NT) + (bias_ref[...] - jnp.abs(scale))
        weights = jnp.exp(scores).astype(BF16)
        mixed = matmul(weights, values, NN)
        mixed = mixed[:, : 2 * head_dim] / mixed[:, 2 * head_dim :]
        result = mixed if result is None else jnp.where(masks[n], mixed, result)
    out_ref[...] = result.astype(out_ref.dtype)


def attend_whole(raw, scale_row, all_scale):
    tokens, width = raw.shape[0], raw.shape[1] // 3
    head_dim = width // all_scale.shape[0]
    lanes = 2 * head_dim
    pairs = width // lanes

    block = pl.BlockSpec((tokens, lanes), lambda n: (0, n))
    triple = pl.BlockSpec((tokens, 3 * lanes), lambda n: (0, n))
    return pl.pallas_call(
        functools.partial(attend_kernel, head_dim),
        out_shape=jax.ShapeDtypeStruct((tokens, width), BF16),
        grid=(pairs,),
        in_specs=[
            pl.BlockSpec(memory_space=pltpu.SMEM),
            pl.BlockSpec((1, tokens), lambda n: (0, 0)),
            pl.BlockSpec((tokens, 1), lambda n: (0, 0)),
            triple,
        ],
        out_specs=block,
        scratch_shapes=[pltpu.VMEM((tokens, tokens), F32)],
        cost_estimate=BRIEF,
        compiler_params=pltpu.CompilerParams(vmem_limit_bytes=VMEM_LIMIT),
    )(all_scale, scale_row[None, :], scale_row[:, None], raw)


def attend_back_kernel(
    head_dim,
    scale_ref,
    row_ref,
    column_ref,
    raw_ref,
    mixed_ref,
    d_mixed_ref,
    out_ref,
    term_ref,
    bias_ref,
):
    pair = pl.program_id(0)

    @pl.when(pair == 0)
    def _():
        bias_ref[...] = jnp.where(column_ref[...] <= row_ref[...], 0.0, HIDDEN)

    lanes = 2 * head_dim
    q, k = raw_ref[:, :lanes].astype(F32), raw_ref[:, lanes : 2 * lanes].astype(F32)
    v, d_mixed = raw_ref[:, 2 * lanes :], d_mixed_ref[...]
    masks = head_masks(q.shape, head_dim)
    k_units = [unit_of(k, mask) for mask in masks]
    k_hat = (k_units[0][0] + k_units[1][0]).astype(BF16)
    products = d_mixed.astype(F32) * mixed_ref[...].astype(F32)
    d_q_all = d_k_all = d_v_all = None
    for n in range(2):
        mask = masks[n]
        scale = scale_ref[2 * pair + n]
        q_unit, q_inverse = unit_of(q, mask)
        q_hat = (q_unit * scale).astype(BF16)
        d_out = jnp.where(mask, d_mixed, jnp.zeros_like(d_mixed))
        offset = jnp.sum(jnp.where(mask, products, 0.0), axis=-1, keepdims=True)
        offset = jnp.transpose(jnp.broadcast_to(offset, products.shape))[:1]
        scores = matmul(k_hat, q_hat, NT) + (bias_ref[...] - jnp.abs(scale))
        weights = jnp.exp(scores)
        weights = weights * (1.0 / jnp.sum(weights, axis=0, keepdims=True))
        d_weights = matmul(v, d_out, NT)
        d_scores = (weights * (d_weights - offset)).astype(BF16)
        d_v = matmul(weights.astype(BF16), d_out, NN)
        d_k = matmul(d_scores, q_hat, NN)
        d_q = jnp.where(mask, matmul(d_scores, k_hat, TN), 0.0)
        d_k = jnp.where(mask, d_k, 0.0)
        k_unit, k_inverse = k_units[n]
        term = d_q * q_unit
        term_n = jnp.sum(term, axis=0, keepdims=True)
        d_q = q_inverse * scale * (d_q - q_unit * jnp.sum(term, axis=-1, keepdims=True))
        d_k = k_inverse * (d_k - k_unit * jnp.sum(d_k * k_unit, axis=-1, keepdims=True))
        if n == 0:
            d_q_all, d_k_all, d_v_all, term_all = d_q, d_k, d_v, term_n
        else:
            d_q_all, d_k_all = d_q_all + d_q, d_k_all + d_k
            d_v_all, term_all = d_v_all + d_v, term_all + term_n
    out_ref[:, :lanes] = d_q_all.astype(out_ref.dtype)
    out_ref[:, lanes : 2 * lanes] = d_k_all.astype(out_ref.dtype)
    out_ref[:, 2 * lanes :] = d_v_all.astype(out_ref.dtype)
    term_ref[...] = jnp.broadcast_to(term_all, term_ref.shape)


def attend_back_whole(raw, mixed, d_mixed, scale_row, all_scale):
    tokens, width = mixed.shape
    heads = all_scale.shape[0]
    head_dim = width // heads
    lanes = 2 * head_dim
    pairs = width // lanes

    block = pl.BlockSpec((tokens, lanes), lambda n: (0, n))
    triple = pl.BlockSpec((tokens, 3 * lanes), lambda n: (0, n))
    d_raw, terms = pl.pallas_call(
        functools.partial(attend_back_kernel, head_dim),
        out_shape=[
            jax.ShapeDtypeStruct((tokens, 3 * width), BF16),
            jax.ShapeDtypeStruct((8, width), F32),
        ],
        grid=(pairs,),
        in_specs=[
            pl.BlockSpec(memory_space=pltpu.SMEM),
            pl.BlockSpec((1, tokens), lambda n: (0, 0)),
            pl.BlockSpec((tokens, 1), lambda n: (0, 0)),
            triple,
            block,
            block,
        ],
        out_specs=[
            triple,
            pl.BlockSpec((8, lanes), lambda n: (0, n)),
        ],
        scratch_shapes=[pltpu.VMEM((tokens, tokens), F32)],
        cost_estimate=BRIEF,
        compiler_params=pltpu.CompilerParams(vmem_limit_bytes=VMEM_LIMIT),
    )(all_scale, scale_row[None, :], scale_row[:, None], raw, mixed, d_mixed)
    return d_raw, jnp.sum(terms[0].reshape(heads, head_dim), axis=1)


def halves(values, c, half):
    keep = lax.dynamic_slice_in_dim(values, c * half, half, axis=1)
    give = lax.dynamic_slice_in_dim(values, (1 - c) * half, half, axis=1)
    return keep, give


def on_device_whole(
    inputs, labels, scale_ids, cotangent, table, w_ada, w_qkv, head_scale, w_proj, w_fc1, w_fc2
):
    width = inputs.shape[2]
    classes, rows = table.shape
    heads = TS * head_scale.shape[0]
    quarter = w_qkv.shape[2] // 2
    hidden_quarter = w_fc1.shape[1] // 2
    z, x, c, t = place()
    position = jnp.stack([z, x, c, t]).astype(jnp.int32)

    where = (z, x, c, t)

    pair = 2 * width // heads


    label_pair = jnp.stack(in_order(labels[0], labels[1], t)).astype(F32)
    label_tile = jnp.broadcast_to(label_pair[:, None], (2, 128))
    scale_tile = jnp.broadcast_to(head_scale[None, :], (8, head_scale.shape[0]))
    qkv_halves = []
    for side in (c, 1 - c):
        columns = [
            lax.dynamic_slice_in_dim(w_qkv[:, n].astype(BF16), side * quarter + j * pair, pair, 1)
            for j in range(quarter // pair)
            for n in range(3)
        ]
        qkv_halves.append(jnp.concatenate(columns, axis=1))
    keep_qkv, give_qkv, label_tile, scale_tile, inputs = hold(
        *qkv_halves, label_tile, scale_tile, inputs
    )
    recv_qkv, label_z = send(give_qkv, to_core), send_z(label_tile)
    keep_qkv, recv_qkv, label_z = hold(keep_qkv, recv_qkv, label_z)
    two_qkv = jnp.stack([keep_qkv, recv_qkv])
    two_qkv, label_z, inputs, scale_tile, rest = hold(
        two_qkv,
        label_z,
        inputs,
        scale_tile,
        (cotangent, w_ada, w_proj, w_fc1, w_fc2, table, scale_ids),
    )
    cotangent, w_ada, w_proj, w_fc1, w_fc2, table, scale_ids = rest
    z_qkv = send_z(two_qkv)
    token_other = send(pick(inputs, 1 - t).astype(BF16), to_t)
    scale_row = pick(scale_ids, t)

    label_rows = jnp.concatenate([label_tile] + label_z)
    label_rows = jnp.concatenate([label_rows, send(label_rows, to_x)])
    label_rows = jnp.concatenate([label_rows, send(label_rows, to_core)])
    all_labels = label_rows[:, 0].astype(jnp.int32)
    one_hot = (all_labels[:, None] == jnp.arange(classes)[None, :]).astype(BF16)
    condition = matmul(one_hot, table.astype(BF16), NN)
    silu_low = jax.nn.silu(condition).astype(BF16)
    ada_low = w_ada.astype(BF16).reshape(rows, 6 * width)
    silu_own = silu_low.reshape(-1, TS, rows)[:, 0]
    partial = matmul(silu_own, ada_low, NN).reshape(CS, XS, ZS, 6 * width)
    partial = partial[0] + send(partial[1], to_core)
    own_part, x_part = partial[0], send(partial[1], to_x)
    w_fc1, w_proj_t, w_fc2_t = w_fc1.astype(BF16), w_proj.astype(BF16).T, w_fc2.astype(BF16).T
    rest_halves = [halves(w_proj_t, c, quarter), halves(w_fc1, c, hidden_quarter)]
    rest_halves.append(halves(w_fc2_t, c, hidden_quarter))
    keep_rest, give_rest = [jnp.concatenate([part[n] for part in rest_halves], 1) for n in range(2)]
    split = quarter + hidden_quarter
    z_qkv, own_part, x_part, token_other, recv_rest = hold(
        z_qkv, own_part, x_part, token_other, send(give_rest, to_core)
    )

    four_qkv = jnp.stack([two_qkv] + z_qkv)
    partial = own_part + x_part
    four_qkv, partial, recv_rest, token_other = hold(four_qkv, partial, recv_rest, token_other)
    near_qkv, far_qkv = send(four_qkv, to_near), send(four_qkv, to_far)
    mod_z = send_terms_z([partial[ZS - k] for k in range(1, ZS)])
    two_mid = jnp.stack([keep_rest[:, :split], recv_rest[:, :split]])
    two_fc2 = jnp.stack([keep_rest[:, split:], recv_rest[:, split:]])
    mod_z, two_mid, two_fc2 = hold(mod_z, two_mid, two_fc2)
    mid_2 = send(two_mid, to_z(2))
    modulation = sum(mod_z, partial[0]).reshape(6, 1, width)
    gain_attn, gain_mlp, scale_attn, scale_mlp, shift_attn, shift_mlp = modulation
    tokens_in = join_image(inputs, token_other, t)
    cotangent_give = pick(cotangent, 1 - t).astype(BF16)
    near_qkv, far_qkv, mid_2, two_mid, cotangent_give, scale_tile = hold(
        near_qkv, far_qkv, mid_2, two_mid, cotangent_give, scale_tile
    )
    last_qkv = send(near_qkv, to_far)
    mid_1, mid_3 = send(two_mid, to_z(1)), send(two_mid, to_z(3))
    scale_other = send(scale_tile, to_t)
    cotangent_other = send(cotangent_give, to_t)
    normed_one, inverse_one = layer_norm(tokens_in)
    hidden_one = (normed_one * (1.0 + scale_attn) + shift_attn).astype(BF16)
    last_qkv, mid_1, mid_3, hidden_one, scale_other, cotangent_other = hold(
        last_qkv, mid_1, mid_3, hidden_one, scale_other, cotangent_other
    )
    scales = jnp.concatenate(in_order(head_scale, scale_other[0], t)).reshape(TS, 2, -1)
    scale_own, scale_oth = pick(scales, c, 1).reshape(-1), pick(scales, 1 - c, 1).reshape(-1)
    four_mid = jnp.stack([two_mid, mid_1, mid_2, mid_3])
    four_mid, last_qkv, two_fc2, hidden_one = hold(four_mid, last_qkv, two_fc2, hidden_one)
    near_mid, far_mid = send(four_mid, to_near), send(four_mid, to_far)
    z_fc2 = send_z(two_fc2)
    (qkv_own,) = assemble([four_qkv, near_qkv, far_qkv, last_qkv], position, [3 * quarter])
    raw_own = matmul(hidden_one, qkv_own, NN).astype(BF16)
    raw_own, qkv_oth = hold(raw_own, send(qkv_own, to_core))
    raw_oth = matmul(hidden_one, qkv_oth, NN).astype(BF16)
    mixed_own = attend_whole(raw_own, scale_row, scale_own)
    mixed_own, near_mid, far_mid, z_fc2, raw_oth = hold(
        mixed_own, near_mid, far_mid, z_fc2, raw_oth
    )
    last_mid = send(near_mid, to_far)
    mixed_oth = attend_whole(raw_oth, scale_row, scale_oth)
    four_fc2 = jnp.stack([two_fc2] + z_fc2)
    mixed_oth, last_mid, four_fc2 = hold(mixed_oth, last_mid, four_fc2)
    near_fc2, far_fc2 = send(four_fc2, to_near), send(four_fc2, to_far)
    proj_own, fc1_own = assemble(
        [four_mid, near_mid, far_mid, last_mid], position, [quarter, hidden_quarter]
    )
    upstream = join_image(cotangent, cotangent_other, t)
    d_branch = (gain_mlp * upstream).astype(BF16)
    proj_oth, d_branch = hold(send(proj_own, to_core), d_branch)
    fc1_oth = send(fc1_own, to_core)
    attended = matmul(mixed_own, proj_own, NT) + matmul(mixed_oth, proj_oth, NT)
    middle = tokens_in + gain_attn * attended
    normed_two, inverse_two = layer_norm(middle)
    hidden_two = (normed_two * (1.0 + scale_mlp) + shift_mlp).astype(BF16)
    hidden_two, fc1_oth = hold(hidden_two, fc1_oth)

    def activate(weights):
        first = (2.0 / jnp.pi) ** 0.5
        before = matmul(hidden_two, weights, NN)
        square = before * before
        gate = 0.5 + 0.5 * jnp.tanh(before * (first + (first * 0.044715) * square))
        active = before * gate
        steep = 2.0 * first + (6.0 * first * 0.044715) * square
        return active.astype(BF16), (gate + active * (1.0 - gate) * steep).astype(BF16)

    active_oth, slope_oth = activate(fc1_oth)
    active_oth, slope_oth, near_fc2, far_fc2 = hold(active_oth, slope_oth, near_fc2, far_fc2)
    last_fc2 = send(near_fc2, to_far)
    active_own, slope_own = activate(fc1_own)
    given = products([(d_branch, active_oth)])
    given, active_own, slope_own, last_fc2 = hold(given, active_own, slope_own, last_fc2)
    added = [send(part, to_core) for part in given]
    (fc2_own,) = assemble([four_fc2, near_fc2, far_fc2, last_fc2], position, [hidden_quarter])
    fc2_own, added = hold(fc2_own, added)
    fc2_oth = send(fc2_own, to_core)
    blocks_fc2 = products([(d_branch, active_own)], added)
    blocks_fc2, fc2_oth = hold(blocks_fc2, fc2_oth)
    far_fc2 = send(scatter_far(blocks_fc2, where), to_far)
    d_before_oth = (matmul(d_branch, fc2_oth, NN) * slope_oth.astype(F32)).astype(BF16)
    d_before_own = (matmul(d_branch, fc2_own, NN) * slope_own.astype(F32)).astype(BF16)
    branch = matmul(active_own, fc2_own, NT) + matmul(active_oth, fc2_oth, NT)
    output_own, output_give = own_and_other(middle + gain_mlp * branch, t)

    d_gain_mlp = jnp.sum(upstream * branch, axis=0)
    d_before_oth, d_before_own, output_give, far_fc2 = hold(
        d_before_oth, d_before_own, output_give, far_fc2
    )
    near_fc2 = send(scatter_near(blocks_fc2, far_fc2, where), to_near)
    d_hidden_two = matmul(d_before_own, fc1_own, NT) + matmul(d_before_oth, fc1_oth, NT)
    d_scale_mlp = jnp.sum(d_hidden_two * normed_two, axis=0)
    d_shift_mlp = jnp.sum(d_hidden_two, axis=0)
    d_middle = upstream + norm_back(d_hidden_two * (1.0 + scale_mlp), normed_two, inverse_two)
    d_gain_attn = jnp.sum(d_middle * attended, axis=0)
    d_attended = (gain_attn * d_middle).astype(BF16)
    given = products([(d_attended, mixed_oth), (hidden_two, d_before_oth)])
    given, d_attended, near_fc2 = hold(given, d_attended, near_fc2)
    z_fc2 = scatter_z(blocks_fc2, far_fc2, near_fc2, where)
    own_fc2, others_fc2 = z_fc2[0], send_terms_z(z_fc2[1:])
    d_mixed_oth = matmul(d_attended, proj_oth, NN).astype(BF16)
    d_mixed_own = matmul(d_attended, proj_own, NN).astype(BF16)
    d_mixed_oth, d_mixed_own, added = hold(d_mixed_oth, d_mixed_own, [send(part, to_core) for part in given])
    blocks_mid = products([(d_attended, mixed_own), (hidden_two, d_before_own)], added)
    blocks_mid, d_mixed_oth, others_fc2 = hold(blocks_mid, d_mixed_oth, others_fc2)
    far_mid = send(scatter_far(blocks_mid, where), to_far)
    d_raw_oth, terms_oth = attend_back_whole(raw_oth, mixed_oth, d_mixed_oth, scale_row, scale_oth)
    given = products([(hidden_one, d_raw_oth)])
    given, far_mid, d_mixed_own = hold(given, far_mid, d_mixed_own)
    near_mid = send(scatter_near(blocks_mid, far_mid, where), to_near)
    added = [send(part, to_core) for part in given]
    output_other = send(output_give, to_t)
    d_raw_own, terms_own = attend_back_whole(raw_own, mixed_own, d_mixed_own, scale_row, scale_own)
    d_raw_own, near_mid, added = hold(d_raw_own, near_mid, added)
    z_mid = scatter_z(blocks_mid, far_mid, near_mid, where)
    own_mid, others_mid = z_mid[0], send_terms_z(z_mid[1:])
    blocks_qkv = products([(hidden_one, d_raw_own)], added)
    blocks_qkv, d_raw_own = hold(blocks_qkv, d_raw_own)
    far_qkv = send(scatter_far(blocks_qkv, where), to_far)
    d_hidden_one = matmul(d_raw_own, qkv_own, NT) + matmul(d_raw_oth, qkv_oth, NT)
    d_scale_attn = jnp.sum(d_hidden_one * normed_one, axis=0)
    d_shift_attn = jnp.sum(d_hidden_one, axis=0)
    d_modulation = jnp.concatenate(
        [d_gain_attn, d_gain_mlp, d_scale_attn, d_scale_mlp, d_shift_attn, d_shift_mlp]
    )
    terms = in_order(terms_own.reshape(TS, -1), terms_oth.reshape(TS, -1), c)
    scale_terms = jnp.concatenate(terms, axis=1).reshape(-1)
    scale_high = lax.reduce_precision(scale_terms, 8, 7)
    row = jnp.concatenate(
        [d_modulation, scale_high, scale_terms - scale_high, jnp.zeros((128 - 2 * heads,), F32)]
    ).astype(BF16)[None, :]
    d_inputs = d_middle + norm_back(d_hidden_one * (1.0 + scale_attn), normed_one, inverse_one)
    inputs_own, inputs_give = own_and_other(d_inputs, t)
    row_other = send(row, to_t)
    far_qkv, inputs_give, row_other, output_other = hold(
        far_qkv, inputs_give, row_other, output_other
    )
    near_give, inputs_give, row_other = hold(
        scatter_near(blocks_qkv, far_qkv, where), inputs_give, row_other
    )
    near_qkv = send(near_give, to_near)
    inputs_other = send(inputs_give, to_t)
    mod_rows = jnp.concatenate([row, row_other])
    near_qkv, mod_z, others_mid = hold(near_qkv, send_z(mod_rows), others_mid)
    z_qkv = scatter_z(blocks_qkv, far_qkv, near_qkv, where)
    z_qkv, mod_z, mod_rows = hold(z_qkv, mod_z, mod_rows)
    own_qkv, others_qkv = z_qkv[0], send_terms_z(z_qkv[1:])
    half_fc2, other_fc2 = scatter_total(own_fc2, others_fc2, where)
    half_mid, other_mid = scatter_total(own_mid, others_mid, where)
    other_rest = send(jnp.concatenate([other_mid, other_fc2], axis=1), to_core)
    mod_rows = jnp.concatenate([mod_rows] + mod_z)
    mod_rows = jnp.concatenate([mod_rows, send(mod_rows, to_x)])
    mod_rows = jnp.concatenate([mod_rows, send(mod_rows, to_core)])

    d_mod_all = mod_rows[:, : 6 * width]
    scale_sum = jnp.sum(mod_rows[:, 6 * width : 6 * width + 2 * heads].astype(F32), axis=0)
    scale_sum = (scale_sum[:heads] + scale_sum[heads:]).reshape(TS, heads // TS)
    grad_scale = pick(scale_sum, t)
    grad_ada = matmul(silu_low, d_mod_all, TN).reshape(rows, 6, width)
    d_silu = matmul(d_mod_all, ada_low, NT)
    _, silu_pull = jax.vjp(jax.nn.silu, condition)
    d_condition = silu_pull(d_silu)[0]
    grad_table = jnp.dot(one_hot.astype(F32).T, d_condition, precision=HIGHEST)

    def joined(own, other):
        return jnp.concatenate(in_order(own, other.astype(F32), c), axis=1)

    grad_proj = joined(half_mid[:, :quarter], other_rest[:, :quarter]).T
    grad_fc1 = joined(half_mid[:, quarter:], other_rest[:, quarter:split])
    grad_fc2 = joined(half_fc2, other_rest[:, split:]).T
    others_qkv, others = hold(
        others_qkv, (grad_ada, grad_table, grad_scale, inputs_other, grad_proj, grad_fc1, grad_fc2)
    )
    grad_ada, grad_table, grad_scale, inputs_other, grad_proj, grad_fc1, grad_fc2 = others
    half_qkv, other_qkv = scatter_total(own_qkv, others_qkv, where)
    other_qkv = send(other_qkv, to_core)

    def part_of(values, n):
        starts = range(n * pair, 3 * quarter, 3 * pair)
        return jnp.concatenate([values[:, start : start + pair] for start in starts], axis=1)

    grad_qkv = [joined(part_of(half_qkv, n), part_of(other_qkv, n)) for n in range(3)]
    return (
        two_images(output_own, output_other, t),
        two_images(inputs_own, inputs_other, t),
        grad_table,
        grad_ada,
        jnp.stack(grad_qkv, axis=1),
        grad_scale,
        grad_proj,
        grad_fc1,
        grad_fc2,
    )


def solution(mesh):
    placed = (
        P("dp", "tensor", None),
        P("dp"),
        P("dp", None),
        P("dp", "tensor", None),
        P(None, "dp"),
        P("dp", None, None),
        P("dp", None, "tensor"),
        P("tensor"),
        P("tensor", "dp"),
        P("dp", "tensor"),
        P("tensor", "dp"),
    )
    fitting = mesh.shape["dp"] == ZS * XS * CS and mesh.shape["tensor"] == TS

    def on_device(inputs, *others):
        fits = fitting and inputs.shape[0] == TS
        return (on_device_whole if fits else on_device_general)(inputs, *others)

    return jax.shard_map(
        on_device,
        mesh=mesh,
        in_specs=placed,
        out_specs=(
            P("dp", "tensor", None),
            P("dp", "tensor", None),
            P(None, "dp"),
            P("dp", None, None),
            P("dp", None, "tensor"),
            P("tensor"),
            P("tensor", "dp"),
            P("dp", "tensor"),
            P("tensor", "dp"),
        ),
        check_vma=False,
    )
```

```python
import functools
import math

import jax
import jax.numpy as jnp
from jax import lax
from jax.experimental import pallas as pl
from jax.experimental.pallas import tpu as pltpu
from jax.sharding import PartitionSpec as P

EPSILON = 1e-06
HIGHEST = lax.Precision.HIGHEST


def layer_norm(values):
    average = jnp.mean(values, axis=-1, keepdims=True)
    centred = values - average
    inverse = lax.rsqrt(jnp.mean(centred * centred, axis=-1, keepdims=True) + EPSILON)
    return (centred * inverse, inverse)


def norm_back(d_normed, normed, inverse):
    return inverse * (
        d_normed
        - jnp.mean(d_normed, axis=-1, keepdims=True)
        - normed * jnp.mean(d_normed * normed, axis=-1, keepdims=True)
    )


def unit_rows(values):
    inverse = lax.rsqrt(jnp.sum(values * values, axis=-1, keepdims=True) + EPSILON)
    return (values * inverse, inverse)


def unit_back(d_unit, unit, inverse):
    return inverse * (d_unit - unit * jnp.sum(d_unit * unit, axis=-1, keepdims=True))


def spread(values):
    return lax.all_gather(values, "tensor", axis=1, tiled=True)


def collect(terms):
    return lax.psum_scatter(
        terms.astype(jnp.bfloat16), "tensor", scatter_dimension=1, tiled=True
    ).astype(jnp.float32)


def masked_scores(queries, keys_in, scale_row):
    scores = jnp.einsum("qhd,khd->hqk", queries, keys_in, preferred_element_type=jnp.float32)
    visible = scale_row[None, :] <= scale_row[:, None]
    return jnp.where(visible[None], scores, -1e30)


def attend_forward(pieces):
    queries, keys_in, values_in, scale_row = pieces
    scores = masked_scores(queries, keys_in, scale_row)
    largest = jnp.max(scores, axis=-1, keepdims=True)
    exponent = jnp.exp(scores - largest)
    denominator = jnp.sum(exponent, axis=-1, keepdims=True)
    attn_probs = (exponent / denominator).astype(jnp.bfloat16)
    mixed = jnp.einsum("hqk,khd->qhd", attn_probs, values_in, preferred_element_type=jnp.float32)
    return (mixed.astype(jnp.bfloat16), (largest + jnp.log(denominator))[..., 0])


def attend_backward(pieces):
    queries, keys_in, values_in, scale_row, log_total, d_mixed = pieces
    scores = masked_scores(queries, keys_in, scale_row)
    attn_probs = jnp.exp(scores - log_total[..., None])
    d_probs = jnp.einsum("qhd,khd->hqk", d_mixed, values_in, preferred_element_type=jnp.float32)
    offset = jnp.sum(attn_probs * d_probs, axis=-1, keepdims=True)
    d_scores = (attn_probs * (d_probs - offset)).astype(jnp.bfloat16)
    d_queries = jnp.einsum("hqk,khd->qhd", d_scores, keys_in, preferred_element_type=jnp.float32)
    d_keys = jnp.einsum("hqk,qhd->khd", d_scores, queries, preferred_element_type=jnp.float32)
    d_values = jnp.einsum(
        "hqk,qhd->khd", attn_probs.astype(jnp.bfloat16), d_mixed, preferred_element_type=jnp.float32
    )
    return (d_queries, d_keys, d_values)


def on_device_general(
    inputs, labels, scale_ids, cotangent, table, w_ada, w_qkv, head_scale, w_proj, w_fc1, w_fc2
):
    images, local_len, model_width = inputs.shape
    full_len = scale_ids.shape[1]
    local_heads = head_scale.shape[0]
    head_dim = w_qkv.shape[2] // local_heads
    classes = table.shape[0]
    gathered = (
        lax.all_gather(table.astype(jnp.bfloat16), "dp", axis=1, tiled=True),
        lax.all_gather(w_qkv.astype(jnp.bfloat16), "dp", axis=0, tiled=True),
        lax.all_gather(w_proj.astype(jnp.bfloat16), "dp", axis=1, tiled=True),
        lax.all_gather(w_fc1.astype(jnp.bfloat16), "dp", axis=0, tiled=True),
        lax.all_gather(w_fc2.astype(jnp.bfloat16), "dp", axis=1, tiled=True),
    )
    table_low, qkv_low, proj_low, fc1_low, fc2_low = gathered
    qkv_flat = qkv_low.reshape(model_width, -1)
    one_hot = labels[:, None] == jnp.arange(classes)[None, :]
    condition = jnp.dot(one_hot.astype(jnp.bfloat16), table_low, preferred_element_type=jnp.float32)
    silu_low = jax.nn.silu(condition).astype(jnp.bfloat16)
    ada_full = lax.all_gather(w_ada.astype(jnp.bfloat16), "dp", axis=0, tiled=True).reshape(
        model_width, 6 * model_width
    )
    modulation = jnp.dot(silu_low, ada_full, preferred_element_type=jnp.float32)
    modulation = modulation.reshape(images, 6, model_width)
    gain_attn = modulation[:, 0, None, :]
    gain_mlp = modulation[:, 1, None, :]
    scale_attn = modulation[:, 2, None, :]
    scale_mlp = modulation[:, 3, None, :]
    shift_attn = modulation[:, 4, None, :]
    shift_mlp = modulation[:, 5, None, :]
    normed_one, inverse_one = layer_norm(inputs)
    hidden_one = spread((normed_one * (1.0 + scale_attn) + shift_attn).astype(jnp.bfloat16))
    projected = jnp.einsum("bld,dc->blc", hidden_one, qkv_flat, preferred_element_type=jnp.float32)
    projected = projected.reshape(images, full_len, 3, local_heads, head_dim)
    q_unit, q_inverse = unit_rows(projected[:, :, 0])
    k_unit, k_inverse = unit_rows(projected[:, :, 1])
    q_hat = (q_unit * head_scale[:, None]).astype(jnp.bfloat16)
    k_hat = k_unit.astype(jnp.bfloat16)
    v_hat = projected[:, :, 2].astype(jnp.bfloat16)
    mixed, log_total = lax.map(attend_forward, (q_hat, k_hat, v_hat, scale_ids))
    mixed_flat = mixed.reshape(images, full_len, local_heads * head_dim)
    attended = collect(
        jnp.einsum("blc,cd->bld", mixed_flat, proj_low, preferred_element_type=jnp.float32)
    )
    middle = inputs + gain_attn * attended
    normed_two, inverse_two = layer_norm(middle)
    hidden_two = spread((normed_two * (1.0 + scale_mlp) + shift_mlp).astype(jnp.bfloat16))
    before = jnp.einsum("bld,df->blf", hidden_two, fc1_low, preferred_element_type=jnp.float32)
    gelu_fn = functools.partial(jax.nn.gelu, approximate=True)
    active_f, gelu_pull = jax.vjp(gelu_fn, before)
    active = active_f.astype(jnp.bfloat16)
    branch = collect(jnp.einsum("blf,fd->bld", active, fc2_low, preferred_element_type=jnp.float32))
    output = middle + gain_mlp * branch
    again = (
        lax.all_gather(w_qkv.astype(jnp.bfloat16), "dp", axis=0, tiled=True),
        lax.all_gather(w_proj.astype(jnp.bfloat16), "dp", axis=1, tiled=True),
        lax.all_gather(w_fc1.astype(jnp.bfloat16), "dp", axis=0, tiled=True),
        lax.all_gather(w_fc2.astype(jnp.bfloat16), "dp", axis=1, tiled=True),
    )
    qkv_back, proj_back, fc1_back, fc2_back = again
    d_gain_mlp = jnp.sum(cotangent * branch, axis=1)
    d_branch = spread((gain_mlp * cotangent).astype(jnp.bfloat16))
    grad_fc2 = jnp.einsum("blf,bld->fd", active, d_branch, preferred_element_type=jnp.float32)
    d_active = jnp.einsum("bld,fd->blf", d_branch, fc2_back, preferred_element_type=jnp.float32)
    d_before = gelu_pull(d_active)[0].astype(jnp.bfloat16)
    grad_fc1 = jnp.einsum("bld,blf->df", hidden_two, d_before, preferred_element_type=jnp.float32)
    d_hidden_two = collect(
        jnp.einsum("blf,df->bld", d_before, fc1_back, preferred_element_type=jnp.float32)
    )
    d_scale_mlp = jnp.sum(d_hidden_two * normed_two, axis=1)
    d_shift_mlp = jnp.sum(d_hidden_two, axis=1)
    d_middle = cotangent + norm_back(d_hidden_two * (1.0 + scale_mlp), normed_two, inverse_two)
    d_gain_attn = jnp.sum(d_middle * attended, axis=1)
    d_attended = spread((gain_attn * d_middle).astype(jnp.bfloat16))
    grad_proj = jnp.einsum(
        "blc,bld->cd", mixed_flat, d_attended, preferred_element_type=jnp.float32
    )
    d_mixed = jnp.einsum("bld,cd->blc", d_attended, proj_back, preferred_element_type=jnp.float32)
    d_mixed = d_mixed.astype(jnp.bfloat16).reshape(images, full_len, local_heads, head_dim)
    d_q_hat, d_k_hat, d_v_hat = lax.map(
        attend_backward, (q_hat, k_hat, v_hat, scale_ids, log_total, d_mixed)
    )
    scale_terms = jnp.sum(d_q_hat * q_unit, axis=(0, 1, 3))
    d_query = unit_back(d_q_hat * head_scale[:, None], q_unit, q_inverse)
    d_key = unit_back(d_k_hat, k_unit, k_inverse)
    d_raw = jnp.stack([d_query, d_key, d_v_hat], axis=2).astype(jnp.bfloat16)
    d_raw = d_raw.reshape(images, full_len, 3 * local_heads * head_dim)
    grad_qkv = jnp.einsum("bld,blc->dc", hidden_one, d_raw, preferred_element_type=jnp.float32)
    grad_qkv = grad_qkv.reshape(model_width, 3, local_heads * head_dim)
    d_hidden_one = collect(
        jnp.einsum(
            "blc,dc->bld",
            d_raw,
            qkv_back.reshape(model_width, -1),
            preferred_element_type=jnp.float32,
        )
    )
    d_scale_attn = jnp.sum(d_hidden_one * normed_one, axis=1)
    d_shift_attn = jnp.sum(d_hidden_one, axis=1)
    d_inputs = d_middle + norm_back(d_hidden_one * (1.0 + scale_attn), normed_one, inverse_one)
    mod_terms_back = jnp.stack(
        [d_gain_attn, d_gain_mlp, d_scale_attn, d_scale_mlp, d_shift_attn, d_shift_mlp], axis=1
    )
    d_modulation = lax.psum(mod_terms_back.astype(jnp.bfloat16), "tensor").astype(jnp.float32)
    d_mod_flat = d_modulation.reshape(images, 6 * model_width)
    grad_scale = lax.psum(scale_terms, "dp")
    ada_terms = jnp.dot(silu_low.astype(jnp.float32).T, d_mod_flat, precision=HIGHEST)
    grad_ada = lax.psum_scatter(
        ada_terms.reshape(model_width, 6, model_width).astype(jnp.bfloat16),
        "dp",
        scatter_dimension=0,
        tiled=True,
    ).astype(jnp.float32)
    d_silu = jnp.dot(d_mod_flat, ada_full.astype(jnp.float32).T, precision=HIGHEST)
    _, silu_pull = jax.vjp(jax.nn.silu, condition)
    d_condition = silu_pull(d_silu)[0]
    table_terms = jnp.dot(one_hot.astype(jnp.float32).T, d_condition, precision=HIGHEST)
    summed = (
        lax.psum_scatter(
            table_terms.astype(jnp.bfloat16), "dp", scatter_dimension=1, tiled=True
        ).astype(jnp.float32),
        lax.psum_scatter(
            grad_qkv.astype(jnp.bfloat16), "dp", scatter_dimension=0, tiled=True
        ).astype(jnp.float32),
        lax.psum_scatter(
            grad_proj.astype(jnp.bfloat16), "dp", scatter_dimension=1, tiled=True
        ).astype(jnp.float32),
        lax.psum_scatter(
            grad_fc1.astype(jnp.bfloat16), "dp", scatter_dimension=0, tiled=True
        ).astype(jnp.float32),
        lax.psum_scatter(
            grad_fc2.astype(jnp.bfloat16), "dp", scatter_dimension=1, tiled=True
        ).astype(jnp.float32),
    )
    grad_table, grad_qkv_own, grad_proj_own, grad_fc1_own, grad_fc2_own = summed
    return (
        output,
        d_inputs,
        grad_table,
        grad_ada,
        grad_qkv_own,
        grad_scale,
        grad_proj_own,
        grad_fc1_own,
        grad_fc2_own,
    )


BF16 = jnp.bfloat16
F32 = jnp.float32
ZS, XS, CS, TS = 4, 2, 2, 2
BOTH = ("dp", "tensor")
NN = (((1,), (0,)), ((), ()))
NT = (((1,), (1,)), ((), ()))
TN = (((0,), (0,)), ((), ()))
HIDDEN = -1e30
MIB = 1024 * 1024
BRIEF = pl.CostEstimate(flops=0, bytes_accessed=0, transcendentals=0)


def perm_of(step):
    pairs = []
    for z in range(ZS):
        for x in range(XS):
            for c in range(CS):
                for t in range(TS):
                    nz, nx, nc, nt = step(z, x, c, t)
                    source = ((z * XS + x) * CS + c) * TS + t
                    target = ((nz * XS + nx) * CS + nc) * TS + nt
                    pairs.append((source, target))
    return pairs


def send(values, step):
    return lax.ppermute(values, BOTH, perm_of(step))


def to_core(z, x, c, t):
    return (z, x, 1 - c, t)


def to_x(z, x, c, t):
    return (z, 1 - x, c, t)


def to_t(z, x, c, t):
    return (z, x, c, 1 - t)


def to_z(k):
    return lambda z, x, c, t: ((z + k) % ZS, x, c, t)


def to_near(z, x, c, t):
    return (z, 1 - x, c, t) if c == 0 else (z, x, c, 1 - t)


def to_far(z, x, c, t):
    return (z, x, c, 1 - t) if c == 0 else (z, 1 - x, c, t)


def pick(values, index, axis=0):
    return lax.dynamic_index_in_dim(values, index, axis, keepdims=False)


def place():
    dp = lax.axis_index("dp")
    t = lax.axis_index("tensor")
    return dp // (XS * CS), (dp // CS) % XS, dp % CS, t


def matmul(left, right, dims):
    return lax.dot_general(left, right, dims, preferred_element_type=F32)


def hold(*values):
    return lax.optimization_barrier(values)


def send_z(values):
    return [send(values, to_z(k)) for k in range(1, ZS)]


def send_terms_z(terms):
    return [send(terms[k - 1], to_z(k)) for k in range(1, ZS)]


def assemble_kernel(widths, crossed, where_ref, *refs):
    pieces, outs, sem = refs[:4], refs[4:-1], refs[-1]
    z, x, c, t = where_ref[0], where_ref[1], where_ref[2], where_ref[3]
    for slot, piece in enumerate(pieces):
        near = (1 - c, c) if crossed else (0, 1)
        dx, dt = [(0, 0), near, (1 - near[0], 1 - near[1]), (1, 1)][slot]
        sx, st = x ^ dx, t ^ dt
        for dz in range(ZS):
            for dc in range(CS):
                sz = (z + ZS - dz) % ZS
                sc = c ^ dc
                row = pl.multiple_of(((sz * XS + sx) * CS + sc) * 64, 64)
                start = 0
                for which, width in enumerate(widths):
                    column = pl.multiple_of(st * width, 128)
                    pltpu.make_async_copy(
                        piece.at[dz, dc, :, pl.ds(start, width)],
                        outs[which].at[pl.ds(row, 64), pl.ds(column, width)],
                        sem.at[which],
                    ).start()
                    start += width
    for which, out in enumerate(outs):
        pltpu.make_async_copy(out, out, sem.at[which]).wait()


def assemble(pieces, position, widths, crossed=True):
    rows = ZS * XS * CS * 64
    return pl.pallas_call(
        functools.partial(assemble_kernel, widths, crossed),
        out_shape=[jax.ShapeDtypeStruct((rows, TS * width), BF16) for width in widths],
        in_specs=[pl.BlockSpec(memory_space=pltpu.SMEM)]
        + [pl.BlockSpec(memory_space=pl.ANY)] * 4,
        out_specs=[pl.BlockSpec(memory_space=pltpu.VMEM)] * len(widths),
        scratch_shapes=[pltpu.SemaphoreType.DMA((len(widths),))],
        cost_estimate=BRIEF,
        compiler_params=pltpu.CompilerParams(vmem_limit_bytes=8 * MIB),
    )(position, *pieces)


def products(factors, added=None):
    terms = [matmul(rows, columns, TN) for rows, columns in factors]
    if added is not None:
        terms = [term + other.astype(F32) for term, other in zip(terms, added)]
    return [term.astype(BF16) for term in terms]


def block(blocks, dx, dt, where):
    z, x, c, t = where
    parts = []
    for values in blocks:
        m = values.shape[1] // TS
        values = lax.dynamic_slice_in_dim(values, (t ^ dt) * m, m, 1)
        values = pick(values.reshape(ZS, XS, CS * 64, m), x ^ dx, 1)
        parts.append(values.reshape(ZS * CS * 64, m))
    return parts[0] if len(parts) == 1 else jnp.concatenate(parts, axis=1)


def scatter_far(blocks, where):
    c = where[2]
    return jnp.stack([block(blocks, 1, 1, where), block(blocks, c, 1 - c, where)])


def scatter_near(blocks, far, where):
    c = where[2]
    return (block(blocks, 1 - c, c, where).astype(F32) + far[0].astype(F32)).astype(BF16)


def scatter_z(blocks, far, near, where):
    z = where[0]
    whole = block(blocks, 0, 0, where).astype(F32) + far[1].astype(F32) + near.astype(F32)
    whole = whole.astype(BF16).reshape(ZS, CS, 64, whole.shape[-1])
    return [pick(whole, (z + k) % ZS) for k in range(ZS)]


def scatter_total(own, others, where):
    c = where[2]
    total = sum(term.astype(F32) for term in [own] + list(others))
    return pick(total, c), pick(total, 1 - c).astype(BF16)


def in_order(own, other, bit):
    return jnp.where(bit == 0, own, other), jnp.where(bit == 0, other, own)


def join_image(values, other, t):
    return jnp.concatenate(in_order(pick(values, t), other.astype(F32), t), axis=0)


def own_and_other(values, t):
    half = values.shape[0] // 2
    own = lax.dynamic_slice_in_dim(values, t * half, half, axis=0)
    give = lax.dynamic_slice_in_dim(values, (1 - t) * half, half, axis=0)
    return own, give.astype(BF16)


def two_images(own, other, t):
    return jnp.stack(in_order(own, other.astype(F32), t))


def unit_of(values, mask):
    squares = jnp.where(mask, values * values, 0.0)
    inverse = lax.rsqrt(jnp.sum(squares, axis=-1, keepdims=True) + EPSILON)
    return jnp.where(mask, values * inverse, 0.0), inverse


def head_masks(shape, head_dim):
    lane = lax.broadcasted_iota(jnp.int32, shape, 1)
    return [(lane >= n * head_dim) & (lane < (n + 1) * head_dim) for n in range(2)]


def attend_kernel(head_dim, scale_ref, row_ref, column_ref, raw_ref, out_ref, bias_ref):
    pair = pl.program_id(0)

    @pl.when(pair == 0)
    def _():
        bias_ref[...] = jnp.where(row_ref[...] <= column_ref[...], 0.0, HIDDEN)

    lanes = 2 * head_dim
    q, k = raw_ref[:, :lanes].astype(F32), raw_ref[:, lanes : 2 * lanes].astype(F32)
    v = raw_ref[:, 2 * lanes :]
    values = jnp.concatenate([v, jnp.ones_like(v)], axis=1)
    masks = head_masks(q.shape, head_dim)
    k_hat = (unit_of(k, masks[0])[0] + unit_of(k, masks[1])[0]).astype(BF16)
    result = None
    for n in range(2):
        scale = scale_ref[2 * pair + n]
        q_hat = (unit_of(q, masks[n])[0] * scale).astype(BF16)
        scores = matmul(q_hat, k_hat, NT) + (bias_ref[...] - jnp.abs(scale))
        weights = jnp.exp(scores).astype(BF16)
        mixed = matmul(weights, values, NN)
        mixed = mixed[:, : 2 * head_dim] / mixed[:, 2 * head_dim :]
        result = mixed if result is None else jnp.where(masks[n], mixed, result)
    out_ref[...] = result.astype(out_ref.dtype)


def attend_whole(raw, scale_row, all_scale):
    tokens, width = raw.shape[0], raw.shape[1] // 3
    head_dim = width // all_scale.shape[0]
    lanes = 2 * head_dim
    pairs = width // lanes

    block = pl.BlockSpec((tokens, lanes), lambda n: (0, n))
    triple = pl.BlockSpec((tokens, 3 * lanes), lambda n: (0, n))
    return pl.pallas_call(
        functools.partial(attend_kernel, head_dim),
        out_shape=jax.ShapeDtypeStruct((tokens, width), BF16),
        grid=(pairs,),
        in_specs=[
            pl.BlockSpec(memory_space=pltpu.SMEM),
            pl.BlockSpec((1, tokens), lambda n: (0, 0)),
            pl.BlockSpec((tokens, 1), lambda n: (0, 0)),
            triple,
        ],
        out_specs=block,
        scratch_shapes=[pltpu.VMEM((tokens, tokens), F32)],
        cost_estimate=BRIEF,
        compiler_params=pltpu.CompilerParams(vmem_limit_bytes=16 * MIB),
    )(all_scale, scale_row[None, :], scale_row[:, None], raw)


def attend_back_kernel(
    head_dim,
    scale_ref,
    row_ref,
    column_ref,
    raw_ref,
    mixed_ref,
    d_mixed_ref,
    out_ref,
    term_ref,
    bias_ref,
):
    pair = pl.program_id(0)

    @pl.when(pair == 0)
    def _():
        bias_ref[...] = jnp.where(column_ref[...] <= row_ref[...], 0.0, HIDDEN)

    lanes = 2 * head_dim
    q, k = raw_ref[:, :lanes].astype(F32), raw_ref[:, lanes : 2 * lanes].astype(F32)
    v, d_mixed = raw_ref[:, 2 * lanes :], d_mixed_ref[...]
    masks = head_masks(q.shape, head_dim)
    k_units = [unit_of(k, mask) for mask in masks]
    k_hat = (k_units[0][0] + k_units[1][0]).astype(BF16)
    products = d_mixed.astype(F32) * mixed_ref[...].astype(F32)
    d_q_all = d_k_all = d_v_all = None
    for n in range(2):
        mask = masks[n]
        scale = scale_ref[2 * pair + n]
        q_unit, q_inverse = unit_of(q, mask)
        q_hat = (q_unit * scale).astype(BF16)
        d_out = jnp.where(mask, d_mixed, jnp.zeros_like(d_mixed))
        offset = jnp.sum(jnp.where(mask, products, 0.0), axis=-1, keepdims=True)
        offset = jnp.transpose(jnp.broadcast_to(offset, products.shape))[:1]
        scores = matmul(k_hat, q_hat, NT) + (bias_ref[...] - jnp.abs(scale))
        weights = jnp.exp(scores)
        weights = weights * (1.0 / jnp.sum(weights, axis=0, keepdims=True))
        d_weights = matmul(v, d_out, NT)
        d_scores = (weights * (d_weights - offset)).astype(BF16)
        d_v = matmul(weights.astype(BF16), d_out, NN)
        d_k = matmul(d_scores, q_hat, NN)
        d_q = jnp.where(mask, matmul(d_scores, k_hat, TN), 0.0)
        d_k = jnp.where(mask, d_k, 0.0)
        k_unit, k_inverse = k_units[n]
        term = d_q * q_unit
        term_n = jnp.sum(term, axis=0, keepdims=True)
        d_q = q_inverse * scale * (d_q - q_unit * jnp.sum(term, axis=-1, keepdims=True))
        d_k = k_inverse * (d_k - k_unit * jnp.sum(d_k * k_unit, axis=-1, keepdims=True))
        if n == 0:
            d_q_all, d_k_all, d_v_all, term_all = d_q, d_k, d_v, term_n
        else:
            d_q_all, d_k_all = d_q_all + d_q, d_k_all + d_k
            d_v_all, term_all = d_v_all + d_v, term_all + term_n
    out_ref[:, :lanes] = d_q_all.astype(out_ref.dtype)
    out_ref[:, lanes : 2 * lanes] = d_k_all.astype(out_ref.dtype)
    out_ref[:, 2 * lanes :] = d_v_all.astype(out_ref.dtype)
    term_ref[...] = jnp.broadcast_to(term_all, term_ref.shape)


def attend_back_whole(raw, mixed, d_mixed, scale_row, all_scale):
    tokens, width = mixed.shape
    heads = all_scale.shape[0]
    head_dim = width // heads
    lanes = 2 * head_dim
    pairs = width // lanes

    block = pl.BlockSpec((tokens, lanes), lambda n: (0, n))
    triple = pl.BlockSpec((tokens, 3 * lanes), lambda n: (0, n))
    d_raw, terms = pl.pallas_call(
        functools.partial(attend_back_kernel, head_dim),
        out_shape=[
            jax.ShapeDtypeStruct((tokens, 3 * width), BF16),
            jax.ShapeDtypeStruct((8, width), F32),
        ],
        grid=(pairs,),
        in_specs=[
            pl.BlockSpec(memory_space=pltpu.SMEM),
            pl.BlockSpec((1, tokens), lambda n: (0, 0)),
            pl.BlockSpec((tokens, 1), lambda n: (0, 0)),
            triple,
            block,
            block,
        ],
        out_specs=[
            triple,
            pl.BlockSpec((8, lanes), lambda n: (0, n)),
        ],
        scratch_shapes=[pltpu.VMEM((tokens, tokens), F32)],
        cost_estimate=BRIEF,
        compiler_params=pltpu.CompilerParams(vmem_limit_bytes=20 * MIB),
    )(all_scale, scale_row[None, :], scale_row[:, None], raw, mixed, d_mixed)
    return d_raw, jnp.sum(terms[0].reshape(heads, head_dim), axis=1)


def halves(values, c, half):
    keep = lax.dynamic_slice_in_dim(values, c * half, half, axis=1)
    give = lax.dynamic_slice_in_dim(values, (1 - c) * half, half, axis=1)
    return keep, give


def on_device_whole(
    inputs, labels, scale_ids, cotangent, table, w_ada, w_qkv, head_scale, w_proj, w_fc1, w_fc2
):
    width = inputs.shape[2]
    classes, rows = table.shape
    heads = TS * head_scale.shape[0]
    quarter = w_qkv.shape[2] // 2
    hidden_quarter = w_fc1.shape[1] // 2
    z, x, c, t = place()
    position = jnp.stack([z, x, c, t]).astype(jnp.int32)

    where = (z, x, c, t)

    pair = 2 * width // heads


    label_pair = jnp.stack(in_order(labels[0], labels[1], t)).astype(F32)
    label_tile = jnp.broadcast_to(label_pair[:, None], (2, 128))
    scale_tile = jnp.broadcast_to(head_scale[None, :], (8, head_scale.shape[0]))
    qkv_halves = []
    for side in (c, 1 - c):
        columns = [
            lax.dynamic_slice_in_dim(w_qkv[:, n].astype(BF16), side * quarter + j * pair, pair, 1)
            for j in range(quarter // pair)
            for n in range(3)
        ]
        qkv_halves.append(jnp.concatenate(columns, axis=1))
    keep_qkv, give_qkv, label_tile, scale_tile, inputs = hold(
        *qkv_halves, label_tile, scale_tile, inputs
    )
    recv_qkv, label_z = send(give_qkv, to_core), send_z(label_tile)
    scale_other = send(scale_tile, to_t)
    keep_qkv, recv_qkv, label_z, scale_other = hold(keep_qkv, recv_qkv, label_z, scale_other)
    two_qkv = jnp.stack([keep_qkv, recv_qkv])
    two_qkv, label_z, inputs, rest = hold(
        two_qkv,
        label_z,
        inputs,
        (cotangent, w_ada, w_proj, w_fc1, w_fc2, table, scale_ids),
    )
    cotangent, w_ada, w_proj, w_fc1, w_fc2, table, scale_ids = rest
    z_qkv = send_z(two_qkv)
    token_other = send(pick(inputs, 1 - t).astype(BF16), to_t)
    scale_row = pick(scale_ids, t)

    label_rows = jnp.concatenate([label_tile] + label_z)
    label_rows = jnp.concatenate([label_rows, send(label_rows, to_x)])
    label_rows = jnp.concatenate([label_rows, send(label_rows, to_core)])
    all_labels = label_rows[:, 0].astype(jnp.int32)
    one_hot = (all_labels[:, None] == jnp.arange(classes)[None, :]).astype(BF16)
    condition = matmul(one_hot, table.astype(BF16), NN)
    silu_low = jax.nn.silu(condition).astype(BF16)
    ada_low = w_ada.astype(BF16).reshape(rows, 6 * width)
    silu_own = silu_low.reshape(-1, TS, rows)[:, 0]
    partial = matmul(silu_own, ada_low, NN).reshape(CS, XS, ZS, 6 * width)
    partial = partial[0] + send(partial[1], to_core)
    own_part, x_part = partial[0], send(partial[1], to_x)
    w_fc1, w_proj_t, w_fc2_t = w_fc1.astype(BF16), w_proj.astype(BF16).T, w_fc2.astype(BF16).T
    rest_halves = [halves(w_proj_t, c, quarter), halves(w_fc1, c, hidden_quarter)]
    rest_halves.append(halves(w_fc2_t, c, hidden_quarter))
    keep_rest, give_rest = [jnp.concatenate([part[n] for part in rest_halves], 1) for n in range(2)]
    split = quarter + hidden_quarter
    z_qkv, own_part, x_part, token_other, recv_rest = hold(
        z_qkv, own_part, x_part, token_other, send(give_rest, to_core)
    )

    four_qkv = jnp.stack([two_qkv] + z_qkv)
    partial = own_part + x_part
    four_qkv, partial, recv_rest, token_other = hold(four_qkv, partial, recv_rest, token_other)
    near_qkv, far_qkv = send(four_qkv, to_t), send(four_qkv, to_x)
    mod_z = send_terms_z([partial[ZS - k] for k in range(1, ZS)])
    two_mid = jnp.stack([keep_rest[:, :split], recv_rest[:, :split]])
    two_fc2 = jnp.stack([keep_rest[:, split:], recv_rest[:, split:]])
    mod_z, two_mid, two_fc2 = hold(mod_z, two_mid, two_fc2)
    mid_2 = send(two_mid, to_z(2))
    modulation = sum(mod_z, partial[0]).reshape(6, 1, width)
    gain_attn, gain_mlp, scale_attn, scale_mlp, shift_attn, shift_mlp = modulation
    tokens_in = join_image(inputs, token_other, t)
    cotangent_give = pick(cotangent, 1 - t).astype(BF16)
    near_qkv, far_qkv, mid_2, two_mid, cotangent_give = hold(
        near_qkv, far_qkv, mid_2, two_mid, cotangent_give
    )
    last_qkv = send(near_qkv, to_x)
    mid_1, mid_3 = send(two_mid, to_z(1)), send(two_mid, to_z(3))
    cotangent_other = send(cotangent_give, to_t)
    normed_one, inverse_one = layer_norm(tokens_in)
    hidden_one = (normed_one * (1.0 + scale_attn) + shift_attn).astype(BF16)
    last_qkv, mid_1, mid_3, hidden_one, cotangent_other = hold(
        last_qkv, mid_1, mid_3, hidden_one, cotangent_other
    )
    scales = jnp.concatenate(in_order(head_scale, scale_other[0], t)).reshape(TS, 2, -1)
    scale_own, scale_oth = pick(scales, c, 1).reshape(-1), pick(scales, 1 - c, 1).reshape(-1)
    four_mid = jnp.stack([two_mid, mid_1, mid_2, mid_3])
    four_mid, last_qkv, two_fc2, hidden_one = hold(four_mid, last_qkv, two_fc2, hidden_one)
    near_mid, far_mid = send(four_mid, to_near), send(four_mid, to_far)
    z_fc2 = send_z(two_fc2)
    (qkv_own,) = assemble(
        [four_qkv, near_qkv, far_qkv, last_qkv], position, [3 * quarter], crossed=False
    )
    raw_own = matmul(hidden_one, qkv_own, NN).astype(BF16)
    raw_own, qkv_oth = hold(raw_own, send(qkv_own, to_core))
    raw_oth = matmul(hidden_one, qkv_oth, NN).astype(BF16)
    mixed_own = attend_whole(raw_own, scale_row, scale_own)
    mixed_own, near_mid, far_mid, z_fc2, raw_oth = hold(
        mixed_own, near_mid, far_mid, z_fc2, raw_oth
    )
    last_mid = send(near_mid, to_far)
    mixed_oth = attend_whole(raw_oth, scale_row, scale_oth)
    four_fc2 = jnp.stack([two_fc2] + z_fc2)
    mixed_oth, last_mid, four_fc2 = hold(mixed_oth, last_mid, four_fc2)
    near_fc2, far_fc2 = send(four_fc2, to_near), send(four_fc2, to_far)
    proj_own, fc1_own = assemble(
        [four_mid, near_mid, far_mid, last_mid], position, [quarter, hidden_quarter]
    )
    upstream = join_image(cotangent, cotangent_other, t)
    d_branch = (gain_mlp * upstream).astype(BF16)
    proj_oth, d_branch = hold(send(proj_own, to_core), d_branch)
    fc1_oth = send(fc1_own, to_core)
    attended = matmul(mixed_own, proj_own, NT) + matmul(mixed_oth, proj_oth, NT)
    middle = tokens_in + gain_attn * attended
    normed_two, inverse_two = layer_norm(middle)
    hidden_two = (normed_two * (1.0 + scale_mlp) + shift_mlp).astype(BF16)
    hidden_two, fc1_oth = hold(hidden_two, fc1_oth)

    def activate(weights):
        first = (2.0 / jnp.pi) ** 0.5
        before = matmul(hidden_two, weights, NN)
        square = before * before
        gate = 0.5 + 0.5 * jnp.tanh(before * (first + (first * 0.044715) * square))
        active = before * gate
        steep = 2.0 * first + (6.0 * first * 0.044715) * square
        return active.astype(BF16), (gate + active * (1.0 - gate) * steep).astype(BF16)

    active_oth, slope_oth = activate(fc1_oth)
    active_oth, slope_oth, near_fc2, far_fc2 = hold(active_oth, slope_oth, near_fc2, far_fc2)
    last_fc2 = send(near_fc2, to_far)
    active_own, slope_own = activate(fc1_own)
    given = products([(d_branch, active_oth)])
    given, active_own, slope_own, last_fc2 = hold(given, active_own, slope_own, last_fc2)
    added = [send(part, to_core) for part in given]
    (fc2_own,) = assemble([four_fc2, near_fc2, far_fc2, last_fc2], position, [hidden_quarter])
    fc2_own, added = hold(fc2_own, added)
    fc2_oth = send(fc2_own, to_core)
    blocks_fc2 = products([(d_branch, active_own)], added)
    blocks_fc2, fc2_oth = hold(blocks_fc2, fc2_oth)
    far_fc2 = send(scatter_far(blocks_fc2, where), to_far)
    d_before_oth = (matmul(d_branch, fc2_oth, NN) * slope_oth.astype(F32)).astype(BF16)
    d_before_own = (matmul(d_branch, fc2_own, NN) * slope_own.astype(F32)).astype(BF16)
    branch = matmul(active_own, fc2_own, NT) + matmul(active_oth, fc2_oth, NT)
    output_own, output_give = own_and_other(middle + gain_mlp * branch, t)

    d_gain_mlp = jnp.sum(upstream * branch, axis=0)
    d_before_oth, d_before_own, output_give, far_fc2 = hold(
        d_before_oth, d_before_own, output_give, far_fc2
    )
    near_fc2 = send(scatter_near(blocks_fc2, far_fc2, where), to_near)
    d_hidden_two = matmul(d_before_own, fc1_own, NT) + matmul(d_before_oth, fc1_oth, NT)
    d_scale_mlp = jnp.sum(d_hidden_two * normed_two, axis=0)
    d_shift_mlp = jnp.sum(d_hidden_two, axis=0)
    d_middle = upstream + norm_back(d_hidden_two * (1.0 + scale_mlp), normed_two, inverse_two)
    d_gain_attn = jnp.sum(d_middle * attended, axis=0)
    d_attended = (gain_attn * d_middle).astype(BF16)
    given = products([(d_attended, mixed_oth), (hidden_two, d_before_oth)])
    given, d_attended, near_fc2 = hold(given, d_attended, near_fc2)
    z_fc2 = scatter_z(blocks_fc2, far_fc2, near_fc2, where)
    own_fc2, others_fc2 = z_fc2[0], send_terms_z(z_fc2[1:])
    d_mixed_oth = matmul(d_attended, proj_oth, NN).astype(BF16)
    d_mixed_own = matmul(d_attended, proj_own, NN).astype(BF16)
    d_mixed_oth, d_mixed_own, added = hold(d_mixed_oth, d_mixed_own, [send(part, to_core) for part in given])
    blocks_mid = products([(d_attended, mixed_own), (hidden_two, d_before_own)], added)
    blocks_mid, d_mixed_oth = hold(blocks_mid, d_mixed_oth)
    far_mid = send(scatter_far(blocks_mid, where), to_far)
    d_raw_oth, terms_oth = attend_back_whole(raw_oth, mixed_oth, d_mixed_oth, scale_row, scale_oth)
    given = products([(hidden_one, d_raw_oth)])
    d_hidden_oth = matmul(d_raw_oth, qkv_oth, NT)
    given, far_mid, d_mixed_own, d_hidden_oth, others_fc2 = hold(
        given, far_mid, d_mixed_own, d_hidden_oth, others_fc2
    )
    near_mid = send(scatter_near(blocks_mid, far_mid, where), to_near)
    added = [send(part, to_core) for part in given]
    output_other = send(output_give, to_t)
    d_raw_own, terms_own = attend_back_whole(raw_own, mixed_own, d_mixed_own, scale_row, scale_own)
    d_raw_own, near_mid, added = hold(d_raw_own, near_mid, added)
    z_mid = scatter_z(blocks_mid, far_mid, near_mid, where)
    own_mid, others_mid = z_mid[0], send_terms_z(z_mid[1:])
    blocks_qkv = products([(hidden_one, d_raw_own)], added)
    blocks_qkv, d_raw_own = hold(blocks_qkv, d_raw_own)
    far_qkv = send(scatter_far(blocks_qkv, where), to_far)
    d_hidden_one = matmul(d_raw_own, qkv_own, NT) + d_hidden_oth
    d_scale_attn = jnp.sum(d_hidden_one * normed_one, axis=0)
    d_shift_attn = jnp.sum(d_hidden_one, axis=0)
    d_modulation = jnp.concatenate(
        [d_gain_attn, d_gain_mlp, d_scale_attn, d_scale_mlp, d_shift_attn, d_shift_mlp]
    )
    terms = in_order(terms_own.reshape(TS, -1), terms_oth.reshape(TS, -1), c)
    scale_terms = jnp.concatenate(terms, axis=1).reshape(-1)
    scale_high = lax.reduce_precision(scale_terms, 8, 7)
    row = jnp.concatenate(
        [d_modulation, scale_high, scale_terms - scale_high, jnp.zeros((128 - 2 * heads,), F32)]
    ).astype(BF16)[None, :]
    d_inputs = d_middle + norm_back(d_hidden_one * (1.0 + scale_attn), normed_one, inverse_one)
    inputs_own, inputs_give = own_and_other(d_inputs, t)
    row_other = send(row, to_t)
    far_qkv, inputs_give, row_other, output_other = hold(
        far_qkv, inputs_give, row_other, output_other
    )
    near_give, inputs_give, row_other = hold(
        scatter_near(blocks_qkv, far_qkv, where), inputs_give, row_other
    )
    near_qkv = send(near_give, to_near)
    inputs_other = send(inputs_give, to_t)
    mod_rows = jnp.concatenate([row, row_other])
    near_qkv, mod_z, others_mid = hold(near_qkv, send_z(mod_rows), others_mid)
    z_qkv = scatter_z(blocks_qkv, far_qkv, near_qkv, where)
    z_qkv, mod_z, mod_rows = hold(z_qkv, mod_z, mod_rows)
    own_qkv, others_qkv = z_qkv[0], send_terms_z(z_qkv[1:])
    half_fc2, other_fc2 = scatter_total(own_fc2, others_fc2, where)
    half_mid, other_mid = scatter_total(own_mid, others_mid, where)
    other_rest = send(jnp.concatenate([other_mid, other_fc2], axis=1), to_core)
    mod_rows = jnp.concatenate([mod_rows] + mod_z)
    mod_rows = jnp.concatenate([mod_rows, send(mod_rows, to_x)])
    mod_rows = jnp.concatenate([mod_rows, send(mod_rows, to_core)])

    d_mod_all = mod_rows[:, : 6 * width]
    scale_sum = jnp.sum(mod_rows[:, 6 * width : 6 * width + 2 * heads].astype(F32), axis=0)
    scale_sum = (scale_sum[:heads] + scale_sum[heads:]).reshape(TS, heads // TS)
    grad_scale = pick(scale_sum, t)
    grad_ada = [
        matmul(silu_low, d_mod_all[:, n * width : (n + 1) * width], TN) for n in range(6)
    ]
    grad_ada = jnp.stack(grad_ada).transpose(1, 0, 2)
    d_silu = matmul(d_mod_all, ada_low, NT)
    _, silu_pull = jax.vjp(jax.nn.silu, condition)
    d_condition = silu_pull(d_silu)[0]
    grad_table = jnp.dot(one_hot.astype(F32).T, d_condition, precision=HIGHEST)

    def joined(own, other):
        return jnp.concatenate(in_order(own, other.astype(F32), c), axis=1)

    grad_proj = joined(half_mid[:, :quarter], other_rest[:, :quarter]).T
    grad_fc1 = joined(half_mid[:, quarter:], other_rest[:, quarter:split])
    grad_fc2 = joined(half_fc2, other_rest[:, split:]).T
    others_qkv, others = hold(
        others_qkv, (grad_ada, grad_table, grad_scale, inputs_other, grad_proj, grad_fc1, grad_fc2)
    )
    grad_ada, grad_table, grad_scale, inputs_other, grad_proj, grad_fc1, grad_fc2 = others
    half_qkv, other_qkv = scatter_total(own_qkv, others_qkv, where)
    other_qkv = send(other_qkv, to_core)

    def part_of(values, n):
        starts = range(n * pair, 3 * quarter, 3 * pair)
        return jnp.concatenate([values[:, start : start + pair] for start in starts], axis=1)

    grad_qkv = [joined(part_of(half_qkv, n), part_of(other_qkv, n)) for n in range(3)]
    return (
        two_images(output_own, output_other, t),
        two_images(inputs_own, inputs_other, t),
        grad_table,
        grad_ada,
        jnp.stack(grad_qkv, axis=1),
        grad_scale,
        grad_proj,
        grad_fc1,
        grad_fc2,
    )


def solution(mesh):
    placed = (
        P("dp", "tensor", None),
        P("dp"),
        P("dp", None),
        P("dp", "tensor", None),
        P(None, "dp"),
        P("dp", None, None),
        P("dp", None, "tensor"),
        P("tensor"),
        P("tensor", "dp"),
        P("dp", "tensor"),
        P("tensor", "dp"),
    )
    fitting = mesh.shape["dp"] == ZS * XS * CS and mesh.shape["tensor"] == TS

    def on_device(inputs, *others):
        fits = fitting and inputs.shape[0] == TS
        return (on_device_whole if fits else on_device_general)(inputs, *others)

    return jax.shard_map(
        on_device,
        mesh=mesh,
        in_specs=placed,
        out_specs=(
            P("dp", "tensor", None),
            P("dp", "tensor", None),
            P(None, "dp"),
            P("dp", None, None),
            P("dp", None, "tensor"),
            P("tensor"),
            P("tensor", "dp"),
            P("dp", "tensor"),
            P("tensor", "dp"),
        ),
        check_vma=False,
    )
```

```python
import functools
import math

import jax
import jax.numpy as jnp
from jax import lax
from jax.experimental import pallas as pl
from jax.experimental.pallas import tpu as pltpu
from jax.sharding import PartitionSpec as P

EPSILON = 1e-06
HIGHEST = lax.Precision.HIGHEST


def layer_norm(values):
    average = jnp.mean(values, axis=-1, keepdims=True)
    centred = values - average
    inverse = lax.rsqrt(jnp.mean(centred * centred, axis=-1, keepdims=True) + EPSILON)
    return (centred * inverse, inverse)


def norm_back(d_normed, normed, inverse):
    return inverse * (
        d_normed
        - jnp.mean(d_normed, axis=-1, keepdims=True)
        - normed * jnp.mean(d_normed * normed, axis=-1, keepdims=True)
    )


def unit_rows(values):
    inverse = lax.rsqrt(jnp.sum(values * values, axis=-1, keepdims=True) + EPSILON)
    return (values * inverse, inverse)


def unit_back(d_unit, unit, inverse):
    return inverse * (d_unit - unit * jnp.sum(d_unit * unit, axis=-1, keepdims=True))


def spread(values):
    return lax.all_gather(values, "tensor", axis=1, tiled=True)


def collect(terms):
    return lax.psum_scatter(
        terms.astype(jnp.bfloat16), "tensor", scatter_dimension=1, tiled=True
    ).astype(jnp.float32)


def masked_scores(queries, keys_in, scale_row):
    scores = jnp.einsum("qhd,khd->hqk", queries, keys_in, preferred_element_type=jnp.float32)
    visible = scale_row[None, :] <= scale_row[:, None]
    return jnp.where(visible[None], scores, -1e30)


def attend_forward(pieces):
    queries, keys_in, values_in, scale_row = pieces
    scores = masked_scores(queries, keys_in, scale_row)
    largest = jnp.max(scores, axis=-1, keepdims=True)
    exponent = jnp.exp(scores - largest)
    denominator = jnp.sum(exponent, axis=-1, keepdims=True)
    attn_probs = (exponent / denominator).astype(jnp.bfloat16)
    mixed = jnp.einsum("hqk,khd->qhd", attn_probs, values_in, preferred_element_type=jnp.float32)
    return (mixed.astype(jnp.bfloat16), (largest + jnp.log(denominator))[..., 0])


def attend_backward(pieces):
    queries, keys_in, values_in, scale_row, log_total, d_mixed = pieces
    scores = masked_scores(queries, keys_in, scale_row)
    attn_probs = jnp.exp(scores - log_total[..., None])
    d_probs = jnp.einsum("qhd,khd->hqk", d_mixed, values_in, preferred_element_type=jnp.float32)
    offset = jnp.sum(attn_probs * d_probs, axis=-1, keepdims=True)
    d_scores = (attn_probs * (d_probs - offset)).astype(jnp.bfloat16)
    d_queries = jnp.einsum("hqk,khd->qhd", d_scores, keys_in, preferred_element_type=jnp.float32)
    d_keys = jnp.einsum("hqk,qhd->khd", d_scores, queries, preferred_element_type=jnp.float32)
    d_values = jnp.einsum(
        "hqk,qhd->khd", attn_probs.astype(jnp.bfloat16), d_mixed, preferred_element_type=jnp.float32
    )
    return (d_queries, d_keys, d_values)


def on_device_general(
    inputs, labels, scale_ids, cotangent, table, w_ada, w_qkv, head_scale, w_proj, w_fc1, w_fc2
):
    images, local_len, model_width = inputs.shape
    full_len = scale_ids.shape[1]
    local_heads = head_scale.shape[0]
    head_dim = w_qkv.shape[2] // local_heads
    classes = table.shape[0]
    gathered = (
        lax.all_gather(table.astype(jnp.bfloat16), "dp", axis=1, tiled=True),
        lax.all_gather(w_qkv.astype(jnp.bfloat16), "dp", axis=0, tiled=True),
        lax.all_gather(w_proj.astype(jnp.bfloat16), "dp", axis=1, tiled=True),
        lax.all_gather(w_fc1.astype(jnp.bfloat16), "dp", axis=0, tiled=True),
        lax.all_gather(w_fc2.astype(jnp.bfloat16), "dp", axis=1, tiled=True),
    )
    table_low, qkv_low, proj_low, fc1_low, fc2_low = gathered
    qkv_flat = qkv_low.reshape(model_width, -1)
    one_hot = labels[:, None] == jnp.arange(classes)[None, :]
    condition = jnp.dot(one_hot.astype(jnp.bfloat16), table_low, preferred_element_type=jnp.float32)
    silu_low = jax.nn.silu(condition).astype(jnp.bfloat16)
    ada_full = lax.all_gather(w_ada.astype(jnp.bfloat16), "dp", axis=0, tiled=True).reshape(
        model_width, 6 * model_width
    )
    modulation = jnp.dot(silu_low, ada_full, preferred_element_type=jnp.float32)
    modulation = modulation.reshape(images, 6, model_width)
    gain_attn = modulation[:, 0, None, :]
    gain_mlp = modulation[:, 1, None, :]
    scale_attn = modulation[:, 2, None, :]
    scale_mlp = modulation[:, 3, None, :]
    shift_attn = modulation[:, 4, None, :]
    shift_mlp = modulation[:, 5, None, :]
    normed_one, inverse_one = layer_norm(inputs)
    hidden_one = spread((normed_one * (1.0 + scale_attn) + shift_attn).astype(jnp.bfloat16))
    projected = jnp.einsum("bld,dc->blc", hidden_one, qkv_flat, preferred_element_type=jnp.float32)
    projected = projected.reshape(images, full_len, 3, local_heads, head_dim)
    q_unit, q_inverse = unit_rows(projected[:, :, 0])
    k_unit, k_inverse = unit_rows(projected[:, :, 1])
    q_hat = (q_unit * head_scale[:, None]).astype(jnp.bfloat16)
    k_hat = k_unit.astype(jnp.bfloat16)
    v_hat = projected[:, :, 2].astype(jnp.bfloat16)
    mixed, log_total = lax.map(attend_forward, (q_hat, k_hat, v_hat, scale_ids))
    mixed_flat = mixed.reshape(images, full_len, local_heads * head_dim)
    attended = collect(
        jnp.einsum("blc,cd->bld", mixed_flat, proj_low, preferred_element_type=jnp.float32)
    )
    middle = inputs + gain_attn * attended
    normed_two, inverse_two = layer_norm(middle)
    hidden_two = spread((normed_two * (1.0 + scale_mlp) + shift_mlp).astype(jnp.bfloat16))
    before = jnp.einsum("bld,df->blf", hidden_two, fc1_low, preferred_element_type=jnp.float32)
    gelu_fn = functools.partial(jax.nn.gelu, approximate=True)
    active_f, gelu_pull = jax.vjp(gelu_fn, before)
    active = active_f.astype(jnp.bfloat16)
    branch = collect(jnp.einsum("blf,fd->bld", active, fc2_low, preferred_element_type=jnp.float32))
    output = middle + gain_mlp * branch
    again = (
        lax.all_gather(w_qkv.astype(jnp.bfloat16), "dp", axis=0, tiled=True),
        lax.all_gather(w_proj.astype(jnp.bfloat16), "dp", axis=1, tiled=True),
        lax.all_gather(w_fc1.astype(jnp.bfloat16), "dp", axis=0, tiled=True),
        lax.all_gather(w_fc2.astype(jnp.bfloat16), "dp", axis=1, tiled=True),
    )
    qkv_back, proj_back, fc1_back, fc2_back = again
    d_gain_mlp = jnp.sum(cotangent * branch, axis=1)
    d_branch = spread((gain_mlp * cotangent).astype(jnp.bfloat16))
    grad_fc2 = jnp.einsum("blf,bld->fd", active, d_branch, preferred_element_type=jnp.float32)
    d_active = jnp.einsum("bld,fd->blf", d_branch, fc2_back, preferred_element_type=jnp.float32)
    d_before = gelu_pull(d_active)[0].astype(jnp.bfloat16)
    grad_fc1 = jnp.einsum("bld,blf->df", hidden_two, d_before, preferred_element_type=jnp.float32)
    d_hidden_two = collect(
        jnp.einsum("blf,df->bld", d_before, fc1_back, preferred_element_type=jnp.float32)
    )
    d_scale_mlp = jnp.sum(d_hidden_two * normed_two, axis=1)
    d_shift_mlp = jnp.sum(d_hidden_two, axis=1)
    d_middle = cotangent + norm_back(d_hidden_two * (1.0 + scale_mlp), normed_two, inverse_two)
    d_gain_attn = jnp.sum(d_middle * attended, axis=1)
    d_attended = spread((gain_attn * d_middle).astype(jnp.bfloat16))
    grad_proj = jnp.einsum(
        "blc,bld->cd", mixed_flat, d_attended, preferred_element_type=jnp.float32
    )
    d_mixed = jnp.einsum("bld,cd->blc", d_attended, proj_back, preferred_element_type=jnp.float32)
    d_mixed = d_mixed.astype(jnp.bfloat16).reshape(images, full_len, local_heads, head_dim)
    d_q_hat, d_k_hat, d_v_hat = lax.map(
        attend_backward, (q_hat, k_hat, v_hat, scale_ids, log_total, d_mixed)
    )
    scale_terms = jnp.sum(d_q_hat * q_unit, axis=(0, 1, 3))
    d_query = unit_back(d_q_hat * head_scale[:, None], q_unit, q_inverse)
    d_key = unit_back(d_k_hat, k_unit, k_inverse)
    d_raw = jnp.stack([d_query, d_key, d_v_hat], axis=2).astype(jnp.bfloat16)
    d_raw = d_raw.reshape(images, full_len, 3 * local_heads * head_dim)
    grad_qkv = jnp.einsum("bld,blc->dc", hidden_one, d_raw, preferred_element_type=jnp.float32)
    grad_qkv = grad_qkv.reshape(model_width, 3, local_heads * head_dim)
    d_hidden_one = collect(
        jnp.einsum(
            "blc,dc->bld",
            d_raw,
            qkv_back.reshape(model_width, -1),
            preferred_element_type=jnp.float32,
        )
    )
    d_scale_attn = jnp.sum(d_hidden_one * normed_one, axis=1)
    d_shift_attn = jnp.sum(d_hidden_one, axis=1)
    d_inputs = d_middle + norm_back(d_hidden_one * (1.0 + scale_attn), normed_one, inverse_one)
    mod_terms_back = jnp.stack(
        [d_gain_attn, d_gain_mlp, d_scale_attn, d_scale_mlp, d_shift_attn, d_shift_mlp], axis=1
    )
    d_modulation = lax.psum(mod_terms_back.astype(jnp.bfloat16), "tensor").astype(jnp.float32)
    d_mod_flat = d_modulation.reshape(images, 6 * model_width)
    grad_scale = lax.psum(scale_terms, "dp")
    ada_terms = jnp.dot(silu_low.astype(jnp.float32).T, d_mod_flat, precision=HIGHEST)
    grad_ada = lax.psum_scatter(
        ada_terms.reshape(model_width, 6, model_width).astype(jnp.bfloat16),
        "dp",
        scatter_dimension=0,
        tiled=True,
    ).astype(jnp.float32)
    d_silu = jnp.dot(d_mod_flat, ada_full.astype(jnp.float32).T, precision=HIGHEST)
    _, silu_pull = jax.vjp(jax.nn.silu, condition)
    d_condition = silu_pull(d_silu)[0]
    table_terms = jnp.dot(one_hot.astype(jnp.float32).T, d_condition, precision=HIGHEST)
    summed = (
        lax.psum_scatter(
            table_terms.astype(jnp.bfloat16), "dp", scatter_dimension=1, tiled=True
        ).astype(jnp.float32),
        lax.psum_scatter(
            grad_qkv.astype(jnp.bfloat16), "dp", scatter_dimension=0, tiled=True
        ).astype(jnp.float32),
        lax.psum_scatter(
            grad_proj.astype(jnp.bfloat16), "dp", scatter_dimension=1, tiled=True
        ).astype(jnp.float32),
        lax.psum_scatter(
            grad_fc1.astype(jnp.bfloat16), "dp", scatter_dimension=0, tiled=True
        ).astype(jnp.float32),
        lax.psum_scatter(
            grad_fc2.astype(jnp.bfloat16), "dp", scatter_dimension=1, tiled=True
        ).astype(jnp.float32),
    )
    grad_table, grad_qkv_own, grad_proj_own, grad_fc1_own, grad_fc2_own = summed
    return (
        output,
        d_inputs,
        grad_table,
        grad_ada,
        grad_qkv_own,
        grad_scale,
        grad_proj_own,
        grad_fc1_own,
        grad_fc2_own,
    )


BF16 = jnp.bfloat16
F32 = jnp.float32
ZS, XS, CS, TS = 4, 2, 2, 2
BOTH = ("dp", "tensor")
NN = (((1,), (0,)), ((), ()))
NT = (((1,), (1,)), ((), ()))
TN = (((0,), (0,)), ((), ()))
HIDDEN = -1e30
MIB = 1024 * 1024
BRIEF = pl.CostEstimate(flops=0, bytes_accessed=0, transcendentals=0)


def perm_of(step):
    pairs = []
    for z in range(ZS):
        for x in range(XS):
            for c in range(CS):
                for t in range(TS):
                    nz, nx, nc, nt = step(z, x, c, t)
                    source = ((z * XS + x) * CS + c) * TS + t
                    target = ((nz * XS + nx) * CS + nc) * TS + nt
                    pairs.append((source, target))
    return pairs


def send(values, step):
    return lax.ppermute(values, BOTH, perm_of(step))


def to_core(z, x, c, t):
    return (z, x, 1 - c, t)


def to_x(z, x, c, t):
    return (z, 1 - x, c, t)


def to_t(z, x, c, t):
    return (z, x, c, 1 - t)


def to_z(k):
    return lambda z, x, c, t: ((z + k) % ZS, x, c, t)


def to_near(z, x, c, t):
    return (z, 1 - x, c, t) if c == 0 else (z, x, c, 1 - t)


def to_far(z, x, c, t):
    return (z, x, c, 1 - t) if c == 0 else (z, 1 - x, c, t)


def pick(values, index, axis=0):
    return lax.dynamic_index_in_dim(values, index, axis, keepdims=False)


def place():
    dp = lax.axis_index("dp")
    t = lax.axis_index("tensor")
    return dp // (XS * CS), (dp // CS) % XS, dp % CS, t


def matmul(left, right, dims):
    return lax.dot_general(left, right, dims, preferred_element_type=F32)


def hold(*values):
    return lax.optimization_barrier(values)


def send_z(values):
    return [send(values, to_z(k)) for k in range(1, ZS)]


def send_terms_z(terms):
    return [send(terms[k - 1], to_z(k)) for k in range(1, ZS)]


def assemble_kernel(widths, crossed, where_ref, *refs):
    pieces, outs, sem = refs[:4], refs[4:-1], refs[-1]
    z, x, c, t = where_ref[0], where_ref[1], where_ref[2], where_ref[3]
    for slot, piece in enumerate(pieces):
        near = (1 - c, c) if crossed else (0, 1)
        dx, dt = [(0, 0), near, (1 - near[0], 1 - near[1]), (1, 1)][slot]
        sx, st = x ^ dx, t ^ dt
        for dz in range(ZS):
            for dc in range(CS):
                sz = (z + ZS - dz) % ZS
                sc = c ^ dc
                row = pl.multiple_of(((sz * XS + sx) * CS + sc) * 64, 64)
                start = 0
                for which, width in enumerate(widths):
                    column = pl.multiple_of(st * width, 128)
                    pltpu.make_async_copy(
                        piece.at[dz, dc, :, pl.ds(start, width)],
                        outs[which].at[pl.ds(row, 64), pl.ds(column, width)],
                        sem.at[which],
                    ).start()
                    start += width
    for which, out in enumerate(outs):
        pltpu.make_async_copy(out, out, sem.at[which]).wait()


def assemble(pieces, position, widths, crossed=True):
    rows = ZS * XS * CS * 64
    return pl.pallas_call(
        functools.partial(assemble_kernel, widths, crossed),
        out_shape=[jax.ShapeDtypeStruct((rows, TS * width), BF16) for width in widths],
        in_specs=[pl.BlockSpec(memory_space=pltpu.SMEM)]
        + [pl.BlockSpec(memory_space=pl.ANY)] * 4,
        out_specs=[pl.BlockSpec(memory_space=pltpu.VMEM)] * len(widths),
        scratch_shapes=[pltpu.SemaphoreType.DMA((len(widths),))],
        cost_estimate=BRIEF,
        compiler_params=pltpu.CompilerParams(vmem_limit_bytes=8 * MIB),
    )(position, *pieces)


def products(factors, added=None):
    terms = [matmul(rows, columns, TN) for rows, columns in factors]
    if added is not None:
        terms = [term + other.astype(F32) for term, other in zip(terms, added)]
    return [term.astype(BF16) for term in terms]


def block(blocks, dx, dt, where):
    z, x, c, t = where
    parts = []
    for values in blocks:
        m = values.shape[1] // TS
        values = lax.dynamic_slice_in_dim(values, (t ^ dt) * m, m, 1)
        values = pick(values.reshape(ZS, XS, CS * 64, m), x ^ dx, 1)
        parts.append(values.reshape(ZS * CS * 64, m))
    return parts[0] if len(parts) == 1 else jnp.concatenate(parts, axis=1)


def scatter_far(blocks, where):
    c = where[2]
    return jnp.stack([block(blocks, 1, 1, where), block(blocks, c, 1 - c, where)])


def scatter_near(blocks, far, where):
    c = where[2]
    return (block(blocks, 1 - c, c, where).astype(F32) + far[0].astype(F32)).astype(BF16)


def scatter_z(blocks, far, near, where):
    z = where[0]
    whole = block(blocks, 0, 0, where).astype(F32) + far[1].astype(F32) + near.astype(F32)
    whole = whole.astype(BF16).reshape(ZS, CS, 64, whole.shape[-1])
    return [pick(whole, (z + k) % ZS) for k in range(ZS)]


def scatter_total(own, others, where):
    c = where[2]
    total = sum(term.astype(F32) for term in [own] + list(others))
    return pick(total, c), pick(total, 1 - c).astype(BF16)


def in_order(own, other, bit):
    return jnp.where(bit == 0, own, other), jnp.where(bit == 0, other, own)


def join_image(values, other, t):
    return jnp.concatenate(in_order(pick(values, t), other.astype(F32), t), axis=0)


def own_and_other(values, t):
    half = values.shape[0] // 2
    own = lax.dynamic_slice_in_dim(values, t * half, half, axis=0)
    give = lax.dynamic_slice_in_dim(values, (1 - t) * half, half, axis=0)
    return own, give.astype(BF16)


def two_images(own, other, t):
    return jnp.stack(in_order(own, other.astype(F32), t))


def unit_of(values, mask):
    squares = jnp.where(mask, values * values, 0.0)
    inverse = lax.rsqrt(jnp.sum(squares, axis=-1, keepdims=True) + EPSILON)
    return jnp.where(mask, values * inverse, 0.0), inverse


def head_masks(shape, head_dim):
    lane = lax.broadcasted_iota(jnp.int32, shape, 1)
    return [(lane >= n * head_dim) & (lane < (n + 1) * head_dim) for n in range(2)]


def attend_kernel(head_dim, scale_ref, row_ref, column_ref, raw_ref, out_ref, bias_ref):
    pair = pl.program_id(0)

    @pl.when(pair == 0)
    def _():
        bias_ref[...] = jnp.where(row_ref[...] <= column_ref[...], 0.0, HIDDEN)

    lanes = 2 * head_dim
    q, k = raw_ref[:, :lanes].astype(F32), raw_ref[:, lanes : 2 * lanes].astype(F32)
    v = raw_ref[:, 2 * lanes :]
    values = jnp.concatenate([v, jnp.ones_like(v)], axis=1)
    masks = head_masks(q.shape, head_dim)
    k_hat = (unit_of(k, masks[0])[0] + unit_of(k, masks[1])[0]).astype(BF16)
    result = None
    for n in range(2):
        scale = scale_ref[2 * pair + n]
        q_hat = (unit_of(q, masks[n])[0] * scale).astype(BF16)
        scores = matmul(q_hat, k_hat, NT) + (bias_ref[...] - jnp.abs(scale))
        weights = jnp.exp(scores).astype(BF16)
        mixed = matmul(weights, values, NN)
        mixed = mixed[:, : 2 * head_dim] / mixed[:, 2 * head_dim :]
        result = mixed if result is None else jnp.where(masks[n], mixed, result)
    out_ref[...] = result.astype(out_ref.dtype)


def attend_whole(raw, scale_row, all_scale):
    tokens, width = raw.shape[0], raw.shape[1] // 3
    head_dim = width // all_scale.shape[0]
    lanes = 2 * head_dim
    pairs = width // lanes

    block = pl.BlockSpec((tokens, lanes), lambda n: (0, n))
    triple = pl.BlockSpec((tokens, 3 * lanes), lambda n: (0, n))
    return pl.pallas_call(
        functools.partial(attend_kernel, head_dim),
        out_shape=jax.ShapeDtypeStruct((tokens, width), BF16),
        grid=(pairs,),
        in_specs=[
            pl.BlockSpec(memory_space=pltpu.SMEM),
            pl.BlockSpec((1, tokens), lambda n: (0, 0)),
            pl.BlockSpec((tokens, 1), lambda n: (0, 0)),
            triple,
        ],
        out_specs=block,
        scratch_shapes=[pltpu.VMEM((tokens, tokens), F32)],
        cost_estimate=BRIEF,
        compiler_params=pltpu.CompilerParams(vmem_limit_bytes=16 * MIB),
    )(all_scale, scale_row[None, :], scale_row[:, None], raw)


def attend_back_kernel(
    head_dim,
    scale_ref,
    row_ref,
    column_ref,
    raw_ref,
    mixed_ref,
    d_mixed_ref,
    out_ref,
    term_ref,
    bias_ref,
):
    pair = pl.program_id(0)

    @pl.when(pair == 0)
    def _():
        bias_ref[...] = jnp.where(column_ref[...] <= row_ref[...], 0.0, HIDDEN)

    lanes = 2 * head_dim
    q, k = raw_ref[:, :lanes].astype(F32), raw_ref[:, lanes : 2 * lanes].astype(F32)
    v, d_mixed = raw_ref[:, 2 * lanes :], d_mixed_ref[...]
    masks = head_masks(q.shape, head_dim)
    k_units = [unit_of(k, mask) for mask in masks]
    k_hat = (k_units[0][0] + k_units[1][0]).astype(BF16)
    products = d_mixed.astype(F32) * mixed_ref[...].astype(F32)
    d_q_all = d_k_all = d_v_all = None
    for n in range(2):
        mask = masks[n]
        scale = scale_ref[2 * pair + n]
        q_unit, q_inverse = unit_of(q, mask)
        q_hat = (q_unit * scale).astype(BF16)
        d_out = jnp.where(mask, d_mixed, jnp.zeros_like(d_mixed))
        offset = jnp.sum(jnp.where(mask, products, 0.0), axis=-1, keepdims=True)
        offset = jnp.transpose(jnp.broadcast_to(offset, products.shape))[:1]
        scores = matmul(k_hat, q_hat, NT) + (bias_ref[...] - jnp.abs(scale))
        weights = jnp.exp(scores)
        weights = weights * (1.0 / jnp.sum(weights, axis=0, keepdims=True))
        d_weights = matmul(v, d_out, NT)
        d_scores = (weights * (d_weights - offset)).astype(BF16)
        d_v = matmul(weights.astype(BF16), d_out, NN)
        d_k = matmul(d_scores, q_hat, NN)
        d_q = jnp.where(mask, matmul(d_scores, k_hat, TN), 0.0)
        d_k = jnp.where(mask, d_k, 0.0)
        k_unit, k_inverse = k_units[n]
        term = d_q * q_unit
        term_n = jnp.sum(term, axis=0, keepdims=True)
        d_q = q_inverse * scale * (d_q - q_unit * jnp.sum(term, axis=-1, keepdims=True))
        d_k = k_inverse * (d_k - k_unit * jnp.sum(d_k * k_unit, axis=-1, keepdims=True))
        if n == 0:
            d_q_all, d_k_all, d_v_all, term_all = d_q, d_k, d_v, term_n
        else:
            d_q_all, d_k_all = d_q_all + d_q, d_k_all + d_k
            d_v_all, term_all = d_v_all + d_v, term_all + term_n
    out_ref[:, :lanes] = d_q_all.astype(out_ref.dtype)
    out_ref[:, lanes : 2 * lanes] = d_k_all.astype(out_ref.dtype)
    out_ref[:, 2 * lanes :] = d_v_all.astype(out_ref.dtype)
    term_ref[...] = jnp.broadcast_to(term_all, term_ref.shape)


def attend_back_whole(raw, mixed, d_mixed, scale_row, all_scale):
    tokens, width = mixed.shape
    heads = all_scale.shape[0]
    head_dim = width // heads
    lanes = 2 * head_dim
    pairs = width // lanes

    block = pl.BlockSpec((tokens, lanes), lambda n: (0, n))
    triple = pl.BlockSpec((tokens, 3 * lanes), lambda n: (0, n))
    d_raw, terms = pl.pallas_call(
        functools.partial(attend_back_kernel, head_dim),
        out_shape=[
            jax.ShapeDtypeStruct((tokens, 3 * width), BF16),
            jax.ShapeDtypeStruct((8, width), F32),
        ],
        grid=(pairs,),
        in_specs=[
            pl.BlockSpec(memory_space=pltpu.SMEM),
            pl.BlockSpec((1, tokens), lambda n: (0, 0)),
            pl.BlockSpec((tokens, 1), lambda n: (0, 0)),
            triple,
            block,
            block,
        ],
        out_specs=[
            triple,
            pl.BlockSpec((8, lanes), lambda n: (0, n)),
        ],
        scratch_shapes=[pltpu.VMEM((tokens, tokens), F32)],
        cost_estimate=BRIEF,
        compiler_params=pltpu.CompilerParams(vmem_limit_bytes=20 * MIB),
    )(all_scale, scale_row[None, :], scale_row[:, None], raw, mixed, d_mixed)
    return d_raw, jnp.sum(terms[0].reshape(heads, head_dim), axis=1)


def halves(values, c, half):
    keep = lax.dynamic_slice_in_dim(values, c * half, half, axis=1)
    give = lax.dynamic_slice_in_dim(values, (1 - c) * half, half, axis=1)
    return keep, give


def on_device_whole(
    inputs, labels, scale_ids, cotangent, table, w_ada, w_qkv, head_scale, w_proj, w_fc1, w_fc2
):
    width = inputs.shape[2]
    classes, rows = table.shape
    heads = TS * head_scale.shape[0]
    quarter = w_qkv.shape[2] // 2
    hidden_quarter = w_fc1.shape[1] // 2
    z, x, c, t = place()
    position = jnp.stack([z, x, c, t]).astype(jnp.int32)

    where = (z, x, c, t)

    pair = 2 * width // heads


    label_pair = jnp.stack(in_order(labels[0], labels[1], t)).astype(F32)
    label_tile = jnp.broadcast_to(label_pair[:, None], (2, 128))
    scale_tile = jnp.broadcast_to(head_scale[None, :], (8, head_scale.shape[0]))
    qkv_halves = []
    for side in (c, 1 - c):
        columns = [
            lax.dynamic_slice_in_dim(w_qkv[:, n].astype(BF16), side * quarter + j * pair, pair, 1)
            for j in range(quarter // pair)
            for n in range(3)
        ]
        qkv_halves.append(jnp.concatenate(columns, axis=1))
    keep_qkv, give_qkv, label_tile, scale_tile, inputs = hold(
        *qkv_halves, label_tile, scale_tile, inputs
    )
    recv_qkv, label_z = send(give_qkv, to_core), send_z(label_tile)
    scale_other = send(scale_tile, to_t)
    keep_qkv, recv_qkv, label_z, scale_other = hold(keep_qkv, recv_qkv, label_z, scale_other)
    two_qkv = jnp.stack([keep_qkv, recv_qkv])
    two_qkv, label_z, inputs, rest = hold(
        two_qkv,
        label_z,
        inputs,
        (cotangent, w_ada, w_proj, w_fc1, w_fc2, table, scale_ids),
    )
    cotangent, w_ada, w_proj, w_fc1, w_fc2, table, scale_ids = rest
    z_qkv = send_z(two_qkv)
    token_other = send(pick(inputs, 1 - t).astype(BF16), to_t)
    scale_row = pick(scale_ids, t)

    label_rows = jnp.concatenate([label_tile] + label_z)
    label_rows = jnp.concatenate([label_rows, send(label_rows, to_x)])
    label_rows = jnp.concatenate([label_rows, send(label_rows, to_core)])
    all_labels = label_rows[:, 0].astype(jnp.int32)
    one_hot = (all_labels[:, None] == jnp.arange(classes)[None, :]).astype(BF16)
    condition = matmul(one_hot, table.astype(BF16), NN)
    silu_low = jax.nn.silu(condition).astype(BF16)
    ada_low = w_ada.astype(BF16).reshape(rows, 6 * width)
    silu_own = silu_low.reshape(-1, TS, rows)[:, 0]
    partial = matmul(silu_own, ada_low, NN).reshape(CS, XS, ZS, 6 * width)
    partial = partial[0] + send(partial[1], to_core)
    own_part, x_part = partial[0], send(partial[1], to_x)
    w_fc1, w_proj_t, w_fc2_t = w_fc1.astype(BF16), w_proj.astype(BF16).T, w_fc2.astype(BF16).T
    rest_halves = [halves(w_proj_t, c, quarter), halves(w_fc1, c, hidden_quarter)]
    rest_halves.append(halves(w_fc2_t, c, hidden_quarter))
    keep_rest, give_rest = [jnp.concatenate([part[n] for part in rest_halves], 1) for n in range(2)]
    split = quarter + hidden_quarter
    z_qkv, own_part, x_part, recv_rest = hold(
        z_qkv, own_part, x_part, send(give_rest, to_core)
    )

    four_qkv = jnp.stack([two_qkv] + z_qkv)
    partial = own_part + x_part
    four_qkv, partial, recv_rest = hold(four_qkv, partial, recv_rest)
    near_qkv, far_qkv = send(four_qkv, to_t), send(four_qkv, to_x)
    mod_z = send_terms_z([partial[ZS - k] for k in range(1, ZS)])
    two_mid = jnp.stack([keep_rest[:, :split], recv_rest[:, :split]])
    two_fc2 = jnp.stack([keep_rest[:, split:], recv_rest[:, split:]])
    mod_z, two_mid, two_fc2, token_other = hold(mod_z, two_mid, two_fc2, token_other)
    mid_2 = send(two_mid, to_z(2))
    modulation = sum(mod_z, partial[0]).reshape(6, 1, width)
    gain_attn, gain_mlp, scale_attn, scale_mlp, shift_attn, shift_mlp = modulation
    tokens_in = join_image(inputs, token_other, t)
    cotangent_give = pick(cotangent, 1 - t).astype(BF16)
    near_qkv, far_qkv, mid_2, two_mid, cotangent_give = hold(
        near_qkv, far_qkv, mid_2, two_mid, cotangent_give
    )
    last_qkv = send(near_qkv, to_x)
    mid_1, mid_3 = send(two_mid, to_z(1)), send(two_mid, to_z(3))
    cotangent_other = send(cotangent_give, to_t)
    normed_one, inverse_one = layer_norm(tokens_in)
    hidden_one = (normed_one * (1.0 + scale_attn) + shift_attn).astype(BF16)
    last_qkv, mid_1, mid_3, hidden_one, cotangent_other = hold(
        last_qkv, mid_1, mid_3, hidden_one, cotangent_other
    )
    scales = jnp.concatenate(in_order(head_scale, scale_other[0], t)).reshape(TS, 2, -1)
    scale_own, scale_oth = pick(scales, c, 1).reshape(-1), pick(scales, 1 - c, 1).reshape(-1)
    four_mid = jnp.stack([two_mid, mid_1, mid_2, mid_3])
    four_mid, last_qkv, two_fc2, hidden_one = hold(four_mid, last_qkv, two_fc2, hidden_one)
    near_mid, far_mid = send(four_mid, to_near), send(four_mid, to_far)
    z_fc2 = send_z(two_fc2)
    (qkv_own,) = assemble(
        [four_qkv, near_qkv, far_qkv, last_qkv], position, [3 * quarter], crossed=False
    )
    raw_own = matmul(hidden_one, qkv_own, NN).astype(BF16)
    raw_own, qkv_oth = hold(raw_own, send(qkv_own, to_core))
    raw_oth = matmul(hidden_one, qkv_oth, NN).astype(BF16)
    mixed_own = attend_whole(raw_own, scale_row, scale_own)
    mixed_own, near_mid, far_mid, z_fc2, raw_oth = hold(
        mixed_own, near_mid, far_mid, z_fc2, raw_oth
    )
    last_mid = send(near_mid, to_far)
    mixed_oth = attend_whole(raw_oth, scale_row, scale_oth)
    four_fc2 = jnp.stack([two_fc2] + z_fc2)
    mixed_oth, last_mid, four_fc2 = hold(mixed_oth, last_mid, four_fc2)
    near_fc2, far_fc2 = send(four_fc2, to_near), send(four_fc2, to_far)
    proj_own, fc1_own = assemble(
        [four_mid, near_mid, far_mid, last_mid], position, [quarter, hidden_quarter]
    )
    upstream = join_image(cotangent, cotangent_other, t)
    d_branch = (gain_mlp * upstream).astype(BF16)
    proj_oth, d_branch = hold(send(proj_own, to_core), d_branch)
    fc1_oth = send(fc1_own, to_core)
    attended = matmul(mixed_own, proj_own, NT) + matmul(mixed_oth, proj_oth, NT)
    middle = tokens_in + gain_attn * attended
    normed_two, inverse_two = layer_norm(middle)
    hidden_two = (normed_two * (1.0 + scale_mlp) + shift_mlp).astype(BF16)
    hidden_two, fc1_oth = hold(hidden_two, fc1_oth)

    def activate(weights):
        first = (2.0 / jnp.pi) ** 0.5
        before = matmul(hidden_two, weights, NN)
        square = before * before
        gate = 0.5 + 0.5 * jnp.tanh(before * (first + (first * 0.044715) * square))
        active = before * gate
        steep = 2.0 * first + (6.0 * first * 0.044715) * square
        return active.astype(BF16), (gate + active * (1.0 - gate) * steep).astype(BF16)

    active_oth, slope_oth = activate(fc1_oth)
    active_oth, slope_oth, near_fc2, far_fc2 = hold(active_oth, slope_oth, near_fc2, far_fc2)
    last_fc2 = send(near_fc2, to_far)
    active_own, slope_own = activate(fc1_own)
    given = products([(d_branch, active_oth)])
    given, active_own, slope_own, last_fc2 = hold(given, active_own, slope_own, last_fc2)
    added = [send(part, to_core) for part in given]
    (fc2_own,) = assemble([four_fc2, near_fc2, far_fc2, last_fc2], position, [hidden_quarter])
    fc2_own, added = hold(fc2_own, added)
    fc2_oth = send(fc2_own, to_core)
    blocks_fc2 = products([(d_branch, active_own)], added)
    blocks_fc2, fc2_oth = hold(blocks_fc2, fc2_oth)
    far_give, blocks_fc2, active_own = hold(scatter_far(blocks_fc2, where), blocks_fc2, active_own)
    far_fc2 = send(far_give, to_far)

    d_before_oth = (matmul(d_branch, fc2_oth, NN) * slope_oth.astype(F32)).astype(BF16)
    d_before_own = (matmul(d_branch, fc2_own, NN) * slope_own.astype(F32)).astype(BF16)
    given = products([(hidden_two, d_before_oth)])
    given, d_before_oth, d_before_own = hold(given, d_before_oth, d_before_own)
    added = [send(part, to_core) for part in given]
    d_hidden_two = matmul(d_before_own, fc1_own, NT) + matmul(d_before_oth, fc1_oth, NT)
    d_scale_mlp = jnp.sum(d_hidden_two * normed_two, axis=0)
    d_shift_mlp = jnp.sum(d_hidden_two, axis=0)
    d_middle = upstream + norm_back(d_hidden_two * (1.0 + scale_mlp), normed_two, inverse_two)
    d_gain_attn = jnp.sum(d_middle * attended, axis=0)
    d_attended = (gain_attn * d_middle).astype(BF16)
    d_attended, added = hold(d_attended, added)
    blocks_fc1 = products([(hidden_two, d_before_own)], added)
    far_give, blocks_fc1, d_attended, far_fc2 = hold(
        scatter_far(blocks_fc1, where), blocks_fc1, d_attended, far_fc2
    )
    near_fc2 = send(scatter_near(blocks_fc2, far_fc2, where), to_near)
    far_fc1 = send(far_give, to_far)
    given = products([(d_attended, mixed_oth)])
    given, d_attended = hold(given, d_attended)
    added = [send(part, to_core) for part in given]
    d_mixed_oth = matmul(d_attended, proj_oth, NN).astype(BF16)
    d_mixed_own = matmul(d_attended, proj_own, NN).astype(BF16)
    d_mixed_oth, d_mixed_own, added = hold(d_mixed_oth, d_mixed_own, added)
    blocks_proj = products([(d_attended, mixed_own)], added)
    blocks_proj, d_mixed_oth = hold(blocks_proj, d_mixed_oth)
    far_proj = send(scatter_far(blocks_proj, where), to_far)
    d_raw_oth, terms_oth = attend_back_whole(raw_oth, mixed_oth, d_mixed_oth, scale_row, scale_oth)
    given = products([(hidden_one, d_raw_oth)])
    given, near_fc2, d_mixed_own = hold(given, near_fc2, d_mixed_own)
    added = [send(part, to_core) for part in given]
    d_raw_own, terms_own = attend_back_whole(raw_own, mixed_own, d_mixed_own, scale_row, scale_own)
    d_raw_own, far_fc1, far_proj, added = hold(d_raw_own, far_fc1, far_proj, added)
    blocks_mid = blocks_proj + blocks_fc1
    far_mid = [jnp.concatenate([far_proj[n], far_fc1[n]], axis=1) for n in range(2)]
    near_give = scatter_near(blocks_mid, far_mid, where)
    z_fc2 = scatter_z(blocks_fc2, far_fc2, near_fc2, where)
    near_give, z_fc2, d_raw_own = hold(near_give, z_fc2, d_raw_own)
    near_mid = send(near_give, to_near)
    own_fc2, others_fc2 = z_fc2[0], send_terms_z(z_fc2[1:])
    blocks_qkv = products([(hidden_one, d_raw_own)], added)
    far_give, blocks_qkv, d_raw_own, d_raw_oth, active_own = hold(
        scatter_far(blocks_qkv, where), blocks_qkv, d_raw_own, d_raw_oth, active_own
    )
    far_qkv = send(far_give, to_far)
    d_hidden_one = matmul(d_raw_own, qkv_own, NT) + matmul(d_raw_oth, qkv_oth, NT)
    d_hidden_one, near_mid, others_fc2 = hold(d_hidden_one, near_mid, others_fc2)
    z_mid = scatter_z(blocks_mid, far_mid, near_mid, where)
    own_mid, others_mid = z_mid[0], send_terms_z(z_mid[1:])
    d_scale_attn = jnp.sum(d_hidden_one * normed_one, axis=0)
    d_shift_attn = jnp.sum(d_hidden_one, axis=0)
    d_inputs = d_middle + norm_back(d_hidden_one * (1.0 + scale_attn), normed_one, inverse_one)
    inputs_own, inputs_give = own_and_other(d_inputs, t)
    far_qkv, inputs_give, d_scale_attn = hold(far_qkv, inputs_give, d_scale_attn)
    near_give, active_own, inputs_give = hold(
        scatter_near(blocks_qkv, far_qkv, where), active_own, inputs_give
    )
    near_qkv = send(near_give, to_near)
    branch = matmul(active_own, fc2_own, NT) + matmul(active_oth, fc2_oth, NT)
    output_own, output_give = own_and_other(middle + gain_mlp * branch, t)
    d_gain_mlp = jnp.sum(upstream * branch, axis=0)
    d_modulation = jnp.concatenate(
        [d_gain_attn, d_gain_mlp, d_scale_attn, d_scale_mlp, d_shift_attn, d_shift_mlp]
    )
    terms = in_order(terms_own.reshape(TS, -1), terms_oth.reshape(TS, -1), c)
    scale_terms = jnp.concatenate(terms, axis=1).reshape(-1)
    scale_high = lax.reduce_precision(scale_terms, 8, 7)
    row = jnp.concatenate(
        [d_modulation, scale_high, scale_terms - scale_high, jnp.zeros((128 - 2 * heads,), F32)]
    ).astype(BF16)[None, :]
    mod_rows = jnp.concatenate([row, send(row, to_t)])
    near_qkv, mod_rows, others_mid = hold(near_qkv, mod_rows, others_mid)
    z_qkv = scatter_z(blocks_qkv, far_qkv, near_qkv, where)
    z_qkv, mod_rows, inputs_give, output_give = hold(z_qkv, mod_rows, inputs_give, output_give)
    own_qkv, others_qkv = z_qkv[0], send_terms_z(z_qkv[1:])
    mod_z = send_z(mod_rows)
    inputs_other, output_other = send(inputs_give, to_t), send(output_give, to_t)
    half_fc2, other_fc2 = scatter_total(own_fc2, others_fc2, where)
    half_mid, other_mid = scatter_total(own_mid, others_mid, where)
    other_rest = send(jnp.concatenate([other_mid, other_fc2], axis=1), to_core)
    mod_rows = jnp.concatenate([mod_rows] + mod_z)
    mod_rows = jnp.concatenate([mod_rows, send(mod_rows, to_x)])
    mod_rows = jnp.concatenate([mod_rows, send(mod_rows, to_core)])

    d_mod_all = mod_rows[:, : 6 * width]
    scale_sum = jnp.sum(mod_rows[:, 6 * width : 6 * width + 2 * heads].astype(F32), axis=0)
    scale_sum = (scale_sum[:heads] + scale_sum[heads:]).reshape(TS, heads // TS)
    grad_scale = pick(scale_sum, t)
    grad_ada = [
        matmul(silu_low, d_mod_all[:, n * width : (n + 1) * width], TN) for n in range(6)
    ]
    grad_ada = jnp.stack(grad_ada).transpose(1, 0, 2)
    d_silu = matmul(d_mod_all, ada_low, NT)
    _, silu_pull = jax.vjp(jax.nn.silu, condition)
    d_condition = silu_pull(d_silu)[0]
    grad_table = jnp.dot(one_hot.astype(F32).T, d_condition, precision=HIGHEST)

    def joined(own, other):
        return jnp.concatenate(in_order(own, other.astype(F32), c), axis=1)

    grad_proj = joined(half_mid[:, :quarter], other_rest[:, :quarter]).T
    grad_fc1 = joined(half_mid[:, quarter:], other_rest[:, quarter:split])
    grad_fc2 = joined(half_fc2, other_rest[:, split:]).T
    others_qkv, others = hold(
        others_qkv, (grad_ada, grad_table, grad_scale, inputs_other, grad_proj, grad_fc1, grad_fc2)
    )
    grad_ada, grad_table, grad_scale, inputs_other, grad_proj, grad_fc1, grad_fc2 = others
    half_qkv, other_qkv = scatter_total(own_qkv, others_qkv, where)
    other_qkv = send(other_qkv, to_core)

    def part_of(values, n):
        starts = range(n * pair, 3 * quarter, 3 * pair)
        return jnp.concatenate([values[:, start : start + pair] for start in starts], axis=1)

    grad_qkv = [joined(part_of(half_qkv, n), part_of(other_qkv, n)) for n in range(3)]
    return (
        two_images(output_own, output_other, t),
        two_images(inputs_own, inputs_other, t),
        grad_table,
        grad_ada,
        jnp.stack(grad_qkv, axis=1),
        grad_scale,
        grad_proj,
        grad_fc1,
        grad_fc2,
    )


def solution(mesh):
    placed = (
        P("dp", "tensor", None),
        P("dp"),
        P("dp", None),
        P("dp", "tensor", None),
        P(None, "dp"),
        P("dp", None, None),
        P("dp", None, "tensor"),
        P("tensor"),
        P("tensor", "dp"),
        P("dp", "tensor"),
        P("tensor", "dp"),
    )
    fitting = mesh.shape["dp"] == ZS * XS * CS and mesh.shape["tensor"] == TS

    def on_device(inputs, *others):
        fits = fitting and inputs.shape[0] == TS
        return (on_device_whole if fits else on_device_general)(inputs, *others)

    return jax.shard_map(
        on_device,
        mesh=mesh,
        in_specs=placed,
        out_specs=(
            P("dp", "tensor", None),
            P("dp", "tensor", None),
            P(None, "dp"),
            P("dp", None, None),
            P("dp", None, "tensor"),
            P("tensor"),
            P("tensor", "dp"),
            P("dp", "tensor"),
            P("tensor", "dp"),
        ),
        check_vma=False,
    )
```

```python
import functools
import math

import jax
import jax.numpy as jnp
from jax import lax
from jax.experimental import pallas as pl
from jax.experimental.pallas import tpu as pltpu
from jax.sharding import PartitionSpec as P

EPSILON = 1e-06
HIGHEST = lax.Precision.HIGHEST


def layer_norm(values):
    average = jnp.mean(values, axis=-1, keepdims=True)
    centred = values - average
    inverse = lax.rsqrt(jnp.mean(centred * centred, axis=-1, keepdims=True) + EPSILON)
    return (centred * inverse, inverse)


def norm_back(d_normed, normed, inverse):
    return inverse * (
        d_normed
        - jnp.mean(d_normed, axis=-1, keepdims=True)
        - normed * jnp.mean(d_normed * normed, axis=-1, keepdims=True)
    )


def unit_rows(values):
    inverse = lax.rsqrt(jnp.sum(values * values, axis=-1, keepdims=True) + EPSILON)
    return (values * inverse, inverse)


def unit_back(d_unit, unit, inverse):
    return inverse * (d_unit - unit * jnp.sum(d_unit * unit, axis=-1, keepdims=True))


def spread(values):
    return lax.all_gather(values, "tensor", axis=1, tiled=True)


def collect(terms):
    return lax.psum_scatter(
        terms.astype(jnp.bfloat16), "tensor", scatter_dimension=1, tiled=True
    ).astype(jnp.float32)


def masked_scores(queries, keys_in, scale_row):
    scores = jnp.einsum("qhd,khd->hqk", queries, keys_in, preferred_element_type=jnp.float32)
    visible = scale_row[None, :] <= scale_row[:, None]
    return jnp.where(visible[None], scores, -1e30)


def attend_forward(pieces):
    queries, keys_in, values_in, scale_row = pieces
    scores = masked_scores(queries, keys_in, scale_row)
    largest = jnp.max(scores, axis=-1, keepdims=True)
    exponent = jnp.exp(scores - largest)
    denominator = jnp.sum(exponent, axis=-1, keepdims=True)
    attn_probs = (exponent / denominator).astype(jnp.bfloat16)
    mixed = jnp.einsum("hqk,khd->qhd", attn_probs, values_in, preferred_element_type=jnp.float32)
    return (mixed.astype(jnp.bfloat16), (largest + jnp.log(denominator))[..., 0])


def attend_backward(pieces):
    queries, keys_in, values_in, scale_row, log_total, d_mixed = pieces
    scores = masked_scores(queries, keys_in, scale_row)
    attn_probs = jnp.exp(scores - log_total[..., None])
    d_probs = jnp.einsum("qhd,khd->hqk", d_mixed, values_in, preferred_element_type=jnp.float32)
    offset = jnp.sum(attn_probs * d_probs, axis=-1, keepdims=True)
    d_scores = (attn_probs * (d_probs - offset)).astype(jnp.bfloat16)
    d_queries = jnp.einsum("hqk,khd->qhd", d_scores, keys_in, preferred_element_type=jnp.float32)
    d_keys = jnp.einsum("hqk,qhd->khd", d_scores, queries, preferred_element_type=jnp.float32)
    d_values = jnp.einsum(
        "hqk,qhd->khd", attn_probs.astype(jnp.bfloat16), d_mixed, preferred_element_type=jnp.float32
    )
    return (d_queries, d_keys, d_values)


def on_device_general(
    inputs, labels, scale_ids, cotangent, table, w_ada, w_qkv, head_scale, w_proj, w_fc1, w_fc2
):
    images, local_len, model_width = inputs.shape
    full_len = scale_ids.shape[1]
    local_heads = head_scale.shape[0]
    head_dim = w_qkv.shape[2] // local_heads
    classes = table.shape[0]
    gathered = (
        lax.all_gather(table.astype(jnp.bfloat16), "dp", axis=1, tiled=True),
        lax.all_gather(w_qkv.astype(jnp.bfloat16), "dp", axis=0, tiled=True),
        lax.all_gather(w_proj.astype(jnp.bfloat16), "dp", axis=1, tiled=True),
        lax.all_gather(w_fc1.astype(jnp.bfloat16), "dp", axis=0, tiled=True),
        lax.all_gather(w_fc2.astype(jnp.bfloat16), "dp", axis=1, tiled=True),
    )
    table_low, qkv_low, proj_low, fc1_low, fc2_low = gathered
    qkv_flat = qkv_low.reshape(model_width, -1)
    one_hot = labels[:, None] == jnp.arange(classes)[None, :]
    condition = jnp.dot(one_hot.astype(jnp.bfloat16), table_low, preferred_element_type=jnp.float32)
    silu_low = jax.nn.silu(condition).astype(jnp.bfloat16)
    ada_full = lax.all_gather(w_ada.astype(jnp.bfloat16), "dp", axis=0, tiled=True).reshape(
        model_width, 6 * model_width
    )
    modulation = jnp.dot(silu_low, ada_full, preferred_element_type=jnp.float32)
    modulation = modulation.reshape(images, 6, model_width)
    gain_attn = modulation[:, 0, None, :]
    gain_mlp = modulation[:, 1, None, :]
    scale_attn = modulation[:, 2, None, :]
    scale_mlp = modulation[:, 3, None, :]
    shift_attn = modulation[:, 4, None, :]
    shift_mlp = modulation[:, 5, None, :]
    normed_one, inverse_one = layer_norm(inputs)
    hidden_one = spread((normed_one * (1.0 + scale_attn) + shift_attn).astype(jnp.bfloat16))
    projected = jnp.einsum("bld,dc->blc", hidden_one, qkv_flat, preferred_element_type=jnp.float32)
    projected = projected.reshape(images, full_len, 3, local_heads, head_dim)
    q_unit, q_inverse = unit_rows(projected[:, :, 0])
    k_unit, k_inverse = unit_rows(projected[:, :, 1])
    q_hat = (q_unit * head_scale[:, None]).astype(jnp.bfloat16)
    k_hat = k_unit.astype(jnp.bfloat16)
    v_hat = projected[:, :, 2].astype(jnp.bfloat16)
    mixed, log_total = lax.map(attend_forward, (q_hat, k_hat, v_hat, scale_ids))
    mixed_flat = mixed.reshape(images, full_len, local_heads * head_dim)
    attended = collect(
        jnp.einsum("blc,cd->bld", mixed_flat, proj_low, preferred_element_type=jnp.float32)
    )
    middle = inputs + gain_attn * attended
    normed_two, inverse_two = layer_norm(middle)
    hidden_two = spread((normed_two * (1.0 + scale_mlp) + shift_mlp).astype(jnp.bfloat16))
    before = jnp.einsum("bld,df->blf", hidden_two, fc1_low, preferred_element_type=jnp.float32)
    gelu_fn = functools.partial(jax.nn.gelu, approximate=True)
    active_f, gelu_pull = jax.vjp(gelu_fn, before)
    active = active_f.astype(jnp.bfloat16)
    branch = collect(jnp.einsum("blf,fd->bld", active, fc2_low, preferred_element_type=jnp.float32))
    output = middle + gain_mlp * branch
    again = (
        lax.all_gather(w_qkv.astype(jnp.bfloat16), "dp", axis=0, tiled=True),
        lax.all_gather(w_proj.astype(jnp.bfloat16), "dp", axis=1, tiled=True),
        lax.all_gather(w_fc1.astype(jnp.bfloat16), "dp", axis=0, tiled=True),
        lax.all_gather(w_fc2.astype(jnp.bfloat16), "dp", axis=1, tiled=True),
    )
    qkv_back, proj_back, fc1_back, fc2_back = again
    d_gain_mlp = jnp.sum(cotangent * branch, axis=1)
    d_branch = spread((gain_mlp * cotangent).astype(jnp.bfloat16))
    grad_fc2 = jnp.einsum("blf,bld->fd", active, d_branch, preferred_element_type=jnp.float32)
    d_active = jnp.einsum("bld,fd->blf", d_branch, fc2_back, preferred_element_type=jnp.float32)
    d_before = gelu_pull(d_active)[0].astype(jnp.bfloat16)
    grad_fc1 = jnp.einsum("bld,blf->df", hidden_two, d_before, preferred_element_type=jnp.float32)
    d_hidden_two = collect(
        jnp.einsum("blf,df->bld", d_before, fc1_back, preferred_element_type=jnp.float32)
    )
    d_scale_mlp = jnp.sum(d_hidden_two * normed_two, axis=1)
    d_shift_mlp = jnp.sum(d_hidden_two, axis=1)
    d_middle = cotangent + norm_back(d_hidden_two * (1.0 + scale_mlp), normed_two, inverse_two)
    d_gain_attn = jnp.sum(d_middle * attended, axis=1)
    d_attended = spread((gain_attn * d_middle).astype(jnp.bfloat16))
    grad_proj = jnp.einsum(
        "blc,bld->cd", mixed_flat, d_attended, preferred_element_type=jnp.float32
    )
    d_mixed = jnp.einsum("bld,cd->blc", d_attended, proj_back, preferred_element_type=jnp.float32)
    d_mixed = d_mixed.astype(jnp.bfloat16).reshape(images, full_len, local_heads, head_dim)
    d_q_hat, d_k_hat, d_v_hat = lax.map(
        attend_backward, (q_hat, k_hat, v_hat, scale_ids, log_total, d_mixed)
    )
    scale_terms = jnp.sum(d_q_hat * q_unit, axis=(0, 1, 3))
    d_query = unit_back(d_q_hat * head_scale[:, None], q_unit, q_inverse)
    d_key = unit_back(d_k_hat, k_unit, k_inverse)
    d_raw = jnp.stack([d_query, d_key, d_v_hat], axis=2).astype(jnp.bfloat16)
    d_raw = d_raw.reshape(images, full_len, 3 * local_heads * head_dim)
    grad_qkv = jnp.einsum("bld,blc->dc", hidden_one, d_raw, preferred_element_type=jnp.float32)
    grad_qkv = grad_qkv.reshape(model_width, 3, local_heads * head_dim)
    d_hidden_one = collect(
        jnp.einsum(
            "blc,dc->bld",
            d_raw,
            qkv_back.reshape(model_width, -1),
            preferred_element_type=jnp.float32,
        )
    )
    d_scale_attn = jnp.sum(d_hidden_one * normed_one, axis=1)
    d_shift_attn = jnp.sum(d_hidden_one, axis=1)
    d_inputs = d_middle + norm_back(d_hidden_one * (1.0 + scale_attn), normed_one, inverse_one)
    mod_terms_back = jnp.stack(
        [d_gain_attn, d_gain_mlp, d_scale_attn, d_scale_mlp, d_shift_attn, d_shift_mlp], axis=1
    )
    d_modulation = lax.psum(mod_terms_back.astype(jnp.bfloat16), "tensor").astype(jnp.float32)
    d_mod_flat = d_modulation.reshape(images, 6 * model_width)
    grad_scale = lax.psum(scale_terms, "dp")
    ada_terms = jnp.dot(silu_low.astype(jnp.float32).T, d_mod_flat, precision=HIGHEST)
    grad_ada = lax.psum_scatter(
        ada_terms.reshape(model_width, 6, model_width).astype(jnp.bfloat16),
        "dp",
        scatter_dimension=0,
        tiled=True,
    ).astype(jnp.float32)
    d_silu = jnp.dot(d_mod_flat, ada_full.astype(jnp.float32).T, precision=HIGHEST)
    _, silu_pull = jax.vjp(jax.nn.silu, condition)
    d_condition = silu_pull(d_silu)[0]
    table_terms = jnp.dot(one_hot.astype(jnp.float32).T, d_condition, precision=HIGHEST)
    summed = (
        lax.psum_scatter(
            table_terms.astype(jnp.bfloat16), "dp", scatter_dimension=1, tiled=True
        ).astype(jnp.float32),
        lax.psum_scatter(
            grad_qkv.astype(jnp.bfloat16), "dp", scatter_dimension=0, tiled=True
        ).astype(jnp.float32),
        lax.psum_scatter(
            grad_proj.astype(jnp.bfloat16), "dp", scatter_dimension=1, tiled=True
        ).astype(jnp.float32),
        lax.psum_scatter(
            grad_fc1.astype(jnp.bfloat16), "dp", scatter_dimension=0, tiled=True
        ).astype(jnp.float32),
        lax.psum_scatter(
            grad_fc2.astype(jnp.bfloat16), "dp", scatter_dimension=1, tiled=True
        ).astype(jnp.float32),
    )
    grad_table, grad_qkv_own, grad_proj_own, grad_fc1_own, grad_fc2_own = summed
    return (
        output,
        d_inputs,
        grad_table,
        grad_ada,
        grad_qkv_own,
        grad_scale,
        grad_proj_own,
        grad_fc1_own,
        grad_fc2_own,
    )


BF16 = jnp.bfloat16
F32 = jnp.float32
ZS, XS, CS, TS = 4, 2, 2, 2
BOTH = ("dp", "tensor")
NN = (((1,), (0,)), ((), ()))
NT = (((1,), (1,)), ((), ()))
TN = (((0,), (0,)), ((), ()))
HIDDEN = -1e30
MIB = 1024 * 1024
BRIEF = pl.CostEstimate(flops=0, bytes_accessed=0, transcendentals=0)


def perm_of(step):
    pairs = []
    for z in range(ZS):
        for x in range(XS):
            for c in range(CS):
                for t in range(TS):
                    nz, nx, nc, nt = step(z, x, c, t)
                    source = ((z * XS + x) * CS + c) * TS + t
                    target = ((nz * XS + nx) * CS + nc) * TS + nt
                    pairs.append((source, target))
    return pairs


def send(values, step):
    return lax.ppermute(values, BOTH, perm_of(step))


def to_core(z, x, c, t):
    return (z, x, 1 - c, t)


def to_x(z, x, c, t):
    return (z, 1 - x, c, t)


def to_t(z, x, c, t):
    return (z, x, c, 1 - t)


def to_z(k):
    return lambda z, x, c, t: ((z + k) % ZS, x, c, t)


def to_z_bit(bit):
    return lambda z, x, c, t: (z ^ bit, x, c, t)


def to_near(z, x, c, t):
    return (z, 1 - x, c, t) if c == 0 else (z, x, c, 1 - t)


def to_far(z, x, c, t):
    return (z, x, c, 1 - t) if c == 0 else (z, 1 - x, c, t)


def pick(values, index, axis=0):
    return lax.dynamic_index_in_dim(values, index, axis, keepdims=False)


def place():
    dp = lax.axis_index("dp")
    t = lax.axis_index("tensor")
    return dp // (XS * CS), (dp // CS) % XS, dp % CS, t


def matmul(left, right, dims):
    return lax.dot_general(left, right, dims, preferred_element_type=F32)


def hold(*values):
    return lax.optimization_barrier(values)


def send_z(values):
    return [send(values, to_z(k)) for k in range(1, ZS)]


def send_terms_z(terms):
    return [send(terms[k - 1], to_z(k)) for k in range(1, ZS)]


def assemble_kernel(widths, crossed, where_ref, *refs):
    pieces, outs, sem = refs[:4], refs[4:-1], refs[-1]
    z, x, c, t = where_ref[0], where_ref[1], where_ref[2], where_ref[3]
    for slot, piece in enumerate(pieces):
        near = (1 - c, c) if crossed else (0, 1)
        dx, dt = [(0, 0), near, (1 - near[0], 1 - near[1]), (1, 1)][slot]
        sx, st = x ^ dx, t ^ dt
        for dz in range(ZS):
            for dc in range(CS):
                sz = (z + ZS - dz) % ZS
                sc = c ^ dc
                row = pl.multiple_of(((sz * XS + sx) * CS + sc) * 64, 64)
                start = 0
                for which, width in enumerate(widths):
                    column = pl.multiple_of(st * width, 128)
                    pltpu.make_async_copy(
                        piece.at[dz, dc, :, pl.ds(start, width)],
                        outs[which].at[pl.ds(row, 64), pl.ds(column, width)],
                        sem.at[which],
                    ).start()
                    start += width
    for which, out in enumerate(outs):
        pltpu.make_async_copy(out, out, sem.at[which]).wait()


def assemble(pieces, position, widths, crossed=True):
    rows = ZS * XS * CS * 64
    return pl.pallas_call(
        functools.partial(assemble_kernel, widths, crossed),
        out_shape=[jax.ShapeDtypeStruct((rows, TS * width), BF16) for width in widths],
        in_specs=[pl.BlockSpec(memory_space=pltpu.SMEM)]
        + [pl.BlockSpec(memory_space=pl.ANY)] * 4,
        out_specs=[pl.BlockSpec(memory_space=pltpu.VMEM)] * len(widths),
        scratch_shapes=[pltpu.SemaphoreType.DMA((len(widths),))],
        cost_estimate=BRIEF,
        compiler_params=pltpu.CompilerParams(vmem_limit_bytes=8 * MIB),
    )(position, *pieces)


def products(factors, added=None):
    terms = [matmul(rows, columns, TN) for rows, columns in factors]
    if added is not None:
        terms = [term + other.astype(F32) for term, other in zip(terms, added)]
    return [term.astype(BF16) for term in terms]


def block(blocks, dx, dt, where):
    z, x, c, t = where
    parts = []
    for values in blocks:
        m = values.shape[1] // TS
        values = lax.dynamic_slice_in_dim(values, (t ^ dt) * m, m, 1)
        values = pick(values.reshape(ZS, XS, CS * 64, m), x ^ dx, 1)
        parts.append(values.reshape(ZS * CS * 64, m))
    return parts[0] if len(parts) == 1 else jnp.concatenate(parts, axis=1)


def scatter_far(blocks, where):
    c = where[2]
    return jnp.stack([block(blocks, 1, 1, where), block(blocks, c, 1 - c, where)])


def scatter_near(blocks, far, where):
    c = where[2]
    return (block(blocks, 1 - c, c, where).astype(F32) + far[0].astype(F32)).astype(BF16)


def scatter_z(blocks, far, near, where):
    z = where[0]
    whole = block(blocks, 0, 0, where).astype(F32) + far[1].astype(F32) + near.astype(F32)
    whole = whole.astype(BF16).reshape(ZS, CS, 64, whole.shape[-1])
    return [pick(whole, (z + k) % ZS) for k in range(ZS)]


def scatter_total(own, others, where):
    c = where[2]
    total = sum(term.astype(F32) for term in [own] + list(others))
    return pick(total, c), pick(total, 1 - c).astype(BF16)


def in_order(own, other, bit):
    return jnp.where(bit == 0, own, other), jnp.where(bit == 0, other, own)


def join_image(values, other, t):
    return jnp.concatenate(in_order(pick(values, t), other.astype(F32), t), axis=0)


def own_and_other(values, t):
    half = values.shape[0] // 2
    own = lax.dynamic_slice_in_dim(values, t * half, half, axis=0)
    give = lax.dynamic_slice_in_dim(values, (1 - t) * half, half, axis=0)
    return own, give.astype(BF16)


def two_images(own, other, t):
    return jnp.stack(in_order(own, other.astype(F32), t))


def unit_of(values, mask):
    squares = jnp.where(mask, values * values, 0.0)
    inverse = lax.rsqrt(jnp.sum(squares, axis=-1, keepdims=True) + EPSILON)
    return jnp.where(mask, values * inverse, 0.0), inverse


def head_masks(shape, head_dim):
    lane = lax.broadcasted_iota(jnp.int32, shape, 1)
    return [(lane >= n * head_dim) & (lane < (n + 1) * head_dim) for n in range(2)]


def attend_kernel(head_dim, scale_ref, row_ref, column_ref, raw_ref, out_ref, bias_ref):
    pair = pl.program_id(0)

    @pl.when(pair == 0)
    def _():
        bias_ref[...] = jnp.where(row_ref[...] <= column_ref[...], 0.0, HIDDEN)

    lanes = 2 * head_dim
    q, k = raw_ref[:, :lanes].astype(F32), raw_ref[:, lanes : 2 * lanes].astype(F32)
    v = raw_ref[:, 2 * lanes :]
    values = jnp.concatenate([v, jnp.ones_like(v)], axis=1)
    masks = head_masks(q.shape, head_dim)
    k_hat = (unit_of(k, masks[0])[0] + unit_of(k, masks[1])[0]).astype(BF16)
    result = None
    for n in range(2):
        scale = scale_ref[2 * pair + n]
        q_hat = (unit_of(q, masks[n])[0] * scale).astype(BF16)
        scores = matmul(q_hat, k_hat, NT) + (bias_ref[...] - jnp.abs(scale))
        weights = jnp.exp(scores).astype(BF16)
        mixed = matmul(weights, values, NN)
        mixed = mixed[:, : 2 * head_dim] / mixed[:, 2 * head_dim :]
        result = mixed if result is None else jnp.where(masks[n], mixed, result)
    out_ref[...] = result.astype(out_ref.dtype)


def attend_whole(raw, scale_row, all_scale):
    tokens, width = raw.shape[0], raw.shape[1] // 3
    head_dim = width // all_scale.shape[0]
    lanes = 2 * head_dim
    pairs = width // lanes

    block = pl.BlockSpec((tokens, lanes), lambda n: (0, n))
    triple = pl.BlockSpec((tokens, 3 * lanes), lambda n: (0, n))
    return pl.pallas_call(
        functools.partial(attend_kernel, head_dim),
        out_shape=jax.ShapeDtypeStruct((tokens, width), BF16),
        grid=(pairs,),
        in_specs=[
            pl.BlockSpec(memory_space=pltpu.SMEM),
            pl.BlockSpec((1, tokens), lambda n: (0, 0)),
            pl.BlockSpec((tokens, 1), lambda n: (0, 0)),
            triple,
        ],
        out_specs=block,
        scratch_shapes=[pltpu.VMEM((tokens, tokens), F32)],
        cost_estimate=BRIEF,
        compiler_params=pltpu.CompilerParams(vmem_limit_bytes=16 * MIB),
    )(all_scale, scale_row[None, :], scale_row[:, None], raw)


def attend_back_kernel(
    head_dim,
    scale_ref,
    row_ref,
    column_ref,
    raw_ref,
    mixed_ref,
    d_mixed_ref,
    out_ref,
    term_ref,
    bias_ref,
):
    pair = pl.program_id(0)

    @pl.when(pair == 0)
    def _():
        bias_ref[...] = jnp.where(column_ref[...] <= row_ref[...], 0.0, HIDDEN)

    lanes = 2 * head_dim
    q, k = raw_ref[:, :lanes].astype(F32), raw_ref[:, lanes : 2 * lanes].astype(F32)
    v, d_mixed = raw_ref[:, 2 * lanes :], d_mixed_ref[...]
    masks = head_masks(q.shape, head_dim)
    k_units = [unit_of(k, mask) for mask in masks]
    k_hat = (k_units[0][0] + k_units[1][0]).astype(BF16)
    products = d_mixed.astype(F32) * mixed_ref[...].astype(F32)
    d_q_all = d_k_all = d_v_all = None
    for n in range(2):
        mask = masks[n]
        scale = scale_ref[2 * pair + n]
        q_unit, q_inverse = unit_of(q, mask)
        q_hat = (q_unit * scale).astype(BF16)
        d_out = jnp.where(mask, d_mixed, jnp.zeros_like(d_mixed))
        offset = jnp.sum(jnp.where(mask, products, 0.0), axis=-1, keepdims=True)
        offset = jnp.transpose(jnp.broadcast_to(offset, products.shape))[:1]
        scores = matmul(k_hat, q_hat, NT) + (bias_ref[...] - jnp.abs(scale))
        weights = jnp.exp(scores)
        weights = weights * (1.0 / jnp.sum(weights, axis=0, keepdims=True))
        d_weights = matmul(v, d_out, NT)
        d_scores = (weights * (d_weights - offset)).astype(BF16)
        d_v = matmul(weights.astype(BF16), d_out, NN)
        d_k = matmul(d_scores, q_hat, NN)
        d_q = jnp.where(mask, matmul(d_scores, k_hat, TN), 0.0)
        d_k = jnp.where(mask, d_k, 0.0)
        k_unit, k_inverse = k_units[n]
        term = d_q * q_unit
        term_n = jnp.sum(term, axis=0, keepdims=True)
        d_q = q_inverse * scale * (d_q - q_unit * jnp.sum(term, axis=-1, keepdims=True))
        d_k = k_inverse * (d_k - k_unit * jnp.sum(d_k * k_unit, axis=-1, keepdims=True))
        if n == 0:
            d_q_all, d_k_all, d_v_all, term_all = d_q, d_k, d_v, term_n
        else:
            d_q_all, d_k_all = d_q_all + d_q, d_k_all + d_k
            d_v_all, term_all = d_v_all + d_v, term_all + term_n
    out_ref[:, :lanes] = d_q_all.astype(out_ref.dtype)
    out_ref[:, lanes : 2 * lanes] = d_k_all.astype(out_ref.dtype)
    out_ref[:, 2 * lanes :] = d_v_all.astype(out_ref.dtype)
    term_ref[...] = jnp.broadcast_to(term_all, term_ref.shape)


def attend_back_whole(raw, mixed, d_mixed, scale_row, all_scale):
    tokens, width = mixed.shape
    heads = all_scale.shape[0]
    head_dim = width // heads
    lanes = 2 * head_dim
    pairs = width // lanes

    block = pl.BlockSpec((tokens, lanes), lambda n: (0, n))
    triple = pl.BlockSpec((tokens, 3 * lanes), lambda n: (0, n))
    d_raw, terms = pl.pallas_call(
        functools.partial(attend_back_kernel, head_dim),
        out_shape=[
            jax.ShapeDtypeStruct((tokens, 3 * width), BF16),
            jax.ShapeDtypeStruct((8, width), F32),
        ],
        grid=(pairs,),
        in_specs=[
            pl.BlockSpec(memory_space=pltpu.SMEM),
            pl.BlockSpec((1, tokens), lambda n: (0, 0)),
            pl.BlockSpec((tokens, 1), lambda n: (0, 0)),
            triple,
            block,
            block,
        ],
        out_specs=[
            triple,
            pl.BlockSpec((8, lanes), lambda n: (0, n)),
        ],
        scratch_shapes=[pltpu.VMEM((tokens, tokens), F32)],
        cost_estimate=BRIEF,
        compiler_params=pltpu.CompilerParams(vmem_limit_bytes=20 * MIB),
    )(all_scale, scale_row[None, :], scale_row[:, None], raw, mixed, d_mixed)
    return d_raw, jnp.sum(terms[0].reshape(heads, head_dim), axis=1)


def halves(values, c, half):
    keep = lax.dynamic_slice_in_dim(values, c * half, half, axis=1)
    give = lax.dynamic_slice_in_dim(values, (1 - c) * half, half, axis=1)
    return keep, give


def on_device_whole(
    inputs, labels, scale_ids, cotangent, table, w_ada, w_qkv, head_scale, w_proj, w_fc1, w_fc2
):
    width = inputs.shape[2]
    classes, rows = table.shape
    heads = TS * head_scale.shape[0]
    quarter = w_qkv.shape[2] // 2
    hidden_quarter = w_fc1.shape[1] // 2
    z, x, c, t = place()
    position = jnp.stack([z, x, c, t]).astype(jnp.int32)

    where = (z, x, c, t)

    pair = 2 * width // heads


    label_pair = jnp.stack(in_order(labels[0], labels[1], t)).astype(F32)
    label_tile = jnp.broadcast_to(label_pair[:, None], (2, 128))
    scale_tile = jnp.broadcast_to(head_scale[None, :], (8, head_scale.shape[0]))
    qkv_halves = []
    for side in (c, 1 - c):
        columns = [
            lax.dynamic_slice_in_dim(w_qkv[:, n].astype(BF16), side * quarter + j * pair, pair, 1)
            for j in range(quarter // pair)
            for n in range(3)
        ]
        qkv_halves.append(jnp.concatenate(columns, axis=1))
    keep_qkv, give_qkv, label_tile, scale_tile, inputs = hold(
        *qkv_halves, label_tile, scale_tile, inputs
    )
    recv_qkv, label_z = send(give_qkv, to_core), send_z(label_tile)
    scale_other = send(scale_tile, to_t)
    keep_qkv, recv_qkv, label_z, scale_other = hold(keep_qkv, recv_qkv, label_z, scale_other)
    two_qkv = jnp.stack([keep_qkv, recv_qkv])
    two_qkv, label_z, inputs, rest = hold(
        two_qkv,
        label_z,
        inputs,
        (cotangent, w_ada, w_proj, w_fc1, w_fc2, table, scale_ids),
    )
    cotangent, w_ada, w_proj, w_fc1, w_fc2, table, scale_ids = rest
    z_qkv = send_z(two_qkv)
    token_other = send(pick(inputs, 1 - t).astype(BF16), to_t)
    scale_row = pick(scale_ids, t)

    odd = z % 2 == 1
    first, third = jnp.where(odd, label_z[0], label_z[2]), jnp.where(odd, label_z[2], label_z[0])
    label_rows = jnp.concatenate([label_tile, first, label_z[1], third])
    label_rows = jnp.concatenate([label_rows, send(label_rows, to_x)])
    label_rows = jnp.concatenate([label_rows, send(label_rows, to_core)])
    all_labels = label_rows[:, 0].astype(jnp.int32)
    one_hot = (all_labels[:, None] == jnp.arange(classes)[None, :]).astype(BF16)
    condition = matmul(one_hot, table.astype(BF16), NN)
    silu_low = jax.nn.silu(condition).astype(BF16)
    ada_low = w_ada.astype(BF16).reshape(rows, 6 * width)
    silu_own = silu_low.reshape(-1, TS, rows)[:, 0]
    partial = matmul(silu_own, ada_low, NN).reshape(CS, XS, ZS, 6 * width)
    partial = partial[0] + send(partial[1], to_core)
    own_part, x_part = partial[0], send(partial[1], to_x)
    w_fc1, w_proj_t, w_fc2_t = w_fc1.astype(BF16), w_proj.astype(BF16).T, w_fc2.astype(BF16).T
    rest_halves = [halves(w_proj_t, c, quarter), halves(w_fc1, c, hidden_quarter)]
    rest_halves.append(halves(w_fc2_t, c, hidden_quarter))
    keep_rest, give_rest = [jnp.concatenate([part[n] for part in rest_halves], 1) for n in range(2)]
    split = quarter + hidden_quarter
    z_qkv, own_part, x_part, recv_rest = hold(
        z_qkv, own_part, x_part, send(give_rest, to_core)
    )

    four_qkv = jnp.stack([two_qkv] + z_qkv)
    partial = own_part + x_part
    two_mid = jnp.stack([keep_rest[:, :split], recv_rest[:, :split]])
    two_fc2 = jnp.stack([keep_rest[:, split:], recv_rest[:, split:]])
    four_qkv, partial, two_mid, two_fc2 = hold(four_qkv, partial, two_mid, two_fc2)
    near_qkv, far_qkv = send(four_qkv, to_t), send(four_qkv, to_x)
    mid_2 = send(two_mid, to_z(2))
    partial = partial[:2] + send(partial[2:], to_z_bit(2))
    mod_part, mod_bit = partial[0], send(partial[1], to_z_bit(1))
    cotangent_give = pick(cotangent, 1 - t).astype(BF16)
    near_qkv, far_qkv, mid_2, two_mid, cotangent_give, mod_part, mod_bit, token_other = hold(
        near_qkv, far_qkv, mid_2, two_mid, cotangent_give, mod_part, mod_bit, token_other
    )
    modulation = (mod_part + mod_bit).reshape(6, 1, width)
    gain_attn, gain_mlp, scale_attn, scale_mlp, shift_attn, shift_mlp = modulation
    tokens_in = join_image(inputs, token_other, t)
    last_qkv = send(near_qkv, to_x)
    mid_1, mid_3 = send(two_mid, to_z(1)), send(two_mid, to_z(3))
    cotangent_other = send(cotangent_give, to_t)
    normed_one, inverse_one = layer_norm(tokens_in)
    hidden_one = (normed_one * (1.0 + scale_attn) + shift_attn).astype(BF16)
    last_qkv, mid_1, mid_3, hidden_one, cotangent_other = hold(
        last_qkv, mid_1, mid_3, hidden_one, cotangent_other
    )
    scales = jnp.concatenate(in_order(head_scale, scale_other[0], t)).reshape(TS, 2, -1)
    scale_own, scale_oth = pick(scales, c, 1).reshape(-1), pick(scales, 1 - c, 1).reshape(-1)
    four_mid = jnp.stack([two_mid, mid_1, mid_2, mid_3])
    four_mid, last_qkv, two_fc2, hidden_one = hold(four_mid, last_qkv, two_fc2, hidden_one)
    near_mid, far_mid = send(four_mid, to_near), send(four_mid, to_far)
    z_fc2 = send_z(two_fc2)
    (qkv_own,) = assemble(
        [four_qkv, near_qkv, far_qkv, last_qkv], position, [3 * quarter], crossed=False
    )
    raw_own = matmul(hidden_one, qkv_own, NN).astype(BF16)
    raw_own, qkv_oth = hold(raw_own, send(qkv_own, to_core))
    raw_oth = matmul(hidden_one, qkv_oth, NN).astype(BF16)
    mixed_own = attend_whole(raw_own, scale_row, scale_own)
    mixed_own, near_mid, far_mid, z_fc2, raw_oth = hold(
        mixed_own, near_mid, far_mid, z_fc2, raw_oth
    )
    last_mid = send(near_mid, to_far)
    mixed_oth = attend_whole(raw_oth, scale_row, scale_oth)
    four_fc2 = jnp.stack([two_fc2] + z_fc2)
    mixed_oth, last_mid, four_fc2 = hold(mixed_oth, last_mid, four_fc2)
    near_fc2, far_fc2 = send(four_fc2, to_near), send(four_fc2, to_far)
    proj_own, fc1_own = assemble(
        [four_mid, near_mid, far_mid, last_mid], position, [quarter, hidden_quarter]
    )
    upstream = join_image(cotangent, cotangent_other, t)
    d_branch = (gain_mlp * upstream).astype(BF16)
    proj_oth, d_branch = hold(send(proj_own, to_core), d_branch)
    fc1_oth = send(fc1_own, to_core)
    attended = matmul(mixed_own, proj_own, NT) + matmul(mixed_oth, proj_oth, NT)
    middle = tokens_in + gain_attn * attended
    normed_two, inverse_two = layer_norm(middle)
    hidden_two = (normed_two * (1.0 + scale_mlp) + shift_mlp).astype(BF16)
    hidden_two, fc1_oth = hold(hidden_two, fc1_oth)

    def activate(weights):
        first = (2.0 / jnp.pi) ** 0.5
        before = matmul(hidden_two, weights, NN)
        square = before * before
        gate = 0.5 + 0.5 * jnp.tanh(before * (first + (first * 0.044715) * square))
        active = before * gate
        steep = 2.0 * first + (6.0 * first * 0.044715) * square
        return active.astype(BF16), (gate + active * (1.0 - gate) * steep).astype(BF16)

    active_oth, slope_oth = activate(fc1_oth)
    active_oth, slope_oth, near_fc2, far_fc2 = hold(active_oth, slope_oth, near_fc2, far_fc2)
    last_fc2 = send(near_fc2, to_far)
    active_own, slope_own = activate(fc1_own)
    given = products([(d_branch, active_oth)])
    given, active_own, slope_own, last_fc2 = hold(given, active_own, slope_own, last_fc2)
    added = [send(part, to_core) for part in given]
    (fc2_own,) = assemble([four_fc2, near_fc2, far_fc2, last_fc2], position, [hidden_quarter])
    fc2_own, added = hold(fc2_own, added)
    fc2_oth = send(fc2_own, to_core)
    blocks_fc2 = products([(d_branch, active_own)], added)
    blocks_fc2, fc2_oth = hold(blocks_fc2, fc2_oth)
    far_give, blocks_fc2, active_own = hold(scatter_far(blocks_fc2, where), blocks_fc2, active_own)
    far_fc2 = send(far_give, to_far)

    d_before_oth = (matmul(d_branch, fc2_oth, NN) * slope_oth.astype(F32)).astype(BF16)
    d_before_own = (matmul(d_branch, fc2_own, NN) * slope_own.astype(F32)).astype(BF16)
    given = products([(hidden_two, d_before_oth)])
    given, d_before_oth, d_before_own = hold(given, d_before_oth, d_before_own)
    added = [send(part, to_core) for part in given]
    d_hidden_two = matmul(d_before_own, fc1_own, NT) + matmul(d_before_oth, fc1_oth, NT)
    d_scale_mlp = jnp.sum(d_hidden_two * normed_two, axis=0)
    d_shift_mlp = jnp.sum(d_hidden_two, axis=0)
    d_middle = upstream + norm_back(d_hidden_two * (1.0 + scale_mlp), normed_two, inverse_two)
    d_gain_attn = jnp.sum(d_middle * attended, axis=0)
    d_attended = (gain_attn * d_middle).astype(BF16)
    d_attended, added = hold(d_attended, added)
    blocks_fc1 = products([(hidden_two, d_before_own)], added)
    far_give, blocks_fc1, d_attended, far_fc2 = hold(
        scatter_far(blocks_fc1, where), blocks_fc1, d_attended, far_fc2
    )
    near_fc2 = send(scatter_near(blocks_fc2, far_fc2, where), to_near)
    far_fc1 = send(far_give, to_far)
    given = products([(d_attended, mixed_oth)])
    given, d_attended = hold(given, d_attended)
    added = [send(part, to_core) for part in given]
    d_mixed_oth = matmul(d_attended, proj_oth, NN).astype(BF16)
    d_mixed_own = matmul(d_attended, proj_own, NN).astype(BF16)
    d_mixed_oth, d_mixed_own, added = hold(d_mixed_oth, d_mixed_own, added)
    blocks_proj = products([(d_attended, mixed_own)], added)
    blocks_proj, d_mixed_oth = hold(blocks_proj, d_mixed_oth)
    far_proj = send(scatter_far(blocks_proj, where), to_far)
    d_raw_oth, terms_oth = attend_back_whole(raw_oth, mixed_oth, d_mixed_oth, scale_row, scale_oth)
    given = products([(hidden_one, d_raw_oth)])
    given, near_fc2, d_mixed_own = hold(given, near_fc2, d_mixed_own)
    added = [send(part, to_core) for part in given]
    d_raw_own, terms_own = attend_back_whole(raw_own, mixed_own, d_mixed_own, scale_row, scale_own)
    d_raw_own, far_fc1, far_proj, added = hold(d_raw_own, far_fc1, far_proj, added)
    blocks_mid = blocks_proj + blocks_fc1
    far_mid = [jnp.concatenate([far_proj[n], far_fc1[n]], axis=1) for n in range(2)]
    near_give = scatter_near(blocks_mid, far_mid, where)
    z_fc2 = scatter_z(blocks_fc2, far_fc2, near_fc2, where)
    near_give, z_fc2, d_raw_own = hold(near_give, z_fc2, d_raw_own)
    near_mid = send(near_give, to_near)
    own_fc2, others_fc2 = z_fc2[0], send_terms_z(z_fc2[1:])
    blocks_qkv = products([(hidden_one, d_raw_own)], added)
    far_give, blocks_qkv, d_raw_own, d_raw_oth, active_own = hold(
        scatter_far(blocks_qkv, where), blocks_qkv, d_raw_own, d_raw_oth, active_own
    )
    far_qkv = send(far_give, to_far)
    d_hidden_one = matmul(d_raw_own, qkv_own, NT) + matmul(d_raw_oth, qkv_oth, NT)
    d_hidden_one, near_mid, others_fc2 = hold(d_hidden_one, near_mid, others_fc2)
    z_mid = scatter_z(blocks_mid, far_mid, near_mid, where)
    own_mid, others_mid = z_mid[0], send_terms_z(z_mid[1:])
    d_scale_attn = jnp.sum(d_hidden_one * normed_one, axis=0)
    d_shift_attn = jnp.sum(d_hidden_one, axis=0)
    d_inputs = d_middle + norm_back(d_hidden_one * (1.0 + scale_attn), normed_one, inverse_one)
    inputs_own, inputs_give = own_and_other(d_inputs, t)
    far_qkv, inputs_give, d_scale_attn = hold(far_qkv, inputs_give, d_scale_attn)
    near_give, active_own, inputs_give = hold(
        scatter_near(blocks_qkv, far_qkv, where), active_own, inputs_give
    )
    near_qkv = send(near_give, to_near)
    branch = matmul(active_own, fc2_own, NT) + matmul(active_oth, fc2_oth, NT)
    output_own, output_give = own_and_other(middle + gain_mlp * branch, t)
    d_gain_mlp = jnp.sum(upstream * branch, axis=0)
    d_modulation = jnp.concatenate(
        [d_gain_attn, d_gain_mlp, d_scale_attn, d_scale_mlp, d_shift_attn, d_shift_mlp]
    )
    terms = in_order(terms_own.reshape(TS, -1), terms_oth.reshape(TS, -1), c)
    scale_terms = jnp.concatenate(terms, axis=1).reshape(-1)
    scale_high = lax.reduce_precision(scale_terms, 8, 7)
    row = jnp.concatenate(
        [d_modulation, scale_high, scale_terms - scale_high, jnp.zeros((128 - 2 * heads,), F32)]
    ).astype(BF16)[None, :]
    mod_rows = jnp.concatenate([row, send(row, to_t)])
    near_qkv, mod_rows, others_mid = hold(near_qkv, mod_rows, others_mid)
    z_qkv = scatter_z(blocks_qkv, far_qkv, near_qkv, where)
    z_qkv, mod_rows, inputs_give, output_give = hold(z_qkv, mod_rows, inputs_give, output_give)
    own_qkv, others_qkv = z_qkv[0], send_terms_z(z_qkv[1:])
    mod_z = send_z(mod_rows)
    inputs_other, output_other = send(inputs_give, to_t), send(output_give, to_t)
    half_fc2, other_fc2 = scatter_total(own_fc2, others_fc2, where)
    half_mid, other_mid = scatter_total(own_mid, others_mid, where)
    other_rest = send(jnp.concatenate([other_mid, other_fc2], axis=1), to_core)
    first, third = jnp.where(odd, mod_z[0], mod_z[2]), jnp.where(odd, mod_z[2], mod_z[0])
    mod_rows = jnp.concatenate([mod_rows, first, mod_z[1], third])
    mod_rows = jnp.concatenate([mod_rows, send(mod_rows, to_x)])
    mod_rows = jnp.concatenate([mod_rows, send(mod_rows, to_core)])

    d_mod_all = mod_rows[:, : 6 * width]
    scale_sum = jnp.sum(mod_rows[:, 6 * width : 6 * width + 2 * heads].astype(F32), axis=0)
    scale_sum = (scale_sum[:heads] + scale_sum[heads:]).reshape(TS, heads // TS)
    grad_scale = pick(scale_sum, t)
    grad_ada = [
        matmul(silu_low, d_mod_all[:, n * width : (n + 1) * width], TN) for n in range(6)
    ]
    grad_ada = jnp.stack(grad_ada).transpose(1, 0, 2)
    d_silu = matmul(d_mod_all, ada_low, NT)
    _, silu_pull = jax.vjp(jax.nn.silu, condition)
    d_condition = silu_pull(d_silu)[0]
    grad_table = jnp.dot(one_hot.astype(F32).T, d_condition, precision=HIGHEST)

    def joined(own, other):
        return jnp.concatenate(in_order(own, other.astype(F32), c), axis=1)

    grad_proj = joined(half_mid[:, :quarter], other_rest[:, :quarter]).T
    grad_fc1 = joined(half_mid[:, quarter:], other_rest[:, quarter:split])
    grad_fc2 = joined(half_fc2, other_rest[:, split:]).T
    others_qkv, others = hold(
        others_qkv, (grad_ada, grad_table, grad_scale, inputs_other, grad_proj, grad_fc1, grad_fc2)
    )
    grad_ada, grad_table, grad_scale, inputs_other, grad_proj, grad_fc1, grad_fc2 = others
    half_qkv, other_qkv = scatter_total(own_qkv, others_qkv, where)
    other_qkv = send(other_qkv, to_core)

    def part_of(values, n):
        starts = range(n * pair, 3 * quarter, 3 * pair)
        return jnp.concatenate([values[:, start : start + pair] for start in starts], axis=1)

    grad_qkv = [joined(part_of(half_qkv, n), part_of(other_qkv, n)) for n in range(3)]
    return (
        two_images(output_own, output_other, t),
        two_images(inputs_own, inputs_other, t),
        grad_table,
        grad_ada,
        jnp.stack(grad_qkv, axis=1),
        grad_scale,
        grad_proj,
        grad_fc1,
        grad_fc2,
    )


def solution(mesh):
    placed = (
        P("dp", "tensor", None),
        P("dp"),
        P("dp", None),
        P("dp", "tensor", None),
        P(None, "dp"),
        P("dp", None, None),
        P("dp", None, "tensor"),
        P("tensor"),
        P("tensor", "dp"),
        P("dp", "tensor"),
        P("tensor", "dp"),
    )
    fitting = mesh.shape["dp"] == ZS * XS * CS and mesh.shape["tensor"] == TS

    def on_device(inputs, *others):
        fits = fitting and inputs.shape[0] == TS
        return (on_device_whole if fits else on_device_general)(inputs, *others)

    return jax.shard_map(
        on_device,
        mesh=mesh,
        in_specs=placed,
        out_specs=(
            P("dp", "tensor", None),
            P("dp", "tensor", None),
            P(None, "dp"),
            P("dp", None, None),
            P("dp", None, "tensor"),
            P("tensor"),
            P("tensor", "dp"),
            P("dp", "tensor"),
            P("tensor", "dp"),
        ),
        check_vma=False,
    )
```

```python
import functools
import math

import jax
import jax.numpy as jnp
from jax import lax
from jax.experimental import pallas as pl
from jax.experimental.pallas import tpu as pltpu
from jax.sharding import PartitionSpec as P

EPSILON = 1e-06
HIGHEST = lax.Precision.HIGHEST


def layer_norm(values):
    average = jnp.mean(values, axis=-1, keepdims=True)
    centred = values - average
    inverse = lax.rsqrt(jnp.mean(centred * centred, axis=-1, keepdims=True) + EPSILON)
    return (centred * inverse, inverse)


def norm_back(d_normed, normed, inverse):
    return inverse * (
        d_normed
        - jnp.mean(d_normed, axis=-1, keepdims=True)
        - normed * jnp.mean(d_normed * normed, axis=-1, keepdims=True)
    )


def unit_rows(values):
    inverse = lax.rsqrt(jnp.sum(values * values, axis=-1, keepdims=True) + EPSILON)
    return (values * inverse, inverse)


def unit_back(d_unit, unit, inverse):
    return inverse * (d_unit - unit * jnp.sum(d_unit * unit, axis=-1, keepdims=True))


def spread(values):
    return lax.all_gather(values, "tensor", axis=1, tiled=True)


def collect(terms):
    return lax.psum_scatter(
        terms.astype(jnp.bfloat16), "tensor", scatter_dimension=1, tiled=True
    ).astype(jnp.float32)


def masked_scores(queries, keys_in, scale_row):
    scores = jnp.einsum("qhd,khd->hqk", queries, keys_in, preferred_element_type=jnp.float32)
    visible = scale_row[None, :] <= scale_row[:, None]
    return jnp.where(visible[None], scores, -1e30)


def attend_forward(pieces):
    queries, keys_in, values_in, scale_row = pieces
    scores = masked_scores(queries, keys_in, scale_row)
    largest = jnp.max(scores, axis=-1, keepdims=True)
    exponent = jnp.exp(scores - largest)
    denominator = jnp.sum(exponent, axis=-1, keepdims=True)
    attn_probs = (exponent / denominator).astype(jnp.bfloat16)
    mixed = jnp.einsum("hqk,khd->qhd", attn_probs, values_in, preferred_element_type=jnp.float32)
    return (mixed.astype(jnp.bfloat16), (largest + jnp.log(denominator))[..., 0])


def attend_backward(pieces):
    queries, keys_in, values_in, scale_row, log_total, d_mixed = pieces
    scores = masked_scores(queries, keys_in, scale_row)
    attn_probs = jnp.exp(scores - log_total[..., None])
    d_probs = jnp.einsum("qhd,khd->hqk", d_mixed, values_in, preferred_element_type=jnp.float32)
    offset = jnp.sum(attn_probs * d_probs, axis=-1, keepdims=True)
    d_scores = (attn_probs * (d_probs - offset)).astype(jnp.bfloat16)
    d_queries = jnp.einsum("hqk,khd->qhd", d_scores, keys_in, preferred_element_type=jnp.float32)
    d_keys = jnp.einsum("hqk,qhd->khd", d_scores, queries, preferred_element_type=jnp.float32)
    d_values = jnp.einsum(
        "hqk,qhd->khd", attn_probs.astype(jnp.bfloat16), d_mixed, preferred_element_type=jnp.float32
    )
    return (d_queries, d_keys, d_values)


def on_device_general(
    inputs, labels, scale_ids, cotangent, table, w_ada, w_qkv, head_scale, w_proj, w_fc1, w_fc2
):
    images, local_len, model_width = inputs.shape
    full_len = scale_ids.shape[1]
    local_heads = head_scale.shape[0]
    head_dim = w_qkv.shape[2] // local_heads
    classes = table.shape[0]
    gathered = (
        lax.all_gather(table.astype(jnp.bfloat16), "dp", axis=1, tiled=True),
        lax.all_gather(w_qkv.astype(jnp.bfloat16), "dp", axis=0, tiled=True),
        lax.all_gather(w_proj.astype(jnp.bfloat16), "dp", axis=1, tiled=True),
        lax.all_gather(w_fc1.astype(jnp.bfloat16), "dp", axis=0, tiled=True),
        lax.all_gather(w_fc2.astype(jnp.bfloat16), "dp", axis=1, tiled=True),
    )
    table_low, qkv_low, proj_low, fc1_low, fc2_low = gathered
    qkv_flat = qkv_low.reshape(model_width, -1)
    one_hot = labels[:, None] == jnp.arange(classes)[None, :]
    condition = jnp.dot(one_hot.astype(jnp.bfloat16), table_low, preferred_element_type=jnp.float32)
    silu_low = jax.nn.silu(condition).astype(jnp.bfloat16)
    ada_full = lax.all_gather(w_ada.astype(jnp.bfloat16), "dp", axis=0, tiled=True).reshape(
        model_width, 6 * model_width
    )
    modulation = jnp.dot(silu_low, ada_full, preferred_element_type=jnp.float32)
    modulation = modulation.reshape(images, 6, model_width)
    gain_attn = modulation[:, 0, None, :]
    gain_mlp = modulation[:, 1, None, :]
    scale_attn = modulation[:, 2, None, :]
    scale_mlp = modulation[:, 3, None, :]
    shift_attn = modulation[:, 4, None, :]
    shift_mlp = modulation[:, 5, None, :]
    normed_one, inverse_one = layer_norm(inputs)
    hidden_one = spread((normed_one * (1.0 + scale_attn) + shift_attn).astype(jnp.bfloat16))
    projected = jnp.einsum("bld,dc->blc", hidden_one, qkv_flat, preferred_element_type=jnp.float32)
    projected = projected.reshape(images, full_len, 3, local_heads, head_dim)
    q_unit, q_inverse = unit_rows(projected[:, :, 0])
    k_unit, k_inverse = unit_rows(projected[:, :, 1])
    q_hat = (q_unit * head_scale[:, None]).astype(jnp.bfloat16)
    k_hat = k_unit.astype(jnp.bfloat16)
    v_hat = projected[:, :, 2].astype(jnp.bfloat16)
    mixed, log_total = lax.map(attend_forward, (q_hat, k_hat, v_hat, scale_ids))
    mixed_flat = mixed.reshape(images, full_len, local_heads * head_dim)
    attended = collect(
        jnp.einsum("blc,cd->bld", mixed_flat, proj_low, preferred_element_type=jnp.float32)
    )
    middle = inputs + gain_attn * attended
    normed_two, inverse_two = layer_norm(middle)
    hidden_two = spread((normed_two * (1.0 + scale_mlp) + shift_mlp).astype(jnp.bfloat16))
    before = jnp.einsum("bld,df->blf", hidden_two, fc1_low, preferred_element_type=jnp.float32)
    gelu_fn = functools.partial(jax.nn.gelu, approximate=True)
    active_f, gelu_pull = jax.vjp(gelu_fn, before)
    active = active_f.astype(jnp.bfloat16)
    branch = collect(jnp.einsum("blf,fd->bld", active, fc2_low, preferred_element_type=jnp.float32))
    output = middle + gain_mlp * branch
    again = (
        lax.all_gather(w_qkv.astype(jnp.bfloat16), "dp", axis=0, tiled=True),
        lax.all_gather(w_proj.astype(jnp.bfloat16), "dp", axis=1, tiled=True),
        lax.all_gather(w_fc1.astype(jnp.bfloat16), "dp", axis=0, tiled=True),
        lax.all_gather(w_fc2.astype(jnp.bfloat16), "dp", axis=1, tiled=True),
    )
    qkv_back, proj_back, fc1_back, fc2_back = again
    d_gain_mlp = jnp.sum(cotangent * branch, axis=1)
    d_branch = spread((gain_mlp * cotangent).astype(jnp.bfloat16))
    grad_fc2 = jnp.einsum("blf,bld->fd", active, d_branch, preferred_element_type=jnp.float32)
    d_active = jnp.einsum("bld,fd->blf", d_branch, fc2_back, preferred_element_type=jnp.float32)
    d_before = gelu_pull(d_active)[0].astype(jnp.bfloat16)
    grad_fc1 = jnp.einsum("bld,blf->df", hidden_two, d_before, preferred_element_type=jnp.float32)
    d_hidden_two = collect(
        jnp.einsum("blf,df->bld", d_before, fc1_back, preferred_element_type=jnp.float32)
    )
    d_scale_mlp = jnp.sum(d_hidden_two * normed_two, axis=1)
    d_shift_mlp = jnp.sum(d_hidden_two, axis=1)
    d_middle = cotangent + norm_back(d_hidden_two * (1.0 + scale_mlp), normed_two, inverse_two)
    d_gain_attn = jnp.sum(d_middle * attended, axis=1)
    d_attended = spread((gain_attn * d_middle).astype(jnp.bfloat16))
    grad_proj = jnp.einsum(
        "blc,bld->cd", mixed_flat, d_attended, preferred_element_type=jnp.float32
    )
    d_mixed = jnp.einsum("bld,cd->blc", d_attended, proj_back, preferred_element_type=jnp.float32)
    d_mixed = d_mixed.astype(jnp.bfloat16).reshape(images, full_len, local_heads, head_dim)
    d_q_hat, d_k_hat, d_v_hat = lax.map(
        attend_backward, (q_hat, k_hat, v_hat, scale_ids, log_total, d_mixed)
    )
    scale_terms = jnp.sum(d_q_hat * q_unit, axis=(0, 1, 3))
    d_query = unit_back(d_q_hat * head_scale[:, None], q_unit, q_inverse)
    d_key = unit_back(d_k_hat, k_unit, k_inverse)
    d_raw = jnp.stack([d_query, d_key, d_v_hat], axis=2).astype(jnp.bfloat16)
    d_raw = d_raw.reshape(images, full_len, 3 * local_heads * head_dim)
    grad_qkv = jnp.einsum("bld,blc->dc", hidden_one, d_raw, preferred_element_type=jnp.float32)
    grad_qkv = grad_qkv.reshape(model_width, 3, local_heads * head_dim)
    d_hidden_one = collect(
        jnp.einsum(
            "blc,dc->bld",
            d_raw,
            qkv_back.reshape(model_width, -1),
            preferred_element_type=jnp.float32,
        )
    )
    d_scale_attn = jnp.sum(d_hidden_one * normed_one, axis=1)
    d_shift_attn = jnp.sum(d_hidden_one, axis=1)
    d_inputs = d_middle + norm_back(d_hidden_one * (1.0 + scale_attn), normed_one, inverse_one)
    mod_terms_back = jnp.stack(
        [d_gain_attn, d_gain_mlp, d_scale_attn, d_scale_mlp, d_shift_attn, d_shift_mlp], axis=1
    )
    d_modulation = lax.psum(mod_terms_back.astype(jnp.bfloat16), "tensor").astype(jnp.float32)
    d_mod_flat = d_modulation.reshape(images, 6 * model_width)
    grad_scale = lax.psum(scale_terms, "dp")
    ada_terms = jnp.dot(silu_low.astype(jnp.float32).T, d_mod_flat, precision=HIGHEST)
    grad_ada = lax.psum_scatter(
        ada_terms.reshape(model_width, 6, model_width).astype(jnp.bfloat16),
        "dp",
        scatter_dimension=0,
        tiled=True,
    ).astype(jnp.float32)
    d_silu = jnp.dot(d_mod_flat, ada_full.astype(jnp.float32).T, precision=HIGHEST)
    _, silu_pull = jax.vjp(jax.nn.silu, condition)
    d_condition = silu_pull(d_silu)[0]
    table_terms = jnp.dot(one_hot.astype(jnp.float32).T, d_condition, precision=HIGHEST)
    summed = (
        lax.psum_scatter(
            table_terms.astype(jnp.bfloat16), "dp", scatter_dimension=1, tiled=True
        ).astype(jnp.float32),
        lax.psum_scatter(
            grad_qkv.astype(jnp.bfloat16), "dp", scatter_dimension=0, tiled=True
        ).astype(jnp.float32),
        lax.psum_scatter(
            grad_proj.astype(jnp.bfloat16), "dp", scatter_dimension=1, tiled=True
        ).astype(jnp.float32),
        lax.psum_scatter(
            grad_fc1.astype(jnp.bfloat16), "dp", scatter_dimension=0, tiled=True
        ).astype(jnp.float32),
        lax.psum_scatter(
            grad_fc2.astype(jnp.bfloat16), "dp", scatter_dimension=1, tiled=True
        ).astype(jnp.float32),
    )
    grad_table, grad_qkv_own, grad_proj_own, grad_fc1_own, grad_fc2_own = summed
    return (
        output,
        d_inputs,
        grad_table,
        grad_ada,
        grad_qkv_own,
        grad_scale,
        grad_proj_own,
        grad_fc1_own,
        grad_fc2_own,
    )


BF16 = jnp.bfloat16
F32 = jnp.float32
ZS, XS, CS, TS = 4, 2, 2, 2
BOTH = ("dp", "tensor")
NN = (((1,), (0,)), ((), ()))
NT = (((1,), (1,)), ((), ()))
TN = (((0,), (0,)), ((), ()))
HIDDEN = -1e30
MOST = 256
MIB = 1024 * 1024
BRIEF = pl.CostEstimate(flops=0, bytes_accessed=0, transcendentals=0)


def perm_of(step):
    pairs = []
    for z in range(ZS):
        for x in range(XS):
            for c in range(CS):
                for t in range(TS):
                    nz, nx, nc, nt = step(z, x, c, t)
                    source = ((z * XS + x) * CS + c) * TS + t
                    target = ((nz * XS + nx) * CS + nc) * TS + nt
                    pairs.append((source, target))
    return pairs


def send(values, step):
    return lax.ppermute(values, BOTH, perm_of(step))


def to_core(z, x, c, t):
    return (z, x, 1 - c, t)


def to_x(z, x, c, t):
    return (z, 1 - x, c, t)


def to_t(z, x, c, t):
    return (z, x, c, 1 - t)


def to_z(k):
    return lambda z, x, c, t: ((z + k) % ZS, x, c, t)


def to_z_bit(bit):
    return lambda z, x, c, t: (z ^ bit, x, c, t)


def to_near(z, x, c, t):
    return (z, 1 - x, c, t) if c == 0 else (z, x, c, 1 - t)


def to_far(z, x, c, t):
    return (z, x, c, 1 - t) if c == 0 else (z, 1 - x, c, t)


def pick(values, index, axis=0):
    return lax.dynamic_index_in_dim(values, index, axis, keepdims=False)


def place():
    dp = lax.axis_index("dp")
    t = lax.axis_index("tensor")
    return dp // (XS * CS), (dp // CS) % XS, dp % CS, t


def matmul(left, right, dims):
    return lax.dot_general(left, right, dims, preferred_element_type=F32)


def hold(*values):
    return lax.optimization_barrier(values)


def send_z(values):
    return [send(values, to_z(k)) for k in range(1, ZS)]


def send_terms_z(terms):
    return [send(terms[k - 1], to_z(k)) for k in range(1, ZS)]


def assemble_kernel(widths, crossed, where_ref, *refs):
    pieces, outs, sem = refs[:4], refs[4:-1], refs[-1]
    z, x, c, t = where_ref[0], where_ref[1], where_ref[2], where_ref[3]
    for slot, piece in enumerate(pieces):
        near = (1 - c, c) if crossed else (0, 1)
        dx, dt = [(0, 0), near, (1 - near[0], 1 - near[1]), (1, 1)][slot]
        sx, st = x ^ dx, t ^ dt
        for dz in range(ZS):
            for dc in range(CS):
                sz = (z + ZS - dz) % ZS
                sc = c ^ dc
                row = pl.multiple_of(((sz * XS + sx) * CS + sc) * 64, 64)
                start = 0
                for which, width in enumerate(widths):
                    column = pl.multiple_of(st * width, 128)
                    pltpu.make_async_copy(
                        piece.at[dz, dc, :, pl.ds(start, width)],
                        outs[which].at[pl.ds(row, 64), pl.ds(column, width)],
                        sem.at[which],
                    ).start()
                    start += width
    for which, out in enumerate(outs):
        pltpu.make_async_copy(out, out, sem.at[which]).wait()


def assemble(pieces, position, widths, crossed=True):
    rows = ZS * XS * CS * 64
    return pl.pallas_call(
        functools.partial(assemble_kernel, widths, crossed),
        out_shape=[jax.ShapeDtypeStruct((rows, TS * width), BF16) for width in widths],
        in_specs=[pl.BlockSpec(memory_space=pltpu.SMEM)]
        + [pl.BlockSpec(memory_space=pl.ANY)] * 4,
        out_specs=[pl.BlockSpec(memory_space=pltpu.VMEM)] * len(widths),
        scratch_shapes=[pltpu.SemaphoreType.DMA((len(widths),))],
        cost_estimate=BRIEF,
        compiler_params=pltpu.CompilerParams(vmem_limit_bytes=8 * MIB),
    )(position, *pieces)


def products(factors, added=None):
    terms = [matmul(rows, columns, TN) for rows, columns in factors]
    if added is not None:
        terms = [term + other.astype(F32) for term, other in zip(terms, added)]
    return [term.astype(BF16) for term in terms]


def block(blocks, dx, dt, where):
    z, x, c, t = where
    parts = []
    for values in blocks:
        m = values.shape[1] // TS
        values = lax.dynamic_slice_in_dim(values, (t ^ dt) * m, m, 1)
        values = pick(values.reshape(ZS, XS, CS * 64, m), x ^ dx, 1)
        parts.append(values.reshape(ZS * CS * 64, m))
    return parts[0] if len(parts) == 1 else jnp.concatenate(parts, axis=1)


def scatter_far(blocks, where):
    c = where[2]
    return jnp.stack([block(blocks, 1, 1, where), block(blocks, c, 1 - c, where)])


def scatter_near(blocks, far, where):
    c = where[2]
    return (block(blocks, 1 - c, c, where).astype(F32) + far[0].astype(F32)).astype(BF16)


def scatter_z(blocks, far, near, where):
    z = where[0]
    whole = block(blocks, 0, 0, where).astype(F32) + far[1].astype(F32) + near.astype(F32)
    whole = whole.astype(BF16).reshape(ZS, CS, 64, whole.shape[-1])
    return [pick(whole, (z + k) % ZS) for k in range(ZS)]


def scatter_total(own, others, where):
    c = where[2]
    total = sum(term.astype(F32) for term in [own] + list(others))
    return pick(total, c), pick(total, 1 - c).astype(BF16)


def in_order(own, other, bit):
    return jnp.where(bit == 0, own, other), jnp.where(bit == 0, other, own)


def join_image(values, other, t):
    return jnp.concatenate(in_order(pick(values, t), other.astype(F32), t), axis=0)


def own_and_other(values, t):
    half = values.shape[0] // 2
    own = lax.dynamic_slice_in_dim(values, t * half, half, axis=0)
    give = lax.dynamic_slice_in_dim(values, (1 - t) * half, half, axis=0)
    return own, give.astype(BF16)


def two_images(own, other, t):
    return jnp.stack(in_order(own, other.astype(F32), t))


def unit_of(values, mask):
    squares = jnp.where(mask, values * values, 0.0)
    inverse = lax.rsqrt(jnp.sum(squares, axis=-1, keepdims=True) + EPSILON)
    return jnp.where(mask, values * inverse, 0.0), inverse


def head_masks(shape, head_dim):
    lane = lax.broadcasted_iota(jnp.int32, shape, 1)
    return [(lane >= n * head_dim) & (lane < (n + 1) * head_dim) for n in range(2)]


def attend_kernel(head_dim, scale_ref, row_ref, column_ref, raw_ref, out_ref, bias_ref):
    pair = pl.program_id(0)

    @pl.when(pair == 0)
    def _():
        bias_ref[...] = jnp.where(row_ref[...] <= column_ref[...], 0.0, HIDDEN)

    lanes = 2 * head_dim
    q, k = raw_ref[:, :lanes].astype(F32), raw_ref[:, lanes : 2 * lanes].astype(F32)
    v = raw_ref[:, 2 * lanes :]
    values = jnp.concatenate([v, jnp.ones_like(v)], axis=1)
    tokens = q.shape[0]
    blocks = [(slice(0, MOST), min(2 * MOST, tokens)), (slice(MOST, tokens), tokens)]
    masks = head_masks(q.shape, head_dim)
    k_hat = (unit_of(k, masks[0])[0] + unit_of(k, masks[1])[0]).astype(BF16)
    result = None
    for n in range(2):
        scale = scale_ref[2 * pair + n]
        q_hat = (unit_of(q, masks[n])[0] * scale).astype(BF16)
        mixed = []
        for rows, count in blocks:
            scores = matmul(q_hat[rows], k_hat[:count], NT) + bias_ref[rows, :count]
            weights = jnp.exp(scores - jnp.abs(scale)).astype(BF16)
            mixed.append(matmul(weights, values[:count], NN))
        mixed = jnp.concatenate(mixed, axis=0)
        mixed = mixed[:, : 2 * head_dim] / mixed[:, 2 * head_dim :]
        result = mixed if result is None else jnp.where(masks[n], mixed, result)
    out_ref[...] = result.astype(out_ref.dtype)


def attend_whole(raw, scale_row, all_scale):
    tokens, width = raw.shape[0], raw.shape[1] // 3
    head_dim = width // all_scale.shape[0]
    lanes = 2 * head_dim
    pairs = width // lanes

    block = pl.BlockSpec((tokens, lanes), lambda n: (0, n))
    triple = pl.BlockSpec((tokens, 3 * lanes), lambda n: (0, n))
    return pl.pallas_call(
        functools.partial(attend_kernel, head_dim),
        out_shape=jax.ShapeDtypeStruct((tokens, width), BF16),
        grid=(pairs,),
        in_specs=[
            pl.BlockSpec(memory_space=pltpu.SMEM),
            pl.BlockSpec((1, tokens), lambda n: (0, 0)),
            pl.BlockSpec((tokens, 1), lambda n: (0, 0)),
            triple,
        ],
        out_specs=block,
        scratch_shapes=[pltpu.VMEM((tokens, tokens), F32)],
        cost_estimate=BRIEF,
        compiler_params=pltpu.CompilerParams(vmem_limit_bytes=16 * MIB),
    )(all_scale, scale_row[None, :], scale_row[:, None], raw)


def attend_back_kernel(
    head_dim,
    scale_ref,
    row_ref,
    column_ref,
    raw_ref,
    mixed_ref,
    d_mixed_ref,
    out_ref,
    term_ref,
    bias_ref,
):
    pair = pl.program_id(0)

    @pl.when(pair == 0)
    def _():
        bias_ref[...] = jnp.where(column_ref[...] <= row_ref[...], 0.0, HIDDEN)

    lanes = 2 * head_dim
    q, k = raw_ref[:, :lanes].astype(F32), raw_ref[:, lanes : 2 * lanes].astype(F32)
    v, d_mixed = raw_ref[:, 2 * lanes :], d_mixed_ref[...]
    masks = head_masks(q.shape, head_dim)
    k_units = [unit_of(k, mask) for mask in masks]
    k_hat = (k_units[0][0] + k_units[1][0]).astype(BF16)
    products = d_mixed.astype(F32) * mixed_ref[...].astype(F32)
    tokens = q.shape[0]
    blocks = [(slice(0, min(2 * MOST, tokens)), 0)]
    if tokens > 2 * MOST:
        blocks.append((slice(2 * MOST, tokens), MOST))
    d_q_all = d_k_all = d_v_all = None
    for n in range(2):
        mask = masks[n]
        scale = scale_ref[2 * pair + n]
        q_unit, q_inverse = unit_of(q, mask)
        q_hat = (q_unit * scale).astype(BF16)
        d_out = jnp.where(mask, d_mixed, jnp.zeros_like(d_mixed))
        offset = jnp.sum(jnp.where(mask, products, 0.0), axis=-1, keepdims=True)
        offset = jnp.transpose(jnp.broadcast_to(offset, products.shape))[:1]
        weights, total = [], 0.0
        for keys, first in blocks:
            scores = matmul(k_hat[keys], q_hat[first:], NT) + bias_ref[keys, first:]
            weights.append(jnp.exp(scores - jnp.abs(scale)))
            part = jnp.sum(weights[-1], axis=0, keepdims=True)
            total = part if first == 0 else jnp.concatenate(
                [total[:, :first], total[:, first:] + part], axis=1
            )
        share = 1.0 / total
        d_q, d_k, d_v = None, [], []
        for (keys, first), raised in zip(blocks, weights):
            probs = raised * share[:, first:]
            d_probs = matmul(v[keys], d_out[first:], NT)
            d_scores = (probs * (d_probs - offset[:, first:])).astype(BF16)
            d_v.append(matmul(probs.astype(BF16), d_out[first:], NN))
            d_k.append(matmul(d_scores, q_hat[first:], NN))
            part = matmul(d_scores, k_hat[keys], TN)
            d_q = part if first == 0 else jnp.concatenate(
                [d_q[:first], d_q[first:] + part], axis=0
            )
        d_v, d_k = jnp.concatenate(d_v, axis=0), jnp.concatenate(d_k, axis=0)
        d_q = jnp.where(mask, d_q, 0.0)
        d_k = jnp.where(mask, d_k, 0.0)
        k_unit, k_inverse = k_units[n]
        term = d_q * q_unit
        term_n = jnp.sum(term, axis=0, keepdims=True)
        d_q = q_inverse * scale * (d_q - q_unit * jnp.sum(term, axis=-1, keepdims=True))
        d_k = k_inverse * (d_k - k_unit * jnp.sum(d_k * k_unit, axis=-1, keepdims=True))
        if n == 0:
            d_q_all, d_k_all, d_v_all, term_all = d_q, d_k, d_v, term_n
        else:
            d_q_all, d_k_all = d_q_all + d_q, d_k_all + d_k
            d_v_all, term_all = d_v_all + d_v, term_all + term_n
    out_ref[:, :lanes] = d_q_all.astype(out_ref.dtype)
    out_ref[:, lanes : 2 * lanes] = d_k_all.astype(out_ref.dtype)
    out_ref[:, 2 * lanes :] = d_v_all.astype(out_ref.dtype)
    term_ref[...] = jnp.broadcast_to(term_all, term_ref.shape)


def attend_back_whole(raw, mixed, d_mixed, scale_row, all_scale):
    tokens, width = mixed.shape
    heads = all_scale.shape[0]
    head_dim = width // heads
    lanes = 2 * head_dim
    pairs = width // lanes

    block = pl.BlockSpec((tokens, lanes), lambda n: (0, n))
    triple = pl.BlockSpec((tokens, 3 * lanes), lambda n: (0, n))
    d_raw, terms = pl.pallas_call(
        functools.partial(attend_back_kernel, head_dim),
        out_shape=[
            jax.ShapeDtypeStruct((tokens, 3 * width), BF16),
            jax.ShapeDtypeStruct((8, width), F32),
        ],
        grid=(pairs,),
        in_specs=[
            pl.BlockSpec(memory_space=pltpu.SMEM),
            pl.BlockSpec((1, tokens), lambda n: (0, 0)),
            pl.BlockSpec((tokens, 1), lambda n: (0, 0)),
            triple,
            block,
            block,
        ],
        out_specs=[
            triple,
            pl.BlockSpec((8, lanes), lambda n: (0, n)),
        ],
        scratch_shapes=[pltpu.VMEM((tokens, tokens), F32)],
        cost_estimate=BRIEF,
        compiler_params=pltpu.CompilerParams(vmem_limit_bytes=20 * MIB),
    )(all_scale, scale_row[None, :], scale_row[:, None], raw, mixed, d_mixed)
    return d_raw, jnp.sum(terms[0].reshape(heads, head_dim), axis=1)


def gelu_and_slope(before):
    first = (2.0 / math.pi) ** 0.5
    square = before * before
    gate = 0.5 + 0.5 * jnp.tanh(before * (first + (first * 0.044715) * square))
    active = before * gate
    steep = 2.0 * first + (6.0 * first * 0.044715) * square
    return active, gate + active * (1.0 - gate) * steep


def activate_kernel(rows_ref, weights_ref, active_ref, slope_ref):
    for start in range(0, weights_ref.shape[1], 256):
        columns = slice(start, start + 256)
        active, slope = gelu_and_slope(matmul(rows_ref[...], weights_ref[:, columns], NN))
        active_ref[:, columns] = active.astype(active_ref.dtype)
        slope_ref[:, columns] = slope.astype(slope_ref.dtype)


def by_columns(kernel, rows, weights, count, tile):
    tokens, width = rows.shape
    columns = weights.shape[1]
    out = pl.BlockSpec((tokens, tile), lambda n: (0, n))
    return pl.pallas_call(
        kernel,
        out_shape=[jax.ShapeDtypeStruct((tokens, columns), BF16)] * count,
        grid=(columns // tile,),
        in_specs=[
            pl.BlockSpec((tokens, width), lambda n: (0, 0)),
            pl.BlockSpec((width, tile), lambda n: (0, n)),
        ],
        out_specs=[out] * count,
        cost_estimate=BRIEF,
        compiler_params=pltpu.CompilerParams(vmem_limit_bytes=20 * MIB),
    )(rows, weights)


def halves(values, c, half):
    keep = lax.dynamic_slice_in_dim(values, c * half, half, axis=1)
    give = lax.dynamic_slice_in_dim(values, (1 - c) * half, half, axis=1)
    return keep, give


def on_device_whole(
    inputs, labels, scale_ids, cotangent, table, w_ada, w_qkv, head_scale, w_proj, w_fc1, w_fc2
):
    width = inputs.shape[2]
    classes, rows = table.shape
    heads = TS * head_scale.shape[0]
    quarter = w_qkv.shape[2] // 2
    hidden_quarter = w_fc1.shape[1] // 2
    z, x, c, t = place()
    position = jnp.stack([z, x, c, t]).astype(jnp.int32)

    where = (z, x, c, t)

    pair = 2 * width // heads


    label_pair = jnp.stack(in_order(labels[0], labels[1], t)).astype(F32)
    label_tile = jnp.broadcast_to(label_pair[:, None], (2, 128))
    scale_tile = jnp.broadcast_to(head_scale[None, :], (8, head_scale.shape[0]))
    qkv_halves = []
    for side in (c, 1 - c):
        columns = [
            lax.dynamic_slice_in_dim(w_qkv[:, n].astype(BF16), side * quarter + j * pair, pair, 1)
            for j in range(quarter // pair)
            for n in range(3)
        ]
        qkv_halves.append(jnp.concatenate(columns, axis=1))
    keep_qkv, give_qkv, label_tile, scale_tile, inputs = hold(
        *qkv_halves, label_tile, scale_tile, inputs
    )
    recv_qkv, label_z = send(give_qkv, to_core), send_z(label_tile)
    scale_other = send(scale_tile, to_t)
    keep_qkv, recv_qkv, label_z, scale_other = hold(keep_qkv, recv_qkv, label_z, scale_other)
    two_qkv = jnp.stack([keep_qkv, recv_qkv])
    two_qkv, label_z, inputs, rest = hold(
        two_qkv,
        label_z,
        inputs,
        (cotangent, w_ada, w_proj, w_fc1, w_fc2, table, scale_ids),
    )
    cotangent, w_ada, w_proj, w_fc1, w_fc2, table, scale_ids = rest
    z_qkv = send_z(two_qkv)
    token_other = send(pick(inputs, 1 - t).astype(BF16), to_t)
    scale_row = pick(scale_ids, t)

    odd = z % 2 == 1
    first, third = jnp.where(odd, label_z[0], label_z[2]), jnp.where(odd, label_z[2], label_z[0])
    label_rows = jnp.concatenate([label_tile, first, label_z[1], third])
    label_rows = jnp.concatenate([label_rows, send(label_rows, to_x)])
    label_rows = jnp.concatenate([label_rows, send(label_rows, to_core)])
    all_labels = label_rows[:, 0].astype(jnp.int32)
    one_hot = (all_labels[:, None] == jnp.arange(classes)[None, :]).astype(BF16)
    condition = matmul(one_hot, table.astype(BF16), NN)
    silu_low = jax.nn.silu(condition).astype(BF16)
    ada_low = w_ada.astype(BF16).reshape(rows, 6 * width)
    silu_own = silu_low.reshape(-1, TS, rows)[:, 0]
    partial = matmul(silu_own, ada_low, NN).reshape(CS, XS, ZS, 6 * width)
    partial = partial[0] + send(partial[1], to_core)
    own_part, x_part = partial[0], send(partial[1], to_x)
    w_fc1, w_proj_t, w_fc2_t = w_fc1.astype(BF16), w_proj.astype(BF16).T, w_fc2.astype(BF16).T
    rest_halves = [halves(w_proj_t, c, quarter), halves(w_fc1, c, hidden_quarter)]
    rest_halves.append(halves(w_fc2_t, c, hidden_quarter))
    keep_rest, give_rest = [jnp.concatenate([part[n] for part in rest_halves], 1) for n in range(2)]
    split = quarter + hidden_quarter
    z_qkv, own_part, x_part, recv_rest = hold(
        z_qkv, own_part, x_part, send(give_rest, to_core)
    )

    four_qkv = jnp.stack([two_qkv] + z_qkv)
    partial = own_part + x_part
    two_mid = jnp.stack([keep_rest[:, :split], recv_rest[:, :split]])
    two_fc2 = jnp.stack([keep_rest[:, split:], recv_rest[:, split:]])
    four_qkv, partial, two_mid, two_fc2 = hold(four_qkv, partial, two_mid, two_fc2)
    near_qkv, far_qkv = send(four_qkv, to_t), send(four_qkv, to_x)
    mid_2 = send(two_mid, to_z(2))
    partial = partial[:2] + send(partial[2:], to_z_bit(2))
    mod_part, mod_bit = partial[0], send(partial[1], to_z_bit(1))
    cotangent_give = pick(cotangent, 1 - t).astype(BF16)
    near_qkv, far_qkv, mid_2, two_mid, cotangent_give, mod_part, mod_bit, token_other = hold(
        near_qkv, far_qkv, mid_2, two_mid, cotangent_give, mod_part, mod_bit, token_other
    )
    modulation = (mod_part + mod_bit).reshape(6, 1, width)
    gain_attn, gain_mlp, scale_attn, scale_mlp, shift_attn, shift_mlp = modulation
    tokens_in = join_image(inputs, token_other, t)
    last_qkv = send(near_qkv, to_x)
    mid_1, mid_3 = send(two_mid, to_z(1)), send(two_mid, to_z(3))
    cotangent_other = send(cotangent_give, to_t)
    normed_one, inverse_one = layer_norm(tokens_in)
    hidden_one = (normed_one * (1.0 + scale_attn) + shift_attn).astype(BF16)
    last_qkv, mid_1, mid_3, hidden_one, cotangent_other = hold(
        last_qkv, mid_1, mid_3, hidden_one, cotangent_other
    )
    scales = jnp.concatenate(in_order(head_scale, scale_other[0], t)).reshape(TS, 2, -1)
    scale_own, scale_oth = pick(scales, c, 1).reshape(-1), pick(scales, 1 - c, 1).reshape(-1)
    four_mid = jnp.stack([two_mid, mid_1, mid_2, mid_3])
    four_mid, last_qkv, two_fc2, hidden_one = hold(four_mid, last_qkv, two_fc2, hidden_one)
    near_mid, far_mid = send(four_mid, to_near), send(four_mid, to_far)
    z_fc2 = send_z(two_fc2)
    (qkv_own,) = assemble(
        [four_qkv, near_qkv, far_qkv, last_qkv], position, [3 * quarter], crossed=False
    )
    raw_own = matmul(hidden_one, qkv_own, NN).astype(BF16)
    raw_own, qkv_oth = hold(raw_own, send(qkv_own, to_core))
    raw_oth = matmul(hidden_one, qkv_oth, NN).astype(BF16)
    mixed_own = attend_whole(raw_own, scale_row, scale_own)
    mixed_own, near_mid, far_mid, z_fc2, raw_oth = hold(
        mixed_own, near_mid, far_mid, z_fc2, raw_oth
    )
    last_mid = send(near_mid, to_far)
    mixed_oth = attend_whole(raw_oth, scale_row, scale_oth)
    four_fc2 = jnp.stack([two_fc2] + z_fc2)
    mixed_oth, last_mid, four_fc2 = hold(mixed_oth, last_mid, four_fc2)
    near_fc2, far_fc2 = send(four_fc2, to_near), send(four_fc2, to_far)
    proj_own, fc1_own = assemble(
        [four_mid, near_mid, far_mid, last_mid], position, [quarter, hidden_quarter]
    )
    upstream = join_image(cotangent, cotangent_other, t)
    d_branch = (gain_mlp * upstream).astype(BF16)
    proj_oth, d_branch = hold(send(proj_own, to_core), d_branch)
    fc1_oth = send(fc1_own, to_core)
    attended = matmul(mixed_own, proj_own, NT) + matmul(mixed_oth, proj_oth, NT)
    middle = tokens_in + gain_attn * attended
    normed_two, inverse_two = layer_norm(middle)
    hidden_two = (normed_two * (1.0 + scale_mlp) + shift_mlp).astype(BF16)
    hidden_two, fc1_oth = hold(hidden_two, fc1_oth)

    def activate(weights):
        active, slope = gelu_and_slope(matmul(hidden_two, weights, NN))
        return active.astype(BF16), slope.astype(BF16)

    active_oth, slope_oth = by_columns(activate_kernel, hidden_two, fc1_oth, 2, 512)
    active_oth, slope_oth, near_fc2, far_fc2 = hold(active_oth, slope_oth, near_fc2, far_fc2)
    last_fc2 = send(near_fc2, to_far)
    active_own, slope_own = activate(fc1_own)
    given = products([(d_branch, active_oth)])
    given, active_own, slope_own, last_fc2 = hold(given, active_own, slope_own, last_fc2)
    added = [send(part, to_core) for part in given]
    (fc2_own,) = assemble([four_fc2, near_fc2, far_fc2, last_fc2], position, [hidden_quarter])
    fc2_own, added = hold(fc2_own, added)
    fc2_oth = send(fc2_own, to_core)
    blocks_fc2 = products([(d_branch, active_own)], added)
    blocks_fc2, fc2_oth = hold(blocks_fc2, fc2_oth)
    far_give, blocks_fc2, active_own = hold(scatter_far(blocks_fc2, where), blocks_fc2, active_own)
    far_fc2 = send(far_give, to_far)

    d_before_oth = (matmul(d_branch, fc2_oth, NN) * slope_oth.astype(F32)).astype(BF16)
    d_before_own = (matmul(d_branch, fc2_own, NN) * slope_own.astype(F32)).astype(BF16)
    given = products([(hidden_two, d_before_oth)])
    given, d_before_oth, d_before_own = hold(given, d_before_oth, d_before_own)
    added = [send(part, to_core) for part in given]
    d_hidden_two = matmul(d_before_own, fc1_own, NT) + matmul(d_before_oth, fc1_oth, NT)
    d_scale_mlp = jnp.sum(d_hidden_two * normed_two, axis=0)
    d_shift_mlp = jnp.sum(d_hidden_two, axis=0)
    d_middle = upstream + norm_back(d_hidden_two * (1.0 + scale_mlp), normed_two, inverse_two)
    d_gain_attn = jnp.sum(d_middle * attended, axis=0)
    d_attended = (gain_attn * d_middle).astype(BF16)
    d_attended, added = hold(d_attended, added)
    blocks_fc1 = products([(hidden_two, d_before_own)], added)
    far_give, blocks_fc1, d_attended, far_fc2 = hold(
        scatter_far(blocks_fc1, where), blocks_fc1, d_attended, far_fc2
    )
    near_fc2 = send(scatter_near(blocks_fc2, far_fc2, where), to_near)
    far_fc1 = send(far_give, to_far)
    given = products([(d_attended, mixed_oth)])
    given, d_attended = hold(given, d_attended)
    added = [send(part, to_core) for part in given]
    d_mixed_oth = matmul(d_attended, proj_oth, NN).astype(BF16)
    d_mixed_own = matmul(d_attended, proj_own, NN).astype(BF16)
    d_mixed_oth, d_mixed_own, added = hold(d_mixed_oth, d_mixed_own, added)
    blocks_proj = products([(d_attended, mixed_own)], added)
    blocks_proj, d_mixed_oth = hold(blocks_proj, d_mixed_oth)
    far_proj = send(scatter_far(blocks_proj, where), to_far)
    d_raw_oth, terms_oth = attend_back_whole(raw_oth, mixed_oth, d_mixed_oth, scale_row, scale_oth)
    given = products([(hidden_one, d_raw_oth)])
    given, near_fc2, d_mixed_own = hold(given, near_fc2, d_mixed_own)
    added = [send(part, to_core) for part in given]
    d_raw_own, terms_own = attend_back_whole(raw_own, mixed_own, d_mixed_own, scale_row, scale_own)
    d_raw_own, far_fc1, far_proj, added = hold(d_raw_own, far_fc1, far_proj, added)
    blocks_mid = blocks_proj + blocks_fc1
    far_mid = [jnp.concatenate([far_proj[n], far_fc1[n]], axis=1) for n in range(2)]
    near_give = scatter_near(blocks_mid, far_mid, where)
    z_fc2 = scatter_z(blocks_fc2, far_fc2, near_fc2, where)
    near_give, z_fc2, d_raw_own = hold(near_give, z_fc2, d_raw_own)
    near_mid = send(near_give, to_near)
    own_fc2, others_fc2 = z_fc2[0], send_terms_z(z_fc2[1:])
    blocks_qkv = products([(hidden_one, d_raw_own)], added)
    far_give, blocks_qkv, d_raw_own, d_raw_oth, active_own = hold(
        scatter_far(blocks_qkv, where), blocks_qkv, d_raw_own, d_raw_oth, active_own
    )
    far_qkv = send(far_give, to_far)
    d_hidden_one = matmul(d_raw_own, qkv_own, NT) + matmul(d_raw_oth, qkv_oth, NT)
    d_hidden_one, near_mid, others_fc2 = hold(d_hidden_one, near_mid, others_fc2)
    z_mid = scatter_z(blocks_mid, far_mid, near_mid, where)
    own_mid, others_mid = z_mid[0], send_terms_z(z_mid[1:])
    d_scale_attn = jnp.sum(d_hidden_one * normed_one, axis=0)
    d_shift_attn = jnp.sum(d_hidden_one, axis=0)
    d_inputs = d_middle + norm_back(d_hidden_one * (1.0 + scale_attn), normed_one, inverse_one)
    inputs_own, inputs_give = own_and_other(d_inputs, t)
    far_qkv, inputs_give, d_scale_attn = hold(far_qkv, inputs_give, d_scale_attn)
    near_give, active_own, inputs_give = hold(
        scatter_near(blocks_qkv, far_qkv, where), active_own, inputs_give
    )
    near_qkv = send(near_give, to_near)
    branch = matmul(active_own, fc2_own, NT) + matmul(active_oth, fc2_oth, NT)
    output_own, output_give = own_and_other(middle + gain_mlp * branch, t)
    d_gain_mlp = jnp.sum(upstream * branch, axis=0)
    d_modulation = jnp.concatenate(
        [d_gain_attn, d_gain_mlp, d_scale_attn, d_scale_mlp, d_shift_attn, d_shift_mlp]
    )
    terms = in_order(terms_own.reshape(TS, -1), terms_oth.reshape(TS, -1), c)
    scale_terms = jnp.concatenate(terms, axis=1).reshape(-1)
    scale_high = lax.reduce_precision(scale_terms, 8, 7)
    row = jnp.concatenate(
        [d_modulation, scale_high, scale_terms - scale_high, jnp.zeros((128 - 2 * heads,), F32)]
    ).astype(BF16)[None, :]
    mod_rows = jnp.concatenate([row, send(row, to_t)])
    near_qkv, mod_rows, others_mid = hold(near_qkv, mod_rows, others_mid)
    z_qkv = scatter_z(blocks_qkv, far_qkv, near_qkv, where)
    z_qkv, mod_rows, inputs_give, output_give = hold(z_qkv, mod_rows, inputs_give, output_give)
    own_qkv, others_qkv = z_qkv[0], send_terms_z(z_qkv[1:])
    mod_z = send_z(mod_rows)
    inputs_other, output_other = send(inputs_give, to_t), send(output_give, to_t)
    half_fc2, other_fc2 = scatter_total(own_fc2, others_fc2, where)
    half_mid, other_mid = scatter_total(own_mid, others_mid, where)
    other_rest = send(jnp.concatenate([other_mid, other_fc2], axis=1), to_core)
    first, third = jnp.where(odd, mod_z[0], mod_z[2]), jnp.where(odd, mod_z[2], mod_z[0])
    mod_rows = jnp.concatenate([mod_rows, first, mod_z[1], third])
    mod_x, inputs_other = hold(send(mod_rows, to_x), inputs_other)
    mod_rows = jnp.concatenate([mod_rows, mod_x])
    mod_rows = jnp.concatenate([mod_rows, send(mod_rows, to_core)])

    d_mod_all = mod_rows[:, : 6 * width]
    scale_sum = jnp.sum(mod_rows[:, 6 * width : 6 * width + 2 * heads].astype(F32), axis=0)
    scale_sum = (scale_sum[:heads] + scale_sum[heads:]).reshape(TS, heads // TS)
    grad_scale = pick(scale_sum, t)
    grad_ada = [
        matmul(silu_low, d_mod_all[:, n * width : (n + 1) * width], TN) for n in range(6)
    ]
    grad_ada = jnp.stack(grad_ada).transpose(1, 0, 2)
    d_silu = matmul(d_mod_all, ada_low, NT)
    _, silu_pull = jax.vjp(jax.nn.silu, condition)
    d_condition = silu_pull(d_silu)[0]
    grad_table = jnp.dot(one_hot.astype(F32).T, d_condition, precision=HIGHEST)

    def joined(own, other):
        return jnp.concatenate(in_order(own, other.astype(F32), c), axis=1)

    grad_proj = joined(half_mid[:, :quarter], other_rest[:, :quarter]).T
    grad_fc1 = joined(half_mid[:, quarter:], other_rest[:, quarter:split])
    grad_fc2 = joined(half_fc2, other_rest[:, split:]).T
    others_qkv, others = hold(
        others_qkv, (grad_ada, grad_table, grad_scale, inputs_other, grad_proj, grad_fc1, grad_fc2)
    )
    grad_ada, grad_table, grad_scale, inputs_other, grad_proj, grad_fc1, grad_fc2 = others
    half_qkv, other_qkv = scatter_total(own_qkv, others_qkv, where)
    other_qkv = send(other_qkv, to_core)

    def part_of(values, n):
        starts = range(n * pair, 3 * quarter, 3 * pair)
        return jnp.concatenate([values[:, start : start + pair] for start in starts], axis=1)

    grad_qkv = [joined(part_of(half_qkv, n), part_of(other_qkv, n)) for n in range(3)]
    return (
        two_images(output_own, output_other, t),
        two_images(inputs_own, inputs_other, t),
        grad_table,
        grad_ada,
        jnp.stack(grad_qkv, axis=1),
        grad_scale,
        grad_proj,
        grad_fc1,
        grad_fc2,
    )


def solution(mesh):
    placed = (
        P("dp", "tensor", None),
        P("dp"),
        P("dp", None),
        P("dp", "tensor", None),
        P(None, "dp"),
        P("dp", None, None),
        P("dp", None, "tensor"),
        P("tensor"),
        P("tensor", "dp"),
        P("dp", "tensor"),
        P("tensor", "dp"),
    )
    fitting = mesh.shape["dp"] == ZS * XS * CS and mesh.shape["tensor"] == TS

    def on_device(inputs, *others):
        fits = fitting and inputs.shape[0] == TS
        return (on_device_whole if fits else on_device_general)(inputs, *others)

    return jax.shard_map(
        on_device,
        mesh=mesh,
        in_specs=placed,
        out_specs=(
            P("dp", "tensor", None),
            P("dp", "tensor", None),
            P(None, "dp"),
            P("dp", None, None),
            P("dp", None, "tensor"),
            P("tensor"),
            P("tensor", "dp"),
            P("dp", "tensor"),
            P("tensor", "dp"),
        ),
        check_vma=False,
    )
```

```python
import functools
import math

import jax
import jax.numpy as jnp
from jax import lax
from jax.experimental import pallas as pl
from jax.experimental.pallas import tpu as pltpu
from jax.sharding import PartitionSpec as P

EPSILON = 1e-06
HIGHEST = lax.Precision.HIGHEST


def layer_norm(values):
    average = jnp.mean(values, axis=-1, keepdims=True)
    centred = values - average
    inverse = lax.rsqrt(jnp.mean(centred * centred, axis=-1, keepdims=True) + EPSILON)
    return (centred * inverse, inverse)


def norm_back(d_normed, normed, inverse):
    return inverse * (
        d_normed
        - jnp.mean(d_normed, axis=-1, keepdims=True)
        - normed * jnp.mean(d_normed * normed, axis=-1, keepdims=True)
    )


def unit_rows(values):
    inverse = lax.rsqrt(jnp.sum(values * values, axis=-1, keepdims=True) + EPSILON)
    return (values * inverse, inverse)


def unit_back(d_unit, unit, inverse):
    return inverse * (d_unit - unit * jnp.sum(d_unit * unit, axis=-1, keepdims=True))


def spread(values):
    return lax.all_gather(values, "tensor", axis=1, tiled=True)


def collect(terms):
    return lax.psum_scatter(
        terms.astype(jnp.bfloat16), "tensor", scatter_dimension=1, tiled=True
    ).astype(jnp.float32)


def masked_scores(queries, keys_in, scale_row):
    scores = jnp.einsum("qhd,khd->hqk", queries, keys_in, preferred_element_type=jnp.float32)
    visible = scale_row[None, :] <= scale_row[:, None]
    return jnp.where(visible[None], scores, -1e30)


def attend_forward(pieces):
    queries, keys_in, values_in, scale_row = pieces
    scores = masked_scores(queries, keys_in, scale_row)
    largest = jnp.max(scores, axis=-1, keepdims=True)
    exponent = jnp.exp(scores - largest)
    denominator = jnp.sum(exponent, axis=-1, keepdims=True)
    attn_probs = (exponent / denominator).astype(jnp.bfloat16)
    mixed = jnp.einsum("hqk,khd->qhd", attn_probs, values_in, preferred_element_type=jnp.float32)
    return (mixed.astype(jnp.bfloat16), (largest + jnp.log(denominator))[..., 0])


def attend_backward(pieces):
    queries, keys_in, values_in, scale_row, log_total, d_mixed = pieces
    scores = masked_scores(queries, keys_in, scale_row)
    attn_probs = jnp.exp(scores - log_total[..., None])
    d_probs = jnp.einsum("qhd,khd->hqk", d_mixed, values_in, preferred_element_type=jnp.float32)
    offset = jnp.sum(attn_probs * d_probs, axis=-1, keepdims=True)
    d_scores = (attn_probs * (d_probs - offset)).astype(jnp.bfloat16)
    d_queries = jnp.einsum("hqk,khd->qhd", d_scores, keys_in, preferred_element_type=jnp.float32)
    d_keys = jnp.einsum("hqk,qhd->khd", d_scores, queries, preferred_element_type=jnp.float32)
    d_values = jnp.einsum(
        "hqk,qhd->khd", attn_probs.astype(jnp.bfloat16), d_mixed, preferred_element_type=jnp.float32
    )
    return (d_queries, d_keys, d_values)


def on_device_general(
    inputs, labels, scale_ids, cotangent, table, w_ada, w_qkv, head_scale, w_proj, w_fc1, w_fc2
):
    images, local_len, model_width = inputs.shape
    full_len = scale_ids.shape[1]
    local_heads = head_scale.shape[0]
    head_dim = w_qkv.shape[2] // local_heads
    classes = table.shape[0]
    gathered = (
        lax.all_gather(table.astype(jnp.bfloat16), "dp", axis=1, tiled=True),
        lax.all_gather(w_qkv.astype(jnp.bfloat16), "dp", axis=0, tiled=True),
        lax.all_gather(w_proj.astype(jnp.bfloat16), "dp", axis=1, tiled=True),
        lax.all_gather(w_fc1.astype(jnp.bfloat16), "dp", axis=0, tiled=True),
        lax.all_gather(w_fc2.astype(jnp.bfloat16), "dp", axis=1, tiled=True),
    )
    table_low, qkv_low, proj_low, fc1_low, fc2_low = gathered
    qkv_flat = qkv_low.reshape(model_width, -1)
    one_hot = labels[:, None] == jnp.arange(classes)[None, :]
    condition = jnp.dot(one_hot.astype(jnp.bfloat16), table_low, preferred_element_type=jnp.float32)
    silu_low = jax.nn.silu(condition).astype(jnp.bfloat16)
    ada_full = lax.all_gather(w_ada.astype(jnp.bfloat16), "dp", axis=0, tiled=True).reshape(
        model_width, 6 * model_width
    )
    modulation = jnp.dot(silu_low, ada_full, preferred_element_type=jnp.float32)
    modulation = modulation.reshape(images, 6, model_width)
    gain_attn = modulation[:, 0, None, :]
    gain_mlp = modulation[:, 1, None, :]
    scale_attn = modulation[:, 2, None, :]
    scale_mlp = modulation[:, 3, None, :]
    shift_attn = modulation[:, 4, None, :]
    shift_mlp = modulation[:, 5, None, :]
    normed_one, inverse_one = layer_norm(inputs)
    hidden_one = spread((normed_one * (1.0 + scale_attn) + shift_attn).astype(jnp.bfloat16))
    projected = jnp.einsum("bld,dc->blc", hidden_one, qkv_flat, preferred_element_type=jnp.float32)
    projected = projected.reshape(images, full_len, 3, local_heads, head_dim)
    q_unit, q_inverse = unit_rows(projected[:, :, 0])
    k_unit, k_inverse = unit_rows(projected[:, :, 1])
    q_hat = (q_unit * head_scale[:, None]).astype(jnp.bfloat16)
    k_hat = k_unit.astype(jnp.bfloat16)
    v_hat = projected[:, :, 2].astype(jnp.bfloat16)
    mixed, log_total = lax.map(attend_forward, (q_hat, k_hat, v_hat, scale_ids))
    mixed_flat = mixed.reshape(images, full_len, local_heads * head_dim)
    attended = collect(
        jnp.einsum("blc,cd->bld", mixed_flat, proj_low, preferred_element_type=jnp.float32)
    )
    middle = inputs + gain_attn * attended
    normed_two, inverse_two = layer_norm(middle)
    hidden_two = spread((normed_two * (1.0 + scale_mlp) + shift_mlp).astype(jnp.bfloat16))
    before = jnp.einsum("bld,df->blf", hidden_two, fc1_low, preferred_element_type=jnp.float32)
    gelu_fn = functools.partial(jax.nn.gelu, approximate=True)
    active_f, gelu_pull = jax.vjp(gelu_fn, before)
    active = active_f.astype(jnp.bfloat16)
    branch = collect(jnp.einsum("blf,fd->bld", active, fc2_low, preferred_element_type=jnp.float32))
    output = middle + gain_mlp * branch
    again = (
        lax.all_gather(w_qkv.astype(jnp.bfloat16), "dp", axis=0, tiled=True),
        lax.all_gather(w_proj.astype(jnp.bfloat16), "dp", axis=1, tiled=True),
        lax.all_gather(w_fc1.astype(jnp.bfloat16), "dp", axis=0, tiled=True),
        lax.all_gather(w_fc2.astype(jnp.bfloat16), "dp", axis=1, tiled=True),
    )
    qkv_back, proj_back, fc1_back, fc2_back = again
    d_gain_mlp = jnp.sum(cotangent * branch, axis=1)
    d_branch = spread((gain_mlp * cotangent).astype(jnp.bfloat16))
    grad_fc2 = jnp.einsum("blf,bld->fd", active, d_branch, preferred_element_type=jnp.float32)
    d_active = jnp.einsum("bld,fd->blf", d_branch, fc2_back, preferred_element_type=jnp.float32)
    d_before = gelu_pull(d_active)[0].astype(jnp.bfloat16)
    grad_fc1 = jnp.einsum("bld,blf->df", hidden_two, d_before, preferred_element_type=jnp.float32)
    d_hidden_two = collect(
        jnp.einsum("blf,df->bld", d_before, fc1_back, preferred_element_type=jnp.float32)
    )
    d_scale_mlp = jnp.sum(d_hidden_two * normed_two, axis=1)
    d_shift_mlp = jnp.sum(d_hidden_two, axis=1)
    d_middle = cotangent + norm_back(d_hidden_two * (1.0 + scale_mlp), normed_two, inverse_two)
    d_gain_attn = jnp.sum(d_middle * attended, axis=1)
    d_attended = spread((gain_attn * d_middle).astype(jnp.bfloat16))
    grad_proj = jnp.einsum(
        "blc,bld->cd", mixed_flat, d_attended, preferred_element_type=jnp.float32
    )
    d_mixed = jnp.einsum("bld,cd->blc", d_attended, proj_back, preferred_element_type=jnp.float32)
    d_mixed = d_mixed.astype(jnp.bfloat16).reshape(images, full_len, local_heads, head_dim)
    d_q_hat, d_k_hat, d_v_hat = lax.map(
        attend_backward, (q_hat, k_hat, v_hat, scale_ids, log_total, d_mixed)
    )
    scale_terms = jnp.sum(d_q_hat * q_unit, axis=(0, 1, 3))
    d_query = unit_back(d_q_hat * head_scale[:, None], q_unit, q_inverse)
    d_key = unit_back(d_k_hat, k_unit, k_inverse)
    d_raw = jnp.stack([d_query, d_key, d_v_hat], axis=2).astype(jnp.bfloat16)
    d_raw = d_raw.reshape(images, full_len, 3 * local_heads * head_dim)
    grad_qkv = jnp.einsum("bld,blc->dc", hidden_one, d_raw, preferred_element_type=jnp.float32)
    grad_qkv = grad_qkv.reshape(model_width, 3, local_heads * head_dim)
    d_hidden_one = collect(
        jnp.einsum(
            "blc,dc->bld",
            d_raw,
            qkv_back.reshape(model_width, -1),
            preferred_element_type=jnp.float32,
        )
    )
    d_scale_attn = jnp.sum(d_hidden_one * normed_one, axis=1)
    d_shift_attn = jnp.sum(d_hidden_one, axis=1)
    d_inputs = d_middle + norm_back(d_hidden_one * (1.0 + scale_attn), normed_one, inverse_one)
    mod_terms_back = jnp.stack(
        [d_gain_attn, d_gain_mlp, d_scale_attn, d_scale_mlp, d_shift_attn, d_shift_mlp], axis=1
    )
    d_modulation = lax.psum(mod_terms_back.astype(jnp.bfloat16), "tensor").astype(jnp.float32)
    d_mod_flat = d_modulation.reshape(images, 6 * model_width)
    grad_scale = lax.psum(scale_terms, "dp")
    ada_terms = jnp.dot(silu_low.astype(jnp.float32).T, d_mod_flat, precision=HIGHEST)
    grad_ada = lax.psum_scatter(
        ada_terms.reshape(model_width, 6, model_width).astype(jnp.bfloat16),
        "dp",
        scatter_dimension=0,
        tiled=True,
    ).astype(jnp.float32)
    d_silu = jnp.dot(d_mod_flat, ada_full.astype(jnp.float32).T, precision=HIGHEST)
    _, silu_pull = jax.vjp(jax.nn.silu, condition)
    d_condition = silu_pull(d_silu)[0]
    table_terms = jnp.dot(one_hot.astype(jnp.float32).T, d_condition, precision=HIGHEST)
    summed = (
        lax.psum_scatter(
            table_terms.astype(jnp.bfloat16), "dp", scatter_dimension=1, tiled=True
        ).astype(jnp.float32),
        lax.psum_scatter(
            grad_qkv.astype(jnp.bfloat16), "dp", scatter_dimension=0, tiled=True
        ).astype(jnp.float32),
        lax.psum_scatter(
            grad_proj.astype(jnp.bfloat16), "dp", scatter_dimension=1, tiled=True
        ).astype(jnp.float32),
        lax.psum_scatter(
            grad_fc1.astype(jnp.bfloat16), "dp", scatter_dimension=0, tiled=True
        ).astype(jnp.float32),
        lax.psum_scatter(
            grad_fc2.astype(jnp.bfloat16), "dp", scatter_dimension=1, tiled=True
        ).astype(jnp.float32),
    )
    grad_table, grad_qkv_own, grad_proj_own, grad_fc1_own, grad_fc2_own = summed
    return (
        output,
        d_inputs,
        grad_table,
        grad_ada,
        grad_qkv_own,
        grad_scale,
        grad_proj_own,
        grad_fc1_own,
        grad_fc2_own,
    )


BF16 = jnp.bfloat16
F32 = jnp.float32
ZS, XS, CS, TS = 4, 2, 2, 2
BOTH = ("dp", "tensor")
NN = (((1,), (0,)), ((), ()))
NT = (((1,), (1,)), ((), ()))
TN = (((0,), (0,)), ((), ()))
HIDDEN = -1e30
MOST = 256
MIB = 1024 * 1024
BRIEF = pl.CostEstimate(flops=0, bytes_accessed=0, transcendentals=0)


def perm_of(step):
    pairs = []
    for z in range(ZS):
        for x in range(XS):
            for c in range(CS):
                for t in range(TS):
                    nz, nx, nc, nt = step(z, x, c, t)
                    source = ((z * XS + x) * CS + c) * TS + t
                    target = ((nz * XS + nx) * CS + nc) * TS + nt
                    pairs.append((source, target))
    return pairs


def send(values, step):
    return lax.ppermute(values, BOTH, perm_of(step))


def to_core(z, x, c, t):
    return (z, x, 1 - c, t)


def to_x(z, x, c, t):
    return (z, 1 - x, c, t)


def to_t(z, x, c, t):
    return (z, x, c, 1 - t)


def to_z(k):
    return lambda z, x, c, t: ((z + k) % ZS, x, c, t)


def to_z_bit(bit):
    return lambda z, x, c, t: (z ^ bit, x, c, t)


def to_near(z, x, c, t):
    return (z, 1 - x, c, t) if c == 0 else (z, x, c, 1 - t)


def to_far(z, x, c, t):
    return (z, x, c, 1 - t) if c == 0 else (z, 1 - x, c, t)


def pick(values, index, axis=0):
    return lax.dynamic_index_in_dim(values, index, axis, keepdims=False)


def place():
    dp = lax.axis_index("dp")
    t = lax.axis_index("tensor")
    return dp // (XS * CS), (dp // CS) % XS, dp % CS, t


def matmul(left, right, dims):
    return lax.dot_general(left, right, dims, preferred_element_type=F32)


def hold(*values):
    return lax.optimization_barrier(values)


def send_z(values):
    return [send(values, to_z(k)) for k in range(1, ZS)]


def send_terms_z(terms):
    return [send(terms[k - 1], to_z(k)) for k in range(1, ZS)]


def assemble_kernel(widths, crossed, where_ref, *refs):
    pieces, outs, sem = refs[:4], refs[4:-1], refs[-1]
    z, x, c, t = where_ref[0], where_ref[1], where_ref[2], where_ref[3]
    for slot, piece in enumerate(pieces):
        near = (1 - c, c) if crossed else (0, 1)
        dx, dt = [(0, 0), near, (1 - near[0], 1 - near[1]), (1, 1)][slot]
        sx, st = x ^ dx, t ^ dt
        for dz in range(ZS):
            for dc in range(CS):
                sz = (z + ZS - dz) % ZS
                sc = c ^ dc
                row = pl.multiple_of(((sz * XS + sx) * CS + sc) * 64, 64)
                start = 0
                for which, width in enumerate(widths):
                    column = pl.multiple_of(st * width, 128)
                    pltpu.make_async_copy(
                        piece.at[dz, dc, :, pl.ds(start, width)],
                        outs[which].at[pl.ds(row, 64), pl.ds(column, width)],
                        sem.at[which],
                    ).start()
                    start += width
    for which, out in enumerate(outs):
        pltpu.make_async_copy(out, out, sem.at[which]).wait()


def assemble(pieces, position, widths, crossed=True):
    rows = ZS * XS * CS * 64
    return pl.pallas_call(
        functools.partial(assemble_kernel, widths, crossed),
        out_shape=[jax.ShapeDtypeStruct((rows, TS * width), BF16) for width in widths],
        in_specs=[pl.BlockSpec(memory_space=pltpu.SMEM)]
        + [pl.BlockSpec(memory_space=pl.ANY)] * 4,
        out_specs=[pl.BlockSpec(memory_space=pltpu.VMEM)] * len(widths),
        scratch_shapes=[pltpu.SemaphoreType.DMA((len(widths),))],
        cost_estimate=BRIEF,
        compiler_params=pltpu.CompilerParams(vmem_limit_bytes=8 * MIB),
    )(position, *pieces)


def products(factors, added=None):
    terms = [matmul(rows, columns, TN) for rows, columns in factors]
    if added is not None:
        terms = [term + other.astype(F32) for term, other in zip(terms, added)]
    return [term.astype(BF16) for term in terms]


def block(blocks, dx, dt, where):
    z, x, c, t = where
    parts = []
    for values in blocks:
        m = values.shape[1] // TS
        values = lax.dynamic_slice_in_dim(values, (t ^ dt) * m, m, 1)
        values = pick(values.reshape(ZS, XS, CS * 64, m), x ^ dx, 1)
        parts.append(values.reshape(ZS * CS * 64, m))
    return parts[0] if len(parts) == 1 else jnp.concatenate(parts, axis=1)


def scatter_far(blocks, where):
    c = where[2]
    return jnp.stack([block(blocks, 1, 1, where), block(blocks, c, 1 - c, where)])


def scatter_near(blocks, far, where):
    c = where[2]
    return (block(blocks, 1 - c, c, where).astype(F32) + far[0].astype(F32)).astype(BF16)


def scatter_z(blocks, far, near, where):
    z = where[0]
    whole = block(blocks, 0, 0, where).astype(F32) + far[1].astype(F32) + near.astype(F32)
    whole = whole.astype(BF16).reshape(ZS, CS, 64, whole.shape[-1])
    return [pick(whole, (z + k) % ZS) for k in range(ZS)]


def scatter_total(own, others, where):
    c = where[2]
    total = sum(term.astype(F32) for term in [own] + list(others))
    return pick(total, c), pick(total, 1 - c).astype(BF16)


def in_order(own, other, bit):
    return jnp.where(bit == 0, own, other), jnp.where(bit == 0, other, own)


def join_image(values, other, t):
    return jnp.concatenate(in_order(pick(values, t), other.astype(F32), t), axis=0)


def own_and_other(values, t):
    half = values.shape[0] // 2
    own = lax.dynamic_slice_in_dim(values, t * half, half, axis=0)
    give = lax.dynamic_slice_in_dim(values, (1 - t) * half, half, axis=0)
    return own, give.astype(BF16)


def two_images(own, other, t):
    return jnp.stack(in_order(own, other.astype(F32), t))


def unit_of(values, mask):
    squares = jnp.where(mask, values * values, 0.0)
    inverse = lax.rsqrt(jnp.sum(squares, axis=-1, keepdims=True) + EPSILON)
    return jnp.where(mask, values * inverse, 0.0), inverse


def head_masks(shape, head_dim):
    lane = lax.broadcasted_iota(jnp.int32, shape, 1)
    return [(lane >= n * head_dim) & (lane < (n + 1) * head_dim) for n in range(2)]


def attend_kernel(head_dim, scale_ref, row_ref, column_ref, raw_ref, out_ref, bias_ref):
    pair = pl.program_id(0)

    @pl.when(pair == 0)
    def _():
        bias_ref[...] = jnp.where(row_ref[...] <= column_ref[...], 0.0, HIDDEN)

    lanes = 2 * head_dim
    q, k = raw_ref[:, :lanes].astype(F32), raw_ref[:, lanes : 2 * lanes].astype(F32)
    v = raw_ref[:, 2 * lanes :]
    values = jnp.concatenate([v, jnp.ones_like(v)], axis=1)
    tokens = q.shape[0]
    blocks = [(slice(0, MOST), min(2 * MOST, tokens)), (slice(MOST, tokens), tokens)]
    masks = head_masks(q.shape, head_dim)
    k_hat = (unit_of(k, masks[0])[0] + unit_of(k, masks[1])[0]).astype(BF16)
    result = None
    for n in range(2):
        scale = scale_ref[2 * pair + n]
        q_hat = (unit_of(q, masks[n])[0] * scale).astype(BF16)
        mixed = []
        for rows, count in blocks:
            scores = matmul(q_hat[rows], k_hat[:count], NT) + bias_ref[rows, :count]
            weights = jnp.exp(scores - jnp.abs(scale)).astype(BF16)
            mixed.append(matmul(weights, values[:count], NN))
        mixed = jnp.concatenate(mixed, axis=0)
        mixed = mixed[:, : 2 * head_dim] / mixed[:, 2 * head_dim :]
        result = mixed if result is None else jnp.where(masks[n], mixed, result)
    out_ref[...] = result.astype(out_ref.dtype)


def attend_whole(raw, scale_row, all_scale):
    tokens, width = raw.shape[0], raw.shape[1] // 3
    head_dim = width // all_scale.shape[0]
    lanes = 2 * head_dim
    pairs = width // lanes

    block = pl.BlockSpec((tokens, lanes), lambda n: (0, n))
    triple = pl.BlockSpec((tokens, 3 * lanes), lambda n: (0, n))
    return pl.pallas_call(
        functools.partial(attend_kernel, head_dim),
        out_shape=jax.ShapeDtypeStruct((tokens, width), BF16),
        grid=(pairs,),
        in_specs=[
            pl.BlockSpec(memory_space=pltpu.SMEM),
            pl.BlockSpec((1, tokens), lambda n: (0, 0)),
            pl.BlockSpec((tokens, 1), lambda n: (0, 0)),
            triple,
        ],
        out_specs=block,
        scratch_shapes=[pltpu.VMEM((tokens, tokens), F32)],
        cost_estimate=BRIEF,
        compiler_params=pltpu.CompilerParams(vmem_limit_bytes=16 * MIB),
    )(all_scale, scale_row[None, :], scale_row[:, None], raw)


def attend_back_kernel(
    head_dim,
    scale_ref,
    row_ref,
    column_ref,
    raw_ref,
    mixed_ref,
    d_mixed_ref,
    out_ref,
    term_ref,
    bias_ref,
):
    pair = pl.program_id(0)

    @pl.when(pair == 0)
    def _():
        bias_ref[...] = jnp.where(column_ref[...] <= row_ref[...], 0.0, HIDDEN)

    lanes = 2 * head_dim
    q, k = raw_ref[:, :lanes].astype(F32), raw_ref[:, lanes : 2 * lanes].astype(F32)
    v, d_mixed = raw_ref[:, 2 * lanes :], d_mixed_ref[...]
    masks = head_masks(q.shape, head_dim)
    k_units = [unit_of(k, mask) for mask in masks]
    k_hat = (k_units[0][0] + k_units[1][0]).astype(BF16)
    products = d_mixed.astype(F32) * mixed_ref[...].astype(F32)
    tokens = q.shape[0]
    blocks = [(slice(0, min(2 * MOST, tokens)), 0)]
    if tokens > 2 * MOST:
        blocks.append((slice(2 * MOST, tokens), MOST))
    d_q_all = d_k_all = d_v_all = None
    for n in range(2):
        mask = masks[n]
        scale = scale_ref[2 * pair + n]
        q_unit, q_inverse = unit_of(q, mask)
        q_hat = (q_unit * scale).astype(BF16)
        d_out = jnp.where(mask, d_mixed, jnp.zeros_like(d_mixed))
        offset = jnp.sum(jnp.where(mask, products, 0.0), axis=-1, keepdims=True)
        offset = jnp.transpose(jnp.broadcast_to(offset, products.shape))[:1]
        weights, total = [], 0.0
        for keys, first in blocks:
            scores = matmul(k_hat[keys], q_hat[first:], NT) + bias_ref[keys, first:]
            weights.append(jnp.exp(scores - jnp.abs(scale)))
            part = jnp.sum(weights[-1], axis=0, keepdims=True)
            total = part if first == 0 else jnp.concatenate(
                [total[:, :first], total[:, first:] + part], axis=1
            )
        share = 1.0 / total
        d_q, d_k, d_v = None, [], []
        for (keys, first), raised in zip(blocks, weights):
            probs = raised * share[:, first:]
            d_probs = matmul(v[keys], d_out[first:], NT)
            d_scores = (probs * (d_probs - offset[:, first:])).astype(BF16)
            d_v.append(matmul(probs.astype(BF16), d_out[first:], NN))
            d_k.append(matmul(d_scores, q_hat[first:], NN))
            part = matmul(d_scores, k_hat[keys], TN)
            d_q = part if first == 0 else jnp.concatenate(
                [d_q[:first], d_q[first:] + part], axis=0
            )
        d_v, d_k = jnp.concatenate(d_v, axis=0), jnp.concatenate(d_k, axis=0)
        d_q = jnp.where(mask, d_q, 0.0)
        d_k = jnp.where(mask, d_k, 0.0)
        k_unit, k_inverse = k_units[n]
        term = d_q * q_unit
        term_n = jnp.sum(term, axis=0, keepdims=True)
        d_q = q_inverse * scale * (d_q - q_unit * jnp.sum(term, axis=-1, keepdims=True))
        d_k = k_inverse * (d_k - k_unit * jnp.sum(d_k * k_unit, axis=-1, keepdims=True))
        if n == 0:
            d_q_all, d_k_all, d_v_all, term_all = d_q, d_k, d_v, term_n
        else:
            d_q_all, d_k_all = d_q_all + d_q, d_k_all + d_k
            d_v_all, term_all = d_v_all + d_v, term_all + term_n
    out_ref[:, :lanes] = d_q_all.astype(out_ref.dtype)
    out_ref[:, lanes : 2 * lanes] = d_k_all.astype(out_ref.dtype)
    out_ref[:, 2 * lanes :] = d_v_all.astype(out_ref.dtype)
    term_ref[...] = jnp.broadcast_to(term_all, term_ref.shape)


def attend_back_whole(raw, mixed, d_mixed, scale_row, all_scale):
    tokens, width = mixed.shape
    heads = all_scale.shape[0]
    head_dim = width // heads
    lanes = 2 * head_dim
    pairs = width // lanes

    block = pl.BlockSpec((tokens, lanes), lambda n: (0, n))
    triple = pl.BlockSpec((tokens, 3 * lanes), lambda n: (0, n))
    d_raw, terms = pl.pallas_call(
        functools.partial(attend_back_kernel, head_dim),
        out_shape=[
            jax.ShapeDtypeStruct((tokens, 3 * width), BF16),
            jax.ShapeDtypeStruct((8, width), F32),
        ],
        grid=(pairs,),
        in_specs=[
            pl.BlockSpec(memory_space=pltpu.SMEM),
            pl.BlockSpec((1, tokens), lambda n: (0, 0)),
            pl.BlockSpec((tokens, 1), lambda n: (0, 0)),
            triple,
            block,
            block,
        ],
        out_specs=[
            triple,
            pl.BlockSpec((8, lanes), lambda n: (0, n)),
        ],
        scratch_shapes=[pltpu.VMEM((tokens, tokens), F32)],
        cost_estimate=BRIEF,
        compiler_params=pltpu.CompilerParams(vmem_limit_bytes=20 * MIB),
    )(all_scale, scale_row[None, :], scale_row[:, None], raw, mixed, d_mixed)
    return d_raw, jnp.sum(terms[0].reshape(heads, head_dim), axis=1)


def gelu_and_slope(before):
    first = (2.0 / math.pi) ** 0.5
    square = before * before
    gate = 0.5 + 0.5 * jnp.tanh(before * (first + (first * 0.044715) * square))
    active = before * gate
    steep = 2.0 * first + (6.0 * first * 0.044715) * square
    return active, gate + active * (1.0 - gate) * steep


def activate_kernel(rows_ref, weights_ref, active_ref, slope_ref):
    for start in range(0, weights_ref.shape[1], 256):
        columns = slice(start, start + 256)
        active, slope = gelu_and_slope(matmul(rows_ref[...], weights_ref[:, columns], NN))
        active_ref[:, columns] = active.astype(active_ref.dtype)
        slope_ref[:, columns] = slope.astype(slope_ref.dtype)


def by_columns(kernel, rows, weights, count, tile):
    tokens, width = rows.shape
    columns = weights.shape[1]
    out = pl.BlockSpec((tokens, tile), lambda n: (0, n))
    return pl.pallas_call(
        kernel,
        out_shape=[jax.ShapeDtypeStruct((tokens, columns), BF16)] * count,
        grid=(columns // tile,),
        in_specs=[
            pl.BlockSpec((tokens, width), lambda n: (0, 0)),
            pl.BlockSpec((width, tile), lambda n: (0, n)),
        ],
        out_specs=[out] * count,
        cost_estimate=BRIEF,
        compiler_params=pltpu.CompilerParams(vmem_limit_bytes=20 * MIB),
    )(rows, weights)


def halves(values, c, half):
    keep = lax.dynamic_slice_in_dim(values, c * half, half, axis=1)
    give = lax.dynamic_slice_in_dim(values, (1 - c) * half, half, axis=1)
    return keep, give


def on_device_whole(
    inputs, labels, scale_ids, cotangent, table, w_ada, w_qkv, head_scale, w_proj, w_fc1, w_fc2
):
    width = inputs.shape[2]
    classes, rows = table.shape
    heads = TS * head_scale.shape[0]
    quarter = w_qkv.shape[2] // 2
    hidden_quarter = w_fc1.shape[1] // 2
    z, x, c, t = place()
    position = jnp.stack([z, x, c, t]).astype(jnp.int32)

    where = (z, x, c, t)

    pair = 2 * width // heads


    label_pair = jnp.stack(in_order(labels[0], labels[1], t)).astype(F32)
    label_tile = jnp.broadcast_to(label_pair[:, None], (2, 128))
    scale_tile = jnp.broadcast_to(head_scale[None, :], (8, head_scale.shape[0]))
    qkv_halves = []
    for side in (c, 1 - c):
        columns = [
            lax.dynamic_slice_in_dim(w_qkv[:, n].astype(BF16), side * quarter + j * pair, pair, 1)
            for j in range(quarter // pair)
            for n in range(3)
        ]
        qkv_halves.append(jnp.concatenate(columns, axis=1))
    keep_qkv, give_qkv, label_tile, scale_tile, inputs = hold(
        *qkv_halves, label_tile, scale_tile, inputs
    )
    recv_qkv, label_z = send(give_qkv, to_core), send_z(label_tile)
    scale_other = send(scale_tile, to_t)
    keep_qkv, recv_qkv, label_z, scale_other = hold(keep_qkv, recv_qkv, label_z, scale_other)
    two_qkv = jnp.stack([keep_qkv, recv_qkv])
    two_qkv, label_z, inputs, rest = hold(
        two_qkv,
        label_z,
        inputs,
        (cotangent, w_ada, w_proj, w_fc1, w_fc2, table, scale_ids),
    )
    cotangent, w_ada, w_proj, w_fc1, w_fc2, table, scale_ids = rest
    z_qkv = send_z(two_qkv)
    token_other = send(pick(inputs, 1 - t).astype(BF16), to_t)
    scale_row = pick(scale_ids, t)

    odd = z % 2 == 1
    first, third = jnp.where(odd, label_z[0], label_z[2]), jnp.where(odd, label_z[2], label_z[0])
    label_rows = jnp.concatenate([label_tile, first, label_z[1], third])
    label_rows = jnp.concatenate([label_rows, send(label_rows, to_x)])
    label_rows = jnp.concatenate([label_rows, send(label_rows, to_core)])
    all_labels = label_rows[:, 0].astype(jnp.int32)
    one_hot = (all_labels[:, None] == jnp.arange(classes)[None, :]).astype(BF16)
    condition = matmul(one_hot, table.astype(BF16), NN)
    silu_low = jax.nn.silu(condition).astype(BF16)
    ada_low = w_ada.astype(BF16).reshape(rows, 6 * width)
    silu_own = silu_low.reshape(-1, TS, rows)[:, 0]
    partial = matmul(silu_own, ada_low, NN).reshape(CS, XS, ZS, 6 * width)
    partial = partial[0] + send(partial[1], to_core)
    own_part, x_part = partial[0], send(partial[1], to_x)
    w_fc1, w_proj_t, w_fc2_t = w_fc1.astype(BF16), w_proj.astype(BF16).T, w_fc2.astype(BF16).T
    rest_halves = [halves(w_proj_t, c, quarter), halves(w_fc1, c, hidden_quarter)]
    rest_halves.append(halves(w_fc2_t, c, hidden_quarter))
    keep_rest, give_rest = [jnp.concatenate([part[n] for part in rest_halves], 1) for n in range(2)]
    split = quarter + hidden_quarter
    z_qkv, own_part, x_part, recv_rest = hold(
        z_qkv, own_part, x_part, send(give_rest, to_core)
    )

    four_qkv = jnp.stack([two_qkv] + z_qkv)
    partial = own_part + x_part
    two_mid = jnp.stack([keep_rest[:, :split], recv_rest[:, :split]])
    two_fc2 = jnp.stack([keep_rest[:, split:], recv_rest[:, split:]])
    four_qkv, partial, two_mid, two_fc2 = hold(four_qkv, partial, two_mid, two_fc2)
    near_qkv, far_qkv = send(four_qkv, to_t), send(four_qkv, to_x)
    mid_2 = send(two_mid, to_z(2))
    partial = partial[:2] + send(partial[2:], to_z_bit(2))
    mod_part, mod_bit = partial[0], send(partial[1], to_z_bit(1))
    cotangent_give = pick(cotangent, 1 - t).astype(BF16)
    near_qkv, far_qkv, mid_2, two_mid, cotangent_give, mod_part, mod_bit, token_other = hold(
        near_qkv, far_qkv, mid_2, two_mid, cotangent_give, mod_part, mod_bit, token_other
    )
    modulation = (mod_part + mod_bit).reshape(6, 1, width)
    gain_attn, gain_mlp, scale_attn, scale_mlp, shift_attn, shift_mlp = modulation
    tokens_in = join_image(inputs, token_other, t)
    last_qkv = send(near_qkv, to_x)
    mid_1, mid_3 = send(two_mid, to_z(1)), send(two_mid, to_z(3))
    cotangent_other = send(cotangent_give, to_t)
    normed_one, inverse_one = layer_norm(tokens_in)
    hidden_one = (normed_one * (1.0 + scale_attn) + shift_attn).astype(BF16)
    last_qkv, mid_1, mid_3, hidden_one, cotangent_other = hold(
        last_qkv, mid_1, mid_3, hidden_one, cotangent_other
    )
    scales = jnp.concatenate(in_order(head_scale, scale_other[0], t)).reshape(TS, 2, -1)
    scale_own, scale_oth = pick(scales, c, 1).reshape(-1), pick(scales, 1 - c, 1).reshape(-1)
    four_mid = jnp.stack([two_mid, mid_1, mid_2, mid_3])
    four_mid, last_qkv, two_fc2, hidden_one = hold(four_mid, last_qkv, two_fc2, hidden_one)
    near_mid, far_mid = send(four_mid, to_near), send(four_mid, to_far)
    z_fc2 = send_z(two_fc2)
    (qkv_own,) = assemble(
        [four_qkv, near_qkv, far_qkv, last_qkv], position, [3 * quarter], crossed=False
    )
    raw_own = matmul(hidden_one, qkv_own, NN).astype(BF16)
    raw_own, qkv_oth = hold(raw_own, send(qkv_own, to_core))
    raw_oth = matmul(hidden_one, qkv_oth, NN).astype(BF16)
    mixed_own = attend_whole(raw_own, scale_row, scale_own)
    mixed_own, near_mid, far_mid, z_fc2, raw_oth = hold(
        mixed_own, near_mid, far_mid, z_fc2, raw_oth
    )
    last_mid = send(near_mid, to_far)
    mixed_oth = attend_whole(raw_oth, scale_row, scale_oth)
    four_fc2 = jnp.stack([two_fc2] + z_fc2)
    mixed_oth, last_mid, four_fc2 = hold(mixed_oth, last_mid, four_fc2)
    near_fc2, far_fc2 = send(four_fc2, to_near), send(four_fc2, to_far)
    proj_own, fc1_own = assemble(
        [four_mid, near_mid, far_mid, last_mid], position, [quarter, hidden_quarter]
    )
    upstream = join_image(cotangent, cotangent_other, t)
    d_branch = (gain_mlp * upstream).astype(BF16)
    proj_oth, d_branch = hold(send(proj_own, to_core), d_branch)
    fc1_oth = send(fc1_own, to_core)
    attended = matmul(mixed_own, proj_own, NT) + matmul(mixed_oth, proj_oth, NT)
    middle = tokens_in + gain_attn * attended
    normed_two, inverse_two = layer_norm(middle)
    hidden_two = (normed_two * (1.0 + scale_mlp) + shift_mlp).astype(BF16)
    hidden_two, fc1_oth = hold(hidden_two, fc1_oth)

    def activate(weights):
        active, slope = gelu_and_slope(matmul(hidden_two, weights, NN))
        return active.astype(BF16), slope.astype(BF16)

    active_oth, slope_oth = by_columns(activate_kernel, hidden_two, fc1_oth, 2, 512)
    active_oth, slope_oth, near_fc2, far_fc2 = hold(active_oth, slope_oth, near_fc2, far_fc2)
    last_fc2 = send(near_fc2, to_far)
    active_own, slope_own = activate(fc1_own)
    given = products([(d_branch, active_oth)])
    given, active_own, slope_own = hold(given, active_own, slope_own)
    added = [send(part, to_core) for part in given]
    last_fc2, active_own = hold(last_fc2, active_own)
    (fc2_own,) = assemble([four_fc2, near_fc2, far_fc2, last_fc2], position, [hidden_quarter])
    fc2_own, added = hold(fc2_own, added)
    fc2_oth = send(fc2_own, to_core)
    blocks_fc2 = products([(d_branch, active_own)], added)
    blocks_fc2, fc2_oth = hold(blocks_fc2, fc2_oth)
    far_give, blocks_fc2, active_own = hold(scatter_far(blocks_fc2, where), blocks_fc2, active_own)
    far_fc2 = send(far_give, to_far)

    d_before_oth = (matmul(d_branch, fc2_oth, NN) * slope_oth.astype(F32)).astype(BF16)
    d_before_own = (matmul(d_branch, fc2_own, NN) * slope_own.astype(F32)).astype(BF16)
    given = products([(hidden_two, d_before_oth)])
    given, d_before_oth, d_before_own = hold(given, d_before_oth, d_before_own)
    added = [send(part, to_core) for part in given]
    d_hidden_two = matmul(d_before_own, fc1_own, NT) + matmul(d_before_oth, fc1_oth, NT)
    d_scale_mlp = jnp.sum(d_hidden_two * normed_two, axis=0)
    d_shift_mlp = jnp.sum(d_hidden_two, axis=0)
    d_middle = upstream + norm_back(d_hidden_two * (1.0 + scale_mlp), normed_two, inverse_two)
    d_gain_attn = jnp.sum(d_middle * attended, axis=0)
    d_attended = (gain_attn * d_middle).astype(BF16)
    d_attended, added = hold(d_attended, added)
    blocks_fc1 = products([(hidden_two, d_before_own)], added)
    far_give, blocks_fc1, d_attended, far_fc2 = hold(
        scatter_far(blocks_fc1, where), blocks_fc1, d_attended, far_fc2
    )
    near_fc2 = send(scatter_near(blocks_fc2, far_fc2, where), to_near)
    far_fc1 = send(far_give, to_far)
    given = products([(d_attended, mixed_oth)])
    given, d_attended = hold(given, d_attended)
    added = [send(part, to_core) for part in given]
    d_mixed_oth = matmul(d_attended, proj_oth, NN).astype(BF16)
    d_mixed_own = matmul(d_attended, proj_own, NN).astype(BF16)
    d_mixed_oth, d_mixed_own, added = hold(d_mixed_oth, d_mixed_own, added)
    blocks_proj = products([(d_attended, mixed_own)], added)
    blocks_proj, d_mixed_oth = hold(blocks_proj, d_mixed_oth)
    far_proj = send(scatter_far(blocks_proj, where), to_far)
    d_raw_oth, terms_oth = attend_back_whole(raw_oth, mixed_oth, d_mixed_oth, scale_row, scale_oth)
    given = products([(hidden_one, d_raw_oth)])
    given, near_fc2, d_mixed_own = hold(given, near_fc2, d_mixed_own)
    added = [send(part, to_core) for part in given]
    d_raw_own, terms_own = attend_back_whole(raw_own, mixed_own, d_mixed_own, scale_row, scale_own)
    d_raw_own, far_fc1, far_proj, added = hold(d_raw_own, far_fc1, far_proj, added)
    blocks_mid = blocks_proj + blocks_fc1
    far_mid = [jnp.concatenate([far_proj[n], far_fc1[n]], axis=1) for n in range(2)]
    near_give = scatter_near(blocks_mid, far_mid, where)
    z_fc2 = scatter_z(blocks_fc2, far_fc2, near_fc2, where)
    near_give, z_fc2, d_raw_own = hold(near_give, z_fc2, d_raw_own)
    near_mid = send(near_give, to_near)
    own_fc2, others_fc2 = z_fc2[0], send_terms_z(z_fc2[1:])
    blocks_qkv = products([(hidden_one, d_raw_own)], added)
    far_give, blocks_qkv, d_raw_own, d_raw_oth, active_own = hold(
        scatter_far(blocks_qkv, where), blocks_qkv, d_raw_own, d_raw_oth, active_own
    )
    far_qkv = send(far_give, to_far)
    d_hidden_one = matmul(d_raw_own, qkv_own, NT) + matmul(d_raw_oth, qkv_oth, NT)
    d_hidden_one, near_mid, others_fc2 = hold(d_hidden_one, near_mid, others_fc2)
    z_mid = scatter_z(blocks_mid, far_mid, near_mid, where)
    own_mid, others_mid = z_mid[0], send_terms_z(z_mid[1:])
    d_scale_attn = jnp.sum(d_hidden_one * normed_one, axis=0)
    d_shift_attn = jnp.sum(d_hidden_one, axis=0)
    d_inputs = d_middle + norm_back(d_hidden_one * (1.0 + scale_attn), normed_one, inverse_one)
    inputs_own, inputs_give = own_and_other(d_inputs, t)
    far_qkv, inputs_give, d_scale_attn = hold(far_qkv, inputs_give, d_scale_attn)
    near_give, active_own, inputs_give = hold(
        scatter_near(blocks_qkv, far_qkv, where), active_own, inputs_give
    )
    near_qkv = send(near_give, to_near)
    branch = matmul(active_own, fc2_own, NT) + matmul(active_oth, fc2_oth, NT)
    output_own, output_give = own_and_other(middle + gain_mlp * branch, t)
    d_gain_mlp = jnp.sum(upstream * branch, axis=0)
    d_modulation = jnp.concatenate(
        [d_gain_attn, d_gain_mlp, d_scale_attn, d_scale_mlp, d_shift_attn, d_shift_mlp]
    )
    terms = in_order(terms_own.reshape(TS, -1), terms_oth.reshape(TS, -1), c)
    scale_terms = jnp.concatenate(terms, axis=1).reshape(-1)
    scale_high = lax.reduce_precision(scale_terms, 8, 7)
    row = jnp.concatenate(
        [d_modulation, scale_high, scale_terms - scale_high, jnp.zeros((128 - 2 * heads,), F32)]
    ).astype(BF16)[None, :]
    mod_rows = jnp.concatenate([row, send(row, to_t)])
    near_qkv, mod_rows, others_mid = hold(near_qkv, mod_rows, others_mid)
    z_qkv = scatter_z(blocks_qkv, far_qkv, near_qkv, where)
    z_qkv, mod_rows, inputs_give, output_give = hold(z_qkv, mod_rows, inputs_give, output_give)
    own_qkv, others_qkv = z_qkv[0], send_terms_z(z_qkv[1:])
    mod_z = send_z(mod_rows)
    inputs_other, output_other = send(inputs_give, to_t), send(output_give, to_t)
    half_fc2, other_fc2 = scatter_total(own_fc2, others_fc2, where)
    half_mid, other_mid = scatter_total(own_mid, others_mid, where)
    other_rest = send(jnp.concatenate([other_mid, other_fc2], axis=1), to_core)
    first, third = jnp.where(odd, mod_z[0], mod_z[2]), jnp.where(odd, mod_z[2], mod_z[0])
    mod_rows = jnp.concatenate([mod_rows, first, mod_z[1], third])
    mod_x, inputs_other = hold(send(mod_rows, to_x), inputs_other)
    mod_rows = jnp.concatenate([mod_rows, mod_x])
    mod_rows = jnp.concatenate([mod_rows, send(mod_rows, to_core)])

    d_mod_all = mod_rows[:, : 6 * width]
    scale_sum = jnp.sum(mod_rows[:, 6 * width : 6 * width + 2 * heads].astype(F32), axis=0)
    scale_sum = (scale_sum[:heads] + scale_sum[heads:]).reshape(TS, heads // TS)
    grad_scale = pick(scale_sum, t)
    grad_ada = [
        matmul(silu_low, d_mod_all[:, n * width : (n + 1) * width], TN) for n in range(6)
    ]
    grad_ada = jnp.stack(grad_ada).transpose(1, 0, 2)
    d_silu = matmul(d_mod_all, ada_low, NT)
    _, silu_pull = jax.vjp(jax.nn.silu, condition)
    d_condition = silu_pull(d_silu)[0]
    grad_table = jnp.dot(one_hot.astype(F32).T, d_condition, precision=HIGHEST)

    def joined(own, other):
        return jnp.concatenate(in_order(own, other.astype(F32), c), axis=1)

    grad_proj = joined(half_mid[:, :quarter], other_rest[:, :quarter]).T
    grad_fc1 = joined(half_mid[:, quarter:], other_rest[:, quarter:split])
    grad_fc2 = joined(half_fc2, other_rest[:, split:]).T
    others_qkv, others = hold(
        others_qkv, (grad_ada, grad_table, grad_scale, inputs_other, grad_proj, grad_fc1, grad_fc2)
    )
    grad_ada, grad_table, grad_scale, inputs_other, grad_proj, grad_fc1, grad_fc2 = others
    half_qkv, other_qkv = scatter_total(own_qkv, others_qkv, where)
    other_qkv = send(other_qkv, to_core)

    def part_of(values, n):
        starts = range(n * pair, 3 * quarter, 3 * pair)
        return jnp.concatenate([values[:, start : start + pair] for start in starts], axis=1)

    grad_qkv = [joined(part_of(half_qkv, n), part_of(other_qkv, n)) for n in range(3)]
    return (
        two_images(output_own, output_other, t),
        two_images(inputs_own, inputs_other, t),
        grad_table,
        grad_ada,
        jnp.stack(grad_qkv, axis=1),
        grad_scale,
        grad_proj,
        grad_fc1,
        grad_fc2,
    )


def solution(mesh):
    placed = (
        P("dp", "tensor", None),
        P("dp"),
        P("dp", None),
        P("dp", "tensor", None),
        P(None, "dp"),
        P("dp", None, None),
        P("dp", None, "tensor"),
        P("tensor"),
        P("tensor", "dp"),
        P("dp", "tensor"),
        P("tensor", "dp"),
    )
    fitting = mesh.shape["dp"] == ZS * XS * CS and mesh.shape["tensor"] == TS

    def on_device(inputs, *others):
        fits = fitting and inputs.shape[0] == TS
        return (on_device_whole if fits else on_device_general)(inputs, *others)

    return jax.shard_map(
        on_device,
        mesh=mesh,
        in_specs=placed,
        out_specs=(
            P("dp", "tensor", None),
            P("dp", "tensor", None),
            P(None, "dp"),
            P("dp", None, None),
            P("dp", None, "tensor"),
            P("tensor"),
            P("tensor", "dp"),
            P("dp", "tensor"),
            P("tensor", "dp"),
        ),
        check_vma=False,
    )
```

```python
import functools
import math

import jax
import jax.numpy as jnp
from jax import lax
from jax.experimental import pallas as pl
from jax.experimental.pallas import tpu as pltpu
from jax.sharding import PartitionSpec as P

EPSILON = 1e-06
HIGHEST = lax.Precision.HIGHEST


def layer_norm(values):
    average = jnp.mean(values, axis=-1, keepdims=True)
    centred = values - average
    inverse = lax.rsqrt(jnp.mean(centred * centred, axis=-1, keepdims=True) + EPSILON)
    return (centred * inverse, inverse)


def norm_back(d_normed, normed, inverse):
    return inverse * (
        d_normed
        - jnp.mean(d_normed, axis=-1, keepdims=True)
        - normed * jnp.mean(d_normed * normed, axis=-1, keepdims=True)
    )


def unit_rows(values):
    inverse = lax.rsqrt(jnp.sum(values * values, axis=-1, keepdims=True) + EPSILON)
    return (values * inverse, inverse)


def unit_back(d_unit, unit, inverse):
    return inverse * (d_unit - unit * jnp.sum(d_unit * unit, axis=-1, keepdims=True))


def spread(values):
    return lax.all_gather(values, "tensor", axis=1, tiled=True)


def collect(terms):
    return lax.psum_scatter(
        terms.astype(jnp.bfloat16), "tensor", scatter_dimension=1, tiled=True
    ).astype(jnp.float32)


def masked_scores(queries, keys_in, scale_row):
    scores = jnp.einsum("qhd,khd->hqk", queries, keys_in, preferred_element_type=jnp.float32)
    visible = scale_row[None, :] <= scale_row[:, None]
    return jnp.where(visible[None], scores, -1e30)


def attend_forward(pieces):
    queries, keys_in, values_in, scale_row = pieces
    scores = masked_scores(queries, keys_in, scale_row)
    largest = jnp.max(scores, axis=-1, keepdims=True)
    exponent = jnp.exp(scores - largest)
    denominator = jnp.sum(exponent, axis=-1, keepdims=True)
    attn_probs = (exponent / denominator).astype(jnp.bfloat16)
    mixed = jnp.einsum("hqk,khd->qhd", attn_probs, values_in, preferred_element_type=jnp.float32)
    return (mixed.astype(jnp.bfloat16), (largest + jnp.log(denominator))[..., 0])


def attend_backward(pieces):
    queries, keys_in, values_in, scale_row, log_total, d_mixed = pieces
    scores = masked_scores(queries, keys_in, scale_row)
    attn_probs = jnp.exp(scores - log_total[..., None])
    d_probs = jnp.einsum("qhd,khd->hqk", d_mixed, values_in, preferred_element_type=jnp.float32)
    offset = jnp.sum(attn_probs * d_probs, axis=-1, keepdims=True)
    d_scores = (attn_probs * (d_probs - offset)).astype(jnp.bfloat16)
    d_queries = jnp.einsum("hqk,khd->qhd", d_scores, keys_in, preferred_element_type=jnp.float32)
    d_keys = jnp.einsum("hqk,qhd->khd", d_scores, queries, preferred_element_type=jnp.float32)
    d_values = jnp.einsum(
        "hqk,qhd->khd", attn_probs.astype(jnp.bfloat16), d_mixed, preferred_element_type=jnp.float32
    )
    return (d_queries, d_keys, d_values)


def on_device_general(
    inputs, labels, scale_ids, cotangent, table, w_ada, w_qkv, head_scale, w_proj, w_fc1, w_fc2
):
    images, local_len, model_width = inputs.shape
    full_len = scale_ids.shape[1]
    local_heads = head_scale.shape[0]
    head_dim = w_qkv.shape[2] // local_heads
    classes = table.shape[0]
    gathered = (
        lax.all_gather(table.astype(jnp.bfloat16), "dp", axis=1, tiled=True),
        lax.all_gather(w_qkv.astype(jnp.bfloat16), "dp", axis=0, tiled=True),
        lax.all_gather(w_proj.astype(jnp.bfloat16), "dp", axis=1, tiled=True),
        lax.all_gather(w_fc1.astype(jnp.bfloat16), "dp", axis=0, tiled=True),
        lax.all_gather(w_fc2.astype(jnp.bfloat16), "dp", axis=1, tiled=True),
    )
    table_low, qkv_low, proj_low, fc1_low, fc2_low = gathered
    qkv_flat = qkv_low.reshape(model_width, -1)
    one_hot = labels[:, None] == jnp.arange(classes)[None, :]
    condition = jnp.dot(one_hot.astype(jnp.bfloat16), table_low, preferred_element_type=jnp.float32)
    silu_low = jax.nn.silu(condition).astype(jnp.bfloat16)
    ada_full = lax.all_gather(w_ada.astype(jnp.bfloat16), "dp", axis=0, tiled=True).reshape(
        model_width, 6 * model_width
    )
    modulation = jnp.dot(silu_low, ada_full, preferred_element_type=jnp.float32)
    modulation = modulation.reshape(images, 6, model_width)
    gain_attn = modulation[:, 0, None, :]
    gain_mlp = modulation[:, 1, None, :]
    scale_attn = modulation[:, 2, None, :]
    scale_mlp = modulation[:, 3, None, :]
    shift_attn = modulation[:, 4, None, :]
    shift_mlp = modulation[:, 5, None, :]
    normed_one, inverse_one = layer_norm(inputs)
    hidden_one = spread((normed_one * (1.0 + scale_attn) + shift_attn).astype(jnp.bfloat16))
    projected = jnp.einsum("bld,dc->blc", hidden_one, qkv_flat, preferred_element_type=jnp.float32)
    projected = projected.reshape(images, full_len, 3, local_heads, head_dim)
    q_unit, q_inverse = unit_rows(projected[:, :, 0])
    k_unit, k_inverse = unit_rows(projected[:, :, 1])
    q_hat = (q_unit * head_scale[:, None]).astype(jnp.bfloat16)
    k_hat = k_unit.astype(jnp.bfloat16)
    v_hat = projected[:, :, 2].astype(jnp.bfloat16)
    mixed, log_total = lax.map(attend_forward, (q_hat, k_hat, v_hat, scale_ids))
    mixed_flat = mixed.reshape(images, full_len, local_heads * head_dim)
    attended = collect(
        jnp.einsum("blc,cd->bld", mixed_flat, proj_low, preferred_element_type=jnp.float32)
    )
    middle = inputs + gain_attn * attended
    normed_two, inverse_two = layer_norm(middle)
    hidden_two = spread((normed_two * (1.0 + scale_mlp) + shift_mlp).astype(jnp.bfloat16))
    before = jnp.einsum("bld,df->blf", hidden_two, fc1_low, preferred_element_type=jnp.float32)
    gelu_fn = functools.partial(jax.nn.gelu, approximate=True)
    active_f, gelu_pull = jax.vjp(gelu_fn, before)
    active = active_f.astype(jnp.bfloat16)
    branch = collect(jnp.einsum("blf,fd->bld", active, fc2_low, preferred_element_type=jnp.float32))
    output = middle + gain_mlp * branch
    again = (
        lax.all_gather(w_qkv.astype(jnp.bfloat16), "dp", axis=0, tiled=True),
        lax.all_gather(w_proj.astype(jnp.bfloat16), "dp", axis=1, tiled=True),
        lax.all_gather(w_fc1.astype(jnp.bfloat16), "dp", axis=0, tiled=True),
        lax.all_gather(w_fc2.astype(jnp.bfloat16), "dp", axis=1, tiled=True),
    )
    qkv_back, proj_back, fc1_back, fc2_back = again
    d_gain_mlp = jnp.sum(cotangent * branch, axis=1)
    d_branch = spread((gain_mlp * cotangent).astype(jnp.bfloat16))
    grad_fc2 = jnp.einsum("blf,bld->fd", active, d_branch, preferred_element_type=jnp.float32)
    d_active = jnp.einsum("bld,fd->blf", d_branch, fc2_back, preferred_element_type=jnp.float32)
    d_before = gelu_pull(d_active)[0].astype(jnp.bfloat16)
    grad_fc1 = jnp.einsum("bld,blf->df", hidden_two, d_before, preferred_element_type=jnp.float32)
    d_hidden_two = collect(
        jnp.einsum("blf,df->bld", d_before, fc1_back, preferred_element_type=jnp.float32)
    )
    d_scale_mlp = jnp.sum(d_hidden_two * normed_two, axis=1)
    d_shift_mlp = jnp.sum(d_hidden_two, axis=1)
    d_middle = cotangent + norm_back(d_hidden_two * (1.0 + scale_mlp), normed_two, inverse_two)
    d_gain_attn = jnp.sum(d_middle * attended, axis=1)
    d_attended = spread((gain_attn * d_middle).astype(jnp.bfloat16))
    grad_proj = jnp.einsum(
        "blc,bld->cd", mixed_flat, d_attended, preferred_element_type=jnp.float32
    )
    d_mixed = jnp.einsum("bld,cd->blc", d_attended, proj_back, preferred_element_type=jnp.float32)
    d_mixed = d_mixed.astype(jnp.bfloat16).reshape(images, full_len, local_heads, head_dim)
    d_q_hat, d_k_hat, d_v_hat = lax.map(
        attend_backward, (q_hat, k_hat, v_hat, scale_ids, log_total, d_mixed)
    )
    scale_terms = jnp.sum(d_q_hat * q_unit, axis=(0, 1, 3))
    d_query = unit_back(d_q_hat * head_scale[:, None], q_unit, q_inverse)
    d_key = unit_back(d_k_hat, k_unit, k_inverse)
    d_raw = jnp.stack([d_query, d_key, d_v_hat], axis=2).astype(jnp.bfloat16)
    d_raw = d_raw.reshape(images, full_len, 3 * local_heads * head_dim)
    grad_qkv = jnp.einsum("bld,blc->dc", hidden_one, d_raw, preferred_element_type=jnp.float32)
    grad_qkv = grad_qkv.reshape(model_width, 3, local_heads * head_dim)
    d_hidden_one = collect(
        jnp.einsum(
            "blc,dc->bld",
            d_raw,
            qkv_back.reshape(model_width, -1),
            preferred_element_type=jnp.float32,
        )
    )
    d_scale_attn = jnp.sum(d_hidden_one * normed_one, axis=1)
    d_shift_attn = jnp.sum(d_hidden_one, axis=1)
    d_inputs = d_middle + norm_back(d_hidden_one * (1.0 + scale_attn), normed_one, inverse_one)
    mod_terms_back = jnp.stack(
        [d_gain_attn, d_gain_mlp, d_scale_attn, d_scale_mlp, d_shift_attn, d_shift_mlp], axis=1
    )
    d_modulation = lax.psum(mod_terms_back.astype(jnp.bfloat16), "tensor").astype(jnp.float32)
    d_mod_flat = d_modulation.reshape(images, 6 * model_width)
    grad_scale = lax.psum(scale_terms, "dp")
    ada_terms = jnp.dot(silu_low.astype(jnp.float32).T, d_mod_flat, precision=HIGHEST)
    grad_ada = lax.psum_scatter(
        ada_terms.reshape(model_width, 6, model_width).astype(jnp.bfloat16),
        "dp",
        scatter_dimension=0,
        tiled=True,
    ).astype(jnp.float32)
    d_silu = jnp.dot(d_mod_flat, ada_full.astype(jnp.float32).T, precision=HIGHEST)
    _, silu_pull = jax.vjp(jax.nn.silu, condition)
    d_condition = silu_pull(d_silu)[0]
    table_terms = jnp.dot(one_hot.astype(jnp.float32).T, d_condition, precision=HIGHEST)
    summed = (
        lax.psum_scatter(
            table_terms.astype(jnp.bfloat16), "dp", scatter_dimension=1, tiled=True
        ).astype(jnp.float32),
        lax.psum_scatter(
            grad_qkv.astype(jnp.bfloat16), "dp", scatter_dimension=0, tiled=True
        ).astype(jnp.float32),
        lax.psum_scatter(
            grad_proj.astype(jnp.bfloat16), "dp", scatter_dimension=1, tiled=True
        ).astype(jnp.float32),
        lax.psum_scatter(
            grad_fc1.astype(jnp.bfloat16), "dp", scatter_dimension=0, tiled=True
        ).astype(jnp.float32),
        lax.psum_scatter(
            grad_fc2.astype(jnp.bfloat16), "dp", scatter_dimension=1, tiled=True
        ).astype(jnp.float32),
    )
    grad_table, grad_qkv_own, grad_proj_own, grad_fc1_own, grad_fc2_own = summed
    return (
        output,
        d_inputs,
        grad_table,
        grad_ada,
        grad_qkv_own,
        grad_scale,
        grad_proj_own,
        grad_fc1_own,
        grad_fc2_own,
    )


BF16 = jnp.bfloat16
F32 = jnp.float32
ZS, XS, CS, TS = 4, 2, 2, 2
BOTH = ("dp", "tensor")
NN = (((1,), (0,)), ((), ()))
NT = (((1,), (1,)), ((), ()))
TN = (((0,), (0,)), ((), ()))
HIDDEN = -1e30
MOST = 256
MIB = 1024 * 1024
BRIEF = pl.CostEstimate(flops=0, bytes_accessed=0, transcendentals=0)


def perm_of(step):
    pairs = []
    for z in range(ZS):
        for x in range(XS):
            for c in range(CS):
                for t in range(TS):
                    nz, nx, nc, nt = step(z, x, c, t)
                    source = ((z * XS + x) * CS + c) * TS + t
                    target = ((nz * XS + nx) * CS + nc) * TS + nt
                    pairs.append((source, target))
    return pairs


def send(values, step):
    return lax.ppermute(values, BOTH, perm_of(step))


def to_core(z, x, c, t):
    return (z, x, 1 - c, t)


def to_x(z, x, c, t):
    return (z, 1 - x, c, t)


def to_t(z, x, c, t):
    return (z, x, c, 1 - t)


def to_z(k):
    return lambda z, x, c, t: ((z + k) % ZS, x, c, t)


def to_z_bit(bit):
    return lambda z, x, c, t: (z ^ bit, x, c, t)


def to_near(z, x, c, t):
    return (z, 1 - x, c, t) if c == 0 else (z, x, c, 1 - t)


def to_far(z, x, c, t):
    return (z, x, c, 1 - t) if c == 0 else (z, 1 - x, c, t)


def pick(values, index, axis=0):
    return lax.dynamic_index_in_dim(values, index, axis, keepdims=False)


def place():
    dp = lax.axis_index("dp")
    t = lax.axis_index("tensor")
    return dp // (XS * CS), (dp // CS) % XS, dp % CS, t


def matmul(left, right, dims):
    return lax.dot_general(left, right, dims, preferred_element_type=F32)


def hold(*values):
    return lax.optimization_barrier(values)


def send_z(values):
    return [send(values, to_z(k)) for k in range(1, ZS)]


def send_terms_z(terms):
    return [send(terms[k - 1], to_z(k)) for k in range(1, ZS)]


def assemble_kernel(widths, crossed, where_ref, *refs):
    pieces, outs, sem = refs[:4], refs[4:-1], refs[-1]
    z, x, c, t = where_ref[0], where_ref[1], where_ref[2], where_ref[3]
    for slot, piece in enumerate(pieces):
        near = (1 - c, c) if crossed else (0, 1)
        dx, dt = [(0, 0), near, (1 - near[0], 1 - near[1]), (1, 1)][slot]
        sx, st = x ^ dx, t ^ dt
        for dz in range(ZS):
            for dc in range(CS):
                sz = (z + ZS - dz) % ZS
                sc = c ^ dc
                row = pl.multiple_of(((sz * XS + sx) * CS + sc) * 64, 64)
                start = 0
                for which, width in enumerate(widths):
                    column = pl.multiple_of(st * width, 128)
                    pltpu.make_async_copy(
                        piece.at[dz, dc, :, pl.ds(start, width)],
                        outs[which].at[pl.ds(row, 64), pl.ds(column, width)],
                        sem.at[which],
                    ).start()
                    start += width
    for which, out in enumerate(outs):
        pltpu.make_async_copy(out, out, sem.at[which]).wait()


def assemble(pieces, position, widths, crossed=True):
    rows = ZS * XS * CS * 64
    return pl.pallas_call(
        functools.partial(assemble_kernel, widths, crossed),
        out_shape=[jax.ShapeDtypeStruct((rows, TS * width), BF16) for width in widths],
        in_specs=[pl.BlockSpec(memory_space=pltpu.SMEM)]
        + [pl.BlockSpec(memory_space=pl.ANY)] * 4,
        out_specs=[pl.BlockSpec(memory_space=pltpu.VMEM)] * len(widths),
        scratch_shapes=[pltpu.SemaphoreType.DMA((len(widths),))],
        cost_estimate=BRIEF,
        compiler_params=pltpu.CompilerParams(vmem_limit_bytes=8 * MIB),
    )(position, *pieces)


def products(factors, added=None):
    terms = [matmul(rows, columns, TN) for rows, columns in factors]
    if added is not None:
        terms = [term + other.astype(F32) for term, other in zip(terms, added)]
    return [term.astype(BF16) for term in terms]


def block(blocks, dx, dt, where):
    z, x, c, t = where
    parts = []
    for values in blocks:
        m = values.shape[1] // TS
        values = lax.dynamic_slice_in_dim(values, (t ^ dt) * m, m, 1)
        values = pick(values.reshape(ZS, XS, CS * 64, m), x ^ dx, 1)
        parts.append(values.reshape(ZS * CS * 64, m))
    return parts[0] if len(parts) == 1 else jnp.concatenate(parts, axis=1)


def scatter_far(blocks, where):
    c = where[2]
    return jnp.stack([block(blocks, 1, 1, where), block(blocks, c, 1 - c, where)])


def scatter_near(blocks, far, where):
    c = where[2]
    return (block(blocks, 1 - c, c, where).astype(F32) + far[0].astype(F32)).astype(BF16)


def scatter_z(blocks, far, near, where):
    z = where[0]
    whole = block(blocks, 0, 0, where).astype(F32) + far[1].astype(F32) + near.astype(F32)
    whole = whole.astype(BF16).reshape(ZS, CS, 64, whole.shape[-1])
    return [pick(whole, (z + k) % ZS) for k in range(ZS)]


def scatter_total(own, others, where):
    c = where[2]
    total = sum(term.astype(F32) for term in [own] + list(others))
    return pick(total, c), pick(total, 1 - c).astype(BF16)


def in_order(own, other, bit):
    return jnp.where(bit == 0, own, other), jnp.where(bit == 0, other, own)


def join_image(values, other, t):
    return jnp.concatenate(in_order(pick(values, t), other.astype(F32), t), axis=0)


def own_and_other(values, t):
    half = values.shape[0] // 2
    own = lax.dynamic_slice_in_dim(values, t * half, half, axis=0)
    give = lax.dynamic_slice_in_dim(values, (1 - t) * half, half, axis=0)
    return own, give.astype(BF16)


def two_images(own, other, t):
    return jnp.stack(in_order(own, other.astype(F32), t))


def unit_of(values, mask):
    squares = jnp.where(mask, values * values, 0.0)
    inverse = lax.rsqrt(jnp.sum(squares, axis=-1, keepdims=True) + EPSILON)
    return jnp.where(mask, values * inverse, 0.0), inverse


def head_masks(shape, head_dim):
    lane = lax.broadcasted_iota(jnp.int32, shape, 1)
    return [(lane >= n * head_dim) & (lane < (n + 1) * head_dim) for n in range(2)]


def attend_kernel(head_dim, scale_ref, row_ref, column_ref, raw_ref, out_ref, bias_ref):
    pair = pl.program_id(0)

    @pl.when(pair == 0)
    def _():
        bias_ref[...] = jnp.where(row_ref[...] <= column_ref[...], 0.0, HIDDEN)

    lanes = 2 * head_dim
    q, k = raw_ref[:, :lanes].astype(F32), raw_ref[:, lanes : 2 * lanes].astype(F32)
    v = raw_ref[:, 2 * lanes :]
    values = jnp.concatenate([v, jnp.ones_like(v)], axis=1)
    tokens = q.shape[0]
    blocks = [(slice(0, MOST), min(2 * MOST, tokens)), (slice(MOST, tokens), tokens)]
    masks = head_masks(q.shape, head_dim)
    k_hat = (unit_of(k, masks[0])[0] + unit_of(k, masks[1])[0]).astype(BF16)
    result = None
    for n in range(2):
        scale = scale_ref[2 * pair + n]
        q_hat = (unit_of(q, masks[n])[0] * scale).astype(BF16)
        mixed = []
        for rows, count in blocks:
            scores = matmul(q_hat[rows], k_hat[:count], NT) + bias_ref[rows, :count]
            weights = jnp.exp(scores - jnp.abs(scale)).astype(BF16)
            mixed.append(matmul(weights, values[:count], NN))
        mixed = jnp.concatenate(mixed, axis=0)
        mixed = mixed[:, : 2 * head_dim] / mixed[:, 2 * head_dim :]
        result = mixed if result is None else jnp.where(masks[n], mixed, result)
    out_ref[...] = result.astype(out_ref.dtype)


def attend_whole(raw, scale_row, all_scale):
    tokens, width = raw.shape[0], raw.shape[1] // 3
    head_dim = width // all_scale.shape[0]
    lanes = 2 * head_dim
    pairs = width // lanes

    block = pl.BlockSpec((tokens, lanes), lambda n: (0, n))
    triple = pl.BlockSpec((tokens, 3 * lanes), lambda n: (0, n))
    return pl.pallas_call(
        functools.partial(attend_kernel, head_dim),
        out_shape=jax.ShapeDtypeStruct((tokens, width), BF16),
        grid=(pairs,),
        in_specs=[
            pl.BlockSpec(memory_space=pltpu.SMEM),
            pl.BlockSpec((1, tokens), lambda n: (0, 0)),
            pl.BlockSpec((tokens, 1), lambda n: (0, 0)),
            triple,
        ],
        out_specs=block,
        scratch_shapes=[pltpu.VMEM((tokens, tokens), F32)],
        cost_estimate=BRIEF,
        compiler_params=pltpu.CompilerParams(vmem_limit_bytes=16 * MIB),
    )(all_scale, scale_row[None, :], scale_row[:, None], raw)


def attend_back_kernel(
    head_dim,
    scale_ref,
    row_ref,
    column_ref,
    raw_ref,
    mixed_ref,
    d_mixed_ref,
    out_ref,
    term_ref,
    bias_ref,
):
    pair = pl.program_id(0)

    @pl.when(pair == 0)
    def _():
        bias_ref[...] = jnp.where(column_ref[...] <= row_ref[...], 0.0, HIDDEN)

    lanes = 2 * head_dim
    q, k = raw_ref[:, :lanes].astype(F32), raw_ref[:, lanes : 2 * lanes].astype(F32)
    v, d_mixed = raw_ref[:, 2 * lanes :], d_mixed_ref[...]
    masks = head_masks(q.shape, head_dim)
    k_units = [unit_of(k, mask) for mask in masks]
    k_hat = (k_units[0][0] + k_units[1][0]).astype(BF16)
    products = d_mixed.astype(F32) * mixed_ref[...].astype(F32)
    tokens = q.shape[0]
    blocks = [(slice(0, min(2 * MOST, tokens)), 0)]
    if tokens > 2 * MOST:
        blocks.append((slice(2 * MOST, tokens), MOST))
    d_q_all = d_k_all = d_v_all = None
    for n in range(2):
        mask = masks[n]
        scale = scale_ref[2 * pair + n]
        q_unit, q_inverse = unit_of(q, mask)
        q_hat = (q_unit * scale).astype(BF16)
        d_out = jnp.where(mask, d_mixed, jnp.zeros_like(d_mixed))
        offset = jnp.sum(jnp.where(mask, products, 0.0), axis=-1, keepdims=True)
        offset = jnp.transpose(jnp.broadcast_to(offset, products.shape))[:1]
        weights, total = [], 0.0
        for keys, first in blocks:
            scores = matmul(k_hat[keys], q_hat[first:], NT) + bias_ref[keys, first:]
            weights.append(jnp.exp(scores - jnp.abs(scale)))
            part = jnp.sum(weights[-1], axis=0, keepdims=True)
            total = part if first == 0 else jnp.concatenate(
                [total[:, :first], total[:, first:] + part], axis=1
            )
        share = 1.0 / total
        d_q, d_k, d_v = None, [], []
        for (keys, first), raised in zip(blocks, weights):
            probs = raised * share[:, first:]
            d_probs = matmul(v[keys], d_out[first:], NT)
            d_scores = (probs * (d_probs - offset[:, first:])).astype(BF16)
            d_v.append(matmul(probs.astype(BF16), d_out[first:], NN))
            d_k.append(matmul(d_scores, q_hat[first:], NN))
            part = matmul(d_scores, k_hat[keys], TN)
            d_q = part if first == 0 else jnp.concatenate(
                [d_q[:first], d_q[first:] + part], axis=0
            )
        d_v, d_k = jnp.concatenate(d_v, axis=0), jnp.concatenate(d_k, axis=0)
        d_q = jnp.where(mask, d_q, 0.0)
        d_k = jnp.where(mask, d_k, 0.0)
        k_unit, k_inverse = k_units[n]
        term = d_q * q_unit
        term_n = jnp.sum(term, axis=0, keepdims=True)
        d_q = q_inverse * scale * (d_q - q_unit * jnp.sum(term, axis=-1, keepdims=True))
        d_k = k_inverse * (d_k - k_unit * jnp.sum(d_k * k_unit, axis=-1, keepdims=True))
        if n == 0:
            d_q_all, d_k_all, d_v_all, term_all = d_q, d_k, d_v, term_n
        else:
            d_q_all, d_k_all = d_q_all + d_q, d_k_all + d_k
            d_v_all, term_all = d_v_all + d_v, term_all + term_n
    out_ref[:, :lanes] = d_q_all.astype(out_ref.dtype)
    out_ref[:, lanes : 2 * lanes] = d_k_all.astype(out_ref.dtype)
    out_ref[:, 2 * lanes :] = d_v_all.astype(out_ref.dtype)
    term_ref[...] = jnp.broadcast_to(term_all, term_ref.shape)


def attend_back_whole(raw, mixed, d_mixed, scale_row, all_scale):
    tokens, width = mixed.shape
    heads = all_scale.shape[0]
    head_dim = width // heads
    lanes = 2 * head_dim
    pairs = width // lanes

    block = pl.BlockSpec((tokens, lanes), lambda n: (0, n))
    triple = pl.BlockSpec((tokens, 3 * lanes), lambda n: (0, n))
    d_raw, terms = pl.pallas_call(
        functools.partial(attend_back_kernel, head_dim),
        out_shape=[
            jax.ShapeDtypeStruct((tokens, 3 * width), BF16),
            jax.ShapeDtypeStruct((8, width), F32),
        ],
        grid=(pairs,),
        in_specs=[
            pl.BlockSpec(memory_space=pltpu.SMEM),
            pl.BlockSpec((1, tokens), lambda n: (0, 0)),
            pl.BlockSpec((tokens, 1), lambda n: (0, 0)),
            triple,
            block,
            block,
        ],
        out_specs=[
            triple,
            pl.BlockSpec((8, lanes), lambda n: (0, n)),
        ],
        scratch_shapes=[pltpu.VMEM((tokens, tokens), F32)],
        cost_estimate=BRIEF,
        compiler_params=pltpu.CompilerParams(vmem_limit_bytes=20 * MIB),
    )(all_scale, scale_row[None, :], scale_row[:, None], raw, mixed, d_mixed)
    return d_raw, jnp.sum(terms[0].reshape(heads, head_dim), axis=1)


def gelu_and_slope(before):
    first = (2.0 / math.pi) ** 0.5
    square = before * before
    gate = 0.5 + 0.5 * jnp.tanh(before * (first + (first * 0.044715) * square))
    active = before * gate
    steep = 2.0 * first + (6.0 * first * 0.044715) * square
    return active, gate + active * (1.0 - gate) * steep


def activate_kernel(rows_ref, weights_ref, active_ref, slope_ref):
    for start in range(0, weights_ref.shape[1], 256):
        columns = slice(start, start + 256)
        active, slope = gelu_and_slope(matmul(rows_ref[...], weights_ref[:, columns], NN))
        active_ref[:, columns] = active.astype(active_ref.dtype)
        slope_ref[:, columns] = slope.astype(slope_ref.dtype)


def by_columns(kernel, rows, weights, count, tile):
    tokens, width = rows.shape
    columns = weights.shape[1]
    out = pl.BlockSpec((tokens, tile), lambda n: (0, n))
    return pl.pallas_call(
        kernel,
        out_shape=[jax.ShapeDtypeStruct((tokens, columns), BF16)] * count,
        grid=(columns // tile,),
        in_specs=[
            pl.BlockSpec((tokens, width), lambda n: (0, 0)),
            pl.BlockSpec((width, tile), lambda n: (0, n)),
        ],
        out_specs=[out] * count,
        cost_estimate=BRIEF,
        compiler_params=pltpu.CompilerParams(vmem_limit_bytes=20 * MIB),
    )(rows, weights)


def halves(values, c, half):
    keep = lax.dynamic_slice_in_dim(values, c * half, half, axis=1)
    give = lax.dynamic_slice_in_dim(values, (1 - c) * half, half, axis=1)
    return keep, give


def on_device_whole(
    inputs, labels, scale_ids, cotangent, table, w_ada, w_qkv, head_scale, w_proj, w_fc1, w_fc2
):
    width = inputs.shape[2]
    classes, rows = table.shape
    heads = TS * head_scale.shape[0]
    quarter = w_qkv.shape[2] // 2
    hidden_quarter = w_fc1.shape[1] // 2
    z, x, c, t = place()
    position = jnp.stack([z, x, c, t]).astype(jnp.int32)

    where = (z, x, c, t)

    pair = 2 * width // heads


    label_pair = jnp.stack(in_order(labels[0], labels[1], t)).astype(F32)
    label_tile = jnp.broadcast_to(label_pair[:, None], (2, 128))
    scale_tile = jnp.broadcast_to(head_scale[None, :], (8, head_scale.shape[0]))
    qkv_halves = []
    for side in (c, 1 - c):
        columns = [
            lax.dynamic_slice_in_dim(w_qkv[:, n].astype(BF16), side * quarter + j * pair, pair, 1)
            for j in range(quarter // pair)
            for n in range(3)
        ]
        qkv_halves.append(jnp.concatenate(columns, axis=1))
    keep_qkv, give_qkv, label_tile, scale_tile, inputs = hold(
        *qkv_halves, label_tile, scale_tile, inputs
    )
    recv_qkv, label_z = send(give_qkv, to_core), send_z(label_tile)
    scale_other = send(scale_tile, to_t)
    keep_qkv, recv_qkv, label_z, scale_other = hold(keep_qkv, recv_qkv, label_z, scale_other)
    two_qkv = jnp.stack([keep_qkv, recv_qkv])
    two_qkv, label_z, inputs, rest = hold(
        two_qkv,
        label_z,
        inputs,
        (cotangent, w_ada, w_proj, w_fc1, w_fc2, table, scale_ids),
    )
    cotangent, w_ada, w_proj, w_fc1, w_fc2, table, scale_ids = rest
    z_qkv = send_z(two_qkv)
    token_other = send(pick(inputs, 1 - t).astype(BF16), to_t)
    scale_row = pick(scale_ids, t)

    odd = z % 2 == 1
    first, third = jnp.where(odd, label_z[0], label_z[2]), jnp.where(odd, label_z[2], label_z[0])
    label_rows = jnp.concatenate([label_tile, first, label_z[1], third])
    label_rows = jnp.concatenate([label_rows, send(label_rows, to_x)])
    label_rows = jnp.concatenate([label_rows, send(label_rows, to_core)])
    all_labels = label_rows[:, 0].astype(jnp.int32)
    one_hot = (all_labels[:, None] == jnp.arange(classes)[None, :]).astype(BF16)
    condition = matmul(one_hot, table.astype(BF16), NN)
    silu_low = jax.nn.silu(condition).astype(BF16)
    ada_low = w_ada.astype(BF16).reshape(rows, 6 * width)
    silu_own = silu_low.reshape(-1, TS, rows)[:, 0]
    partial = matmul(silu_own, ada_low, NN).reshape(CS, XS, ZS, 6 * width)
    partial = partial[0] + send(partial[1], to_core)
    own_part, x_part = partial[0], send(partial[1], to_x)
    w_fc1, w_proj_t, w_fc2_t = w_fc1.astype(BF16), w_proj.astype(BF16).T, w_fc2.astype(BF16).T
    rest_halves = [halves(w_proj_t, c, quarter), halves(w_fc1, c, hidden_quarter)]
    rest_halves.append(halves(w_fc2_t, c, hidden_quarter))
    keep_rest, give_rest = [jnp.concatenate([part[n] for part in rest_halves], 1) for n in range(2)]
    split = quarter + hidden_quarter
    z_qkv, own_part, x_part, recv_rest = hold(
        z_qkv, own_part, x_part, send(give_rest, to_core)
    )

    four_qkv = jnp.stack([two_qkv] + z_qkv)
    partial = own_part + x_part
    two_mid = jnp.stack([keep_rest[:, :split], recv_rest[:, :split]])
    two_fc2 = jnp.stack([keep_rest[:, split:], recv_rest[:, split:]])
    four_qkv, partial, two_mid, two_fc2 = hold(four_qkv, partial, two_mid, two_fc2)
    near_qkv, far_qkv = send(four_qkv, to_t), send(four_qkv, to_x)
    mid_2 = send(two_mid, to_z(2))
    partial = partial[:2] + send(partial[2:], to_z_bit(2))
    mod_part, mod_bit = partial[0], send(partial[1], to_z_bit(1))
    cotangent_give = pick(cotangent, 1 - t).astype(BF16)
    near_qkv, far_qkv, mid_2, two_mid, cotangent_give, mod_part, mod_bit, token_other = hold(
        near_qkv, far_qkv, mid_2, two_mid, cotangent_give, mod_part, mod_bit, token_other
    )
    modulation = (mod_part + mod_bit).reshape(6, 1, width)
    gain_attn, gain_mlp, scale_attn, scale_mlp, shift_attn, shift_mlp = modulation
    tokens_in = join_image(inputs, token_other, t)
    last_qkv = send(near_qkv, to_x)
    mid_1, mid_3 = send(two_mid, to_z(1)), send(two_mid, to_z(3))
    cotangent_other = send(cotangent_give, to_t)
    normed_one, inverse_one = layer_norm(tokens_in)
    hidden_one = (normed_one * (1.0 + scale_attn) + shift_attn).astype(BF16)
    last_qkv, mid_1, mid_3, hidden_one, cotangent_other = hold(
        last_qkv, mid_1, mid_3, hidden_one, cotangent_other
    )
    scales = jnp.concatenate(in_order(head_scale, scale_other[0], t)).reshape(TS, 2, -1)
    scale_own, scale_oth = pick(scales, c, 1).reshape(-1), pick(scales, 1 - c, 1).reshape(-1)
    four_mid = jnp.stack([two_mid, mid_1, mid_2, mid_3])
    four_mid, last_qkv, two_fc2, hidden_one = hold(four_mid, last_qkv, two_fc2, hidden_one)
    near_mid, far_mid = send(four_mid, to_near), send(four_mid, to_far)
    z_fc2 = send_z(two_fc2)
    (qkv_own,) = assemble(
        [four_qkv, near_qkv, far_qkv, last_qkv], position, [3 * quarter], crossed=False
    )
    raw_own = matmul(hidden_one, qkv_own, NN).astype(BF16)
    raw_own, qkv_oth = hold(raw_own, send(qkv_own, to_core))
    raw_oth = matmul(hidden_one, qkv_oth, NN).astype(BF16)
    mixed_own = attend_whole(raw_own, scale_row, scale_own)
    mixed_own, near_mid, far_mid, z_fc2, raw_oth = hold(
        mixed_own, near_mid, far_mid, z_fc2, raw_oth
    )
    last_mid = send(near_mid, to_far)
    mixed_oth = attend_whole(raw_oth, scale_row, scale_oth)
    four_fc2 = jnp.stack([two_fc2] + z_fc2)
    mixed_oth, last_mid, four_fc2 = hold(mixed_oth, last_mid, four_fc2)
    near_fc2, far_fc2 = send(four_fc2, to_near), send(four_fc2, to_far)
    proj_own, fc1_own = assemble(
        [four_mid, near_mid, far_mid, last_mid], position, [quarter, hidden_quarter]
    )
    upstream = join_image(cotangent, cotangent_other, t)
    d_branch = (gain_mlp * upstream).astype(BF16)
    proj_oth, d_branch = hold(send(proj_own, to_core), d_branch)
    fc1_oth = send(fc1_own, to_core)
    attended = matmul(mixed_own, proj_own, NT) + matmul(mixed_oth, proj_oth, NT)
    middle = tokens_in + gain_attn * attended
    normed_two, inverse_two = layer_norm(middle)
    hidden_two = (normed_two * (1.0 + scale_mlp) + shift_mlp).astype(BF16)
    hidden_two, fc1_oth = hold(hidden_two, fc1_oth)

    def activate(weights):
        active, slope = gelu_and_slope(matmul(hidden_two, weights, NN))
        return active.astype(BF16), slope.astype(BF16)

    active_oth, slope_oth = by_columns(activate_kernel, hidden_two, fc1_oth, 2, 512)
    active_oth, slope_oth, near_fc2, far_fc2 = hold(active_oth, slope_oth, near_fc2, far_fc2)
    last_fc2 = send(near_fc2, to_far)
    active_own, slope_own = activate(fc1_own)
    given = products([(d_branch, active_oth)])
    given, active_own, slope_own = hold(given, active_own, slope_own)
    added = [send(part, to_core) for part in given]
    last_fc2, active_own = hold(last_fc2, active_own)
    (fc2_own,) = assemble([four_fc2, near_fc2, far_fc2, last_fc2], position, [hidden_quarter])
    fc2_own, active_own = hold(fc2_own, active_own)
    fc2_oth = send(fc2_own, to_core)
    blocks_fc2 = products([(d_branch, active_own)], added)
    blocks_fc2, fc2_oth = hold(blocks_fc2, fc2_oth)
    far_give, blocks_fc2, active_own = hold(scatter_far(blocks_fc2, where), blocks_fc2, active_own)
    far_fc2 = send(far_give, to_far)

    d_before_oth = (matmul(d_branch, fc2_oth, NN) * slope_oth.astype(F32)).astype(BF16)
    d_before_own = (matmul(d_branch, fc2_own, NN) * slope_own.astype(F32)).astype(BF16)
    given = products([(hidden_two, d_before_oth)])
    given, d_before_oth, d_before_own = hold(given, d_before_oth, d_before_own)
    added = [send(part, to_core) for part in given]
    d_hidden_two = matmul(d_before_own, fc1_own, NT) + matmul(d_before_oth, fc1_oth, NT)
    d_scale_mlp = jnp.sum(d_hidden_two * normed_two, axis=0)
    d_shift_mlp = jnp.sum(d_hidden_two, axis=0)
    d_middle = upstream + norm_back(d_hidden_two * (1.0 + scale_mlp), normed_two, inverse_two)
    d_gain_attn = jnp.sum(d_middle * attended, axis=0)
    d_attended = (gain_attn * d_middle).astype(BF16)
    d_attended, added = hold(d_attended, added)
    blocks_fc1 = products([(hidden_two, d_before_own)], added)
    far_give, blocks_fc1, d_attended, far_fc2 = hold(
        scatter_far(blocks_fc1, where), blocks_fc1, d_attended, far_fc2
    )
    near_fc2 = send(scatter_near(blocks_fc2, far_fc2, where), to_near)
    far_fc1 = send(far_give, to_far)
    given = products([(d_attended, mixed_oth)])
    given, d_attended = hold(given, d_attended)
    added = [send(part, to_core) for part in given]
    d_mixed_oth = matmul(d_attended, proj_oth, NN).astype(BF16)
    d_mixed_own = matmul(d_attended, proj_own, NN).astype(BF16)
    d_mixed_oth, d_mixed_own, added = hold(d_mixed_oth, d_mixed_own, added)
    blocks_proj = products([(d_attended, mixed_own)], added)
    blocks_proj, d_mixed_oth = hold(blocks_proj, d_mixed_oth)
    far_proj = send(scatter_far(blocks_proj, where), to_far)
    d_raw_oth, terms_oth = attend_back_whole(raw_oth, mixed_oth, d_mixed_oth, scale_row, scale_oth)
    given = products([(hidden_one, d_raw_oth)])
    given, near_fc2, d_mixed_own = hold(given, near_fc2, d_mixed_own)
    added = [send(part, to_core) for part in given]
    d_raw_own, terms_own = attend_back_whole(raw_own, mixed_own, d_mixed_own, scale_row, scale_own)
    d_raw_own, far_fc1, far_proj, added = hold(d_raw_own, far_fc1, far_proj, added)
    blocks_mid = blocks_proj + blocks_fc1
    far_mid = [jnp.concatenate([far_proj[n], far_fc1[n]], axis=1) for n in range(2)]
    near_give = scatter_near(blocks_mid, far_mid, where)
    z_fc2 = scatter_z(blocks_fc2, far_fc2, near_fc2, where)
    near_give, z_fc2, d_raw_own = hold(near_give, z_fc2, d_raw_own)
    near_mid = send(near_give, to_near)
    own_fc2, others_fc2 = z_fc2[0], send_terms_z(z_fc2[1:])
    blocks_qkv = products([(hidden_one, d_raw_own)], added)
    far_give, blocks_qkv, d_raw_own, d_raw_oth, active_own = hold(
        scatter_far(blocks_qkv, where), blocks_qkv, d_raw_own, d_raw_oth, active_own
    )
    far_qkv = send(far_give, to_far)
    d_hidden_one = matmul(d_raw_own, qkv_own, NT) + matmul(d_raw_oth, qkv_oth, NT)
    d_hidden_one, near_mid, others_fc2 = hold(d_hidden_one, near_mid, others_fc2)
    z_mid = scatter_z(blocks_mid, far_mid, near_mid, where)
    own_mid, others_mid = z_mid[0], send_terms_z(z_mid[1:])
    d_scale_attn = jnp.sum(d_hidden_one * normed_one, axis=0)
    d_shift_attn = jnp.sum(d_hidden_one, axis=0)
    d_inputs = d_middle + norm_back(d_hidden_one * (1.0 + scale_attn), normed_one, inverse_one)
    inputs_own, inputs_give = own_and_other(d_inputs, t)
    far_qkv, inputs_give, d_scale_attn = hold(far_qkv, inputs_give, d_scale_attn)
    near_give, active_own, inputs_give = hold(
        scatter_near(blocks_qkv, far_qkv, where), active_own, inputs_give
    )
    near_qkv = send(near_give, to_near)
    branch = matmul(active_own, fc2_own, NT) + matmul(active_oth, fc2_oth, NT)
    output_own, output_give = own_and_other(middle + gain_mlp * branch, t)
    d_gain_mlp = jnp.sum(upstream * branch, axis=0)
    d_modulation = jnp.concatenate(
        [d_gain_attn, d_gain_mlp, d_scale_attn, d_scale_mlp, d_shift_attn, d_shift_mlp]
    )
    terms = in_order(terms_own.reshape(TS, -1), terms_oth.reshape(TS, -1), c)
    scale_terms = jnp.concatenate(terms, axis=1).reshape(-1)
    scale_high = lax.reduce_precision(scale_terms, 8, 7)
    row = jnp.concatenate(
        [d_modulation, scale_high, scale_terms - scale_high, jnp.zeros((128 - 2 * heads,), F32)]
    ).astype(BF16)[None, :]
    mod_rows = jnp.concatenate([row, send(row, to_t)])
    near_qkv, mod_rows, others_mid = hold(near_qkv, mod_rows, others_mid)
    z_qkv = scatter_z(blocks_qkv, far_qkv, near_qkv, where)
    z_qkv, mod_rows, inputs_give, output_give = hold(z_qkv, mod_rows, inputs_give, output_give)
    own_qkv, others_qkv = z_qkv[0], send_terms_z(z_qkv[1:])
    mod_z = send_z(mod_rows)
    inputs_other, output_other = send(inputs_give, to_t), send(output_give, to_t)
    half_fc2, other_fc2 = scatter_total(own_fc2, others_fc2, where)
    half_mid, other_mid = scatter_total(own_mid, others_mid, where)
    other_rest = send(jnp.concatenate([other_mid, other_fc2], axis=1), to_core)
    first, third = jnp.where(odd, mod_z[0], mod_z[2]), jnp.where(odd, mod_z[2], mod_z[0])
    mod_rows = jnp.concatenate([mod_rows, first, mod_z[1], third])
    mod_x, inputs_other = hold(send(mod_rows, to_x), inputs_other)
    mod_rows = jnp.concatenate([mod_rows, mod_x])
    mod_rows = jnp.concatenate([mod_rows, send(mod_rows, to_core)])

    d_mod_all = mod_rows[:, : 6 * width]
    scale_sum = jnp.sum(mod_rows[:, 6 * width : 6 * width + 2 * heads].astype(F32), axis=0)
    scale_sum = (scale_sum[:heads] + scale_sum[heads:]).reshape(TS, heads // TS)
    grad_scale = pick(scale_sum, t)
    grad_ada = [
        matmul(silu_low, d_mod_all[:, n * width : (n + 1) * width], TN) for n in range(6)
    ]
    grad_ada = jnp.stack(grad_ada).transpose(1, 0, 2)
    d_silu = matmul(d_mod_all, ada_low, NT)
    _, silu_pull = jax.vjp(jax.nn.silu, condition)
    d_condition = silu_pull(d_silu)[0]
    grad_table = jnp.dot(one_hot.astype(F32).T, d_condition, precision=HIGHEST)

    def joined(own, other):
        return jnp.concatenate(in_order(own, other.astype(F32), c), axis=1)

    grad_proj = joined(half_mid[:, :quarter], other_rest[:, :quarter]).T
    grad_fc1 = joined(half_mid[:, quarter:], other_rest[:, quarter:split])
    grad_fc2 = joined(half_fc2, other_rest[:, split:]).T
    others_qkv, others = hold(
        others_qkv, (grad_ada, grad_table, grad_scale, inputs_other, grad_proj, grad_fc1, grad_fc2)
    )
    grad_ada, grad_table, grad_scale, inputs_other, grad_proj, grad_fc1, grad_fc2 = others
    half_qkv, other_qkv = scatter_total(own_qkv, others_qkv, where)
    other_qkv = send(other_qkv, to_core)

    def part_of(values, n):
        starts = range(n * pair, 3 * quarter, 3 * pair)
        return jnp.concatenate([values[:, start : start + pair] for start in starts], axis=1)

    grad_qkv = [joined(part_of(half_qkv, n), part_of(other_qkv, n)) for n in range(3)]
    return (
        two_images(output_own, output_other, t),
        two_images(inputs_own, inputs_other, t),
        grad_table,
        grad_ada,
        jnp.stack(grad_qkv, axis=1),
        grad_scale,
        grad_proj,
        grad_fc1,
        grad_fc2,
    )


def solution(mesh):
    placed = (
        P("dp", "tensor", None),
        P("dp"),
        P("dp", None),
        P("dp", "tensor", None),
        P(None, "dp"),
        P("dp", None, None),
        P("dp", None, "tensor"),
        P("tensor"),
        P("tensor", "dp"),
        P("dp", "tensor"),
        P("tensor", "dp"),
    )
    fitting = mesh.shape["dp"] == ZS * XS * CS and mesh.shape["tensor"] == TS

    def on_device(inputs, *others):
        fits = fitting and inputs.shape[0] == TS
        return (on_device_whole if fits else on_device_general)(inputs, *others)

    return jax.shard_map(
        on_device,
        mesh=mesh,
        in_specs=placed,
        out_specs=(
            P("dp", "tensor", None),
            P("dp", "tensor", None),
            P(None, "dp"),
            P("dp", None, None),
            P("dp", None, "tensor"),
            P("tensor"),
            P("tensor", "dp"),
            P("dp", "tensor"),
            P("tensor", "dp"),
        ),
        check_vma=False,
    )
```
